32 devices in a mesh: wide: 8 (over z, x), narrow: 4 (over y, core).
Axes of the slice: x: 2, y: 2, z: 4, core: 2. Of those that a mesh axis runs over, the one named last changes fastest.
Arguments:
- tokens_in: bfloat16 [8192, 2048], P(('wide', 'narrow')), may hold values from -6 to 6
- segment_starts: int32 [8192], P(('wide', 'narrow')), may hold values 0 or 1
- cotangent: bfloat16 [8192, 2048], P(('wide', 'narrow')), may hold values from -6 to 6
- norm1_gain: bfloat16 [2048], P(('wide', 'narrow')), may hold values from 0.25 to 1.75
- rec_gate_weight: bfloat16 [2048, 2560], P(('wide', 'narrow')), may hold values from -0.125 to 0.125
- rec_in_weight: bfloat16 [2048, 2560], P(('wide', 'narrow')), may hold values from -0.125 to 0.125
- conv_weight: bfloat16 [2560, 4], P(('wide', 'narrow')), may hold values from -3 to 3
- conv_bias: bfloat16 [2560], P(('wide', 'narrow')), may hold values from -3 to 3
- gate_a_weight: bfloat16 [2560, 160], P(('wide', 'narrow')), may hold values from -0.5 to 0.5
- gate_a_bias: bfloat16 [2560], P(('wide', 'narrow')), may hold values from -4 to 4
- gate_x_weight: bfloat16 [2560, 160], P(('wide', 'narrow')), may hold values from -0.5 to 0.5
- gate_x_bias: bfloat16 [2560], P(('wide', 'narrow')), may hold values from -4 to 4
- decay_rate: bfloat16 [2560], P(('wide', 'narrow')), may hold values from 7.772446e-05 to 0.049804688
- rec_out_weight: bfloat16 [2560, 2048], P(('wide', 'narrow')), may hold values from -0.125 to 0.125
- norm2_gain: bfloat16 [2048], P(('wide', 'narrow')), may hold values from 0.25 to 1.75
- mlp_gate_weight: bfloat16 [2048, 6144], P(('wide', 'narrow')), may hold values from -0.125 to 0.125
- mlp_up_weight: bfloat16 [2048, 6144], P(('wide', 'narrow')), may hold values from -0.125 to 0.125
- mlp_down_weight: bfloat16 [6144, 2048], P(('wide', 'narrow')), may hold values from -0.078125 to 0.078125
Outputs:
- layer_out: bfloat16 [8192, 2048], P(('wide', 'narrow'))
- grad_tokens: float32 [8192, 2048], P(('wide', 'narrow'))
- grad_norm1_gain: float32 [2048], P(('wide', 'narrow'))
- grad_rec_gate_weight: float32 [2048, 2560], P(('wide', 'narrow'))
- grad_rec_in_weight: float32 [2048, 2560], P(('wide', 'narrow'))
- grad_conv_weight: float32 [2560, 4], P(('wide', 'narrow'))
- grad_conv_bias: float32 [2560], P(('wide', 'narrow'))
- grad_gate_a_weight: float32 [2560, 160], P(('wide', 'narrow'))
- grad_gate_a_bias: float32 [2560], P(('wide', 'narrow'))
- grad_gate_x_weight: float32 [2560, 160], P(('wide', 'narrow'))
- grad_gate_x_bias: float32 [2560], P(('wide', 'narrow'))
- grad_decay_rate: float32 [2560], P(('wide', 'narrow'))
- grad_rec_out_weight: float32 [2560, 2048], P(('wide', 'narrow'))
- grad_norm2_gain: float32 [2048], P(('wide', 'narrow'))
- grad_mlp_gate_weight: float32 [2048, 6144], P(('wide', 'narrow'))
- grad_mlp_up_weight: float32 [2048, 6144], P(('wide', 'narrow'))
- grad_mlp_down_weight: float32 [6144, 2048], P(('wide', 'narrow'))
The draws below stay inside these ranges and needn't reach their ends.
Inputs may be any that keep to these rules, and one draw needn't show every extreme that they name: `segment_starts`: documents run on across the boundaries between devices.
All inputs are finite; a program needn't handle non-finite values.
Results may differ from the reference program's by a relative error of at most 0.011.
Values may be sent and summed in bfloat16 or wider, within the bound.
A program may use at most 512 MiB of HBM per device.

```python
import math
from functools import partial
import jax
import jax.numpy as jnp
from jax import lax

D = 2048
FF = 6144
NB = 16
BLK = 160
CONV = 4
TOK_DEV = 256
R = 2560
TOKENS = 8192


def with_ends(values, stream_key, least, top_value):
    longest = values.shape.index(max(values.shape))
    spots = []
    for shift in (0, 1):
        where = [jax.random.randint(jax.random.fold_in(stream_key, axis), (), 0, length) for axis, length in enumerate(values.shape)]
        where[longest] = (where[longest] + shift) % values.shape[longest]
        spots.append(tuple(where))
    return values.at[spots[0]].set(least).at[spots[1]].set(top_value)


def levels(stream_key, shape, cuts, smallest, top_value):
    loudness, own = 1.0, jax.random.fold_in(stream_key, 6)
    for dim, parts in cuts:
        heights = jnp.exp(jax.random.uniform(jax.random.fold_in(own, dim), (parts,), jnp.float32, smallest / len(cuts), top_value / len(cuts)))
        loudness = loudness * jnp.repeat(heights, shape[dim] // parts).reshape([-1 if axis == dim else 1 for axis in range(len(shape))])
    return loudness


def gaussian(own_key, extent, spread, bound, split=(), kind=jnp.bfloat16):
    loudness = levels(own_key, extent, split, -0.22, 0.18) if split else 1.0
    entries = jax.random.normal(own_key, extent, jnp.float32) * spread * loudness
    return jnp.minimum(jnp.maximum(entries, -bound), bound).astype(kind)


def setup_inputs(seed: int = 0) -> dict:
    splits = jax.random.split(jax.random.key(seed), 19)
    tokens_in = gaussian(splits[0], (TOKENS, D), 1.0, 6.0, ((0, 32),))
    segment_starts = with_ends((jax.random.randint(splits[1], (TOKENS,), 0, 4 * TOK_DEV) < 1).astype(jnp.int32), jax.random.fold_in(splits[1], 1), 0, 1)
    cotangent = gaussian(splits[2], (TOKENS, D), 1.0, 6.0, ((0, 32),))
    norm1_gain = jnp.clip(1.0 + 0.15 * jax.random.normal(splits[3], (D,), jnp.float32), 0.25, 1.75).astype(jnp.bfloat16)
    rec_gate_weight = gaussian(splits[4], (D, R), D ** -0.5, 0.125, ((0, 32),))
    rec_in_weight = gaussian(splits[5], (D, R), D ** -0.5, 0.125, ((0, 32),))
    conv_weight = gaussian(splits[6], (R, CONV), CONV ** -0.5, 3.0, ((0, 32),))
    conv_bias = gaussian(splits[7], (R,), 0.5, 3.0, ((0, 32),))
    gate_a_weight = gaussian(splits[8], (R, BLK), BLK ** -0.5, 0.5, ((0, 32),))
    gate_a_bias = gaussian(splits[9], (R,), 1.0, 4.0, ((0, 32),))
    gate_x_weight = gaussian(splits[10], (R, BLK), BLK ** -0.5, 0.5, ((0, 32),))
    gate_x_bias = gaussian(splits[11], (R,), 1.0, 4.0, ((0, 32),))
    decay_rate = jnp.clip(jnp.exp(math.log(0.049804688) - 6.46269442 * jax.random.uniform(splits[12], (R,), jnp.float32) ** levels(splits[12], (R,), ((0, 32),), -0.2, 0.2)), 7.772445678710938e-05, 0.049804688).astype(jnp.bfloat16)
    rec_out_weight = gaussian(splits[13], (R, D), R ** -0.5, 0.125, ((0, 32),))
    norm2_gain = jnp.clip(1.0 + 0.15 * jax.random.normal(splits[14], (D,), jnp.float32), 0.25, 1.75).astype(jnp.bfloat16)
    mlp_gate_weight = gaussian(splits[15], (D, FF), D ** -0.5, 0.125, ((0, 32),))
    mlp_up_weight = gaussian(splits[16], (D, FF), D ** -0.5, 0.125, ((0, 32),))
    mlp_down_weight = gaussian(splits[17], (FF, D), FF ** -0.5, 0.078125, ((0, 32),))
    return {"tokens_in": tokens_in, "segment_starts": segment_starts, "cotangent": cotangent, "norm1_gain": norm1_gain, "rec_gate_weight": rec_gate_weight, "rec_in_weight": rec_in_weight, "conv_weight": conv_weight, "conv_bias": conv_bias, "gate_a_weight": gate_a_weight, "gate_a_bias": gate_a_bias, "gate_x_weight": gate_x_weight, "gate_x_bias": gate_x_bias, "decay_rate": decay_rate, "rec_out_weight": rec_out_weight, "norm2_gain": norm2_gain, "mlp_gate_weight": mlp_gate_weight, "mlp_up_weight": mlp_up_weight, "mlp_down_weight": mlp_down_weight}


@jax.custom_vjp
def low(v):
    return lax.optimization_barrier(v.astype(jnp.bfloat16)).astype(jnp.float32)

@jax.custom_vjp
def low_back(v):
    return v

def low_keep(v):
    return (low(v), None)

def low_pass(kept, grad):
    return (grad,)

def back_keep(v):
    return (v, None)

def back_low(kept, grad):
    return (low(grad),)
low.defvjp(low_keep, low_pass)
low_back.defvjp(back_keep, back_low)
norm_eps = 1e-06
decay_scale = 8.0
push_shift = 0.05
highest = lax.Precision.HIGHEST

def rms_scale(tok_rows, gain):
    return tok_rows * lax.rsqrt(lax.optimization_barrier(jnp.mean(tok_rows * tok_rows, axis=-1, keepdims=True)) + norm_eps) * gain

def gelu_tanh(values):
    return jax.nn.gelu(values, approximate=True)

def combine_pairs(earlier, later):
    return (earlier[0] * later[0], later[0] * earlier[1] + later[1])

def conv_apply(extended, conv_taps, conv_offset, ids_ext, seg_block):
    row_total = seg_block.shape[0]
    tap_total = conv_taps.shape[1]
    summed = jnp.zeros((row_total, conv_taps.shape[0]), jnp.float32) + conv_offset
    for tap_index in range(tap_total):
        begin = tap_total - 1 - tap_index
        window = extended[begin:begin + row_total]
        same_doc = (ids_ext[begin:begin + row_total] == seg_block).astype(jnp.float32)
        summed = summed + conv_taps[:, tap_index] * window * same_doc[:, None]
    return summed

def gate_math(logit_a, logit_b, conved, rates, open_mask):
    gate_a = jax.nn.sigmoid(logit_a)
    gate_x = jax.nn.sigmoid(logit_b)
    decay = jnp.exp(-decay_scale * gate_a * rates)
    keep_all = decay * open_mask
    push_all = jnp.sqrt(1.0 - decay * decay + push_shift) * gate_x * conved
    return (keep_all, push_all)

def layer_block(weights, carry_in, pieces):
    gain_first, gate_whole, branch_whole, conv_taps, conv_offset, decay_whole, decay_bias, input_whole, input_bias, decay_rates, output_whole, gain_second, mlp_gate_whole, mlp_up_whole, mlp_down_whole = weights
    state_in, tail_rows, tail_ids = carry_in
    tok_rows, seg_block = pieces
    row_total = tok_rows.shape[0]
    tail_len = CONV - 1
    normed = low(rms_scale(tok_rows, gain_first))
    gate_pre = low_back(jnp.dot(normed, gate_whole, precision=highest))
    branch_in = low_back(low(jnp.dot(normed, branch_whole, precision=highest)))
    extended = jnp.concatenate([tail_rows, branch_in], axis=0)
    ids_ext = jnp.concatenate([tail_ids, seg_block])
    conved = low_back(low(conv_apply(extended, conv_taps, conv_offset, ids_ext, seg_block)))
    conved_blocks = conved.reshape(row_total, NB, BLK)
    logit_a = low_back(jnp.einsum('tnb,nbc->tnc', conved_blocks, decay_whole.reshape(NB, BLK, BLK), precision=highest).reshape(row_total, NB * BLK) + decay_bias)
    logit_b = low_back(jnp.einsum('tnb,nbc->tnc', conved_blocks, input_whole.reshape(NB, BLK, BLK), precision=highest).reshape(row_total, NB * BLK) + input_bias)
    open_mask = (ids_ext[tail_len - 1:tail_len - 1 + row_total] == seg_block).astype(jnp.float32)[:, None]
    keep_all, push_all = gate_math(logit_a, logit_b, conved, decay_rates, open_mask)
    keep_prod, local_state = lax.associative_scan(combine_pairs, (keep_all, push_all), axis=0)
    state_all = keep_prod * state_in + local_state
    mixed = low(state_all * gelu_tanh(gate_pre))
    middle = tok_rows + low_back(jnp.dot(mixed, output_whole, precision=highest))
    normed_two = low(rms_scale(middle, gain_second))
    mlp_gate = low_back(jnp.dot(normed_two, mlp_gate_whole, precision=highest))
    mlp_up = low_back(jnp.dot(normed_two, mlp_up_whole, precision=highest))
    hidden = low(gelu_tanh(mlp_gate) * mlp_up)
    result = middle + jnp.dot(hidden, mlp_down_whole, precision=highest)
    carry_out = (state_all[row_total - 1], branch_in[row_total - tail_len:], seg_block[row_total - tail_len:])
    return (carry_out, result)

def reference(tokens_in, segment_starts, cotangent, norm1_gain, rec_gate_weight, rec_in_weight, conv_weight, conv_bias, gate_a_weight, gate_a_bias, gate_x_weight, gate_x_bias, decay_rate, rec_out_weight, norm2_gain, mlp_gate_weight, mlp_up_weight, mlp_down_weight):
    block_rows = min(4096, TOKENS)
    width_rnn = NB * BLK
    seg_all = jnp.cumsum(segment_starts).astype(jnp.int32)
    seg_blocks = seg_all.reshape(-1, block_rows)
    weights_f = tuple((weight_arg.astype(jnp.float32) for weight_arg in (norm1_gain, rec_gate_weight, rec_in_weight, conv_weight, conv_bias, gate_a_weight, gate_a_bias, gate_x_weight, gate_x_bias, decay_rate, rec_out_weight, norm2_gain, mlp_gate_weight, mlp_up_weight, mlp_down_weight)))

    def layer_forward(tokens_f, weights):
        carry_init = (jnp.zeros((width_rnn,), jnp.float32), jnp.zeros((CONV - 1, width_rnn), jnp.float32), jnp.full((CONV - 1,), -1, jnp.int32))
        stepper = jax.checkpoint(partial(layer_block, weights))
        carry_end, results = lax.scan(stepper, carry_init, (tokens_f.reshape(-1, block_rows, D), seg_blocks))
        return results.reshape(TOKENS, D)
    layer_f, layer_back = jax.vjp(layer_forward, tokens_in.astype(jnp.float32), weights_f)
    grad_tokens, grads = layer_back(cotangent.astype(jnp.float32))
    return (layer_f.astype(jnp.bfloat16), grad_tokens, grads[0], grads[1], grads[2], grads[3], grads[4], grads[5], grads[6], grads[7], grads[8], grads[9], grads[10], grads[11], grads[12], grads[13], grads[14])
```

```python
import functools

import jax
import jax.numpy as jnp
from jax import lax
from jax.experimental import pallas as pl
from jax.experimental.pallas import tpu as pltpu
from jax.sharding import Mesh
from jax.sharding import PartitionSpec as P

BLK = 160
CONV = 4
TAIL = CONV - 1
LANES = 128
FEAT = ("x", "y", "c")
NF = 8

norm_eps = 1e-06
decay_scale = 8.0
push_shift = 0.05
f32 = jnp.float32
bf16 = jnp.bfloat16
MESH = pl.DeviceIdType.MESH
contract_last = (((1,), (1,)), ((), ()))
contract_first = (((0,), (0,)), ((), ()))
VMEM_LIMIT = 56 * 2**20


def cost(micros, flops=0):
    return pl.CostEstimate(
        flops=int(flops), bytes_accessed=int(micros * 3.0e6), transcendentals=0
    )


def hbm_spec():
    return pl.BlockSpec(memory_space=pl.ANY)


def vmem_spec():
    return pl.BlockSpec(memory_space=pltpu.VMEM)


def greet(peers):
    barrier = pltpu.get_barrier_semaphore()
    for device in peers:
        pl.semaphore_signal(barrier, inc=1, device_id=device, device_id_type=MESH)
    pl.semaphore_wait(barrier, len(peers))


def feature_place():
    return tuple(lax.axis_index(name) for name in FEAT)


def remote(src, dst, send_sem, recv_sem, device):
    return pltpu.make_async_remote_copy(
        src_ref=src,
        dst_ref=dst,
        send_sem=send_sem,
        recv_sem=recv_sem,
        device_id=device,
        device_id_type=MESH,
    )


def gather_kernel(x_ref, o_ref, local_sem, ssem, rsem):
    x, y, c = feature_place()
    mine = x * 4 + y * 2 + c
    from_x = (1 - x) * 4 + y * 2 + c
    from_y = x * 4 + (1 - y) * 2 + c
    from_d = (1 - x) * 4 + (1 - y) * 2 + c
    to_x, to_y, to_c = {"x": 1 - x}, {"y": 1 - y}, {"c": 1 - c}
    half = x_ref.shape[0] // 2
    top, low = pl.ds(0, half), pl.ds(half, half)
    greet((to_x, to_y, to_c))

    def copy(i, src, dst, device):
        return remote(src, dst, ssem.at[i], rsem.at[i], device)

    own = pltpu.make_async_copy(x_ref, o_ref.at[mine], local_sem)
    x_top = copy(0, x_ref.at[top], o_ref.at[mine, top], to_x)
    x_low = copy(1, x_ref.at[low], o_ref.at[mine, low], to_x)
    y_low = copy(2, x_ref.at[low], o_ref.at[mine, low], to_y)
    y_top = copy(3, x_ref.at[top], o_ref.at[mine, top], to_y)
    c_own = copy(4, x_ref, o_ref.at[mine], to_c)
    y_fwd = copy(5, o_ref.at[from_x, top], o_ref.at[from_x, top], to_y)
    x_fwd = copy(6, o_ref.at[from_y, low], o_ref.at[from_y, low], to_x)
    c_x = copy(7, o_ref.at[from_x], o_ref.at[from_x], to_c)
    c_y = copy(8, o_ref.at[from_y], o_ref.at[from_y], to_c)
    c_d = copy(9, o_ref.at[from_d], o_ref.at[from_d], to_c)
    for one in (x_top, y_low, x_low, y_top, c_own, own):
        one.start()
    x_top.wait_recv()
    y_fwd.start()
    y_low.wait_recv()
    x_fwd.start()
    x_low.wait_recv()
    c_x.start()
    y_top.wait_recv()
    c_y.start()
    y_fwd.wait_recv()
    x_fwd.wait_recv()
    c_d.start()
    for one in (c_own, c_x, c_y, c_d):
        one.wait_recv()
    for one in (x_top, x_low, y_low, y_top, c_own, y_fwd, x_fwd, c_x, c_y, c_d):
        one.wait_send()
    own.wait()


def gather_feature(block):
    rows, width = block.shape
    out = pl.pallas_call(
        gather_kernel,
        out_shape=jax.ShapeDtypeStruct((NF, rows, width), block.dtype),
        in_specs=[vmem_spec()],
        out_specs=hbm_spec(),
        scratch_shapes=[
            pltpu.SemaphoreType.DMA,
            pltpu.SemaphoreType.DMA((10,)),
            pltpu.SemaphoreType.DMA((10,)),
        ],
        compiler_params=pltpu.CompilerParams(
            collective_id=0, has_side_effects=True, vmem_limit_bytes=VMEM_LIMIT
        ),
        cost_estimate=cost(40),
        name="gather_feature",
    )(block)
    return out.reshape(NF * rows, width)


def scatter_kernel(
    p_ref, o_ref, own, other, total, rx, ry, relay, rx_last, ry_last, lsem, ssem, rsem
):
    x, y, c = feature_place()
    to_x, to_y, to_c = {"x": 1 - x}, {"y": 1 - y}, {"c": 1 - c}
    rows, width = o_ref.shape
    half = rows // 2
    top, low = pl.ds(0, half), pl.ds(half, half)
    step = 16
    chips = (
        x * 2 + y,
        (1 - x) * 2 + y,
        x * 2 + (1 - y),
        (1 - x) * 2 + (1 - y),
    )

    def copy(i, src, dst, device):
        return remote(src, dst, ssem.at[i], rsem.at[i], device)

    loads = [
        pltpu.make_async_copy(p_ref.at[chips[r] * 2 + c], own.at[r], lsem.at[r]) for r in range(4)
    ]
    for r in (3, 1, 2, 0):
        loads[r].start()
    greet((to_x, to_y, to_c))
    cross = [
        copy(r, p_ref.at[chips[r] * 2 + (1 - c)], other.at[r], to_c) for r in range(4)
    ]
    for r in (3, 1, 2, 0):
        cross[r].start()

    def add_into(r):
        loads[r].wait()
        cross[r].wait_recv()

        def body(i, none):
            at = pl.ds(pl.multiple_of(i * step, step), step)
            total[r, at] = (own[r, at].astype(f32) + other[r, at].astype(f32)).astype(total.dtype)
            return none

        lax.fori_loop(0, rows // step, body, 0)

    x_diag = copy(4, total.at[3, top], rx.at[1], to_x)
    y_diag = copy(5, total.at[3, low], ry.at[1], to_y)
    x_near = copy(6, total.at[1, top], rx.at[0], to_x)
    y_near = copy(7, total.at[2, low], ry.at[0], to_y)
    y_last = copy(8, relay.at[0], ry_last, to_y)
    x_last = copy(9, relay.at[1], rx_last, to_x)

    add_into(3)
    x_diag.start()
    y_diag.start()
    add_into(1)
    x_near.start()
    add_into(2)
    y_near.start()
    loads[0].wait()
    cross[0].wait_recv()

    def relay_add(slot, r, start, got):
        def body(i, none):
            at = pl.ds(pl.multiple_of(i * step, step), step)
            here = pl.ds(pl.multiple_of(start + i * step, step), step)
            relay[slot, at] = (total[r, here].astype(f32) + got[1, at].astype(f32)).astype(
                relay.dtype
            )
            return none

        lax.fori_loop(0, half // step, body, 0)

    x_diag.wait_recv()
    relay_add(0, 2, 0, rx)
    y_last.start()
    y_diag.wait_recv()
    relay_add(1, 1, half, ry)
    x_last.start()

    def finish(start, near, last):
        def body(i, none):
            at = pl.ds(pl.multiple_of(i * step, step), step)
            here = pl.ds(pl.multiple_of(start + i * step, step), step)
            o_ref[here] = (own[0, here].astype(f32) + other[0, here].astype(f32)) + (
                near[0, at].astype(f32) + last[at].astype(f32)
            )
            return none

        lax.fori_loop(0, half // step, body, 0)

    x_near.wait_recv()
    y_last.wait_recv()
    finish(0, rx, ry_last)
    y_near.wait_recv()
    x_last.wait_recv()
    finish(half, ry, rx_last)
    for one in cross + [x_diag, y_diag, x_near, y_near, x_last, y_last]:
        one.wait_send()


def scatter_feature(partial):
    rows, width = partial.shape[0] // NF, partial.shape[1]
    half = rows // 2
    kind = partial.dtype
    return pl.pallas_call(
        scatter_kernel,
        out_shape=jax.ShapeDtypeStruct((rows, width), f32),
        in_specs=[hbm_spec()],
        out_specs=vmem_spec(),
        scratch_shapes=[
            pltpu.VMEM((4, rows, width), kind),
            pltpu.VMEM((4, rows, width), kind),
            pltpu.VMEM((4, rows, width), kind),
            pltpu.VMEM((2, half, width), kind),
            pltpu.VMEM((2, half, width), kind),
            pltpu.VMEM((2, half, width), kind),
            pltpu.VMEM((half, width), kind),
            pltpu.VMEM((half, width), kind),
            pltpu.SemaphoreType.DMA((4,)),
            pltpu.SemaphoreType.DMA((10,)),
            pltpu.SemaphoreType.DMA((10,)),
        ],
        compiler_params=pltpu.CompilerParams(
            collective_id=1, has_side_effects=True, vmem_limit_bytes=VMEM_LIMIT
        ),
        cost_estimate=cost(45),
        name="scatter_feature",
    )(partial.reshape(NF, rows, width))


def exchange_kernel(axes, x_ref, o_ref, local_sem, ssem, rsem):
    place = [lax.axis_index(name) for name in axes]
    count = 2 ** len(axes)

    def rank(coords):
        total = 0
        for one in coords:
            total = total * 2 + one
        return total

    mine = rank(place)
    flips = []
    for mask in range(1, count):
        bits = [(mask // 2 ** (len(axes) - 1 - i)) % 2 for i in range(len(axes))]
        coords = [1 - p if bit else p for p, bit in zip(place, bits)]
        device = {name: q for name, q, bit in zip(axes, coords, bits) if bit}
        flips.append((rank(coords), device))
    own = pltpu.make_async_copy(x_ref.at[mine], o_ref.at[mine], local_sem)
    own.start()
    greet([device for _, device in flips])
    copies = [
        remote(x_ref.at[target], o_ref.at[mine], ssem.at[i], rsem.at[i], device)
        for i, (target, device) in enumerate(flips)
    ]
    for one in reversed(copies):
        one.start()
    for one in copies:
        one.wait()
    own.wait()


def exchange(blocks, axes, ident):
    count = 2 ** len(axes)
    return pl.pallas_call(
        functools.partial(exchange_kernel, axes),
        out_shape=jax.ShapeDtypeStruct(blocks.shape, blocks.dtype),
        in_specs=[vmem_spec()],
        out_specs=hbm_spec(),
        scratch_shapes=[
            pltpu.SemaphoreType.DMA,
            pltpu.SemaphoreType.DMA((count - 1,)),
            pltpu.SemaphoreType.DMA((count - 1,)),
        ],
        compiler_params=pltpu.CompilerParams(
            collective_id=ident, has_side_effects=True, vmem_limit_bytes=VMEM_LIMIT
        ),
        cost_estimate=cost(15),
        name="exchange",
    )(blocks)


def groups_kernel(count, x_ref, o_ref, local_sem, ssem, rsem):
    z = lax.axis_index("z")
    own = pltpu.make_async_copy(x_ref, o_ref.at[z], local_sem)
    own.start()
    targets = [{"z": lax.rem(z + hop, count)} for hop in range(1, count)]
    greet(targets)
    copies = [
        remote(x_ref, o_ref.at[z], ssem.at[i], rsem.at[i], device)
        for i, device in enumerate(targets)
    ]
    for one in copies:
        one.start()
    for one in copies:
        one.wait()
    own.wait()


def gather_groups(block, count, ident):
    return pl.pallas_call(
        functools.partial(groups_kernel, count),
        out_shape=jax.ShapeDtypeStruct((count,) + block.shape, block.dtype),
        in_specs=[vmem_spec()],
        out_specs=vmem_spec(),
        scratch_shapes=[
            pltpu.SemaphoreType.DMA,
            pltpu.SemaphoreType.DMA((count - 1,)),
            pltpu.SemaphoreType.DMA((count - 1,)),
        ],
        compiler_params=pltpu.CompilerParams(collective_id=ident, has_side_effects=True),
        cost_estimate=cost(5),
        name="gather_groups",
    )(block)


def gelu_tanh(values):
    return jax.nn.gelu(values, approximate=True)


def sigmoid(v):
    return 1.0 / (1.0 + jnp.exp(-v))


def gelu_pair(v):
    root = 0.7978845608028654
    cube = 0.044715
    square = v * v
    t = jnp.tanh(root * (v + cube * square * v))
    value = 0.5 * v * (1.0 + t)
    slope = 0.5 * (1.0 + t) + 0.5 * v * (1.0 - t * t) * root * (1.0 + 3.0 * cube * square)
    return value, slope


def tile_scan(keep, push, reverse):
    rows = lax.broadcasted_iota(jnp.int32, keep.shape, 0)
    count = keep.shape[0]
    hop = 1
    while hop < count:
        if reverse:
            inside = rows < count - hop
            shift = count - hop
        else:
            inside = rows >= hop
            shift = hop
        keep_near = jnp.where(inside, pltpu.roll(keep, shift, 0), 1.0)
        push_near = jnp.where(inside, pltpu.roll(push, shift, 0), 0.0)
        push = push + keep * push_near
        keep = keep * keep_near
        hop *= 2
    return keep, push


def conv_of(ext, masks, taps, offset, rows):
    value = offset + taps[0:1] * ext[pl.ds(8, rows)]
    for k in range(1, CONV):
        value = value + taps[k : k + 1] * ext[pl.ds(8 - k, rows)] * masks[:, k - 1 : k]
    return value


def forward_kernel(
    branch_ref,
    halo_ref,
    mask_ref,
    small_ref,
    wa_ref,
    wx_ref,
    conved_ref,
    keep_ref,
    prod_ref,
    state_ref,
    ext,
    carry,
):
    rows = branch_ref.shape[0]
    step = pl.program_id(0)

    @pl.when(step == 0)
    def _():
        ext[pl.ds(0, 8)] = halo_ref[...]
        carry[0:1] = jnp.ones_like(carry[0:1])
        carry[1:2] = jnp.zeros_like(carry[1:2])

    @pl.when(step > 0)
    def _():
        ext[pl.ds(0, 8)] = ext[pl.ds(rows, 8)]

    ext[pl.ds(8, rows)] = branch_ref[...].astype(f32)
    masks = mask_ref[...]
    conved = conv_of(ext, masks, small_ref, small_ref[4:5], rows).astype(bf16)
    conved_ref[...] = conved
    logit_a = jnp.dot(conved, wa_ref[...], preferred_element_type=f32) + small_ref[5:6]
    logit_x = jnp.dot(conved, wx_ref[...], preferred_element_type=f32) + small_ref[6:7]
    decay = jnp.exp(-decay_scale * sigmoid(logit_a) * small_ref[7:8])
    keep_ref[...] = decay * masks[:, 0:1]
    state_ref[...] = (
        jnp.sqrt(1.0 - decay * decay + push_shift) * sigmoid(logit_x) * conved.astype(f32)
    )

    def body(i, held):
        prod_in, state_in = held
        at = pl.ds(pl.multiple_of(i * 8, 8), 8)
        keep, push = tile_scan(keep_ref[at], state_ref[at], False)
        state = push + keep * state_in
        prod = keep * prod_in
        prod_ref[at] = prod
        state_ref[at] = state
        return prod[7:8], state[7:8]

    prod_out, state_out = lax.fori_loop(0, rows // 8, body, (carry[0:1], carry[1:2]))
    carry[0:1] = prod_out
    carry[1:2] = state_out


def forward_scan(branch_in, halo, masks, small, wa, wx, chunk):
    rows, width = branch_in.shape
    tile = pl.BlockSpec((chunk, width), lambda i: (i, 0))
    whole = lambda a: pl.BlockSpec(a.shape, lambda i: (0, 0))
    full = jax.ShapeDtypeStruct((rows, width), f32)
    return pl.pallas_call(
        forward_kernel,
        grid=(rows // chunk,),
        out_shape=(jax.ShapeDtypeStruct((rows, width), bf16), full, full, full),
        in_specs=[
            tile,
            whole(halo),
            pl.BlockSpec((chunk, masks.shape[1]), lambda i: (i, 0)),
            whole(small),
            whole(wa),
            whole(wx),
        ],
        out_specs=(tile, tile, tile, tile),
        scratch_shapes=[pltpu.VMEM((chunk + 8, width), f32), pltpu.VMEM((8, width), f32)],
        compiler_params=pltpu.CompilerParams(vmem_limit_bytes=VMEM_LIMIT),
        cost_estimate=cost(20),
        name="forward_scan",
    )(branch_in, halo, masks, small, wa, wx)


def adjoint_kernel(d_mixed_ref, gate_ref, keep_ref, prod_ref, adj_ref, keep_next, carry):
    rows = d_mixed_ref.shape[0]
    step = pl.program_id(0)

    @pl.when(step == 0)
    def _():
        keep_next[pl.ds(rows, 8)] = jnp.ones_like(keep_next[pl.ds(rows, 8)])
        carry[0:1] = jnp.ones_like(carry[0:1])
        carry[1:2] = jnp.zeros_like(carry[1:2])

    @pl.when(step > 0)
    def _():
        keep_next[pl.ds(rows, 8)] = keep_next[pl.ds(0, 8)]

    keep_next[pl.ds(0, rows)] = keep_ref[...]
    prod_ref[...] = keep_next[pl.ds(1, rows)]
    adj_ref[...] = d_mixed_ref[...] * gelu_tanh(gate_ref[...])
    tiles = rows // 8

    def body(i, held):
        prod_in, adj_in = held
        at = pl.ds(pl.multiple_of((tiles - 1 - i) * 8, 8), 8)
        keep, push = tile_scan(prod_ref[at], adj_ref[at], True)
        adj = push + keep * adj_in
        prod = keep * prod_in
        prod_ref[at] = prod
        adj_ref[at] = adj
        return prod[0:1], adj[0:1]

    prod_out, adj_out = lax.fori_loop(0, tiles, body, (carry[0:1], carry[1:2]))
    carry[0:1] = prod_out
    carry[1:2] = adj_out


def adjoint_scan(d_mixed, gate_pre, keep, chunk):
    rows, width = keep.shape
    last = rows // chunk - 1
    tile = pl.BlockSpec((chunk, width), lambda i: (last - i, 0))
    full = jax.ShapeDtypeStruct((rows, width), f32)
    return pl.pallas_call(
        adjoint_kernel,
        grid=(rows // chunk,),
        out_shape=(full, full),
        in_specs=[tile, tile, tile],
        out_specs=(tile, tile),
        scratch_shapes=[pltpu.VMEM((chunk + 8, width), f32), pltpu.VMEM((8, width), f32)],
        compiler_params=pltpu.CompilerParams(vmem_limit_bytes=VMEM_LIMIT),
        cost_estimate=cost(12),
        name="adjoint_scan",
    )(d_mixed, gate_pre, keep)


def backward_kernel(
    d_mixed_ref,
    gate_ref,
    state_ref,
    prod_ref,
    state_before_ref,
    prod_before_ref,
    adj_ref,
    adj_prod_ref,
    branch_ref,
    branch_before_ref,
    halo_ref,
    conved_ref,
    mask_ref,
    small_ref,
    enter_ref,
    wa_ref,
    wx_ref,
    d_gate_ref,
    d_branch_ref,
    sums_ref,
    edge_ref,
    ga_ref,
    gx_ref,
    ext,
    state_ext,
    later,
):
    rows, width = d_mixed_ref.shape
    step = pl.program_id(0)
    steps = pl.num_programs(0)
    state_in = enter_ref[0:1]
    adj_in = enter_ref[1:2]

    @pl.when(step == 0)
    def _():
        sums_ref[...] = jnp.zeros_like(sums_ref)
        ga_ref[...] = jnp.zeros_like(ga_ref)
        gx_ref[...] = jnp.zeros_like(gx_ref)
        for k in range(TAIL):
            later[k, pl.ds(rows, 8)] = jnp.zeros((8, width), f32)

    @pl.when(step > 0)
    def _():
        for k in range(TAIL):
            later[k, pl.ds(rows, 8)] = later[k, pl.ds(0, 8)]

    first = step == steps - 1

    @pl.when(first)
    def _():
        ext[pl.ds(0, 8)] = halo_ref[...]
        state_ext[pl.ds(0, 8)] = jnp.broadcast_to(state_in, (8, width))

    @pl.when(jnp.logical_not(first))
    def _():
        ext[pl.ds(0, 8)] = branch_before_ref[...].astype(f32)[8:16]
        state_ext[pl.ds(0, 8)] = state_before_ref[...] + prod_before_ref[...] * state_in

    ext[pl.ds(8, rows)] = branch_ref[...].astype(f32)
    state = state_ref[...] + prod_ref[...] * state_in
    state_ext[pl.ds(8, rows)] = state
    _, slope = gelu_pair(gate_ref[...])
    d_gate_ref[...] = (d_mixed_ref[...] * state * slope).astype(bf16)
    adjoint = adj_ref[...] + adj_prod_ref[...] * adj_in
    state_prev = state_ext[pl.ds(7, rows)]
    masks = mask_ref[...]
    conved_low = conved_ref[...]
    conved = conved_low.astype(f32)
    rates = small_ref[7:8]
    gate_a = sigmoid(
        jnp.dot(conved_low, wa_ref[...], preferred_element_type=f32) + small_ref[5:6]
    )
    gate_x = sigmoid(
        jnp.dot(conved_low, wx_ref[...], preferred_element_type=f32) + small_ref[6:7]
    )
    decay = jnp.exp(-decay_scale * gate_a * rates)
    root = jnp.sqrt(1.0 - decay * decay + push_shift)
    d_decay = adjoint * (state_prev * masks[:, 0:1] - gate_x * conved * decay / root)
    slope_a = -decay_scale * d_decay * decay * gate_a
    d_logit_a = (slope_a * rates * (1.0 - gate_a)).astype(bf16)
    through = adjoint * root * gate_x
    d_logit_x = (through * conved * (1.0 - gate_x)).astype(bf16)
    d_conved = (
        through
        + lax.dot_general(d_logit_a, wa_ref[...], contract_last, preferred_element_type=f32)
        + lax.dot_general(d_logit_x, wx_ref[...], contract_last, preferred_element_type=f32)
    )
    d_conved = d_conved.astype(bf16).astype(f32)
    ga_ref[...] += lax.dot_general(
        conved_low, d_logit_a, contract_first, preferred_element_type=f32
    )
    gx_ref[...] += lax.dot_general(
        conved_low, d_logit_x, contract_first, preferred_element_type=f32
    )

    def total(v):
        return jnp.sum(v, axis=0, keepdims=True)

    sums_ref[0:1] += total(d_conved * ext[pl.ds(8, rows)])
    for k in range(1, CONV):
        masked = d_conved * masks[:, k - 1 : k]
        later[k - 1, pl.ds(0, rows)] = masked
        sums_ref[k : k + 1] += total(masked * ext[pl.ds(8 - k, rows)])
    sums_ref[4:5] += total(d_conved)
    sums_ref[5:6] += total(d_logit_a.astype(f32))
    sums_ref[6:7] += total(d_logit_x.astype(f32))
    sums_ref[7:8] += total(slope_a)
    d_branch = small_ref[0:1] * d_conved
    for k in range(1, CONV):
        d_branch = d_branch + small_ref[k : k + 1] * later[k - 1, pl.ds(k, rows)]
    d_branch_ref[...] = d_branch.astype(bf16)

    @pl.when(first)
    def _():
        for back in range(1, CONV):
            value = jnp.zeros((1, width), f32)
            for k in range(back, CONV):
                value = value + small_ref[k : k + 1] * later[k - 1, pl.ds(k - back, 1)]
            edge_ref[8 - back : 9 - back] = value
        edge_ref[0 : 8 - TAIL] = jnp.zeros((8 - TAIL, width), f32)


def backward_scan(
    d_mixed, gate_pre, state, prod, adj, adj_prod, branch_in, halo, conved, masks, small, enter,
    wa, wx, chunk,
):
    rows, width = state.shape
    last = rows // chunk - 1
    tile = pl.BlockSpec((chunk, width), lambda i: (last - i, 0))

    def before(size):
        per = chunk // size
        return pl.BlockSpec((size, width), lambda i: (jnp.maximum((last - i) * per - 1, 0), 0))

    whole = lambda a: pl.BlockSpec(a.shape, lambda i: (0, 0))
    low = jax.ShapeDtypeStruct((rows, width), bf16)
    pinned = lambda shape: pl.BlockSpec(shape, lambda i: (0, 0))
    return pl.pallas_call(
        backward_kernel,
        grid=(rows // chunk,),
        out_shape=(
            low,
            low,
            jax.ShapeDtypeStruct((8, width), f32),
            jax.ShapeDtypeStruct((8, width), f32),
            jax.ShapeDtypeStruct((width, width), f32),
            jax.ShapeDtypeStruct((width, width), f32),
        ),
        in_specs=[
            tile,
            tile,
            tile,
            tile,
            before(8),
            before(8),
            tile,
            tile,
            tile,
            before(16),
            whole(halo),
            tile,
            pl.BlockSpec((chunk, masks.shape[1]), lambda i: (last - i, 0)),
            whole(small),
            whole(enter),
            whole(wa),
            whole(wx),
        ],
        out_specs=(
            tile,
            tile,
            pinned((8, width)),
            pinned((8, width)),
            pinned((width, width)),
            pinned((width, width)),
        ),
        scratch_shapes=[
            pltpu.VMEM((chunk + 8, width), f32),
            pltpu.VMEM((chunk + 8, width), f32),
            pltpu.VMEM((TAIL, chunk + 8, width), f32),
        ],
        compiler_params=pltpu.CompilerParams(vmem_limit_bytes=VMEM_LIMIT),
        cost_estimate=cost(25),
        name="backward_scan",
    )(
        d_mixed, gate_pre, state, prod, state, prod, adj, adj_prod, branch_in, branch_in, halo,
        conved, masks, small, enter, wa, wx,
    )


def pad_lanes(rows, width):
    have = rows.shape[-1]
    return jnp.pad(rows, ((0, 0), (0, width - have)))


def inverse_rms(rows):
    return lax.rsqrt(jnp.mean(rows * rows, axis=-1, keepdims=True) + norm_eps)


def norm_back(rows, scale, e):
    return scale * e - rows * (scale * scale * scale) * jnp.mean(e * rows, axis=-1, keepdims=True)


def on_device(
    tokens_in,
    segment_starts,
    cotangent,
    norm1_gain,
    rec_gate_weight,
    rec_in_weight,
    conv_weight,
    conv_bias,
    gate_a_weight,
    gate_a_bias,
    gate_x_weight,
    gate_x_bias,
    decay_rate,
    rec_out_weight,
    norm2_gain,
    mlp_gate_weight,
    mlp_up_weight,
    mlp_down_weight,
):
    count = lax.axis_size("z")
    z = lax.axis_index("z")
    spread = count // 2
    swap_axes = FEAT[len(FEAT) - (spread.bit_length() - 1) :]
    outer = NF // spread
    rows_tok, width = tokens_in.shape
    group_rows = NF * rows_tok
    chan_rows = conv_weight.shape[0]
    chans = chan_rows * count
    rows_w = rec_gate_weight.shape[0]
    ff_rows = mlp_down_weight.shape[0]
    ff = ff_rows * count
    chunk = 256

    def split_chan(w):
        return (
            w.reshape(rows_w, spread, 2, outer, BLK)
            .transpose(3, 1, 0, 2, 4)
            .reshape(NF, rows_w, chans)
        )

    def join_chan(w):
        return (
            w.reshape(outer, spread, rows_w, 2, BLK)
            .transpose(2, 1, 3, 0, 4)
            .reshape(rows_w, NF * chans)
        )

    def split_ff(w):
        return (
            w.reshape(rows_w, count, NF, ff_rows).transpose(2, 0, 1, 3).reshape(NF, rows_w, ff)
        )

    def join_ff(w):
        return (
            w.reshape(NF, rows_w, count, ff_rows).transpose(1, 2, 0, 3).reshape(rows_w, NF * ff)
        )

    pack = jnp.concatenate(
        [
            rec_out_weight,
            gate_a_weight,
            gate_x_weight,
            conv_weight,
            conv_bias[:, None],
            gate_a_bias[:, None],
            gate_x_bias[:, None],
            decay_rate[:, None],
        ],
        axis=1,
    )
    used = pack.shape[1]
    pack_width = -(-used // LANES) * LANES
    pack = pad_lanes(pack, pack_width)
    pack_all = lax.all_gather(pack, "z", axis=0, tiled=True)

    extra = jnp.concatenate(
        [
            pad_lanes(segment_starts.astype(bf16)[None], 2 * chans),
            pad_lanes(norm1_gain[None], 2 * chans),
            pad_lanes(norm2_gain[None], 2 * chans),
            jnp.zeros((13, 2 * chans), bf16),
        ],
        axis=0,
    )
    rec_send = jnp.concatenate(
        [
            jnp.concatenate(
                [split_chan(rec_gate_weight), split_chan(rec_in_weight)],
                axis=2,
            ),
            jnp.broadcast_to(extra[None], (NF, 16, 2 * chans)),
        ],
        axis=1,
    )
    rec_got = exchange(rec_send, FEAT, 3)
    w_rec = lax.all_gather(
        rec_got[:, :rows_w].reshape(NF * rows_w, 2 * chans), "z", axis=0, tiled=True
    )
    starts = rec_got[:, rows_w, :rows_tok].reshape(group_rows).astype(f32)

    plane_gains = jnp.stack(
        [
            rec_got[:, rows_w + 1, :rows_w].reshape(NF * rows_w),
            rec_got[:, rows_w + 2, :rows_w].reshape(NF * rows_w),
        ]
    ).astype(f32)
    gains = gather_groups(jnp.pad(plane_gains, ((0, 6), (0, 0))), count, 7)
    gain_one = gains[:, 0].reshape(1, width)
    gain_two = gains[:, 1].reshape(1, width)

    tok = tokens_in.astype(f32)
    tok_group = gather_feature(tokens_in).astype(f32)
    normed = (tok_group * inverse_rms(tok_group) * gain_one).astype(bf16)

    mlp_send = jnp.concatenate([split_ff(mlp_gate_weight), split_ff(mlp_up_weight)], axis=2)
    mlp_got = exchange(mlp_send, FEAT, 4)
    w_mlp = lax.all_gather(mlp_got.reshape(NF * rows_w, 2 * ff), "z", axis=0, tiled=True)
    w_down = lax.all_gather(mlp_down_weight, "z", axis=0, tiled=True)

    pack_swap = exchange(pack_all.reshape(spread, 2, chan_rows, pack_width), swap_axes, 5)
    mine = pack_swap.transpose(1, 0, 2, 3).reshape(chans, pack_width)
    w_out = mine[:, :width]
    small = mine[:, width + 2 * BLK : used].astype(f32).T

    unit = lax.broadcasted_iota(jnp.int32, (chans, chans), 0) // BLK
    same_block = unit == lax.broadcasted_iota(jnp.int32, (chans, chans), 1) // BLK

    def block_diag(w):
        return jnp.where(same_block, jnp.concatenate([w, w], axis=1), jnp.zeros((), w.dtype))

    wa = block_diag(mine[:, width : width + BLK])
    wx = block_diag(mine[:, width + BLK : width + 2 * BLK])

    open_one = 1.0 - starts
    ahead = jnp.concatenate([jnp.ones((TAIL,), f32), open_one])
    open_two = open_one * ahead[TAIL - 1 : TAIL - 1 + group_rows]
    open_three = open_two * ahead[TAIL - 2 : TAIL - 2 + group_rows]
    masks = jnp.stack([open_one, open_two, open_three], axis=1)
    end = open_one[group_rows - 2 :]
    later_open = jnp.stack([end[0] * end[1], end[1], jnp.ones((), f32)])[:, None]

    rec_pre = jnp.dot(normed, w_rec, preferred_element_type=f32)
    gate_pre = rec_pre[:, :chans]
    branch_in = rec_pre[:, chans:].astype(bf16)
    lane_pad = -(-chans // LANES) * LANES

    def over_groups(rows):
        total = rows.shape[0]
        block = jnp.pad(rows, ((8 - total, 0), (0, lane_pad - chans)))
        return gather_groups(block, count, 2)[:, 8 - total :, :chans]

    tails = over_groups(branch_in[group_rows - TAIL :].astype(f32) * later_open)
    before = lax.dynamic_index_in_dim(tails, jnp.maximum(z - 1, 0), 0, False)
    before = jnp.where(z > 0, before, 0.0)
    halo = jnp.pad(before, ((8 - TAIL, 0), (0, 0)))
    conved, keep, prod, state_local = forward_scan(branch_in, halo, masks, small, wa, wx, chunk)
    ends = over_groups(jnp.stack([prod[group_rows - 1], state_local[group_rows - 1]]))
    state_in = jnp.zeros((chans,), f32)
    for hop in range(count - 1):
        state_in = jnp.where(hop < z, ends[hop, 0] * state_in + ends[hop, 1], state_in)
    mixed = ((state_local + prod * state_in) * gelu_tanh(gate_pre)).astype(bf16)
    middle = tok + scatter_feature(jnp.dot(mixed, w_out, preferred_element_type=f32).astype(bf16))

    scale_two = inverse_rms(middle)
    normed_two = gather_feature((middle * scale_two * gain_two).astype(bf16))
    cot_own, normed_two = lax.optimization_barrier((cotangent, normed_two))
    cot = gather_feature(cot_own)
    mlp_pre = jnp.dot(normed_two, w_mlp, preferred_element_type=f32)
    d_hidden = lax.dot_general(cot, w_down, contract_last, preferred_element_type=f32)
    mlp_gate, mlp_up = mlp_pre[:, :ff], mlp_pre[:, ff:]
    act, slope = gelu_pair(mlp_gate)
    hidden = (act * mlp_up).astype(bf16)
    d_mlp = jnp.concatenate(
        [(d_hidden * mlp_up * slope).astype(bf16), (d_hidden * act).astype(bf16)], axis=1
    )
    down_part = lax.dot_general(
        hidden, cot, contract_first, preferred_element_type=f32
    ).astype(bf16)
    mlp_part = lax.dot_general(
        normed_two, d_mlp, contract_first, preferred_element_type=f32
    ).astype(bf16)
    d_mlp, down_part, mlp_part = lax.optimization_barrier((d_mlp, down_part, mlp_part))
    down_sum = lax.psum_scatter(down_part, "z", scatter_dimension=0, tiled=True)
    mlp_sum = lax.psum_scatter(mlp_part, "z", scatter_dimension=0, tiled=True)
    e_two = gain_two * scatter_feature(
        lax.dot_general(d_mlp, w_mlp, contract_last, preferred_element_type=f32).astype(bf16)
    )
    d_middle = cotangent.astype(f32) + norm_back(middle, scale_two, e_two)
    d_rec = gather_feature(d_middle.astype(bf16))

    d_mixed = lax.dot_general(d_rec, w_out, contract_last, preferred_element_type=f32)
    adj_prod, adj_local = adjoint_scan(d_mixed, gate_pre, keep, chunk)
    heads = over_groups(jnp.stack([keep[0] * adj_prod[0], keep[0] * adj_local[0]]))
    adj_in = jnp.zeros((chans,), f32)
    for hop in range(count - 1, 0, -1):
        adj_in = jnp.where(hop > z, heads[hop, 0] * adj_in + heads[hop, 1], adj_in)
    enter = jnp.pad(jnp.stack([state_in, adj_in]), ((0, 6), (0, 0)))
    d_gate, d_branch, sums, edge, grad_a, grad_x = backward_scan(
        d_mixed, gate_pre, state_local, prod, adj_local, adj_prod, branch_in, halo, conved, masks,
        small, enter, wa, wx, chunk,
    )
    edges = over_groups(edge[8 - TAIL :])
    after = lax.dynamic_index_in_dim(edges, jnp.minimum(z + 1, count - 1), 0, False)
    after = jnp.where(z < count - 1, after, 0.0) * later_open
    tail_sum = (d_branch[group_rows - TAIL :].astype(f32) + after).astype(bf16)
    d_branch = jnp.concatenate([d_branch[: group_rows - TAIL], tail_sum], axis=0)
    d_rec_pre = jnp.concatenate([d_gate, d_branch], axis=1)
    rec_part = lax.dot_general(
        normed, d_rec_pre, contract_first, preferred_element_type=f32
    ).astype(bf16)
    fold = (
        lax.broadcasted_iota(jnp.int32, (chans, BLK), 0) % BLK
        == lax.broadcasted_iota(jnp.int32, (chans, BLK), 1)
    ).astype(bf16)

    def diagonal(w):
        kept = jnp.where(same_block, w, 0.0).astype(bf16)
        return jnp.dot(kept, fold, preferred_element_type=f32).astype(bf16)

    grad_out = lax.dot_general(mixed, d_rec, contract_first, preferred_element_type=f32)
    back_pack = jnp.concatenate(
        [grad_out.astype(bf16), diagonal(grad_a), diagonal(grad_x), sums.T.astype(bf16)], axis=1
    )
    back_pack = pad_lanes(back_pack, pack_width)
    back_pack = back_pack.reshape(2, spread, chan_rows, pack_width).transpose(1, 0, 2, 3)
    back_swap = exchange(back_pack, swap_axes, 5).reshape(count * chan_rows, pack_width)
    d_rec_pre, rec_part, back_swap, hidden, mlp_sum, down_sum = lax.optimization_barrier(
        (d_rec_pre, rec_part, back_swap, hidden, mlp_sum, down_sum)
    )
    rec_sum = lax.psum_scatter(rec_part, "z", scatter_dimension=0, tiled=True)
    pack_sum = lax.psum_scatter(back_swap, "z", scatter_dimension=0, tiled=True).astype(f32)
    e_one = gain_one * scatter_feature(
        lax.dot_general(d_rec_pre, w_rec, contract_last, preferred_element_type=f32).astype(bf16)
    )
    grad_tokens = d_middle + norm_back(tok, inverse_rms(tok), e_one)
    layer_out = (
        middle
        + scatter_feature(jnp.dot(hidden, w_down, preferred_element_type=f32).astype(bf16))
    ).astype(bf16)

    mlp_back = exchange(mlp_sum.reshape(NF, rows_w, 2 * ff), FEAT, 4).astype(f32)
    grad_gate, grad_up = join_ff(mlp_back[:, :, :ff]), join_ff(mlp_back[:, :, ff:])
    rec_back = exchange(rec_sum.reshape(NF, rows_w, 2 * chans), FEAT, 6).astype(f32)
    grad_rec_gate = join_chan(rec_back[:, :, :chans])
    grad_rec_in = join_chan(rec_back[:, :, chans:])

    def gain_grad(gain, w_one, g_one, w_two, g_two):
        total = jnp.sum(w_one.astype(f32) * g_one + w_two.astype(f32) * g_two, axis=1)
        return total / gain.astype(f32)

    base = width + 2 * BLK
    return (
        layer_out,
        grad_tokens,
        gain_grad(norm1_gain, rec_gate_weight, grad_rec_gate, rec_in_weight, grad_rec_in),
        grad_rec_gate,
        grad_rec_in,
        pack_sum[:, base : base + CONV],
        pack_sum[:, base + CONV],
        pack_sum[:, width : width + BLK],
        pack_sum[:, base + CONV + 1],
        pack_sum[:, width + BLK : base],
        pack_sum[:, base + CONV + 2],
        pack_sum[:, base + CONV + 3],
        pack_sum[:, :width],
        gain_grad(norm2_gain, mlp_gate_weight, grad_gate, mlp_up_weight, grad_up),
        grad_gate,
        grad_up,
        down_sum.astype(f32),
    )


def solution(mesh):
    wide, narrow = mesh.shape["wide"], mesh.shape["narrow"]
    groups = wide * narrow // NF
    grid = Mesh(mesh.devices.reshape((groups,) + (2,) * len(FEAT)), ("z",) + FEAT)
    flat = P(("z",) + FEAT)
    wide_rows = P(("z",) + FEAT, None)
    one, two = flat, wide_rows
    return jax.shard_map(
        on_device,
        mesh=grid,
        in_specs=(
            two, one, two, one, two, two, two, one, two, one, two, one, one, two, one, two, two, two,
        ),
        out_specs=(
            two, two, one, two, two, two, one, two, one, two, one, one, two, one, two, two, two,
        ),
        check_vma=False,
    )
```

```python
import functools

import jax
import jax.numpy as jnp
from jax import lax
from jax.experimental import pallas as pl
from jax.experimental.pallas import tpu as pltpu
from jax.sharding import Mesh
from jax.sharding import PartitionSpec as P

BLK = 160
CONV = 4
TAIL = CONV - 1
LANES = 128
FEAT = ("x", "y", "c")
NF = 8
OWN, ACROSS_Y, ACROSS_X, DIAGONAL = 0, 1, 2, 3

norm_eps = 1e-06
decay_scale = 8.0
push_shift = 0.05
f32 = jnp.float32
bf16 = jnp.bfloat16
MESH = pl.DeviceIdType.MESH
contract_last = (((1,), (1,)), ((), ()))
contract_first = (((0,), (0,)), ((), ()))
VMEM_LIMIT = 56 * 2**20


def cost(micros, flops=0):
    return pl.CostEstimate(
        flops=int(flops), bytes_accessed=int(micros * 3.0e6), transcendentals=0
    )


def hbm_spec():
    return pl.BlockSpec(memory_space=pl.ANY)


def vmem_spec():
    return pl.BlockSpec(memory_space=pltpu.VMEM)


def greet(peers):
    barrier = pltpu.get_barrier_semaphore()
    for device in peers:
        pl.semaphore_signal(barrier, inc=1, device_id=device, device_id_type=MESH)
    pl.semaphore_wait(barrier, len(peers))


def feature_place():
    return tuple(lax.axis_index(name) for name in FEAT)


def remote(src, dst, send_sem, recv_sem, device):
    return pltpu.make_async_remote_copy(
        src_ref=src,
        dst_ref=dst,
        send_sem=send_sem,
        recv_sem=recv_sem,
        device_id=device,
        device_id_type=MESH,
    )


def gather_kernel(x_ref, o_ref, local_sem, ssem, rsem):
    x, y, c = feature_place()
    to_x, to_y, to_c = {"x": 1 - x}, {"y": 1 - y}, {"c": 1 - c}
    half = x_ref.shape[0] // 2
    top, low = pl.ds(0, half), pl.ds(half, half)
    greet((to_x, to_y, to_c))

    def copy(i, src, dst, device):
        return remote(src, dst, ssem.at[i], rsem.at[i], device)

    own = pltpu.make_async_copy(x_ref, o_ref.at[OWN], local_sem)
    x_top = copy(0, x_ref.at[top], o_ref.at[ACROSS_X, top], to_x)
    x_low = copy(1, x_ref.at[low], o_ref.at[ACROSS_X, low], to_x)
    y_low = copy(2, x_ref.at[low], o_ref.at[ACROSS_Y, low], to_y)
    y_top = copy(3, x_ref.at[top], o_ref.at[ACROSS_Y, top], to_y)
    c_own = copy(4, x_ref, o_ref.at[4 + OWN], to_c)
    y_fwd = copy(5, o_ref.at[ACROSS_X, top], o_ref.at[DIAGONAL, top], to_y)
    x_fwd = copy(6, o_ref.at[ACROSS_Y, low], o_ref.at[DIAGONAL, low], to_x)
    c_x = copy(7, o_ref.at[ACROSS_X], o_ref.at[4 + ACROSS_X], to_c)
    c_y = copy(8, o_ref.at[ACROSS_Y], o_ref.at[4 + ACROSS_Y], to_c)
    c_d = copy(9, o_ref.at[DIAGONAL], o_ref.at[4 + DIAGONAL], to_c)
    for one in (x_top, y_low, x_low, y_top, c_own, own):
        one.start()
    x_top.wait_recv()
    y_fwd.start()
    y_low.wait_recv()
    x_fwd.start()
    x_low.wait_recv()
    c_x.start()
    y_top.wait_recv()
    c_y.start()
    y_fwd.wait_recv()
    x_fwd.wait_recv()
    c_d.start()
    for one in (c_own, c_x, c_y, c_d):
        one.wait_recv()
    for one in (x_top, x_low, y_low, y_top, c_own, y_fwd, x_fwd, c_x, c_y, c_d):
        one.wait_send()
    own.wait()


def gather_feature(block):
    rows, width = block.shape
    out = pl.pallas_call(
        gather_kernel,
        out_shape=jax.ShapeDtypeStruct((NF, rows, width), block.dtype),
        in_specs=[vmem_spec()],
        out_specs=hbm_spec(),
        scratch_shapes=[
            pltpu.SemaphoreType.DMA,
            pltpu.SemaphoreType.DMA((10,)),
            pltpu.SemaphoreType.DMA((10,)),
        ],
        compiler_params=pltpu.CompilerParams(
            collective_id=0, has_side_effects=True, vmem_limit_bytes=VMEM_LIMIT
        ),
        cost_estimate=cost(40),
        name="gather_feature",
    )(block)
    return out.reshape(NF * rows, width)


def scatter_kernel(
    p_ref, o_ref, own, other, total, rx, ry, relay, rx_last, ry_last, lsem, ssem, rsem
):
    x, y, c = feature_place()
    to_x, to_y, to_c = {"x": 1 - x}, {"y": 1 - y}, {"c": 1 - c}
    rows, width = o_ref.shape
    half = rows // 2
    top, low = pl.ds(0, half), pl.ds(half, half)
    step = 16
    def copy(i, src, dst, device):
        return remote(src, dst, ssem.at[i], rsem.at[i], device)

    loads = [
        pltpu.make_async_copy(p_ref.at[r], own.at[r], lsem.at[r]) for r in range(4)
    ]
    for r in (DIAGONAL, ACROSS_X, ACROSS_Y, OWN):
        loads[r].start()
    greet((to_x, to_y, to_c))
    cross = [copy(r, p_ref.at[4 + r], other.at[r], to_c) for r in range(4)]
    for r in (DIAGONAL, ACROSS_X, ACROSS_Y, OWN):
        cross[r].start()

    def add_into(r):
        loads[r].wait()
        cross[r].wait_recv()

        def body(i, none):
            at = pl.ds(pl.multiple_of(i * step, step), step)
            total[r, at] = (own[r, at].astype(f32) + other[r, at].astype(f32)).astype(total.dtype)
            return none

        lax.fori_loop(0, rows // step, body, 0)

    x_diag = copy(4, total.at[DIAGONAL, top], rx.at[1], to_x)
    y_diag = copy(5, total.at[DIAGONAL, low], ry.at[1], to_y)
    x_near = copy(6, total.at[ACROSS_X, top], rx.at[0], to_x)
    y_near = copy(7, total.at[ACROSS_Y, low], ry.at[0], to_y)
    y_last = copy(8, relay.at[0], ry_last, to_y)
    x_last = copy(9, relay.at[1], rx_last, to_x)

    add_into(DIAGONAL)
    x_diag.start()
    y_diag.start()
    add_into(ACROSS_X)
    x_near.start()
    add_into(ACROSS_Y)
    y_near.start()
    loads[OWN].wait()
    cross[OWN].wait_recv()

    def relay_add(slot, r, start, got):
        def body(i, none):
            at = pl.ds(pl.multiple_of(i * step, step), step)
            here = pl.ds(pl.multiple_of(start + i * step, step), step)
            relay[slot, at] = (total[r, here].astype(f32) + got[1, at].astype(f32)).astype(
                relay.dtype
            )
            return none

        lax.fori_loop(0, half // step, body, 0)

    x_diag.wait_recv()
    relay_add(0, ACROSS_Y, 0, rx)
    y_last.start()
    y_diag.wait_recv()
    relay_add(1, ACROSS_X, half, ry)
    x_last.start()

    def finish(start, near, last):
        def body(i, none):
            at = pl.ds(pl.multiple_of(i * step, step), step)
            here = pl.ds(pl.multiple_of(start + i * step, step), step)
            o_ref[here] = (own[OWN, here].astype(f32) + other[OWN, here].astype(f32)) + (
                near[0, at].astype(f32) + last[at].astype(f32)
            )
            return none

        lax.fori_loop(0, half // step, body, 0)

    x_near.wait_recv()
    y_last.wait_recv()
    finish(0, rx, ry_last)
    y_near.wait_recv()
    x_last.wait_recv()
    finish(half, ry, rx_last)
    for one in cross + [x_diag, y_diag, x_near, y_near, x_last, y_last]:
        one.wait_send()


def scatter_feature(partial):
    rows, width = partial.shape[0] // NF, partial.shape[1]
    half = rows // 2
    kind = partial.dtype
    return pl.pallas_call(
        scatter_kernel,
        out_shape=jax.ShapeDtypeStruct((rows, width), f32),
        in_specs=[hbm_spec()],
        out_specs=vmem_spec(),
        scratch_shapes=[
            pltpu.VMEM((4, rows, width), kind),
            pltpu.VMEM((4, rows, width), kind),
            pltpu.VMEM((4, rows, width), kind),
            pltpu.VMEM((2, half, width), kind),
            pltpu.VMEM((2, half, width), kind),
            pltpu.VMEM((2, half, width), kind),
            pltpu.VMEM((half, width), kind),
            pltpu.VMEM((half, width), kind),
            pltpu.SemaphoreType.DMA((4,)),
            pltpu.SemaphoreType.DMA((10,)),
            pltpu.SemaphoreType.DMA((10,)),
        ],
        compiler_params=pltpu.CompilerParams(
            collective_id=1, has_side_effects=True, vmem_limit_bytes=VMEM_LIMIT
        ),
        cost_estimate=cost(45),
        name="scatter_feature",
    )(partial.reshape(NF, rows, width))


def across(value, axis):
    return lax.ppermute(value, axis, [(0, 1), (1, 0)])


def hold(*values):
    return lax.optimization_barrier(values)


def gather_near(block):
    return across(block, "x"), across(block, "y")


def gather_diagonal(by_x, by_y):
    half = by_x.shape[0] // 2
    return across(by_x[:half], "y"), across(by_y[half:], "x")


def gather_chip(block, by_x, by_y, d_top, d_low):
    return jnp.concatenate([block, by_y, by_x, d_top, d_low])


def scatter_near(mine, theirs_got):
    rows = mine.shape[0] // 4
    kind = theirs_got.dtype
    total = (mine.astype(f32) + theirs_got.astype(f32)).astype(kind)
    total = total.reshape(4, 2, rows // 2, mine.shape[1])
    by_x = across(total[2:, 0], "x")
    by_y = across(jnp.stack([total[ACROSS_Y, 1], total[DIAGONAL, 1]]), "y")
    return total, by_x, by_y


def scatter_relay(total, by_x, by_y):
    kind = total.dtype
    y_last = across((total[ACROSS_Y, 0].astype(f32) + by_x[1].astype(f32)).astype(kind), "y")
    x_last = across((total[ACROSS_X, 1].astype(f32) + by_y[1].astype(f32)).astype(kind), "x")
    return y_last, x_last


def scatter_sum(total, by_x, by_y, y_last, x_last):
    upper = total[OWN, 0].astype(f32) + by_x[0].astype(f32) + y_last.astype(f32)
    lower = total[OWN, 1].astype(f32) + by_y[0].astype(f32) + x_last.astype(f32)
    return jnp.concatenate([upper, lower])


def exchange_kernel(axes, x_ref, o_ref, local_sem, ssem, rsem):
    place = [lax.axis_index(name) for name in axes]
    count = 2 ** len(axes)

    def rank(coords):
        total = 0
        for one in coords:
            total = total * 2 + one
        return total

    mine = rank(place)
    flips = []
    for mask in range(1, count):
        bits = [(mask // 2 ** (len(axes) - 1 - i)) % 2 for i in range(len(axes))]
        coords = [1 - p if bit else p for p, bit in zip(place, bits)]
        device = {name: q for name, q, bit in zip(axes, coords, bits) if bit}
        flips.append((rank(coords), device))
    own = pltpu.make_async_copy(x_ref.at[mine], o_ref.at[mine], local_sem)
    own.start()
    greet([device for _, device in flips])
    copies = [
        remote(x_ref.at[target], o_ref.at[mine], ssem.at[i], rsem.at[i], device)
        for i, (target, device) in enumerate(flips)
    ]
    for one in reversed(copies):
        one.start()
    for one in copies:
        one.wait()
    own.wait()


def exchange(blocks, axes, ident):
    count = 2 ** len(axes)
    return pl.pallas_call(
        functools.partial(exchange_kernel, axes),
        out_shape=jax.ShapeDtypeStruct(blocks.shape, blocks.dtype),
        in_specs=[vmem_spec()],
        out_specs=hbm_spec(),
        scratch_shapes=[
            pltpu.SemaphoreType.DMA,
            pltpu.SemaphoreType.DMA((count - 1,)),
            pltpu.SemaphoreType.DMA((count - 1,)),
        ],
        compiler_params=pltpu.CompilerParams(
            collective_id=ident, has_side_effects=True, vmem_limit_bytes=VMEM_LIMIT
        ),
        cost_estimate=cost(15),
        name="exchange",
    )(blocks)


def groups_kernel(count, x_ref, o_ref, local_sem, ssem, rsem):
    z = lax.axis_index("z")
    own = pltpu.make_async_copy(x_ref, o_ref.at[z], local_sem)
    own.start()
    targets = [{"z": lax.rem(z + hop, count)} for hop in range(1, count)]
    greet(targets)
    copies = [
        remote(x_ref, o_ref.at[z], ssem.at[i], rsem.at[i], device)
        for i, device in enumerate(targets)
    ]
    for one in copies:
        one.start()
    for one in copies:
        one.wait()
    own.wait()


def gather_groups(block, count, ident):
    return pl.pallas_call(
        functools.partial(groups_kernel, count),
        out_shape=jax.ShapeDtypeStruct((count,) + block.shape, block.dtype),
        in_specs=[vmem_spec()],
        out_specs=vmem_spec(),
        scratch_shapes=[
            pltpu.SemaphoreType.DMA,
            pltpu.SemaphoreType.DMA((count - 1,)),
            pltpu.SemaphoreType.DMA((count - 1,)),
        ],
        compiler_params=pltpu.CompilerParams(collective_id=ident, has_side_effects=True),
        cost_estimate=cost(5),
        name="gather_groups",
    )(block)


def gelu_tanh(values):
    return jax.nn.gelu(values, approximate=True)


def sigmoid(v):
    return 1.0 / (1.0 + jnp.exp(-v))


def gelu_pair(v):
    root = 0.7978845608028654
    cube = 0.044715
    square = v * v
    t = jnp.tanh(root * (v + cube * square * v))
    value = 0.5 * v * (1.0 + t)
    slope = 0.5 * (1.0 + t) + 0.5 * v * (1.0 - t * t) * root * (1.0 + 3.0 * cube * square)
    return value, slope


def tile_scan(keep, push, reverse):
    rows = lax.broadcasted_iota(jnp.int32, keep.shape, 0)
    count = keep.shape[0]
    hop = 1
    while hop < count:
        if reverse:
            inside = rows < count - hop
            shift = count - hop
        else:
            inside = rows >= hop
            shift = hop
        keep_near = jnp.where(inside, pltpu.roll(keep, shift, 0), 1.0)
        push_near = jnp.where(inside, pltpu.roll(push, shift, 0), 0.0)
        push = push + keep * push_near
        keep = keep * keep_near
        hop *= 2
    return keep, push


def conv_of(ext, masks, taps, offset, rows):
    value = offset + taps[0:1] * ext[pl.ds(8, rows)]
    for k in range(1, CONV):
        value = value + taps[k : k + 1] * ext[pl.ds(8 - k, rows)] * masks[:, k - 1 : k]
    return value


def forward_kernel(
    order_ref,
    branch_ref,
    halo_ref,
    mask_ref,
    small_ref,
    wa_ref,
    wx_ref,
    conved_ref,
    keep_ref,
    prod_ref,
    state_ref,
    ends_ref,
    ext,
    carry,
):
    rows = branch_ref.shape[0]
    step = pl.program_id(0)

    @pl.when(step == 0)
    def _():
        ext[pl.ds(0, 8)] = halo_ref[...]
        carry[0:1] = jnp.ones_like(carry[0:1])
        carry[1:2] = jnp.zeros_like(carry[1:2])

    @pl.when(step > 0)
    def _():
        ext[pl.ds(0, 8)] = ext[pl.ds(rows, 8)]

    ext[pl.ds(8, rows)] = branch_ref[...].astype(f32)
    masks = mask_ref[...]
    conved = conv_of(ext, masks, small_ref, small_ref[4:5], rows).astype(bf16)
    conved_ref[...] = conved
    logit_a = jnp.dot(conved, wa_ref[...], preferred_element_type=f32) + small_ref[5:6]
    logit_x = jnp.dot(conved, wx_ref[...], preferred_element_type=f32) + small_ref[6:7]
    decay = jnp.exp(-decay_scale * sigmoid(logit_a) * small_ref[7:8])
    keep_ref[...] = decay * masks[:, 0:1]
    state_ref[...] = (
        jnp.sqrt(1.0 - decay * decay + push_shift) * sigmoid(logit_x) * conved.astype(f32)
    )

    def body(i, held):
        prod_in, state_in = held
        at = pl.ds(pl.multiple_of(i * 8, 8), 8)
        keep, push = tile_scan(keep_ref[at], state_ref[at], False)
        state = push + keep * state_in
        prod = keep * prod_in
        prod_ref[at] = prod
        state_ref[at] = state
        return prod[7:8], state[7:8]

    prod_out, state_out = lax.fori_loop(0, rows // 8, body, (carry[0:1], carry[1:2]))
    carry[0:1] = prod_out
    carry[1:2] = state_out
    ends_ref[0:1] = prod_out
    ends_ref[1:2] = state_out
    ends_ref[2:8] = jnp.zeros_like(ends_ref[2:8])


def forward_scan(order, branch_in, halo, masks, small, wa, wx, chunk):
    rows, width = branch_in.shape
    tile = pl.BlockSpec((chunk, width), lambda i, order: (order[i], 0))
    whole = lambda a: pl.BlockSpec(a.shape, lambda i, order: (0, 0))
    full = jax.ShapeDtypeStruct((rows, width), f32)
    return pl.pallas_call(
        forward_kernel,
        out_shape=(
            jax.ShapeDtypeStruct((rows, width), bf16),
            full,
            full,
            full,
            jax.ShapeDtypeStruct((8, width), f32),
        ),
        grid_spec=pltpu.PrefetchScalarGridSpec(
            num_scalar_prefetch=1,
            grid=(rows // chunk,),
            in_specs=[
                tile,
                whole(halo),
                pl.BlockSpec((chunk, masks.shape[1]), lambda i, order: (i, 0)),
                whole(small),
                whole(wa),
                whole(wx),
            ],
            out_specs=(tile, tile, tile, tile, pl.BlockSpec((8, width), lambda i, order: (0, 0))),
            scratch_shapes=[pltpu.VMEM((chunk + 8, width), f32), pltpu.VMEM((8, width), f32)],
        ),
        compiler_params=pltpu.CompilerParams(vmem_limit_bytes=VMEM_LIMIT),
        cost_estimate=cost(15),
        name="forward_scan",
    )(order, branch_in, halo, masks, small, wa, wx)


def adjoint_kernel(
    order_ref, d_mixed_ref, gate_ref, keep_ref, prod_ref, adj_ref, heads_ref, keep_next, carry
):
    rows = d_mixed_ref.shape[0]
    step = pl.program_id(0)

    @pl.when(step == 0)
    def _():
        keep_next[pl.ds(rows, 8)] = jnp.ones_like(keep_next[pl.ds(rows, 8)])
        carry[0:1] = jnp.ones_like(carry[0:1])
        carry[1:2] = jnp.zeros_like(carry[1:2])

    @pl.when(step > 0)
    def _():
        keep_next[pl.ds(rows, 8)] = keep_next[pl.ds(0, 8)]

    keep_next[pl.ds(0, rows)] = keep_ref[...]
    prod_ref[...] = keep_next[pl.ds(1, rows)]
    adj_ref[...] = d_mixed_ref[...] * gelu_tanh(gate_ref[...])
    tiles = rows // 8

    def body(i, held):
        prod_in, adj_in = held
        at = pl.ds(pl.multiple_of((tiles - 1 - i) * 8, 8), 8)
        keep, push = tile_scan(prod_ref[at], adj_ref[at], True)
        adj = push + keep * adj_in
        prod = keep * prod_in
        prod_ref[at] = prod
        adj_ref[at] = adj
        return prod[0:1], adj[0:1]

    prod_out, adj_out = lax.fori_loop(0, tiles, body, (carry[0:1], carry[1:2]))
    carry[0:1] = prod_out
    carry[1:2] = adj_out
    heads_ref[0:1] = keep_ref[0:1] * prod_out
    heads_ref[1:2] = keep_ref[0:1] * adj_out
    heads_ref[2:8] = jnp.zeros_like(heads_ref[2:8])


def adjoint_scan(order, d_mixed, gate_pre, keep, chunk):
    rows, width = keep.shape
    last = rows // chunk - 1
    tile = pl.BlockSpec((chunk, width), lambda i, order: (order[last - i], 0))
    full = jax.ShapeDtypeStruct((rows, width), f32)
    return pl.pallas_call(
        adjoint_kernel,
        out_shape=(full, full, jax.ShapeDtypeStruct((8, width), f32)),
        grid_spec=pltpu.PrefetchScalarGridSpec(
            num_scalar_prefetch=1,
            grid=(rows // chunk,),
            in_specs=[tile, tile, tile],
            out_specs=(tile, tile, pl.BlockSpec((8, width), lambda i, order: (0, 0))),
            scratch_shapes=[pltpu.VMEM((chunk + 8, width), f32), pltpu.VMEM((8, width), f32)],
        ),
        compiler_params=pltpu.CompilerParams(vmem_limit_bytes=VMEM_LIMIT),
        cost_estimate=cost(12),
        name="adjoint_scan",
    )(order, d_mixed, gate_pre, keep)


def backward_kernel(
    order_ref,
    d_mixed_ref,
    gate_ref,
    state_ref,
    prod_ref,
    state_before_ref,
    prod_before_ref,
    adj_ref,
    adj_prod_ref,
    branch_ref,
    branch_before_ref,
    halo_ref,
    conved_ref,
    mask_ref,
    small_ref,
    enter_ref,
    wa_ref,
    wx_ref,
    d_pre_ref,
    sums_ref,
    edge_ref,
    ga_ref,
    gx_ref,
    ext,
    state_ext,
    later,
):
    rows, width = d_mixed_ref.shape
    step = pl.program_id(0)
    steps = pl.num_programs(0)
    state_in = enter_ref[0:1]
    adj_in = enter_ref[1:2]

    @pl.when(step == 0)
    def _():
        sums_ref[...] = jnp.zeros_like(sums_ref)
        ga_ref[...] = jnp.zeros_like(ga_ref)
        gx_ref[...] = jnp.zeros_like(gx_ref)
        for k in range(TAIL):
            later[k, pl.ds(rows, 8)] = jnp.zeros((8, width), f32)

    @pl.when(step > 0)
    def _():
        for k in range(TAIL):
            later[k, pl.ds(rows, 8)] = later[k, pl.ds(0, 8)]

    first = step == steps - 1

    @pl.when(first)
    def _():
        ext[pl.ds(0, 8)] = halo_ref[...]
        state_ext[pl.ds(0, 8)] = jnp.broadcast_to(state_in, (8, width))

    @pl.when(jnp.logical_not(first))
    def _():
        ext[pl.ds(0, 8)] = branch_before_ref[...].astype(f32)[8:16]
        state_ext[pl.ds(0, 8)] = state_before_ref[...] + prod_before_ref[...] * state_in

    ext[pl.ds(8, rows)] = branch_ref[...].astype(f32)
    state = state_ref[...] + prod_ref[...] * state_in
    state_ext[pl.ds(8, rows)] = state
    _, slope = gelu_pair(gate_ref[...])
    d_pre_ref[:, 0:width] = (d_mixed_ref[...] * state * slope).astype(bf16)
    adjoint = adj_ref[...] + adj_prod_ref[...] * adj_in
    state_prev = state_ext[pl.ds(7, rows)]
    masks = mask_ref[...]
    conved_low = conved_ref[...]
    conved = conved_low.astype(f32)
    rates = small_ref[7:8]
    gate_a = sigmoid(
        jnp.dot(conved_low, wa_ref[...], preferred_element_type=f32) + small_ref[5:6]
    )
    gate_x = sigmoid(
        jnp.dot(conved_low, wx_ref[...], preferred_element_type=f32) + small_ref[6:7]
    )
    decay = jnp.exp(-decay_scale * gate_a * rates)
    root = jnp.sqrt(1.0 - decay * decay + push_shift)
    d_decay = adjoint * (state_prev * masks[:, 0:1] - gate_x * conved * decay / root)
    slope_a = -decay_scale * d_decay * decay * gate_a
    d_logit_a = (slope_a * rates * (1.0 - gate_a)).astype(bf16)
    through = adjoint * root * gate_x
    d_logit_x = (through * conved * (1.0 - gate_x)).astype(bf16)
    d_conved = (
        through
        + lax.dot_general(d_logit_a, wa_ref[...], contract_last, preferred_element_type=f32)
        + lax.dot_general(d_logit_x, wx_ref[...], contract_last, preferred_element_type=f32)
    )
    d_conved = d_conved.astype(bf16).astype(f32)
    ga_ref[...] += lax.dot_general(
        conved_low, d_logit_a, contract_first, preferred_element_type=f32
    )
    gx_ref[...] += lax.dot_general(
        conved_low, d_logit_x, contract_first, preferred_element_type=f32
    )

    def total(v):
        return jnp.sum(v, axis=0, keepdims=True)

    sums_ref[0:1] += total(d_conved * ext[pl.ds(8, rows)])
    for k in range(1, CONV):
        masked = d_conved * masks[:, k - 1 : k]
        later[k - 1, pl.ds(0, rows)] = masked
        sums_ref[k : k + 1] += total(masked * ext[pl.ds(8 - k, rows)])
    sums_ref[4:5] += total(d_conved)
    sums_ref[5:6] += total(d_logit_a.astype(f32))
    sums_ref[6:7] += total(d_logit_x.astype(f32))
    sums_ref[7:8] += total(slope_a)
    d_branch = small_ref[0:1] * d_conved
    for k in range(1, CONV):
        d_branch = d_branch + small_ref[k : k + 1] * later[k - 1, pl.ds(k, rows)]
    d_pre_ref[:, width : 2 * width] = d_branch.astype(bf16)

    @pl.when(first)
    def _():
        for back in range(1, CONV):
            value = jnp.zeros((1, width), f32)
            for k in range(back, CONV):
                value = value + small_ref[k : k + 1] * later[k - 1, pl.ds(k - back, 1)]
            edge_ref[8 - back : 9 - back] = value
        edge_ref[0 : 8 - TAIL] = jnp.zeros((8 - TAIL, width), f32)


def backward_scan(
    order, d_mixed, gate_pre, state, prod, adj, adj_prod, branch_in, halo, conved, masks, small,
    enter, wa, wx, chunk,
):
    rows, width = state.shape
    last = rows // chunk - 1
    tile = pl.BlockSpec((chunk, width), lambda i, order: (order[last - i], 0))

    def before(size):
        per = chunk // size
        return pl.BlockSpec(
            (size, width),
            lambda i, order: (order[jnp.maximum(last - i - 1, 0)] * per + per - 1, 0),
        )

    pinned = lambda shape: pl.BlockSpec(shape, lambda i, order: (0, 0))
    whole = lambda a: pinned(a.shape)
    return pl.pallas_call(
        backward_kernel,
        out_shape=(
            jax.ShapeDtypeStruct((rows, 2 * width), bf16),
            jax.ShapeDtypeStruct((8, width), f32),
            jax.ShapeDtypeStruct((8, width), f32),
            jax.ShapeDtypeStruct((width, width), f32),
            jax.ShapeDtypeStruct((width, width), f32),
        ),
        grid_spec=pltpu.PrefetchScalarGridSpec(
            num_scalar_prefetch=1,
            grid=(rows // chunk,),
            in_specs=[
                tile,
                tile,
                tile,
                tile,
                before(8),
                before(8),
                tile,
                tile,
                tile,
                before(16),
                whole(halo),
                tile,
                pl.BlockSpec((chunk, masks.shape[1]), lambda i, order: (last - i, 0)),
                whole(small),
                whole(enter),
                whole(wa),
                whole(wx),
            ],
            out_specs=(
                pl.BlockSpec((chunk, 2 * width), lambda i, order: (order[last - i], 0)),
                pinned((8, width)),
                pinned((8, width)),
                pinned((width, width)),
                pinned((width, width)),
            ),
            scratch_shapes=[
                pltpu.VMEM((chunk + 8, width), f32),
                pltpu.VMEM((chunk + 8, width), f32),
                pltpu.VMEM((TAIL, chunk + 8, width), f32),
            ],
        ),
        compiler_params=pltpu.CompilerParams(vmem_limit_bytes=VMEM_LIMIT),
        cost_estimate=cost(21),
        name="backward_scan",
    )(
        order, d_mixed, gate_pre, state, prod, state, prod, adj, adj_prod, branch_in, branch_in,
        halo, conved, masks, small, enter, wa, wx,
    )


def gated_kernel(n_ref, cot_ref, w_ref, down_ref, hidden_ref, d_ref):
    ff = down_ref.shape[0]
    tile = 256
    normed = n_ref[...]
    cot = cot_ref[...]

    def body(j, none):
        at = pl.ds(pl.multiple_of(j * tile, tile), tile)
        up_at = pl.ds(pl.multiple_of(ff + j * tile, tile), tile)
        gate = jnp.dot(normed, w_ref[:, at], preferred_element_type=f32)
        up = jnp.dot(normed, w_ref[:, up_at], preferred_element_type=f32)
        d_hidden = lax.dot_general(cot, down_ref[at], contract_last, preferred_element_type=f32)
        act, slope = gelu_pair(gate)
        hidden_ref[:, at] = (act * up).astype(bf16)
        d_ref[:, at] = (d_hidden * up * slope).astype(bf16)
        d_ref[:, up_at] = (d_hidden * act).astype(bf16)
        return none

    lax.fori_loop(0, ff // tile, body, 0)


def gated_unit(normed, cot, w_mlp, w_down):
    rows, width = normed.shape
    ff = w_down.shape[0]
    steps = 4
    tile = rows // steps
    row = lambda size: pl.BlockSpec((tile, size), lambda i: (i, 0))
    once = lambda a: pl.BlockSpec(a.shape, lambda i: (0, 0), pipeline_mode=pl.Buffered(1))
    return pl.pallas_call(
        gated_kernel,
        grid=(steps,),
        out_shape=(
            jax.ShapeDtypeStruct((rows, ff), bf16),
            jax.ShapeDtypeStruct((rows, 2 * ff), bf16),
        ),
        in_specs=[row(width), row(width), once(w_mlp), once(w_down)],
        out_specs=(row(ff), row(2 * ff)),
        compiler_params=pltpu.CompilerParams(vmem_limit_bytes=VMEM_LIMIT),
        cost_estimate=pl.CostEstimate(
            flops=6 * rows * width * ff, bytes_accessed=40 * 2**20, transcendentals=rows * ff
        ),
        name="gated_unit",
    )(normed, cot, w_mlp, w_down)


def split_kernel(moves, a_ref, b_ref, o_ref):
    for source, block, at, start, size in moves:
        ref = (a_ref, b_ref)[source]
        o_ref[block, :, at : at + size] = ref[:, start : start + size]


def join_kernel(moves, x_ref, a_ref, b_ref, g_ref, oa_ref, ob_ref, og_ref):
    for source, block, at, start, size in moves:
        ref = (oa_ref, ob_ref)[source]
        ref[:, start : start + size] = x_ref[block, :, at : at + size].astype(f32)
    total = jnp.sum(a_ref[...].astype(f32) * oa_ref[...], axis=1, keepdims=True) + jnp.sum(
        b_ref[...].astype(f32) * ob_ref[...], axis=1, keepdims=True
    )
    og_ref[...] = total / g_ref[...]


def split_blocks(a, b, moves):
    rows, width = a.shape
    return pl.pallas_call(
        functools.partial(split_kernel, moves),
        out_shape=jax.ShapeDtypeStruct((NF, rows, 2 * width // NF), a.dtype),
        compiler_params=pltpu.CompilerParams(vmem_limit_bytes=VMEM_LIMIT),
        cost_estimate=cost(4),
        name="split_blocks",
    )(a, b)


def join_blocks(x, a, b, gain, moves):
    rows, width = a.shape
    out = jax.ShapeDtypeStruct((rows, width), f32)
    return pl.pallas_call(
        functools.partial(join_kernel, moves),
        out_shape=(out, out, jax.ShapeDtypeStruct((rows, 1), f32)),
        compiler_params=pltpu.CompilerParams(vmem_limit_bytes=VMEM_LIMIT),
        cost_estimate=cost(5),
        name="join_blocks",
    )(x, a, b, gain)


def pad_lanes(rows, width):
    have = rows.shape[-1]
    return jnp.pad(rows, ((0, 0), (0, width - have)))


def inverse_rms(rows):
    return lax.rsqrt(jnp.mean(rows * rows, axis=-1, keepdims=True) + norm_eps)


def norm_back(rows, scale, e):
    return scale * e - rows * (scale * scale * scale) * jnp.mean(e * rows, axis=-1, keepdims=True)


def on_device(
    tokens_in,
    segment_starts,
    cotangent,
    norm1_gain,
    rec_gate_weight,
    rec_in_weight,
    conv_weight,
    conv_bias,
    gate_a_weight,
    gate_a_bias,
    gate_x_weight,
    gate_x_bias,
    decay_rate,
    rec_out_weight,
    norm2_gain,
    mlp_gate_weight,
    mlp_up_weight,
    mlp_down_weight,
):
    count = lax.axis_size("z")
    z = lax.axis_index("z")
    spread = count // 2
    swap_axes = FEAT[len(FEAT) - (spread.bit_length() - 1) :]
    outer = NF // spread
    rows_tok, width = tokens_in.shape
    group_rows = NF * rows_tok
    chan_rows = conv_weight.shape[0]
    chans = chan_rows * count
    rows_w = rec_gate_weight.shape[0]
    ff_rows = mlp_down_weight.shape[0]
    ff = ff_rows * count
    chunk = 256

    chan_moves = [
        (
            source,
            k * spread + e,
            source * chans + zz * BLK,
            ((2 * e + zz) * outer + k) * BLK,
            BLK,
        )
        for source in range(2)
        for k in range(outer)
        for e in range(spread)
        for zz in range(2)
    ]
    ff_moves = [
        (source, f, source * ff + group * ff_rows, (group * NF + f) * ff_rows, ff_rows)
        for source in range(2)
        for f in range(NF)
        for group in range(count)
    ]
    place = [lax.axis_index(name) for name in FEAT]
    time = jnp.arange(NF, dtype=jnp.int32)
    bit = lambda value, here: jnp.where(value == here, 0, 1)
    order = (
        bit(time % 2, place[2]) * 4 + bit(time // 4, place[0]) * 2 + bit((time // 2) % 2, place[1])
    ).astype(jnp.int32)
    final = order[NF - 1] * rows_tok + rows_tok - 8

    pack = jnp.concatenate(
        [
            rec_out_weight,
            gate_a_weight,
            gate_x_weight,
            conv_weight,
            conv_bias[:, None],
            gate_a_bias[:, None],
            gate_x_bias[:, None],
            decay_rate[:, None],
        ],
        axis=1,
    )
    used = pack.shape[1]
    pack_width = -(-used // LANES) * LANES
    pack = pad_lanes(pack, pack_width)

    extra = jnp.concatenate(
        [
            pad_lanes(segment_starts.astype(bf16)[None], 2 * chans),
            pad_lanes(norm1_gain[None], 2 * chans),
            pad_lanes(norm2_gain[None], 2 * chans),
            jnp.zeros((13, 2 * chans), bf16),
        ],
        axis=0,
    )
    rec_send = jnp.concatenate(
        [
            split_blocks(rec_gate_weight, rec_in_weight, chan_moves),
            jnp.broadcast_to(extra[None], (NF, 16, 2 * chans)),
        ],
        axis=1,
    )
    rec_send, pack = hold(rec_send, pack)
    pack_all = lax.all_gather(pack, "z", axis=0, tiled=True)
    rec_got = exchange(rec_send, FEAT, 3)
    w_rec = lax.all_gather(
        rec_got[:, :rows_w].reshape(NF * rows_w, 2 * chans), "z", axis=0, tiled=True
    )
    tokens_own, rec_got = hold(tokens_in, rec_got)
    tok_group = gather_feature(tokens_own)
    pack_swap = exchange(pack_all.reshape(spread, 2, chan_rows, pack_width), swap_axes, 5)
    starts = rec_got[:, rows_w, :rows_tok].reshape(group_rows).astype(f32)

    plane_gains = jnp.stack(
        [
            rec_got[:, rows_w + 1, :rows_w].reshape(NF * rows_w),
            rec_got[:, rows_w + 2, :rows_w].reshape(NF * rows_w),
        ]
    ).astype(f32)
    gains = gather_groups(jnp.pad(plane_gains, ((0, 6), (0, 0))), count, 7)
    gain_one = gains[:, 0].reshape(1, width)
    gain_two = gains[:, 1].reshape(1, width)

    tok = tokens_in.astype(f32)
    tok_group = tok_group.astype(f32)
    normed = (tok_group * inverse_rms(tok_group) * gain_one).astype(bf16)
    normed, pack_swap, mlp_gate_in = hold(normed, pack_swap, mlp_gate_weight)
    mlp_send = split_blocks(mlp_gate_in, mlp_up_weight, ff_moves)
    mlp_got = exchange(mlp_send, FEAT, 4)

    w_rec, down_in = hold(w_rec, mlp_down_weight)
    w_mlp = lax.all_gather(mlp_got.reshape(NF * rows_w, 2 * ff), "z", axis=0, tiled=True)
    w_down = lax.all_gather(down_in, "z", axis=0, tiled=True)

    mine = pack_swap.transpose(1, 0, 2, 3).reshape(chans, pack_width)
    w_out = mine[:, :width]
    small = mine[:, width + 2 * BLK : used].astype(f32).T

    unit = lax.broadcasted_iota(jnp.int32, (chans, chans), 0) // BLK
    same_block = unit == lax.broadcasted_iota(jnp.int32, (chans, chans), 1) // BLK

    def block_diag(w):
        return jnp.where(same_block, jnp.concatenate([w, w], axis=1), jnp.zeros((), w.dtype))

    wa = block_diag(mine[:, width : width + BLK])
    wx = block_diag(mine[:, width + BLK : width + 2 * BLK])

    open_one = 1.0 - starts
    ahead = jnp.concatenate([jnp.ones((TAIL,), f32), open_one])
    open_two = open_one * ahead[TAIL - 1 : TAIL - 1 + group_rows]
    open_three = open_two * ahead[TAIL - 2 : TAIL - 2 + group_rows]
    masks = jnp.stack([open_one, open_two, open_three], axis=1)
    end = open_one[group_rows - 2 :]
    later_open = jnp.concatenate(
        [jnp.zeros((8 - TAIL,), f32), (end[0] * end[1])[None], end[1:], jnp.ones((1,), f32)]
    )[:, None]

    rec_pre = jnp.dot(normed, w_rec, preferred_element_type=f32)
    rec_pre, cot_own = hold(rec_pre, cotangent)
    cot_x, cot_y = gather_near(cot_own)
    gate_pre = rec_pre[:, :chans]
    branch_in = rec_pre[:, chans:].astype(bf16)
    tails = gather_groups(
        lax.dynamic_slice_in_dim(branch_in, final, 8, 0).astype(f32) * later_open, count, 2
    )
    halo = jnp.where(z > 0, lax.dynamic_index_in_dim(tails, jnp.maximum(z - 1, 0), 0, False), 0.0)
    conved, keep, prod, state_local, ends = forward_scan(
        order, branch_in, halo, masks, small, wa, wx, chunk
    )
    ends, cot_x, cot_y = hold(ends, cot_x, cot_y)
    cot_top, cot_low = gather_diagonal(cot_x, cot_y)
    ends = gather_groups(ends, count, 2)
    state_in = jnp.zeros((1, chans), f32)
    for hop in range(count - 1):
        state_in = jnp.where(hop < z, ends[hop, 0:1] * state_in + ends[hop, 1:2], state_in)
    mixed = ((state_local + prod * state_in) * gelu_tanh(gate_pre)).astype(bf16)
    mixed_out = jnp.dot(mixed, w_out, preferred_element_type=f32).astype(bf16)
    mixed_out, cot_top, cot_low = hold(mixed_out, cot_top, cot_low)
    cot_chip = gather_chip(cotangent, cot_x, cot_y, cot_top, cot_low)
    cot = jnp.concatenate([cot_chip, across(cot_chip, "c")])
    middle = tok + scatter_feature(mixed_out)

    scale_two = inverse_rms(middle)
    normed_two = gather_feature((middle * scale_two * gain_two).astype(bf16))
    hidden, d_mlp = gated_unit(normed_two, cot, w_mlp, w_down)
    half_rows = group_rows // 2

    def back_rows(d, w):
        return lax.dot_general(d, w, contract_last, preferred_element_type=f32)

    e_theirs = back_rows(d_mlp[half_rows:], w_mlp).astype(bf16)
    e_got = across(e_theirs, "c")
    d_mlp, e_theirs = hold(d_mlp, e_theirs)
    e_mine = back_rows(d_mlp[:half_rows], w_mlp)
    e_total, e_x, e_y = scatter_near(e_mine, e_got)
    e_total, hidden = hold(e_total, hidden)
    down_part = lax.dot_general(
        hidden, cot, contract_first, preferred_element_type=f32
    ).astype(bf16)
    out_theirs = jnp.dot(hidden[half_rows:], w_down, preferred_element_type=f32).astype(bf16)
    down_part, e_x, e_y, hidden, out_theirs = hold(down_part, e_x, e_y, hidden, out_theirs)
    down_sum = lax.psum_scatter(down_part, "z", scatter_dimension=0, tiled=True)
    e_last = scatter_relay(e_total, e_x, e_y)
    out_mine = jnp.dot(hidden[:half_rows], w_down, preferred_element_type=f32).astype(bf16)
    out_mine, *e_last = hold(out_mine, *e_last)
    e_two = gain_two * scatter_sum(e_total, e_x, e_y, *e_last)
    d_middle = cotangent.astype(f32) + norm_back(middle, scale_two, e_two)
    d_own = d_middle.astype(bf16)
    d_x, d_y = gather_near(d_own)
    d_own, d_mlp, out_theirs = hold(d_own, d_mlp, out_theirs)
    mlp_part = lax.dot_general(
        normed_two, d_mlp, contract_first, preferred_element_type=f32
    ).astype(bf16)
    d_x, d_y, mlp_part, out_theirs = hold(d_x, d_y, mlp_part, out_theirs)
    mlp_sum = lax.psum_scatter(mlp_part, "z", scatter_dimension=0, tiled=True)
    d_top, d_low = gather_diagonal(d_x, d_y)
    out_got = across(out_theirs, "c")
    d_chip = gather_chip(d_own, d_x, d_y, d_top, d_low)
    d_rec = jnp.concatenate([d_chip, across(d_chip, "c")])
    d_rec, out_got = hold(d_rec, out_got)
    out_total, out_x, out_y = scatter_near(out_mine, out_got)

    d_mixed = lax.dot_general(d_rec, w_out, contract_last, preferred_element_type=f32)
    adj_prod, adj_local, heads = adjoint_scan(order, d_mixed, gate_pre, keep, chunk)
    heads, out_x, out_y = hold(heads, out_x, out_y)
    out_last = scatter_relay(out_total, out_x, out_y)
    heads = gather_groups(heads, count, 2)
    adj_in = jnp.zeros((1, chans), f32)
    for hop in range(count - 1, 0, -1):
        adj_in = jnp.where(hop > z, heads[hop, 0:1] * adj_in + heads[hop, 1:2], adj_in)
    enter = jnp.concatenate([state_in, adj_in, jnp.zeros((6, chans), f32)])
    d_rec_pre, sums, edge, grad_a, grad_x = backward_scan(
        order, d_mixed, gate_pre, state_local, prod, adj_local, adj_prod, branch_in, halo, conved,
        masks, small, enter, wa, wx, chunk,
    )
    edges = gather_groups(edge, count, 2)
    after = lax.dynamic_index_in_dim(edges, jnp.minimum(z + 1, count - 1), 0, False)
    after = jnp.where(z < count - 1, after, 0.0) * later_open
    tail_sum = lax.dynamic_slice_in_dim(d_rec_pre, final, 8, 0).astype(f32) + jnp.pad(
        after, ((0, 0), (chans, 0))
    )
    d_rec_pre = lax.dynamic_update_slice_in_dim(d_rec_pre, tail_sum.astype(bf16), final, 0)
    rec_part = lax.dot_general(
        normed, d_rec_pre, contract_first, preferred_element_type=f32
    ).astype(bf16)
    rec_part, d_rec_pre, grad_a, grad_x, sums, mixed, *out_last = hold(
        rec_part, d_rec_pre, grad_a, grad_x, sums, mixed, *out_last
    )
    layer_out = (middle + scatter_sum(out_total, out_x, out_y, *out_last)).astype(bf16)
    rec_part, mlp_sum, down_sum = hold(rec_part, mlp_sum, down_sum)
    rec_sum = lax.psum_scatter(rec_part, "z", scatter_dimension=0, tiled=True)
    one_theirs = back_rows(d_rec_pre[half_rows:], w_rec).astype(bf16)
    one_got = across(one_theirs, "c")
    d_rec_pre, one_theirs = hold(d_rec_pre, one_theirs)
    one_mine = back_rows(d_rec_pre[:half_rows], w_rec)
    one_total, one_x, one_y = scatter_near(one_mine, one_got)
    one_total, mixed, grad_a, grad_x = hold(one_total, mixed, grad_a, grad_x)
    fold = (
        lax.broadcasted_iota(jnp.int32, (chans, BLK), 0) % BLK
        == lax.broadcasted_iota(jnp.int32, (chans, BLK), 1)
    ).astype(bf16)

    def diagonal(w):
        kept = jnp.where(same_block, w, 0.0).astype(bf16)
        return jnp.dot(kept, fold, preferred_element_type=f32).astype(bf16)

    grad_out = lax.dot_general(mixed, d_rec, contract_first, preferred_element_type=f32)
    back_pack = jnp.concatenate(
        [grad_out.astype(bf16), diagonal(grad_a), diagonal(grad_x), sums.T.astype(bf16)], axis=1
    )
    back_pack = pad_lanes(back_pack, pack_width)
    back_pack = back_pack.reshape(2, spread, chan_rows, pack_width).transpose(1, 0, 2, 3)
    back_swap = exchange(back_pack, swap_axes, 5).reshape(count * chan_rows, pack_width)
    one_x, one_y, back_swap, rec_sum = hold(one_x, one_y, back_swap, rec_sum)
    pack_sum = lax.psum_scatter(back_swap, "z", scatter_dimension=0, tiled=True).astype(f32)
    one_last = scatter_relay(one_total, one_x, one_y)
    e_one = gain_one * scatter_sum(one_total, one_x, one_y, *one_last)
    grad_tokens = d_middle + norm_back(tok, inverse_rms(tok), e_one)

    mlp_sum, *one_last = hold(mlp_sum, *one_last)
    mlp_back = exchange(mlp_sum.reshape(NF, rows_w, 2 * ff), FEAT, 4)
    grad_gate, grad_up, grad_gain_two = join_blocks(
        mlp_back, mlp_gate_weight, mlp_up_weight, norm2_gain.astype(f32)[:, None], ff_moves
    )
    rec_back = exchange(rec_sum.reshape(NF, rows_w, 2 * chans), FEAT, 6)
    grad_rec_gate, grad_rec_in, grad_gain_one = join_blocks(
        rec_back, rec_gate_weight, rec_in_weight, norm1_gain.astype(f32)[:, None], chan_moves
    )

    base = width + 2 * BLK
    return (
        layer_out,
        grad_tokens,
        grad_gain_one[:, 0],
        grad_rec_gate,
        grad_rec_in,
        pack_sum[:, base : base + CONV],
        pack_sum[:, base + CONV],
        pack_sum[:, width : width + BLK],
        pack_sum[:, base + CONV + 1],
        pack_sum[:, width + BLK : base],
        pack_sum[:, base + CONV + 2],
        pack_sum[:, base + CONV + 3],
        pack_sum[:, :width],
        grad_gain_two[:, 0],
        grad_gate,
        grad_up,
        down_sum.astype(f32),
    )


def solution(mesh):
    wide, narrow = mesh.shape["wide"], mesh.shape["narrow"]
    groups = wide * narrow // NF
    grid = Mesh(mesh.devices.reshape((groups,) + (2,) * len(FEAT)), ("z",) + FEAT)
    flat = P(("z",) + FEAT)
    wide_rows = P(("z",) + FEAT, None)
    one, two = flat, wide_rows
    return jax.shard_map(
        on_device,
        mesh=grid,
        in_specs=(
            two, one, two, one, two, two, two, one, two, one, two, one, one, two, one, two, two, two,
        ),
        out_specs=(
            two, two, one, two, two, two, one, two, one, two, one, one, two, one, two, two, two,
        ),
        check_vma=False,
    )
```

```python
import functools

import jax
import jax.numpy as jnp
from jax import lax
from jax.experimental import pallas as pl
from jax.experimental.pallas import tpu as pltpu
from jax.sharding import Mesh
from jax.sharding import PartitionSpec as P

BLK = 160
CONV = 4
TAIL = CONV - 1
LANES = 128
FEAT = ("x", "y", "c")
NF = 8
OWN, ACROSS_Y, ACROSS_X, DIAGONAL = 0, 1, 2, 3

norm_eps = 1e-06
decay_scale = 8.0
push_shift = 0.05
f32 = jnp.float32
bf16 = jnp.bfloat16
MESH = pl.DeviceIdType.MESH
contract_last = (((1,), (1,)), ((), ()))
contract_first = (((0,), (0,)), ((), ()))
VMEM_LIMIT = 56 * 2**20


def cost(micros, flops=0):
    return pl.CostEstimate(
        flops=int(flops), bytes_accessed=int(micros * 3.0e6), transcendentals=0
    )


def hbm_spec():
    return pl.BlockSpec(memory_space=pl.ANY)


def vmem_spec():
    return pl.BlockSpec(memory_space=pltpu.VMEM)


def greet(peers):
    barrier = pltpu.get_barrier_semaphore()
    for device in peers:
        pl.semaphore_signal(barrier, inc=1, device_id=device, device_id_type=MESH)
    pl.semaphore_wait(barrier, len(peers))


def feature_place():
    return tuple(lax.axis_index(name) for name in FEAT)


def remote(src, dst, send_sem, recv_sem, device):
    return pltpu.make_async_remote_copy(
        src_ref=src,
        dst_ref=dst,
        send_sem=send_sem,
        recv_sem=recv_sem,
        device_id=device,
        device_id_type=MESH,
    )


def gather_kernel(*refs):
    if len(refs) == 5:
        x_ref, o_ref, local_sem, ssem, rsem = refs
        extra = ()
    else:
        x_ref, b_ref, o_ref, e_ref, local_sem, ssem, rsem, *sems = refs
        extra = exchange_parts(FEAT, b_ref, e_ref, *sems)
    x, y, c = feature_place()
    to_x, to_y, to_c = {"x": 1 - x}, {"y": 1 - y}, {"c": 1 - c}
    half = x_ref.shape[0] // 2
    top, low = pl.ds(0, half), pl.ds(half, half)
    greet(extra[0] if extra else (to_x, to_y, to_c))

    def copy(i, src, dst, device):
        return remote(src, dst, ssem.at[i], rsem.at[i], device)

    own = pltpu.make_async_copy(x_ref, o_ref.at[OWN], local_sem)
    x_top = copy(0, x_ref.at[top], o_ref.at[ACROSS_X, top], to_x)
    x_low = copy(1, x_ref.at[low], o_ref.at[ACROSS_X, low], to_x)
    y_low = copy(2, x_ref.at[low], o_ref.at[ACROSS_Y, low], to_y)
    y_top = copy(3, x_ref.at[top], o_ref.at[ACROSS_Y, top], to_y)
    c_own = copy(4, x_ref, o_ref.at[4 + OWN], to_c)
    y_fwd = copy(5, o_ref.at[ACROSS_X, top], o_ref.at[DIAGONAL, top], to_y)
    x_fwd = copy(6, o_ref.at[ACROSS_Y, low], o_ref.at[DIAGONAL, low], to_x)
    c_x = copy(7, o_ref.at[ACROSS_X], o_ref.at[4 + ACROSS_X], to_c)
    c_y = copy(8, o_ref.at[ACROSS_Y], o_ref.at[4 + ACROSS_Y], to_c)
    c_d = copy(9, o_ref.at[DIAGONAL], o_ref.at[4 + DIAGONAL], to_c)
    for one in (x_top, y_low, x_low, y_top, c_own, own):
        one.start()
    if extra:
        extra[1].start()
        for one in extra[2]:
            one.start()
    x_top.wait_recv()
    y_fwd.start()
    y_low.wait_recv()
    x_fwd.start()
    x_low.wait_recv()
    c_x.start()
    y_top.wait_recv()
    c_y.start()
    y_fwd.wait_recv()
    x_fwd.wait_recv()
    c_d.start()
    for one in (c_own, c_x, c_y, c_d):
        one.wait_recv()
    for one in (x_top, x_low, y_low, y_top, c_own, y_fwd, x_fwd, c_x, c_y, c_d):
        one.wait_send()
    own.wait()
    if extra:
        for one in extra[2]:
            one.wait()
        extra[1].wait()


def gather_feature(block):
    rows, width = block.shape
    out = pl.pallas_call(
        gather_kernel,
        out_shape=jax.ShapeDtypeStruct((NF, rows, width), block.dtype),
        in_specs=[vmem_spec()],
        out_specs=hbm_spec(),
        scratch_shapes=[
            pltpu.SemaphoreType.DMA,
            pltpu.SemaphoreType.DMA((10,)),
            pltpu.SemaphoreType.DMA((10,)),
        ],
        compiler_params=pltpu.CompilerParams(
            collective_id=0, has_side_effects=True, vmem_limit_bytes=VMEM_LIMIT
        ),
        cost_estimate=cost(40),
        name="gather_feature",
    )(block)
    return out.reshape(NF * rows, width)


def scatter_kernel(
    p_ref, o_ref, own, other, total, rx, ry, relay, rx_last, ry_last, lsem, ssem, rsem
):
    x, y, c = feature_place()
    to_x, to_y, to_c = {"x": 1 - x}, {"y": 1 - y}, {"c": 1 - c}
    rows, width = o_ref.shape
    half = rows // 2
    top, low = pl.ds(0, half), pl.ds(half, half)
    step = 16
    def copy(i, src, dst, device):
        return remote(src, dst, ssem.at[i], rsem.at[i], device)

    loads = [
        pltpu.make_async_copy(p_ref.at[r], own.at[r], lsem.at[r]) for r in range(4)
    ]
    for r in (DIAGONAL, ACROSS_X, ACROSS_Y, OWN):
        loads[r].start()
    greet((to_x, to_y, to_c))
    cross = [copy(r, p_ref.at[4 + r], other.at[r], to_c) for r in range(4)]
    for r in (DIAGONAL, ACROSS_X, ACROSS_Y, OWN):
        cross[r].start()

    def add_into(r):
        loads[r].wait()
        cross[r].wait_recv()

        def body(i, none):
            at = pl.ds(pl.multiple_of(i * step, step), step)
            total[r, at] = (own[r, at].astype(f32) + other[r, at].astype(f32)).astype(total.dtype)
            return none

        lax.fori_loop(0, rows // step, body, 0)

    x_diag = copy(4, total.at[DIAGONAL, top], rx.at[1], to_x)
    y_diag = copy(5, total.at[DIAGONAL, low], ry.at[1], to_y)
    x_near = copy(6, total.at[ACROSS_X, top], rx.at[0], to_x)
    y_near = copy(7, total.at[ACROSS_Y, low], ry.at[0], to_y)
    y_last = copy(8, relay.at[0], ry_last, to_y)
    x_last = copy(9, relay.at[1], rx_last, to_x)

    add_into(DIAGONAL)
    x_diag.start()
    y_diag.start()
    add_into(ACROSS_X)
    x_near.start()
    add_into(ACROSS_Y)
    y_near.start()
    loads[OWN].wait()
    cross[OWN].wait_recv()

    def relay_add(slot, r, start, got):
        def body(i, none):
            at = pl.ds(pl.multiple_of(i * step, step), step)
            here = pl.ds(pl.multiple_of(start + i * step, step), step)
            relay[slot, at] = (total[r, here].astype(f32) + got[1, at].astype(f32)).astype(
                relay.dtype
            )
            return none

        lax.fori_loop(0, half // step, body, 0)

    x_diag.wait_recv()
    relay_add(0, ACROSS_Y, 0, rx)
    y_last.start()
    y_diag.wait_recv()
    relay_add(1, ACROSS_X, half, ry)
    x_last.start()

    def finish(start, near, last):
        def body(i, none):
            at = pl.ds(pl.multiple_of(i * step, step), step)
            here = pl.ds(pl.multiple_of(start + i * step, step), step)
            o_ref[here] = (own[OWN, here].astype(f32) + other[OWN, here].astype(f32)) + (
                near[0, at].astype(f32) + last[at].astype(f32)
            )
            return none

        lax.fori_loop(0, half // step, body, 0)

    x_near.wait_recv()
    y_last.wait_recv()
    finish(0, rx, ry_last)
    y_near.wait_recv()
    x_last.wait_recv()
    finish(half, ry, rx_last)
    for one in cross + [x_diag, y_diag, x_near, y_near, x_last, y_last]:
        one.wait_send()


def scatter_feature(partial):
    rows, width = partial.shape[0] // NF, partial.shape[1]
    half = rows // 2
    kind = partial.dtype
    return pl.pallas_call(
        scatter_kernel,
        out_shape=jax.ShapeDtypeStruct((rows, width), f32),
        in_specs=[hbm_spec()],
        out_specs=vmem_spec(),
        scratch_shapes=[
            pltpu.VMEM((4, rows, width), kind),
            pltpu.VMEM((4, rows, width), kind),
            pltpu.VMEM((4, rows, width), kind),
            pltpu.VMEM((2, half, width), kind),
            pltpu.VMEM((2, half, width), kind),
            pltpu.VMEM((2, half, width), kind),
            pltpu.VMEM((half, width), kind),
            pltpu.VMEM((half, width), kind),
            pltpu.SemaphoreType.DMA((4,)),
            pltpu.SemaphoreType.DMA((10,)),
            pltpu.SemaphoreType.DMA((10,)),
        ],
        compiler_params=pltpu.CompilerParams(
            collective_id=1, has_side_effects=True, vmem_limit_bytes=VMEM_LIMIT
        ),
        cost_estimate=cost(45),
        name="scatter_feature",
    )(partial.reshape(NF, rows, width))


def across(value, axis):
    return lax.ppermute(value, axis, [(0, 1), (1, 0)])


def hold(*values):
    return lax.optimization_barrier(values)


def gather_near(block):
    return across(block, "x"), across(block, "y")


def gather_diagonal(by_x, by_y):
    half = by_x.shape[0] // 2
    return across(by_x[:half], "y"), across(by_y[half:], "x")


def gather_chip(block, by_x, by_y, d_top, d_low):
    return jnp.concatenate([block, by_y, by_x, d_top, d_low])


def scatter_total(mine, theirs_got):
    rows = mine.shape[0] // 4
    kind = theirs_got.dtype
    mine, theirs_got = hold(mine, theirs_got)
    total = (mine.astype(f32) + theirs_got.astype(f32)).astype(kind)
    return total.reshape(4, 2, rows // 2, mine.shape[1])


def scatter_sides(total):
    by_x = across(total[2:, 0], "x")
    by_y = across(jnp.stack([total[ACROSS_Y, 1], total[DIAGONAL, 1]]), "y")
    return by_x, by_y


def scatter_near(mine, theirs_got):
    total = scatter_total(mine, theirs_got)
    return (total,) + scatter_sides(total)


def scatter_relay(total, by_x, by_y):
    kind = total.dtype
    y_last = across((total[ACROSS_Y, 0].astype(f32) + by_x[1].astype(f32)).astype(kind), "y")
    x_last = across((total[ACROSS_X, 1].astype(f32) + by_y[1].astype(f32)).astype(kind), "x")
    return y_last, x_last


def scatter_sum(total, by_x, by_y, y_last, x_last):
    upper = total[OWN, 0].astype(f32) + by_x[0].astype(f32) + y_last.astype(f32)
    lower = total[OWN, 1].astype(f32) + by_y[0].astype(f32) + x_last.astype(f32)
    return jnp.concatenate([upper, lower])


def gather_tail_kernel(x_ref, bx_ref, by_ref, o_ref, lsem, ssem, rsem):
    x, y, c = feature_place()
    to_x, to_y, to_c = {"x": 1 - x}, {"y": 1 - y}, {"c": 1 - c}
    half = x_ref.shape[0] // 2
    top, low = pl.ds(0, half), pl.ds(half, half)

    def copy(i, src, dst, device):
        return remote(src, dst, ssem.at[i], rsem.at[i], device)

    places = ((x_ref, OWN), (by_ref, ACROSS_Y), (bx_ref, ACROSS_X))
    local = [
        pltpu.make_async_copy(ref, o_ref.at[slot], lsem.at[i])
        for i, (ref, slot) in enumerate(places)
    ]
    greet((to_x, to_y, to_c))
    y_fwd = copy(0, bx_ref.at[top], o_ref.at[DIAGONAL, top], to_y)
    x_fwd = copy(1, by_ref.at[low], o_ref.at[DIAGONAL, low], to_x)
    cross = [
        copy(2 + i, ref, o_ref.at[4 + slot], to_c) for i, (ref, slot) in enumerate(places)
    ]
    last = copy(5, o_ref.at[DIAGONAL], o_ref.at[4 + DIAGONAL], to_c)
    for one in [y_fwd, x_fwd] + cross + local:
        one.start()
    y_fwd.wait_recv()
    x_fwd.wait_recv()
    last.start()
    for one in cross + [last]:
        one.wait_recv()
    for one in cross + [y_fwd, x_fwd, last]:
        one.wait_send()
    for one in local:
        one.wait()


def gather_tail(block, by_x, by_y):
    rows, width = block.shape
    out = pl.pallas_call(
        gather_tail_kernel,
        out_shape=jax.ShapeDtypeStruct((NF, rows, width), block.dtype),
        in_specs=[vmem_spec()] * 3,
        out_specs=hbm_spec(),
        scratch_shapes=[
            pltpu.SemaphoreType.DMA((3,)),
            pltpu.SemaphoreType.DMA((6,)),
            pltpu.SemaphoreType.DMA((6,)),
        ],
        compiler_params=pltpu.CompilerParams(
            collective_id=8, has_side_effects=True, vmem_limit_bytes=VMEM_LIMIT
        ),
        cost_estimate=cost(16),
        name="gather_tail",
    )(block, by_x, by_y)
    return out.reshape(NF * rows, width)


def scatter_tail_kernel(
    t_ref, bx_ref, by_ref, o_ref, near, own, bx, by, relay, last, lsem, ssem, rsem
):
    x, y, c = feature_place()
    to_x, to_y = {"x": 1 - x}, {"y": 1 - y}
    half = o_ref.shape[0] // 2
    step = 16

    def load(i, src, dst):
        one = pltpu.make_async_copy(src, dst, lsem.at[i])
        one.start()
        return one

    loads = [
        load(0, t_ref.at[ACROSS_Y, 0], near.at[0]),
        load(1, bx_ref, bx),
        load(2, t_ref.at[ACROSS_X, 1], near.at[1]),
        load(3, by_ref, by),
        load(4, t_ref.at[OWN], own),
    ]
    greet((to_x, to_y))
    sends = [
        remote(relay.at[0], last.at[0], ssem.at[0], rsem.at[0], to_y),
        remote(relay.at[1], last.at[1], ssem.at[1], rsem.at[1], to_x),
    ]

    def tiles(body):
        def one(i, none):
            body(pl.ds(pl.multiple_of(i * step, step), step), i * step)
            return none

        lax.fori_loop(0, half // step, one, 0)

    for side, got in ((0, bx), (1, by)):
        loads[2 * side].wait()
        loads[2 * side + 1].wait()

        def add(at, _, side=side, got=got):
            relay[side, at] = (near[side, at].astype(f32) + got[1, at].astype(f32)).astype(
                relay.dtype
            )

        tiles(add)
        sends[side].start()
    loads[4].wait()
    for side, got in ((0, bx), (1, by)):

        def base(at, start, side=side, got=got):
            here = pl.ds(pl.multiple_of(side * half + start, step), step)
            o_ref[here] = own[side, at].astype(f32) + got[0, at].astype(f32)

        tiles(base)
    for side in range(2):
        sends[side].wait_recv()

        def finish(at, start, side=side):
            here = pl.ds(pl.multiple_of(side * half + start, step), step)
            o_ref[here] = o_ref[here] + last[side, at].astype(f32)

        tiles(finish)
    for one in sends:
        one.wait_send()


def scatter_tail(total, by_x, by_y):
    half, width = total.shape[2:]
    kind = total.dtype
    pair = pltpu.VMEM((2, half, width), kind)
    return pl.pallas_call(
        scatter_tail_kernel,
        out_shape=jax.ShapeDtypeStruct((2 * half, width), f32),
        in_specs=[hbm_spec()] * 3,
        out_specs=vmem_spec(),
        scratch_shapes=[pair] * 6
        + [
            pltpu.SemaphoreType.DMA((5,)),
            pltpu.SemaphoreType.DMA((2,)),
            pltpu.SemaphoreType.DMA((2,)),
        ],
        compiler_params=pltpu.CompilerParams(
            collective_id=9, has_side_effects=True, vmem_limit_bytes=VMEM_LIMIT
        ),
        cost_estimate=cost(16),
        name="scatter_tail",
    )(total, by_x, by_y)


def exchange_parts(axes, x_ref, o_ref, local_sem, ssem, rsem):
    place = [lax.axis_index(name) for name in axes]
    count = 2 ** len(axes)

    def rank(coords):
        total = 0
        for one in coords:
            total = total * 2 + one
        return total

    mine = rank(place)
    own = pltpu.make_async_copy(x_ref.at[mine], o_ref.at[mine], local_sem)
    peers, copies = [], []
    for mask in range(count - 1, 0, -1):
        bits = [(mask // 2 ** (len(axes) - 1 - i)) % 2 for i in range(len(axes))]
        coords = [1 - p if bit else p for p, bit in zip(place, bits)]
        device = {name: q for name, q, bit in zip(axes, coords, bits) if bit}
        peers.append(device)
        copies.append(
            remote(
                x_ref.at[rank(coords)],
                o_ref.at[mine],
                ssem.at[mask - 1],
                rsem.at[mask - 1],
                device,
            )
        )
    return peers, own, copies


def exchange_kernel(axes, *refs):
    count = (len(refs) - 3) // 2
    sources, targets = refs[:count], refs[count : 2 * count]
    local_sem, ssem, rsem = refs[2 * count :]
    parts = [
        exchange_parts(axes, sources[i], targets[i], local_sem.at[i], ssem.at[i], rsem.at[i])
        for i in range(count)
    ]
    for _, own, _ in parts:
        own.start()
    greet(parts[0][0])
    for _, _, copies in parts:
        for one in copies:
            one.start()
    for _, own, copies in parts:
        for one in copies:
            one.wait()
        own.wait()


def exchange(arrays, axes, ident):
    peers = 2 ** len(axes) - 1
    count = len(arrays)
    return pl.pallas_call(
        functools.partial(exchange_kernel, axes),
        out_shape=tuple(jax.ShapeDtypeStruct(a.shape, a.dtype) for a in arrays),
        in_specs=[vmem_spec()] * count,
        out_specs=(hbm_spec(),) * count,
        scratch_shapes=[
            pltpu.SemaphoreType.DMA((count,)),
            pltpu.SemaphoreType.DMA((count, peers)),
            pltpu.SemaphoreType.DMA((count, peers)),
        ],
        compiler_params=pltpu.CompilerParams(
            collective_id=ident, has_side_effects=True, vmem_limit_bytes=VMEM_LIMIT
        ),
        cost_estimate=cost(15),
        name="exchange",
    )(*arrays)


def gather_exchange(block, blocks):
    rows, width = block.shape
    out, got = pl.pallas_call(
        gather_kernel,
        out_shape=(
            jax.ShapeDtypeStruct((NF, rows, width), block.dtype),
            jax.ShapeDtypeStruct(blocks.shape, blocks.dtype),
        ),
        in_specs=[vmem_spec()] * 2,
        out_specs=(hbm_spec(),) * 2,
        scratch_shapes=[
            pltpu.SemaphoreType.DMA,
            pltpu.SemaphoreType.DMA((10,)),
            pltpu.SemaphoreType.DMA((10,)),
            pltpu.SemaphoreType.DMA,
            pltpu.SemaphoreType.DMA((NF - 1,)),
            pltpu.SemaphoreType.DMA((NF - 1,)),
        ],
        compiler_params=pltpu.CompilerParams(
            collective_id=4, has_side_effects=True, vmem_limit_bytes=VMEM_LIMIT
        ),
        cost_estimate=cost(55),
        name="gather_exchange",
    )(block, blocks)
    return out.reshape(NF * rows, width), got


def groups_kernel(count, x_ref, o_ref, local_sem, ssem, rsem):
    z = lax.axis_index("z")
    own = pltpu.make_async_copy(x_ref, o_ref.at[z], local_sem)
    own.start()
    targets = [{"z": lax.rem(z + hop, count)} for hop in range(1, count)]
    greet(targets)
    copies = [
        remote(x_ref, o_ref.at[z], ssem.at[i], rsem.at[i], device)
        for i, device in enumerate(targets)
    ]
    for one in copies:
        one.start()
    for one in copies:
        one.wait()
    own.wait()


def gather_groups(block, count, ident):
    return pl.pallas_call(
        functools.partial(groups_kernel, count),
        out_shape=jax.ShapeDtypeStruct((count,) + block.shape, block.dtype),
        in_specs=[vmem_spec()],
        out_specs=vmem_spec(),
        scratch_shapes=[
            pltpu.SemaphoreType.DMA,
            pltpu.SemaphoreType.DMA((count - 1,)),
            pltpu.SemaphoreType.DMA((count - 1,)),
        ],
        compiler_params=pltpu.CompilerParams(collective_id=ident, has_side_effects=True),
        cost_estimate=cost(5),
        name="gather_groups",
    )(block)


def gelu_tanh(values):
    return jax.nn.gelu(values, approximate=True)


def sigmoid(v):
    return 1.0 / (1.0 + jnp.exp(-v))


def gelu_pair(v):
    root = 0.7978845608028654
    cube = 0.044715
    square = v * v
    t = jnp.tanh(root * (v + cube * square * v))
    value = 0.5 * v * (1.0 + t)
    slope = 0.5 * (1.0 + t) + 0.5 * v * (1.0 - t * t) * root * (1.0 + 3.0 * cube * square)
    return value, slope


def tile_scan(keep, push, reverse):
    rows = lax.broadcasted_iota(jnp.int32, keep.shape, 0)
    count = keep.shape[0]
    hop = 1
    while hop < count:
        if reverse:
            inside = rows < count - hop
            shift = count - hop
        else:
            inside = rows >= hop
            shift = hop
        keep_near = jnp.where(inside, pltpu.roll(keep, shift, 0), 1.0)
        push_near = jnp.where(inside, pltpu.roll(push, shift, 0), 0.0)
        push = push + keep * push_near
        keep = keep * keep_near
        hop *= 2
    return keep, push


def conv_of(ext, masks, taps, offset, rows):
    value = offset + taps[0:1] * ext[pl.ds(8, rows)]
    for k in range(1, CONV):
        value = value + taps[k : k + 1] * ext[pl.ds(8 - k, rows)] * masks[:, k - 1 : k]
    return value


def forward_kernel(
    order_ref,
    pre_ref,
    halo_ref,
    mask_ref,
    small_ref,
    wa_ref,
    wx_ref,
    branch_ref,
    conved_ref,
    keep_ref,
    prod_ref,
    state_ref,
    ends_ref,
    ext,
    carry,
):
    rows, width = branch_ref.shape
    step = pl.program_id(0)
    branch = pre_ref[:, width : 2 * width].astype(bf16)
    branch_ref[...] = branch

    @pl.when(step == 0)
    def _():
        ext[pl.ds(0, 8)] = halo_ref[...]
        carry[0:1] = jnp.ones_like(carry[0:1])
        carry[1:2] = jnp.zeros_like(carry[1:2])

    @pl.when(step > 0)
    def _():
        ext[pl.ds(0, 8)] = ext[pl.ds(rows, 8)]

    ext[pl.ds(8, rows)] = branch.astype(f32)
    masks = mask_ref[...]
    conved = conv_of(ext, masks, small_ref, small_ref[4:5], rows).astype(bf16)
    conved_ref[...] = conved
    logit_a = jnp.dot(conved, wa_ref[...], preferred_element_type=f32) + small_ref[5:6]
    logit_x = jnp.dot(conved, wx_ref[...], preferred_element_type=f32) + small_ref[6:7]
    decay = jnp.exp(-decay_scale * sigmoid(logit_a) * small_ref[7:8])
    keep_ref[...] = decay * masks[:, 0:1]
    state_ref[...] = (
        jnp.sqrt(1.0 - decay * decay + push_shift) * sigmoid(logit_x) * conved.astype(f32)
    )

    def body(i, held):
        prod_in, state_in = held
        at = pl.ds(pl.multiple_of(i * 8, 8), 8)
        keep, push = tile_scan(keep_ref[at], state_ref[at], False)
        state = push + keep * state_in
        prod = keep * prod_in
        prod_ref[at] = prod
        state_ref[at] = state
        return prod[7:8], state[7:8]

    prod_out, state_out = lax.fori_loop(0, rows // 8, body, (carry[0:1], carry[1:2]))
    carry[0:1] = prod_out
    carry[1:2] = state_out
    ends_ref[0:1] = prod_out
    ends_ref[1:2] = state_out
    ends_ref[2:8] = jnp.zeros_like(ends_ref[2:8])


def forward_scan(order, rec_pre, halo, masks, small, wa, wx, chunk):
    rows, width = rec_pre.shape[0], rec_pre.shape[1] // 2
    tile = pl.BlockSpec((chunk, width), lambda i, order: (order[i], 0))
    whole = lambda a: pl.BlockSpec(a.shape, lambda i, order: (0, 0))
    full = jax.ShapeDtypeStruct((rows, width), f32)
    low = jax.ShapeDtypeStruct((rows, width), bf16)
    return pl.pallas_call(
        forward_kernel,
        out_shape=(
            low,
            low,
            full,
            full,
            full,
            jax.ShapeDtypeStruct((8, width), f32),
        ),
        grid_spec=pltpu.PrefetchScalarGridSpec(
            num_scalar_prefetch=1,
            grid=(rows // chunk,),
            in_specs=[
                pl.BlockSpec((chunk, 2 * width), lambda i, order: (order[i], 0)),
                whole(halo),
                pl.BlockSpec((chunk, masks.shape[1]), lambda i, order: (i, 0)),
                whole(small),
                whole(wa),
                whole(wx),
            ],
            out_specs=(tile,) * 5 + (pl.BlockSpec((8, width), lambda i, order: (0, 0)),),
            scratch_shapes=[pltpu.VMEM((chunk + 8, width), f32), pltpu.VMEM((8, width), f32)],
        ),
        compiler_params=pltpu.CompilerParams(vmem_limit_bytes=VMEM_LIMIT),
        cost_estimate=cost(15),
        name="forward_scan",
    )(order, rec_pre, halo, masks, small, wa, wx)


def adjoint_kernel(
    order_ref, d_mixed_ref, pre_ref, keep_ref, prod_ref, adj_ref, heads_ref, keep_next, carry
):
    rows = d_mixed_ref.shape[0]
    step = pl.program_id(0)

    @pl.when(step == 0)
    def _():
        keep_next[pl.ds(rows, 8)] = jnp.ones_like(keep_next[pl.ds(rows, 8)])
        carry[0:1] = jnp.ones_like(carry[0:1])
        carry[1:2] = jnp.zeros_like(carry[1:2])

    @pl.when(step > 0)
    def _():
        keep_next[pl.ds(rows, 8)] = keep_next[pl.ds(0, 8)]

    keep_next[pl.ds(0, rows)] = keep_ref[...]
    prod_ref[...] = keep_next[pl.ds(1, rows)]
    adj_ref[...] = d_mixed_ref[...] * gelu_tanh(pre_ref[:, 0 : adj_ref.shape[1]])
    tiles = rows // 8

    def body(i, held):
        prod_in, adj_in = held
        at = pl.ds(pl.multiple_of((tiles - 1 - i) * 8, 8), 8)
        keep, push = tile_scan(prod_ref[at], adj_ref[at], True)
        adj = push + keep * adj_in
        prod = keep * prod_in
        prod_ref[at] = prod
        adj_ref[at] = adj
        return prod[0:1], adj[0:1]

    prod_out, adj_out = lax.fori_loop(0, tiles, body, (carry[0:1], carry[1:2]))
    carry[0:1] = prod_out
    carry[1:2] = adj_out
    heads_ref[0:1] = keep_ref[0:1] * prod_out
    heads_ref[1:2] = keep_ref[0:1] * adj_out
    heads_ref[2:8] = jnp.zeros_like(heads_ref[2:8])


def adjoint_scan(order, d_mixed, rec_pre, keep, chunk):
    rows, width = keep.shape
    last = rows // chunk - 1
    tile = pl.BlockSpec((chunk, width), lambda i, order: (order[last - i], 0))
    full = jax.ShapeDtypeStruct((rows, width), f32)
    return pl.pallas_call(
        adjoint_kernel,
        out_shape=(full, full, jax.ShapeDtypeStruct((8, width), f32)),
        grid_spec=pltpu.PrefetchScalarGridSpec(
            num_scalar_prefetch=1,
            grid=(rows // chunk,),
            in_specs=[
                tile,
                pl.BlockSpec((chunk, 2 * width), lambda i, order: (order[last - i], 0)),
                tile,
            ],
            out_specs=(tile, tile, pl.BlockSpec((8, width), lambda i, order: (0, 0))),
            scratch_shapes=[pltpu.VMEM((chunk + 8, width), f32), pltpu.VMEM((8, width), f32)],
        ),
        compiler_params=pltpu.CompilerParams(vmem_limit_bytes=VMEM_LIMIT),
        cost_estimate=cost(12),
        name="adjoint_scan",
    )(order, d_mixed, rec_pre, keep)


def backward_kernel(
    order_ref,
    d_mixed_ref,
    pre_ref,
    state_ref,
    prod_ref,
    state_before_ref,
    prod_before_ref,
    adj_ref,
    adj_prod_ref,
    branch_ref,
    branch_before_ref,
    halo_ref,
    conved_ref,
    mask_ref,
    small_ref,
    enter_ref,
    wa_ref,
    wx_ref,
    d_pre_ref,
    sums_ref,
    edge_ref,
    ga_ref,
    gx_ref,
    ext,
    state_ext,
    later,
):
    rows, width = d_mixed_ref.shape
    step = pl.program_id(0)
    steps = pl.num_programs(0)
    state_in = enter_ref[0:1]
    adj_in = enter_ref[1:2]

    @pl.when(step == 0)
    def _():
        sums_ref[...] = jnp.zeros_like(sums_ref)
        ga_ref[...] = jnp.zeros_like(ga_ref)
        gx_ref[...] = jnp.zeros_like(gx_ref)
        for k in range(TAIL):
            later[k, pl.ds(rows, 8)] = jnp.zeros((8, width), f32)

    @pl.when(step > 0)
    def _():
        for k in range(TAIL):
            later[k, pl.ds(rows, 8)] = later[k, pl.ds(0, 8)]

    first = step == steps - 1

    @pl.when(first)
    def _():
        ext[pl.ds(0, 8)] = halo_ref[...]
        state_ext[pl.ds(0, 8)] = jnp.broadcast_to(state_in, (8, width))

    @pl.when(jnp.logical_not(first))
    def _():
        ext[pl.ds(0, 8)] = branch_before_ref[...].astype(f32)[8:16]
        state_ext[pl.ds(0, 8)] = state_before_ref[...] + prod_before_ref[...] * state_in

    ext[pl.ds(8, rows)] = branch_ref[...].astype(f32)
    state = state_ref[...] + prod_ref[...] * state_in
    state_ext[pl.ds(8, rows)] = state
    _, slope = gelu_pair(pre_ref[:, 0:width])
    d_pre_ref[:, 0:width] = (d_mixed_ref[...] * state * slope).astype(bf16)
    adjoint = adj_ref[...] + adj_prod_ref[...] * adj_in
    state_prev = state_ext[pl.ds(7, rows)]
    masks = mask_ref[...]
    conved_low = conved_ref[...]
    conved = conved_low.astype(f32)
    rates = small_ref[7:8]
    gate_a = sigmoid(
        jnp.dot(conved_low, wa_ref[...], preferred_element_type=f32) + small_ref[5:6]
    )
    gate_x = sigmoid(
        jnp.dot(conved_low, wx_ref[...], preferred_element_type=f32) + small_ref[6:7]
    )
    decay = jnp.exp(-decay_scale * gate_a * rates)
    root = jnp.sqrt(1.0 - decay * decay + push_shift)
    d_decay = adjoint * (state_prev * masks[:, 0:1] - gate_x * conved * decay / root)
    slope_a = -decay_scale * d_decay * decay * gate_a
    d_logit_a = (slope_a * rates * (1.0 - gate_a)).astype(bf16)
    through = adjoint * root * gate_x
    d_logit_x = (through * conved * (1.0 - gate_x)).astype(bf16)
    d_conved = (
        through
        + lax.dot_general(d_logit_a, wa_ref[...], contract_last, preferred_element_type=f32)
        + lax.dot_general(d_logit_x, wx_ref[...], contract_last, preferred_element_type=f32)
    )
    d_conved = d_conved.astype(bf16).astype(f32)
    ga_ref[...] += lax.dot_general(
        conved_low, d_logit_a, contract_first, preferred_element_type=f32
    )
    gx_ref[...] += lax.dot_general(
        conved_low, d_logit_x, contract_first, preferred_element_type=f32
    )

    def total(v):
        return jnp.sum(v, axis=0, keepdims=True)

    sums_ref[0:1] += total(d_conved * ext[pl.ds(8, rows)])
    for k in range(1, CONV):
        masked = d_conved * masks[:, k - 1 : k]
        later[k - 1, pl.ds(0, rows)] = masked
        sums_ref[k : k + 1] += total(masked * ext[pl.ds(8 - k, rows)])
    sums_ref[4:5] += total(d_conved)
    sums_ref[5:6] += total(d_logit_a.astype(f32))
    sums_ref[6:7] += total(d_logit_x.astype(f32))
    sums_ref[7:8] += total(slope_a)
    d_branch = small_ref[0:1] * d_conved
    for k in range(1, CONV):
        d_branch = d_branch + small_ref[k : k + 1] * later[k - 1, pl.ds(k, rows)]
    d_pre_ref[:, width : 2 * width] = d_branch.astype(bf16)

    @pl.when(first)
    def _():
        for back in range(1, CONV):
            value = jnp.zeros((1, width), f32)
            for k in range(back, CONV):
                value = value + small_ref[k : k + 1] * later[k - 1, pl.ds(k - back, 1)]
            edge_ref[8 - back : 9 - back] = value
        edge_ref[0 : 8 - TAIL] = jnp.zeros((8 - TAIL, width), f32)


def backward_scan(
    order, d_mixed, rec_pre, state, prod, adj, adj_prod, branch_in, halo, conved, masks, small,
    enter, wa, wx, chunk,
):
    rows, width = state.shape
    last = rows // chunk - 1
    tile = pl.BlockSpec((chunk, width), lambda i, order: (order[last - i], 0))

    def before(size):
        per = chunk // size
        return pl.BlockSpec(
            (size, width),
            lambda i, order: (order[jnp.maximum(last - i - 1, 0)] * per + per - 1, 0),
        )

    pinned = lambda shape: pl.BlockSpec(shape, lambda i, order: (0, 0))
    whole = lambda a: pinned(a.shape)
    return pl.pallas_call(
        backward_kernel,
        out_shape=(
            jax.ShapeDtypeStruct((rows, 2 * width), bf16),
            jax.ShapeDtypeStruct((8, width), f32),
            jax.ShapeDtypeStruct((8, width), f32),
            jax.ShapeDtypeStruct((width, width), f32),
            jax.ShapeDtypeStruct((width, width), f32),
        ),
        grid_spec=pltpu.PrefetchScalarGridSpec(
            num_scalar_prefetch=1,
            grid=(rows // chunk,),
            in_specs=[
                tile,
                pl.BlockSpec((chunk, 2 * width), lambda i, order: (order[last - i], 0)),
                tile,
                tile,
                before(8),
                before(8),
                tile,
                tile,
                tile,
                before(16),
                whole(halo),
                tile,
                pl.BlockSpec((chunk, masks.shape[1]), lambda i, order: (last - i, 0)),
                whole(small),
                whole(enter),
                whole(wa),
                whole(wx),
            ],
            out_specs=(
                pl.BlockSpec((chunk, 2 * width), lambda i, order: (order[last - i], 0)),
                pinned((8, width)),
                pinned((8, width)),
                pinned((width, width)),
                pinned((width, width)),
            ),
            scratch_shapes=[
                pltpu.VMEM((chunk + 8, width), f32),
                pltpu.VMEM((chunk + 8, width), f32),
                pltpu.VMEM((TAIL, chunk + 8, width), f32),
            ],
        ),
        compiler_params=pltpu.CompilerParams(vmem_limit_bytes=VMEM_LIMIT),
        cost_estimate=cost(21),
        name="backward_scan",
    )(
        order, d_mixed, rec_pre, state, prod, state, prod, adj, adj_prod, branch_in, branch_in,
        halo, conved, masks, small, enter, wa, wx,
    )


def gated_kernel(n_ref, mine_ref, theirs_ref, w_ref, down_ref, hidden_ref, d_ref):
    ff = down_ref.shape[0]
    tile = 256
    normed = n_ref[...]
    cot = lax.select(
        pl.program_id(0) < pl.num_programs(0) // 2, mine_ref[...], theirs_ref[...]
    )

    def body(j, none):
        at = pl.ds(pl.multiple_of(j * tile, tile), tile)
        up_at = pl.ds(pl.multiple_of(ff + j * tile, tile), tile)
        gate = jnp.dot(normed, w_ref[:, at], preferred_element_type=f32)
        up = jnp.dot(normed, w_ref[:, up_at], preferred_element_type=f32)
        d_hidden = lax.dot_general(cot, down_ref[at], contract_last, preferred_element_type=f32)
        act, slope = gelu_pair(gate)
        hidden_ref[:, at] = (act * up).astype(bf16)
        d_ref[:, at] = (d_hidden * up * slope).astype(bf16)
        d_ref[:, up_at] = (d_hidden * act).astype(bf16)
        return none

    lax.fori_loop(0, ff // tile, body, 0)


def gated_unit(normed, cot_mine, cot_theirs, w_mlp, w_down):
    rows, width = normed.shape
    ff = w_down.shape[0]
    steps = 4
    tile = rows // steps
    row = lambda size: pl.BlockSpec((tile, size), lambda i: (i, 0))
    once = lambda a: pl.BlockSpec(a.shape, lambda i: (0, 0), pipeline_mode=pl.Buffered(1))
    return pl.pallas_call(
        gated_kernel,
        grid=(steps,),
        out_shape=(
            jax.ShapeDtypeStruct((rows, ff), bf16),
            jax.ShapeDtypeStruct((rows, 2 * ff), bf16),
        ),
        in_specs=[
            row(width),
            pl.BlockSpec((tile, width), lambda i: (jnp.minimum(i, steps // 2 - 1), 0)),
            pl.BlockSpec((tile, width), lambda i: (jnp.maximum(i - steps // 2, 0), 0)),
            once(w_mlp),
            once(w_down),
        ],
        out_specs=(row(ff), row(2 * ff)),
        compiler_params=pltpu.CompilerParams(vmem_limit_bytes=VMEM_LIMIT),
        cost_estimate=pl.CostEstimate(
            flops=6 * rows * width * ff, bytes_accessed=40 * 2**20, transcendentals=rows * ff
        ),
        name="gated_unit",
    )(normed, cot_mine, cot_theirs, w_mlp, w_down)


def split_kernel(moves, a_ref, b_ref, o_ref):
    for source, block, at, start, size in moves:
        ref = (a_ref, b_ref)[source]
        o_ref[block, :, at : at + size] = ref[:, start : start + size]


def join_kernel(moves, x_ref, a_ref, b_ref, g_ref, oa_ref, ob_ref, og_ref):
    for source, block, at, start, size in moves:
        ref = (oa_ref, ob_ref)[source]
        ref[:, start : start + size] = x_ref[block, :, at : at + size].astype(f32)
    total = jnp.sum(a_ref[...].astype(f32) * oa_ref[...], axis=1, keepdims=True) + jnp.sum(
        b_ref[...].astype(f32) * ob_ref[...], axis=1, keepdims=True
    )
    wide = jnp.broadcast_to(total / g_ref[...], (total.shape[0], LANES))
    og_ref[...] = wide.T[0:1]


def split_blocks(a, b, moves):
    rows, width = a.shape
    return pl.pallas_call(
        functools.partial(split_kernel, moves),
        out_shape=jax.ShapeDtypeStruct((NF, rows, 2 * width // NF), a.dtype),
        compiler_params=pltpu.CompilerParams(vmem_limit_bytes=VMEM_LIMIT),
        cost_estimate=cost(4),
        name="split_blocks",
    )(a, b)


def join_blocks(x, a, b, gain, moves):
    rows, width = a.shape
    out = jax.ShapeDtypeStruct((rows, width), f32)
    return pl.pallas_call(
        functools.partial(join_kernel, moves),
        out_shape=(out, out, jax.ShapeDtypeStruct((1, rows), f32)),
        compiler_params=pltpu.CompilerParams(vmem_limit_bytes=VMEM_LIMIT),
        cost_estimate=cost(5),
        name="join_blocks",
    )(x, a, b, gain)


def unpack_kernel(x_ref, out_ref, ga_ref, gx_ref, taps_ref, *row_refs):
    width = out_ref.shape[1]
    base = width + 2 * BLK
    out_ref[...] = x_ref[:, 0:width].astype(f32)
    ga_ref[...] = x_ref[:, width : width + BLK].astype(f32)
    gx_ref[...] = x_ref[:, width + BLK : base].astype(f32)
    last = base - base % LANES
    small = x_ref[:, last : last + LANES].astype(f32)
    taps_ref[...] = small[:, base - last : base - last + CONV]
    turned = small.T
    for i, ref in enumerate(row_refs):
        at = base - last + CONV + i
        ref[...] = turned[at : at + 1]


def unpack_sums(x, width):
    rows = x.shape[0]
    shape = lambda *dims: jax.ShapeDtypeStruct(dims, f32)
    return pl.pallas_call(
        unpack_kernel,
        out_shape=(shape(rows, width), shape(rows, BLK), shape(rows, BLK), shape(rows, CONV))
        + (shape(1, rows),) * 4,
        compiler_params=pltpu.CompilerParams(vmem_limit_bytes=VMEM_LIMIT),
        cost_estimate=cost(2),
        name="unpack_sums",
    )(x)


def pad_lanes(rows, width):
    have = rows.shape[-1]
    return jnp.pad(rows, ((0, 0), (0, width - have)))


def inverse_rms(rows):
    return lax.rsqrt(jnp.mean(rows * rows, axis=-1, keepdims=True) + norm_eps)


def norm_back(rows, scale, e):
    return scale * e - rows * (scale * scale * scale) * jnp.mean(e * rows, axis=-1, keepdims=True)


def on_device(
    tokens_in,
    segment_starts,
    cotangent,
    norm1_gain,
    rec_gate_weight,
    rec_in_weight,
    conv_weight,
    conv_bias,
    gate_a_weight,
    gate_a_bias,
    gate_x_weight,
    gate_x_bias,
    decay_rate,
    rec_out_weight,
    norm2_gain,
    mlp_gate_weight,
    mlp_up_weight,
    mlp_down_weight,
):
    count = lax.axis_size("z")
    z = lax.axis_index("z")
    spread = count // 2
    swap_axes = FEAT[len(FEAT) - (spread.bit_length() - 1) :]
    outer = NF // spread
    rows_tok, width = tokens_in.shape
    group_rows = NF * rows_tok
    chan_rows = conv_weight.shape[0]
    chans = chan_rows * count
    rows_w = rec_gate_weight.shape[0]
    ff_rows = mlp_down_weight.shape[0]
    ff = ff_rows * count
    chunk = 256

    chan_moves = [
        (
            source,
            k * spread + e,
            source * chans + zz * BLK,
            ((2 * e + zz) * outer + k) * BLK,
            BLK,
        )
        for source in range(2)
        for k in range(outer)
        for e in range(spread)
        for zz in range(2)
    ]
    ff_moves = [
        (source, f, source * ff + group * ff_rows, (group * NF + f) * ff_rows, ff_rows)
        for source in range(2)
        for f in range(NF)
        for group in range(count)
    ]
    place = [lax.axis_index(name) for name in FEAT]
    time = jnp.arange(NF, dtype=jnp.int32)
    bit = lambda value, here: jnp.where(value == here, 0, 1)
    order = (
        bit(time % 2, place[2]) * 4 + bit(time // 4, place[0]) * 2 + bit((time // 2) % 2, place[1])
    ).astype(jnp.int32)
    final = order[NF - 1] * rows_tok + rows_tok - 8

    pack = jnp.concatenate(
        [
            rec_out_weight,
            gate_a_weight,
            gate_x_weight,
            conv_weight,
            conv_bias[:, None],
            gate_a_bias[:, None],
            gate_x_bias[:, None],
            decay_rate[:, None],
        ],
        axis=1,
    )
    used = pack.shape[1]
    pack_width = -(-used // LANES) * LANES
    pack = pad_lanes(pack, pack_width)

    extra = jnp.concatenate(
        [
            pad_lanes(segment_starts.astype(bf16)[None], 2 * chans),
            pad_lanes(norm1_gain[None], 2 * chans),
            pad_lanes(norm2_gain[None], 2 * chans),
            jnp.zeros((13, 2 * chans), bf16),
        ],
        axis=0,
    )
    rec_send = jnp.concatenate(
        [
            split_blocks(rec_gate_weight, rec_in_weight, chan_moves),
            jnp.broadcast_to(extra[None], (NF, 16, 2 * chans)),
        ],
        axis=1,
    )
    pack_all = lax.all_gather(pack, "z", axis=0, tiled=True)
    (rec_got,) = exchange([rec_send], FEAT, 3)
    starts = rec_got[:, rows_w, :rows_tok].reshape(group_rows).astype(f32)

    plane_gains = jnp.stack(
        [
            rec_got[:, rows_w + 1, :rows_w].reshape(NF * rows_w),
            rec_got[:, rows_w + 2, :rows_w].reshape(NF * rows_w),
        ]
    ).astype(f32)
    gains = gather_groups(jnp.pad(plane_gains, ((0, 6), (0, 0))), count, 7)
    w_rec = lax.all_gather(
        rec_got[:, :rows_w].reshape(NF * rows_w, 2 * chans), "z", axis=0, tiled=True
    )
    mlp_send = split_blocks(mlp_gate_weight, mlp_up_weight, ff_moves)
    tokens_own, gains = hold(tokens_in, gains)
    tok_group, mlp_got = gather_exchange(tokens_own, mlp_send)
    tok_group, pack_all = hold(tok_group, pack_all)
    (pack_swap,) = exchange(
        [pack_all.reshape(spread, 2, chan_rows, pack_width)], swap_axes, 5
    )
    gain_one = gains[:, 0].reshape(1, width)
    gain_two = gains[:, 1].reshape(1, width)

    tok = tokens_in.astype(f32)
    tok_group = tok_group.astype(f32)
    normed = (tok_group * inverse_rms(tok_group) * gain_one).astype(bf16)

    w_mlp = lax.all_gather(mlp_got.reshape(NF * rows_w, 2 * ff), "z", axis=0, tiled=True)
    w_down = lax.all_gather(mlp_down_weight, "z", axis=0, tiled=True)

    mine = pack_swap.transpose(1, 0, 2, 3).reshape(chans, pack_width)
    w_out = mine[:, :width]
    small = mine[:, width + 2 * BLK : used].astype(f32).T

    unit = lax.broadcasted_iota(jnp.int32, (chans, chans), 0) // BLK
    same_block = unit == lax.broadcasted_iota(jnp.int32, (chans, chans), 1) // BLK

    def block_diag(w):
        return jnp.where(same_block, jnp.concatenate([w, w], axis=1), jnp.zeros((), w.dtype))

    wa = block_diag(mine[:, width : width + BLK])
    wx = block_diag(mine[:, width + BLK : width + 2 * BLK])

    open_one = 1.0 - starts
    ahead = jnp.concatenate([jnp.ones((TAIL,), f32), open_one])
    open_two = open_one * ahead[TAIL - 1 : TAIL - 1 + group_rows]
    open_three = open_two * ahead[TAIL - 2 : TAIL - 2 + group_rows]
    masks = jnp.stack([open_one, open_two, open_three], axis=1)
    end = open_one[group_rows - 2 :]
    later_open = jnp.concatenate(
        [jnp.zeros((8 - TAIL,), f32), (end[0] * end[1])[None], end[1:], jnp.ones((1,), f32)]
    )[:, None]

    rec_pre = jnp.dot(normed, w_rec, preferred_element_type=f32)
    rec_pre, cot_own = hold(rec_pre, cotangent)
    cot_x, cot_y = gather_near(cot_own)
    edge_rows = lax.dynamic_slice_in_dim(rec_pre, final, 8, 0)[:, chans:].astype(bf16)
    tails = gather_groups(edge_rows.astype(f32) * later_open, count, 2)
    halo = jnp.where(z > 0, lax.dynamic_index_in_dim(tails, jnp.maximum(z - 1, 0), 0, False), 0.0)
    branch_in, conved, keep, prod, state_local, ends = forward_scan(
        order, rec_pre, halo, masks, small, wa, wx, chunk
    )
    ends, cot_x, cot_y = hold(ends, cot_x, cot_y)
    cot_top, cot_low = gather_diagonal(cot_x, cot_y)
    ends = gather_groups(ends, count, 2)
    state_in = jnp.zeros((1, chans), f32)
    for hop in range(count - 1):
        state_in = jnp.where(hop < z, ends[hop, 0:1] * state_in + ends[hop, 1:2], state_in)
    mixed = ((state_local + prod * state_in) * gelu_tanh(rec_pre[:, :chans])).astype(bf16)
    mixed_out = jnp.dot(mixed, w_out, preferred_element_type=f32).astype(bf16)
    mixed_out, cot_top, cot_low = hold(mixed_out, cot_top, cot_low)
    cot_chip = gather_chip(cotangent, cot_x, cot_y, cot_top, cot_low)
    cot_got = across(cot_chip, "c")
    middle = tok + scatter_feature(mixed_out)

    scale_two = inverse_rms(middle)
    normed_two = gather_feature((middle * scale_two * gain_two).astype(bf16))
    hidden, d_mlp = gated_unit(normed_two, cot_chip, cot_got, w_mlp, w_down)
    half_rows = group_rows // 2

    def back_rows(d, w):
        return lax.dot_general(d, w, contract_last, preferred_element_type=f32).astype(bf16)

    def over_rows(a, b_mine, b_theirs):
        return (
            lax.dot_general(a[:half_rows], b_mine, contract_first, preferred_element_type=f32)
            + lax.dot_general(a[half_rows:], b_theirs, contract_first, preferred_element_type=f32)
        ).astype(bf16)

    e_theirs = back_rows(d_mlp[half_rows:], w_mlp)
    d_mlp, e_theirs = hold(d_mlp, e_theirs)
    e_got = across(e_theirs, "c")
    e_mine = back_rows(d_mlp[:half_rows], w_mlp)
    e_total, e_x, e_y = scatter_near(e_mine, e_got)
    e_total, hidden = hold(e_total, hidden)
    down_part = over_rows(hidden, cot_chip, cot_got)
    down_part, hidden = hold(down_part, hidden)
    down_sum = lax.psum_scatter(down_part, "z", scatter_dimension=0, tiled=True)
    out_theirs = jnp.dot(hidden[half_rows:], w_down, preferred_element_type=f32).astype(bf16)
    out_got = across(out_theirs, "c")
    out_mine = jnp.dot(hidden[:half_rows], w_down, preferred_element_type=f32).astype(bf16)
    out_mine, out_got, e_x, e_y = hold(out_mine, out_got, e_x, e_y)
    e_two = gain_two * scatter_tail(e_total, e_x, e_y)
    d_middle = cotangent.astype(f32) + norm_back(middle, scale_two, e_two)
    d_own = d_middle.astype(bf16)
    d_x, d_y = gather_near(d_own)
    d_own, d_mlp, out_mine, out_got = hold(d_own, d_mlp, out_mine, out_got)
    mlp_part = lax.dot_general(
        normed_two, d_mlp, contract_first, preferred_element_type=f32
    ).astype(bf16)
    out_total = scatter_total(out_mine, out_got)
    d_x, d_y, mlp_part, out_total = hold(d_x, d_y, mlp_part, out_total)
    mlp_sum = lax.psum_scatter(mlp_part, "z", scatter_dimension=0, tiled=True)
    d_rec = gather_tail(d_own, d_x, d_y)
    d_rec, down_sum, out_total = hold(d_rec, down_sum, out_total)
    out_x, out_y = scatter_sides(out_total)

    d_mixed = lax.dot_general(d_rec, w_out, contract_last, preferred_element_type=f32)
    adj_prod, adj_local, heads = adjoint_scan(order, d_mixed, rec_pre, keep, chunk)
    heads = gather_groups(heads, count, 2)
    heads, out_x, out_y = hold(heads, out_x, out_y)
    out_last = scatter_relay(out_total, out_x, out_y)
    adj_in = jnp.zeros((1, chans), f32)
    for hop in range(count - 1, 0, -1):
        adj_in = jnp.where(hop > z, heads[hop, 0:1] * adj_in + heads[hop, 1:2], adj_in)
    enter = jnp.concatenate([state_in, adj_in, jnp.zeros((6, chans), f32)])
    d_rec_pre, sums, edge, grad_a, grad_x = backward_scan(
        order, d_mixed, rec_pre, state_local, prod, adj_local, adj_prod, branch_in, halo, conved,
        masks, small, enter, wa, wx, chunk,
    )
    edges = gather_groups(edge, count, 2)
    after = lax.dynamic_index_in_dim(edges, jnp.minimum(z + 1, count - 1), 0, False)
    after = jnp.where(z < count - 1, after, 0.0) * later_open
    tail_sum = lax.dynamic_slice_in_dim(d_rec_pre, final, 8, 0).astype(f32) + jnp.pad(
        after, ((0, 0), (chans, 0))
    )
    d_rec_pre = lax.dynamic_update_slice_in_dim(d_rec_pre, tail_sum.astype(bf16), final, 0)
    rec_part = lax.dot_general(
        normed, d_rec_pre, contract_first, preferred_element_type=f32
    ).astype(bf16)
    rec_part, d_rec_pre, grad_a, grad_x, sums, mixed, *out_last = hold(
        rec_part, d_rec_pre, grad_a, grad_x, sums, mixed, *out_last
    )
    layer_out = (middle + scatter_sum(out_total, out_x, out_y, *out_last)).astype(bf16)
    rec_part, mlp_sum = hold(rec_part, mlp_sum)
    rec_sum = lax.psum_scatter(rec_part, "z", scatter_dimension=0, tiled=True)
    one_theirs = back_rows(d_rec_pre[half_rows:], w_rec)
    d_rec_pre, one_theirs = hold(d_rec_pre, one_theirs)
    one_got = across(one_theirs, "c")
    one_mine = back_rows(d_rec_pre[:half_rows], w_rec)
    one_total, one_x, one_y = scatter_near(one_mine, one_got)
    one_total, mixed, grad_a, grad_x = hold(one_total, mixed, grad_a, grad_x)
    fold = (
        lax.broadcasted_iota(jnp.int32, (chans, BLK), 0) % BLK
        == lax.broadcasted_iota(jnp.int32, (chans, BLK), 1)
    ).astype(bf16)

    def diagonal(w):
        kept = jnp.where(same_block, w, 0.0).astype(bf16)
        return jnp.dot(kept, fold, preferred_element_type=f32).astype(bf16)

    back_pack = jnp.concatenate(
        [
            lax.dot_general(
                mixed, d_rec, contract_first, preferred_element_type=f32
            ).astype(bf16),
            diagonal(grad_a),
            diagonal(grad_x),
            sums.T.astype(bf16),
        ],
        axis=1,
    )
    back_pack = pad_lanes(back_pack, pack_width)
    back_pack = back_pack.reshape(2, spread, chan_rows, pack_width).transpose(1, 0, 2, 3)
    (back_swap,) = exchange([back_pack], swap_axes, 5)
    back_swap = back_swap.reshape(count * chan_rows, pack_width)
    one_x, one_y, back_swap, mlp_sum, rec_sum = hold(one_x, one_y, back_swap, mlp_sum, rec_sum)
    pack_sum = lax.psum_scatter(back_swap, "z", scatter_dimension=0, tiled=True)
    one_last = scatter_relay(one_total, one_x, one_y)
    mlp_back, rec_back = exchange(
        [mlp_sum.reshape(NF, rows_w, 2 * ff), rec_sum.reshape(NF, rows_w, 2 * chans)], FEAT, 6
    )
    mlp_back, rec_back, *one_last = hold(mlp_back, rec_back, *one_last)
    e_one = gain_one * scatter_sum(one_total, one_x, one_y, *one_last)
    grad_tokens = d_middle + norm_back(tok, inverse_rms(tok), e_one)
    grad_gate, grad_up, grad_gain_two = join_blocks(
        mlp_back, mlp_gate_weight, mlp_up_weight, norm2_gain.astype(f32)[:, None], ff_moves
    )
    grad_rec_gate, grad_rec_in, grad_gain_one = join_blocks(
        rec_back, rec_gate_weight, rec_in_weight, norm1_gain.astype(f32)[:, None], chan_moves
    )

    grad_out, grad_a, grad_x, grad_taps, *grad_rows = unpack_sums(pack_sum, width)
    grad_offset, grad_a_bias, grad_x_bias, grad_rate = (r.reshape(chan_rows) for r in grad_rows)
    return (
        layer_out,
        grad_tokens,
        grad_gain_one.reshape(rows_w),
        grad_rec_gate,
        grad_rec_in,
        grad_taps,
        grad_offset,
        grad_a,
        grad_a_bias,
        grad_x,
        grad_x_bias,
        grad_rate,
        grad_out,
        grad_gain_two.reshape(rows_w),
        grad_gate,
        grad_up,
        down_sum.astype(f32),
    )


def solution(mesh):
    wide, narrow = mesh.shape["wide"], mesh.shape["narrow"]
    groups = wide * narrow // NF
    grid = Mesh(mesh.devices.reshape((groups,) + (2,) * len(FEAT)), ("z",) + FEAT)
    flat = P(("z",) + FEAT)
    wide_rows = P(("z",) + FEAT, None)
    one, two = flat, wide_rows
    return jax.shard_map(
        on_device,
        mesh=grid,
        in_specs=(
            two, one, two, one, two, two, two, one, two, one, two, one, one, two, one, two, two, two,
        ),
        out_specs=(
            two, two, one, two, two, two, one, two, one, two, one, one, two, one, two, two, two,
        ),
        check_vma=False,
    )
```

```python
import functools

import jax
import jax.numpy as jnp
from jax import lax
from jax.experimental import pallas as pl
from jax.experimental.pallas import tpu as pltpu
from jax.sharding import Mesh
from jax.sharding import PartitionSpec as P

BLK = 160
CONV = 4
TAIL = CONV - 1
LANES = 128
FEAT = ("x", "y", "c")
NF = 8
OWN, ACROSS_Y, ACROSS_X, DIAGONAL = 0, 1, 2, 3

norm_eps = 1e-06
decay_scale = 8.0
push_shift = 0.05
f32 = jnp.float32
bf16 = jnp.bfloat16
MESH = pl.DeviceIdType.MESH
contract_last = (((1,), (1,)), ((), ()))
contract_first = (((0,), (0,)), ((), ()))
VMEM_LIMIT = 56 * 2**20


def cost(micros, flops=0):
    return pl.CostEstimate(
        flops=int(flops), bytes_accessed=int(micros * 3.0e6), transcendentals=0
    )


def hbm_spec():
    return pl.BlockSpec(memory_space=pl.ANY)


def vmem_spec():
    return pl.BlockSpec(memory_space=pltpu.VMEM)


def greet(peers):
    barrier = pltpu.get_barrier_semaphore()
    for device in peers:
        pl.semaphore_signal(barrier, inc=1, device_id=device, device_id_type=MESH)
    pl.semaphore_wait(barrier, len(peers))


def feature_place():
    return tuple(lax.axis_index(name) for name in FEAT)


def remote(src, dst, send_sem, recv_sem, device):
    return pltpu.make_async_remote_copy(
        src_ref=src,
        dst_ref=dst,
        send_sem=send_sem,
        recv_sem=recv_sem,
        device_id=device,
        device_id_type=MESH,
    )


def gather_kernel(*refs):
    if len(refs) == 5:
        x_ref, o_ref, local_sem, ssem, rsem = refs
        extra = ()
    else:
        x_ref, b_ref, o_ref, e_ref, local_sem, ssem, rsem, *sems = refs
        extra = exchange_parts(FEAT, b_ref, e_ref, *sems)
    x, y, c = feature_place()
    to_x, to_y, to_c = {"x": 1 - x}, {"y": 1 - y}, {"c": 1 - c}
    half = x_ref.shape[0] // 2
    top, low = pl.ds(0, half), pl.ds(half, half)
    greet(extra[0] if extra else (to_x, to_y, to_c))

    def copy(i, src, dst, device):
        return remote(src, dst, ssem.at[i], rsem.at[i], device)

    own = pltpu.make_async_copy(x_ref, o_ref.at[OWN], local_sem)
    x_top = copy(0, x_ref.at[top], o_ref.at[ACROSS_X, top], to_x)
    x_low = copy(1, x_ref.at[low], o_ref.at[ACROSS_X, low], to_x)
    y_low = copy(2, x_ref.at[low], o_ref.at[ACROSS_Y, low], to_y)
    y_top = copy(3, x_ref.at[top], o_ref.at[ACROSS_Y, top], to_y)
    c_own = copy(4, x_ref, o_ref.at[4 + OWN], to_c)
    y_fwd = copy(5, o_ref.at[ACROSS_X, top], o_ref.at[DIAGONAL, top], to_y)
    x_fwd = copy(6, o_ref.at[ACROSS_Y, low], o_ref.at[DIAGONAL, low], to_x)
    c_x = copy(7, o_ref.at[ACROSS_X], o_ref.at[4 + ACROSS_X], to_c)
    c_y = copy(8, o_ref.at[ACROSS_Y], o_ref.at[4 + ACROSS_Y], to_c)
    c_d = copy(9, o_ref.at[DIAGONAL], o_ref.at[4 + DIAGONAL], to_c)
    for one in (x_top, y_low, x_low, y_top, c_own, own):
        one.start()
    if extra:
        extra[1].start()
        for one in extra[2]:
            one.start()
    x_top.wait_recv()
    y_fwd.start()
    y_low.wait_recv()
    x_fwd.start()
    x_low.wait_recv()
    c_x.start()
    y_top.wait_recv()
    c_y.start()
    y_fwd.wait_recv()
    x_fwd.wait_recv()
    c_d.start()
    for one in (c_own, c_x, c_y, c_d):
        one.wait_recv()
    for one in (x_top, x_low, y_low, y_top, c_own, y_fwd, x_fwd, c_x, c_y, c_d):
        one.wait_send()
    own.wait()
    if extra:
        for one in extra[2]:
            one.wait()
        extra[1].wait()


def gather_feature(block):
    rows, width = block.shape
    out = pl.pallas_call(
        gather_kernel,
        out_shape=jax.ShapeDtypeStruct((NF, rows, width), block.dtype),
        in_specs=[vmem_spec()],
        out_specs=hbm_spec(),
        scratch_shapes=[
            pltpu.SemaphoreType.DMA,
            pltpu.SemaphoreType.DMA((10,)),
            pltpu.SemaphoreType.DMA((10,)),
        ],
        compiler_params=pltpu.CompilerParams(
            collective_id=0, has_side_effects=True, vmem_limit_bytes=VMEM_LIMIT
        ),
        cost_estimate=cost(40),
        name="gather_feature",
    )(block)
    return out.reshape(NF * rows, width)


def scatter_flow(
    p_theirs, o_ref, own, other, total, rx, ry, relay, rx_last, ry_last, ssem, rsem,
    peers, begin, stage, ready
):
    x, y, c = feature_place()
    to_x, to_y, to_c = {"x": 1 - x}, {"y": 1 - y}, {"c": 1 - c}
    rows, width = o_ref.shape
    half = rows // 2
    top, low = pl.ds(0, half), pl.ds(half, half)
    step = 16

    def copy(i, src, dst, device):
        return remote(src, dst, ssem.at[i], rsem.at[i], device)

    greet(peers or (to_x, to_y, to_c))
    begin()
    cross = [copy(r, p_theirs(r), other.at[r], to_c) for r in range(4)]

    def add_into(r):
        ready(r)
        cross[r].wait_recv()

        def body(i, none):
            at = pl.ds(pl.multiple_of(i * step, step), step)
            total[r, at] = (own[r, at].astype(f32) + other[r, at].astype(f32)).astype(total.dtype)
            return none

        lax.fori_loop(0, rows // step, body, 0)

    x_diag = copy(4, total.at[DIAGONAL, top], rx.at[1], to_x)
    y_diag = copy(5, total.at[DIAGONAL, low], ry.at[1], to_y)
    x_near = copy(6, total.at[ACROSS_X, top], rx.at[0], to_x)
    y_near = copy(7, total.at[ACROSS_Y, low], ry.at[0], to_y)
    y_last = copy(8, relay.at[0], ry_last, to_y)
    x_last = copy(9, relay.at[1], rx_last, to_x)

    stage(DIAGONAL, cross)
    stage(ACROSS_X, cross)
    add_into(DIAGONAL)
    x_diag.start()
    y_diag.start()
    stage(ACROSS_Y, cross)
    add_into(ACROSS_X)
    x_near.start()
    stage(OWN, cross)
    add_into(ACROSS_Y)
    y_near.start()
    ready(OWN)
    cross[OWN].wait_recv()

    def relay_add(slot, r, start, got):
        def body(i, none):
            at = pl.ds(pl.multiple_of(i * step, step), step)
            here = pl.ds(pl.multiple_of(start + i * step, step), step)
            relay[slot, at] = (total[r, here].astype(f32) + got[1, at].astype(f32)).astype(
                relay.dtype
            )
            return none

        lax.fori_loop(0, half // step, body, 0)

    x_diag.wait_recv()
    relay_add(0, ACROSS_Y, 0, rx)
    y_last.start()
    y_diag.wait_recv()
    relay_add(1, ACROSS_X, half, ry)
    x_last.start()

    def finish(start, near, last):
        def body(i, none):
            at = pl.ds(pl.multiple_of(i * step, step), step)
            here = pl.ds(pl.multiple_of(start + i * step, step), step)
            o_ref[here] = (own[OWN, here].astype(f32) + other[OWN, here].astype(f32)) + (
                near[0, at].astype(f32) + last[at].astype(f32)
            )
            return none

        lax.fori_loop(0, half // step, body, 0)

    x_near.wait_recv()
    y_last.wait_recv()
    finish(0, rx, ry_last)
    y_near.wait_recv()
    x_last.wait_recv()
    finish(half, ry, rx_last)
    for one in cross + [x_diag, y_diag, x_near, y_near, x_last, y_last]:
        one.wait_send()


def scatter_kernel(
    p_ref, o_ref, own, other, total, rx, ry, relay, rx_last, ry_last, lsem, ssem, rsem
):
    loads = [pltpu.make_async_copy(p_ref.at[r], own.at[r], lsem.at[r]) for r in range(4)]
    for r in (DIAGONAL, ACROSS_X, ACROSS_Y, OWN):
        loads[r].start()
    scatter_flow(
        lambda r: p_ref.at[4 + r], o_ref, own, other, total, rx, ry, relay, rx_last, ry_last,
        ssem, rsem, None, lambda: None, lambda r, cross: cross[r].start(),
        lambda r: loads[r].wait(),
    )


def scatter_dot_kernel(
    a_ref, w_ref, b_ref, o_ref, e_ref, theirs, own, other, total, rx, ry, relay, rx_last, ry_last,
    ssem, rsem, local_sem, xssem, xrsem
):
    peers, kept, copies = exchange_parts(FEAT, b_ref, e_ref, local_sem, xssem, xrsem)
    rows, width = o_ref.shape
    tile = 512

    def begin():
        kept.start()
        for one in copies:
            one.start()

    def dot_into(block, ref, r):
        rows_in = a_ref[pl.ds(block * rows, rows)]

        def body(j, none):
            at = pl.ds(pl.multiple_of(j * tile, tile), tile)
            ref[r, :, at] = lax.dot_general(
                rows_in, w_ref[at], contract_last, preferred_element_type=f32
            ).astype(ref.dtype)
            return none

        lax.fori_loop(0, width // tile, body, 0)

    def stage(r, cross):
        dot_into(4 + r, theirs, r)
        cross[r].start()
        dot_into(r, own, r)

    scatter_flow(
        lambda r: theirs.at[r], o_ref, own, other, total, rx, ry, relay, rx_last, ry_last,
        ssem, rsem, peers, begin, stage, lambda r: None,
    )
    for one in copies:
        one.wait()
    kept.wait()


def scatter_dot(rows_in, w, blocks):
    rows, width = rows_in.shape[0] // NF, w.shape[0]
    half = rows // 2
    kind = rows_in.dtype
    four = pltpu.VMEM((4, rows, width), kind)
    two = pltpu.VMEM((2, half, width), kind)
    one = pltpu.VMEM((half, width), kind)
    return pl.pallas_call(
        scatter_dot_kernel,
        out_shape=(
            jax.ShapeDtypeStruct((rows, width), f32),
            jax.ShapeDtypeStruct(blocks.shape, blocks.dtype),
        ),
        in_specs=[vmem_spec()] * 3,
        out_specs=(vmem_spec(), hbm_spec()),
        scratch_shapes=[four] * 4
        + [two] * 3
        + [one] * 2
        + [
            pltpu.SemaphoreType.DMA((10,)),
            pltpu.SemaphoreType.DMA((10,)),
            pltpu.SemaphoreType.DMA,
            pltpu.SemaphoreType.DMA((NF - 1,)),
            pltpu.SemaphoreType.DMA((NF - 1,)),
        ],
        compiler_params=pltpu.CompilerParams(
            collective_id=11, has_side_effects=True, vmem_limit_bytes=VMEM_LIMIT
        ),
        cost_estimate=cost(55),
        name="scatter_dot",
    )(rows_in, w, blocks)


def scatter_feature(partial):
    rows, width = partial.shape[0] // NF, partial.shape[1]
    half = rows // 2
    kind = partial.dtype
    return pl.pallas_call(
        scatter_kernel,
        out_shape=jax.ShapeDtypeStruct((rows, width), f32),
        in_specs=[hbm_spec()],
        out_specs=vmem_spec(),
        scratch_shapes=[
            pltpu.VMEM((4, rows, width), kind),
            pltpu.VMEM((4, rows, width), kind),
            pltpu.VMEM((4, rows, width), kind),
            pltpu.VMEM((2, half, width), kind),
            pltpu.VMEM((2, half, width), kind),
            pltpu.VMEM((2, half, width), kind),
            pltpu.VMEM((half, width), kind),
            pltpu.VMEM((half, width), kind),
            pltpu.SemaphoreType.DMA((4,)),
            pltpu.SemaphoreType.DMA((10,)),
            pltpu.SemaphoreType.DMA((10,)),
        ],
        compiler_params=pltpu.CompilerParams(
            collective_id=1, has_side_effects=True, vmem_limit_bytes=VMEM_LIMIT
        ),
        cost_estimate=cost(45),
        name="scatter_feature",
    )(partial.reshape(NF, rows, width))


def across(value, axis):
    return lax.ppermute(value, axis, [(0, 1), (1, 0)])


def hold(*values):
    return lax.optimization_barrier(values)


def gather_near(block):
    return across(block, "x"), across(block, "y")


def gather_diagonal(by_x, by_y):
    half = by_x.shape[0] // 2
    return across(by_x[:half], "y"), across(by_y[half:], "x")


def gather_chip(block, by_x, by_y, d_top, d_low):
    return jnp.concatenate([block, by_y, by_x, d_top, d_low])


def scatter_halves(mine, got):
    shape = (4, 2, mine.shape[0] // 8, mine.shape[1])
    return mine.reshape(shape), got.reshape(shape)


def add_low(a, b):
    return (a.astype(f32) + b.astype(f32)).astype(a.dtype)


def scatter_sends(mine, got):
    mine, got = scatter_halves(mine, got)
    by_x = add_low(mine[ACROSS_X:, 0], got[ACROSS_X:, 0])
    by_y = add_low(mine[ACROSS_Y::2, 1], got[ACROSS_Y::2, 1])
    return by_x, by_y


def scatter_keeps(mine, got):
    mine, got = scatter_halves(mine, got)
    near_y = add_low(mine[ACROSS_Y, 0], got[ACROSS_Y, 0])
    near_x = add_low(mine[ACROSS_X, 1], got[ACROSS_X, 1])
    return near_y, near_x, add_low(mine[OWN], got[OWN])


def scatter_near(mine, got):
    mine, got = hold(mine, got)
    by_x, by_y = scatter_sends(mine, got)
    by_x, by_y, mine, got = hold(by_x, by_y, mine, got)
    return scatter_keeps(mine, got), across(by_x, "x"), across(by_y, "y")


def scatter_relay(keeps, by_x, by_y):
    near_y, near_x, _ = keeps
    return across(add_low(near_y, by_x[1]), "y"), across(add_low(near_x, by_y[1]), "x")


def scatter_sum(keeps, by_x, by_y, y_last, x_last):
    own = keeps[2].astype(f32)
    upper = own[0] + by_x[0].astype(f32) + y_last.astype(f32)
    lower = own[1] + by_y[0].astype(f32) + x_last.astype(f32)
    return jnp.concatenate([upper, lower])


def gather_tail_kernel(x_ref, bx_ref, by_ref, o_ref, lsem, ssem, rsem):
    x, y, c = feature_place()
    to_x, to_y, to_c = {"x": 1 - x}, {"y": 1 - y}, {"c": 1 - c}
    half = x_ref.shape[0] // 2
    top, low = pl.ds(0, half), pl.ds(half, half)

    def copy(i, src, dst, device):
        return remote(src, dst, ssem.at[i], rsem.at[i], device)

    places = ((x_ref, OWN), (by_ref, ACROSS_Y), (bx_ref, ACROSS_X))
    local = [
        pltpu.make_async_copy(ref, o_ref.at[slot], lsem.at[i])
        for i, (ref, slot) in enumerate(places)
    ]
    greet((to_x, to_y, to_c))
    y_fwd = copy(0, bx_ref.at[top], o_ref.at[DIAGONAL, top], to_y)
    x_fwd = copy(1, by_ref.at[low], o_ref.at[DIAGONAL, low], to_x)
    cross = [
        copy(2 + i, ref, o_ref.at[4 + slot], to_c) for i, (ref, slot) in enumerate(places)
    ]
    last = copy(5, o_ref.at[DIAGONAL], o_ref.at[4 + DIAGONAL], to_c)
    for one in [y_fwd, x_fwd] + cross + local:
        one.start()
    y_fwd.wait_recv()
    x_fwd.wait_recv()
    last.start()
    for one in cross + [last]:
        one.wait_recv()
    for one in cross + [y_fwd, x_fwd, last]:
        one.wait_send()
    for one in local:
        one.wait()


def gather_tail(block, by_x, by_y):
    rows, width = block.shape
    out = pl.pallas_call(
        gather_tail_kernel,
        out_shape=jax.ShapeDtypeStruct((NF, rows, width), block.dtype),
        in_specs=[vmem_spec()] * 3,
        out_specs=hbm_spec(),
        scratch_shapes=[
            pltpu.SemaphoreType.DMA((3,)),
            pltpu.SemaphoreType.DMA((6,)),
            pltpu.SemaphoreType.DMA((6,)),
        ],
        compiler_params=pltpu.CompilerParams(
            collective_id=8, has_side_effects=True, vmem_limit_bytes=VMEM_LIMIT
        ),
        cost_estimate=cost(16),
        name="gather_tail",
    )(block, by_x, by_y)
    return out.reshape(NF * rows, width)


def scatter_tail_kernel(
    ny_ref, nx_ref, own_ref, bx_ref, by_ref, o_ref, near, own, bx, by, relay, last, lsem, ssem, rsem
):
    x, y, c = feature_place()
    to_x, to_y = {"x": 1 - x}, {"y": 1 - y}
    half = o_ref.shape[0] // 2
    step = 16

    def load(i, src, dst):
        one = pltpu.make_async_copy(src, dst, lsem.at[i])
        one.start()
        return one

    loads = [
        load(0, ny_ref, near.at[0]),
        load(1, bx_ref, bx),
        load(2, nx_ref, near.at[1]),
        load(3, by_ref, by),
        load(4, own_ref, own),
    ]
    greet((to_x, to_y))
    sends = [
        remote(relay.at[0], last.at[0], ssem.at[0], rsem.at[0], to_y),
        remote(relay.at[1], last.at[1], ssem.at[1], rsem.at[1], to_x),
    ]

    def tiles(body):
        def one(i, none):
            body(pl.ds(pl.multiple_of(i * step, step), step), i * step)
            return none

        lax.fori_loop(0, half // step, one, 0)

    for side, got in ((0, bx), (1, by)):
        loads[2 * side].wait()
        loads[2 * side + 1].wait()

        def add(at, _, side=side, got=got):
            relay[side, at] = (near[side, at].astype(f32) + got[1, at].astype(f32)).astype(
                relay.dtype
            )

        tiles(add)
        sends[side].start()
    loads[4].wait()
    for side, got in ((0, bx), (1, by)):

        def base(at, start, side=side, got=got):
            here = pl.ds(pl.multiple_of(side * half + start, step), step)
            o_ref[here] = own[side, at].astype(f32) + got[0, at].astype(f32)

        tiles(base)
    for side in range(2):
        sends[side].wait_recv()

        def finish(at, start, side=side):
            here = pl.ds(pl.multiple_of(side * half + start, step), step)
            o_ref[here] = o_ref[here] + last[side, at].astype(f32)

        tiles(finish)
    for one in sends:
        one.wait_send()


def scatter_tail(keeps, by_x, by_y):
    _, half, width = by_x.shape
    kind = by_x.dtype
    pair = pltpu.VMEM((2, half, width), kind)
    return pl.pallas_call(
        scatter_tail_kernel,
        out_shape=jax.ShapeDtypeStruct((2 * half, width), f32),
        in_specs=[hbm_spec()] * 5,
        out_specs=vmem_spec(),
        scratch_shapes=[pair] * 6
        + [
            pltpu.SemaphoreType.DMA((5,)),
            pltpu.SemaphoreType.DMA((2,)),
            pltpu.SemaphoreType.DMA((2,)),
        ],
        compiler_params=pltpu.CompilerParams(
            collective_id=9, has_side_effects=True, vmem_limit_bytes=VMEM_LIMIT
        ),
        cost_estimate=cost(16),
        name="scatter_tail",
    )(*keeps, by_x, by_y)


def exchange_parts(axes, x_ref, o_ref, local_sem, ssem, rsem):
    place = [lax.axis_index(name) for name in axes]
    count = 2 ** len(axes)

    def rank(coords):
        total = 0
        for one in coords:
            total = total * 2 + one
        return total

    mine = rank(place)
    own = pltpu.make_async_copy(x_ref.at[mine], o_ref.at[mine], local_sem)
    peers, copies = [], []
    for mask in range(count - 1, 0, -1):
        bits = [(mask // 2 ** (len(axes) - 1 - i)) % 2 for i in range(len(axes))]
        coords = [1 - p if bit else p for p, bit in zip(place, bits)]
        device = {name: q for name, q, bit in zip(axes, coords, bits) if bit}
        peers.append(device)
        copies.append(
            remote(
                x_ref.at[rank(coords)],
                o_ref.at[mine],
                ssem.at[mask - 1],
                rsem.at[mask - 1],
                device,
            )
        )
    return peers, own, copies


def exchange_kernel(axes, *refs):
    count = (len(refs) - 3) // 2
    sources, targets = refs[:count], refs[count : 2 * count]
    local_sem, ssem, rsem = refs[2 * count :]
    parts = [
        exchange_parts(axes, sources[i], targets[i], local_sem.at[i], ssem.at[i], rsem.at[i])
        for i in range(count)
    ]
    for _, own, _ in parts:
        own.start()
    greet(parts[0][0])
    for _, _, copies in parts:
        for one in copies:
            one.start()
    for _, own, copies in parts:
        for one in copies:
            one.wait()
        own.wait()


def exchange(arrays, axes, ident):
    peers = 2 ** len(axes) - 1
    count = len(arrays)
    return pl.pallas_call(
        functools.partial(exchange_kernel, axes),
        out_shape=tuple(jax.ShapeDtypeStruct(a.shape, a.dtype) for a in arrays),
        in_specs=[vmem_spec()] * count,
        out_specs=(hbm_spec(),) * count,
        scratch_shapes=[
            pltpu.SemaphoreType.DMA((count,)),
            pltpu.SemaphoreType.DMA((count, peers)),
            pltpu.SemaphoreType.DMA((count, peers)),
        ],
        compiler_params=pltpu.CompilerParams(
            collective_id=ident, has_side_effects=True, vmem_limit_bytes=VMEM_LIMIT
        ),
        cost_estimate=cost(15),
        name="exchange",
    )(*arrays)


def gather_exchange(block, blocks):
    rows, width = block.shape
    out, got = pl.pallas_call(
        gather_kernel,
        out_shape=(
            jax.ShapeDtypeStruct((NF, rows, width), block.dtype),
            jax.ShapeDtypeStruct(blocks.shape, blocks.dtype),
        ),
        in_specs=[vmem_spec()] * 2,
        out_specs=(hbm_spec(),) * 2,
        scratch_shapes=[
            pltpu.SemaphoreType.DMA,
            pltpu.SemaphoreType.DMA((10,)),
            pltpu.SemaphoreType.DMA((10,)),
            pltpu.SemaphoreType.DMA,
            pltpu.SemaphoreType.DMA((NF - 1,)),
            pltpu.SemaphoreType.DMA((NF - 1,)),
        ],
        compiler_params=pltpu.CompilerParams(
            collective_id=4, has_side_effects=True, vmem_limit_bytes=VMEM_LIMIT
        ),
        cost_estimate=cost(55),
        name="gather_exchange",
    )(block, blocks)
    return out.reshape(NF * rows, width), got


def groups_kernel(count, x_ref, o_ref, local_sem, ssem, rsem):
    z = lax.axis_index("z")
    own = pltpu.make_async_copy(x_ref, o_ref.at[z], local_sem)
    own.start()
    targets = [{"z": lax.rem(z + hop, count)} for hop in range(1, count)]
    greet(targets)
    copies = [
        remote(x_ref, o_ref.at[z], ssem.at[i], rsem.at[i], device)
        for i, device in enumerate(targets)
    ]
    for one in copies:
        one.start()
    for one in copies:
        one.wait()
    own.wait()


def gather_groups(block, count, ident):
    return pl.pallas_call(
        functools.partial(groups_kernel, count),
        out_shape=jax.ShapeDtypeStruct((count,) + block.shape, block.dtype),
        in_specs=[vmem_spec()],
        out_specs=vmem_spec(),
        scratch_shapes=[
            pltpu.SemaphoreType.DMA,
            pltpu.SemaphoreType.DMA((count - 1,)),
            pltpu.SemaphoreType.DMA((count - 1,)),
        ],
        compiler_params=pltpu.CompilerParams(collective_id=ident, has_side_effects=True),
        cost_estimate=cost(5),
        name="gather_groups",
    )(block)


def gelu_tanh(values):
    return jax.nn.gelu(values, approximate=True)


def sigmoid(v):
    return 0.5 + 0.5 * jnp.tanh(0.5 * v)


def gelu_pair(v):
    root = 0.7978845608028654
    cube = 0.044715
    square = v * v
    t = jnp.tanh(root * (v + cube * square * v))
    value = 0.5 * v * (1.0 + t)
    slope = 0.5 * (1.0 + t) + 0.5 * v * (1.0 - t * t) * root * (1.0 + 3.0 * cube * square)
    return value, slope


def tile_scan(keep, push, reverse):
    rows = lax.broadcasted_iota(jnp.int32, keep.shape, 0)
    count = keep.shape[0]
    hop = 1
    while hop < count:
        if reverse:
            inside = rows < count - hop
            shift = count - hop
        else:
            inside = rows >= hop
            shift = hop
        keep_near = jnp.where(inside, pltpu.roll(keep, shift, 0), 1.0)
        push_near = jnp.where(inside, pltpu.roll(push, shift, 0), 0.0)
        push = push + keep * push_near
        keep = keep * keep_near
        hop *= 2
    return keep, push


def conv_of(ext, masks, taps, offset, rows):
    value = offset + taps[0:1] * ext[pl.ds(8, rows)]
    for k in range(1, CONV):
        value = value + taps[k : k + 1] * ext[pl.ds(8 - k, rows)] * masks[:, k - 1 : k]
    return value


def forward_kernel(
    order_ref,
    pre_ref,
    halo_ref,
    mask_ref,
    small_ref,
    wa_ref,
    wx_ref,
    branch_ref,
    conved_ref,
    keep_ref,
    prod_ref,
    state_ref,
    ends_ref,
    ext,
    carry,
):
    rows, width = branch_ref.shape
    step = pl.program_id(0)
    branch = pre_ref[:, width : 2 * width].astype(bf16)
    branch_ref[...] = branch

    @pl.when(step == 0)
    def _():
        ext[pl.ds(0, 8)] = halo_ref[...]
        carry[0:1] = jnp.ones_like(carry[0:1])
        carry[1:2] = jnp.zeros_like(carry[1:2])

    @pl.when(step > 0)
    def _():
        ext[pl.ds(0, 8)] = ext[pl.ds(rows, 8)]

    ext[pl.ds(8, rows)] = branch.astype(f32)
    masks = mask_ref[...]
    conved = conv_of(ext, masks, small_ref, small_ref[4:5], rows).astype(bf16)
    conved_ref[...] = conved
    logit_a = jnp.dot(conved, wa_ref[...], preferred_element_type=f32) + small_ref[5:6]
    logit_x = jnp.dot(conved, wx_ref[...], preferred_element_type=f32) + small_ref[6:7]
    decay = jnp.exp(-decay_scale * sigmoid(logit_a) * small_ref[7:8])
    keep_ref[...] = decay * masks[:, 0:1]
    state_ref[...] = (
        jnp.sqrt(1.0 - decay * decay + push_shift) * sigmoid(logit_x) * conved.astype(f32)
    )

    def body(i, held):
        prod_in, state_in = held
        at = pl.ds(pl.multiple_of(i * 8, 8), 8)
        keep, push = tile_scan(keep_ref[at], state_ref[at], False)
        state = push + keep * state_in
        prod = keep * prod_in
        prod_ref[at] = prod
        state_ref[at] = state
        return prod[7:8], state[7:8]

    prod_out, state_out = lax.fori_loop(
        0, rows // 8, body, (carry[0:1], carry[1:2]), unroll=4
    )
    carry[0:1] = prod_out
    carry[1:2] = state_out
    ends_ref[0:1] = prod_out
    ends_ref[1:2] = state_out
    ends_ref[2:8] = jnp.zeros_like(ends_ref[2:8])


def forward_scan(order, rec_pre, halo, masks, small, wa, wx, chunk):
    rows, width = rec_pre.shape[0], rec_pre.shape[1] // 2
    tile = pl.BlockSpec((chunk, width), lambda i, order: (order[i], 0))
    whole = lambda a: pl.BlockSpec(a.shape, lambda i, order: (0, 0))
    full = jax.ShapeDtypeStruct((rows, width), f32)
    low = jax.ShapeDtypeStruct((rows, width), bf16)
    return pl.pallas_call(
        forward_kernel,
        out_shape=(
            low,
            low,
            full,
            full,
            full,
            jax.ShapeDtypeStruct((8, width), f32),
        ),
        grid_spec=pltpu.PrefetchScalarGridSpec(
            num_scalar_prefetch=1,
            grid=(rows // chunk,),
            in_specs=[
                pl.BlockSpec((chunk, 2 * width), lambda i, order: (order[i], 0)),
                whole(halo),
                pl.BlockSpec((chunk, masks.shape[1]), lambda i, order: (i, 0)),
                whole(small),
                whole(wa),
                whole(wx),
            ],
            out_specs=(tile,) * 5 + (pl.BlockSpec((8, width), lambda i, order: (0, 0)),),
            scratch_shapes=[pltpu.VMEM((chunk + 8, width), f32), pltpu.VMEM((8, width), f32)],
        ),
        compiler_params=pltpu.CompilerParams(vmem_limit_bytes=VMEM_LIMIT),
        cost_estimate=cost(15),
        name="forward_scan",
    )(order, rec_pre, halo, masks, small, wa, wx)


def adjoint_kernel(
    order_ref, d_mixed_ref, pre_ref, keep_ref, prod_ref, adj_ref, heads_ref, keep_next, carry
):
    rows = d_mixed_ref.shape[0]
    step = pl.program_id(0)

    @pl.when(step == 0)
    def _():
        keep_next[pl.ds(rows, 8)] = jnp.ones_like(keep_next[pl.ds(rows, 8)])
        carry[0:1] = jnp.ones_like(carry[0:1])
        carry[1:2] = jnp.zeros_like(carry[1:2])

    @pl.when(step > 0)
    def _():
        keep_next[pl.ds(rows, 8)] = keep_next[pl.ds(0, 8)]

    keep_next[pl.ds(0, rows)] = keep_ref[...]
    prod_ref[...] = keep_next[pl.ds(1, rows)]
    adj_ref[...] = d_mixed_ref[...] * gelu_tanh(pre_ref[:, 0 : adj_ref.shape[1]])
    tiles = rows // 8

    def body(i, held):
        prod_in, adj_in = held
        at = pl.ds(pl.multiple_of((tiles - 1 - i) * 8, 8), 8)
        keep, push = tile_scan(prod_ref[at], adj_ref[at], True)
        adj = push + keep * adj_in
        prod = keep * prod_in
        prod_ref[at] = prod
        adj_ref[at] = adj
        return prod[0:1], adj[0:1]

    prod_out, adj_out = lax.fori_loop(
        0, tiles, body, (carry[0:1], carry[1:2]), unroll=4
    )
    carry[0:1] = prod_out
    carry[1:2] = adj_out
    heads_ref[0:1] = keep_ref[0:1] * prod_out
    heads_ref[1:2] = keep_ref[0:1] * adj_out
    heads_ref[2:8] = jnp.zeros_like(heads_ref[2:8])


def adjoint_scan(order, d_mixed, rec_pre, keep, chunk):
    rows, width = keep.shape
    last = rows // chunk - 1
    tile = pl.BlockSpec((chunk, width), lambda i, order: (order[last - i], 0))
    full = jax.ShapeDtypeStruct((rows, width), f32)
    return pl.pallas_call(
        adjoint_kernel,
        out_shape=(full, full, jax.ShapeDtypeStruct((8, width), f32)),
        grid_spec=pltpu.PrefetchScalarGridSpec(
            num_scalar_prefetch=1,
            grid=(rows // chunk,),
            in_specs=[
                tile,
                pl.BlockSpec((chunk, 2 * width), lambda i, order: (order[last - i], 0)),
                tile,
            ],
            out_specs=(tile, tile, pl.BlockSpec((8, width), lambda i, order: (0, 0))),
            scratch_shapes=[pltpu.VMEM((chunk + 8, width), f32), pltpu.VMEM((8, width), f32)],
        ),
        compiler_params=pltpu.CompilerParams(vmem_limit_bytes=VMEM_LIMIT),
        cost_estimate=cost(12),
        name="adjoint_scan",
    )(order, d_mixed, rec_pre, keep)


def backward_kernel(
    order_ref,
    d_mixed_ref,
    pre_ref,
    state_ref,
    prod_ref,
    state_before_ref,
    prod_before_ref,
    adj_ref,
    adj_prod_ref,
    branch_ref,
    branch_before_ref,
    halo_ref,
    conved_ref,
    mask_ref,
    small_ref,
    enter_ref,
    wa_ref,
    wx_ref,
    d_pre_ref,
    sums_ref,
    edge_ref,
    ga_ref,
    gx_ref,
    ext,
    state_ext,
    later,
):
    rows, width = d_mixed_ref.shape
    step = pl.program_id(0)
    steps = pl.num_programs(0)
    state_in = enter_ref[0:1]
    adj_in = enter_ref[1:2]

    @pl.when(step == 0)
    def _():
        sums_ref[...] = jnp.zeros_like(sums_ref)
        ga_ref[...] = jnp.zeros_like(ga_ref)
        gx_ref[...] = jnp.zeros_like(gx_ref)
        for k in range(TAIL):
            later[k, pl.ds(rows, 8)] = jnp.zeros((8, width), f32)

    @pl.when(step > 0)
    def _():
        for k in range(TAIL):
            later[k, pl.ds(rows, 8)] = later[k, pl.ds(0, 8)]

    first = step == steps - 1

    @pl.when(first)
    def _():
        ext[pl.ds(0, 8)] = halo_ref[...]
        state_ext[pl.ds(0, 8)] = jnp.broadcast_to(state_in, (8, width))

    @pl.when(jnp.logical_not(first))
    def _():
        ext[pl.ds(0, 8)] = branch_before_ref[...].astype(f32)[8:16]
        state_ext[pl.ds(0, 8)] = state_before_ref[...] + prod_before_ref[...] * state_in

    ext[pl.ds(8, rows)] = branch_ref[...].astype(f32)
    state = state_ref[...] + prod_ref[...] * state_in
    state_ext[pl.ds(8, rows)] = state
    _, slope = gelu_pair(pre_ref[:, 0:width])
    d_pre_ref[:, 0:width] = (d_mixed_ref[...] * state * slope).astype(bf16)
    adjoint = adj_ref[...] + adj_prod_ref[...] * adj_in
    state_prev = state_ext[pl.ds(7, rows)]
    masks = mask_ref[...]
    conved_low = conved_ref[...]
    conved = conved_low.astype(f32)
    rates = small_ref[7:8]
    gate_a = sigmoid(
        jnp.dot(conved_low, wa_ref[...], preferred_element_type=f32) + small_ref[5:6]
    )
    gate_x = sigmoid(
        jnp.dot(conved_low, wx_ref[...], preferred_element_type=f32) + small_ref[6:7]
    )
    decay = jnp.exp(-decay_scale * gate_a * rates)
    square = 1.0 - decay * decay + push_shift
    inverse = lax.rsqrt(square)
    root = square * inverse
    d_decay = adjoint * (state_prev * masks[:, 0:1] - gate_x * conved * decay * inverse)
    slope_a = -decay_scale * d_decay * decay * gate_a
    d_logit_a = (slope_a * rates * (1.0 - gate_a)).astype(bf16)
    through = adjoint * root * gate_x
    d_logit_x = (through * conved * (1.0 - gate_x)).astype(bf16)
    d_conved = (
        through
        + lax.dot_general(d_logit_a, wa_ref[...], contract_last, preferred_element_type=f32)
        + lax.dot_general(d_logit_x, wx_ref[...], contract_last, preferred_element_type=f32)
    )
    d_conved = d_conved.astype(bf16).astype(f32)
    ga_ref[...] += lax.dot_general(
        conved_low, d_logit_a, contract_first, preferred_element_type=f32
    )
    gx_ref[...] += lax.dot_general(
        conved_low, d_logit_x, contract_first, preferred_element_type=f32
    )

    def total(v):
        return jnp.sum(v, axis=0, keepdims=True)

    sums_ref[0:1] += total(d_conved * ext[pl.ds(8, rows)])
    for k in range(1, CONV):
        masked = d_conved * masks[:, k - 1 : k]
        later[k - 1, pl.ds(0, rows)] = masked
        sums_ref[k : k + 1] += total(masked * ext[pl.ds(8 - k, rows)])
    sums_ref[4:5] += total(d_conved)
    sums_ref[5:6] += total(d_logit_a.astype(f32))
    sums_ref[6:7] += total(d_logit_x.astype(f32))
    sums_ref[7:8] += total(slope_a)
    d_branch = small_ref[0:1] * d_conved
    for k in range(1, CONV):
        d_branch = d_branch + small_ref[k : k + 1] * later[k - 1, pl.ds(k, rows)]
    d_pre_ref[:, width : 2 * width] = d_branch.astype(bf16)

    @pl.when(first)
    def _():
        for back in range(1, CONV):
            value = jnp.zeros((1, width), f32)
            for k in range(back, CONV):
                value = value + small_ref[k : k + 1] * later[k - 1, pl.ds(k - back, 1)]
            edge_ref[8 - back : 9 - back] = value
        edge_ref[0 : 8 - TAIL] = jnp.zeros((8 - TAIL, width), f32)


def backward_scan(
    order, d_mixed, rec_pre, state, prod, adj, adj_prod, branch_in, halo, conved, masks, small,
    enter, wa, wx, chunk,
):
    rows, width = state.shape
    last = rows // chunk - 1
    tile = pl.BlockSpec((chunk, width), lambda i, order: (order[last - i], 0))

    def before(size):
        per = chunk // size
        return pl.BlockSpec(
            (size, width),
            lambda i, order: (order[jnp.maximum(last - i - 1, 0)] * per + per - 1, 0),
        )

    pinned = lambda shape: pl.BlockSpec(shape, lambda i, order: (0, 0))
    whole = lambda a: pinned(a.shape)
    return pl.pallas_call(
        backward_kernel,
        out_shape=(
            jax.ShapeDtypeStruct((rows, 2 * width), bf16),
            jax.ShapeDtypeStruct((8, width), f32),
            jax.ShapeDtypeStruct((8, width), f32),
            jax.ShapeDtypeStruct((width, width), f32),
            jax.ShapeDtypeStruct((width, width), f32),
        ),
        grid_spec=pltpu.PrefetchScalarGridSpec(
            num_scalar_prefetch=1,
            grid=(rows // chunk,),
            in_specs=[
                tile,
                pl.BlockSpec((chunk, 2 * width), lambda i, order: (order[last - i], 0)),
                tile,
                tile,
                before(8),
                before(8),
                tile,
                tile,
                tile,
                before(16),
                whole(halo),
                tile,
                pl.BlockSpec((chunk, masks.shape[1]), lambda i, order: (last - i, 0)),
                whole(small),
                whole(enter),
                whole(wa),
                whole(wx),
            ],
            out_specs=(
                pl.BlockSpec((chunk, 2 * width), lambda i, order: (order[last - i], 0)),
                pinned((8, width)),
                pinned((8, width)),
                pinned((width, width)),
                pinned((width, width)),
            ),
            scratch_shapes=[
                pltpu.VMEM((chunk + 8, width), f32),
                pltpu.VMEM((chunk + 8, width), f32),
                pltpu.VMEM((TAIL, chunk + 8, width), f32),
            ],
        ),
        compiler_params=pltpu.CompilerParams(vmem_limit_bytes=VMEM_LIMIT),
        cost_estimate=cost(21),
        name="backward_scan",
    )(
        order, d_mixed, rec_pre, state, prod, state, prod, adj, adj_prod, branch_in, branch_in,
        halo, conved, masks, small, enter, wa, wx,
    )


def gated_kernel(n_ref, mine_ref, theirs_ref, w_ref, down_ref, hidden_ref, d_ref):
    ff = down_ref.shape[0]
    tile = 256
    normed = n_ref[...]
    cot = lax.select(
        pl.program_id(0) < pl.num_programs(0) // 2, mine_ref[...], theirs_ref[...]
    )

    def body(j, none):
        at = pl.ds(pl.multiple_of(j * tile, tile), tile)
        up_at = pl.ds(pl.multiple_of(ff + j * tile, tile), tile)
        gate = jnp.dot(normed, w_ref[:, at], preferred_element_type=f32)
        up = jnp.dot(normed, w_ref[:, up_at], preferred_element_type=f32)
        d_hidden = lax.dot_general(cot, down_ref[at], contract_last, preferred_element_type=f32)
        act, slope = gelu_pair(gate)
        hidden_ref[:, at] = (act * up).astype(bf16)
        d_ref[:, at] = (d_hidden * up * slope).astype(bf16)
        d_ref[:, up_at] = (d_hidden * act).astype(bf16)
        return none

    lax.fori_loop(0, ff // tile, body, 0)


def gated_unit(normed, cot_mine, cot_theirs, w_mlp, w_down):
    rows, width = normed.shape
    ff = w_down.shape[0]
    steps = 4
    tile = rows // steps
    row = lambda size: pl.BlockSpec((tile, size), lambda i: (i, 0))
    once = lambda a: pl.BlockSpec(a.shape, lambda i: (0, 0), pipeline_mode=pl.Buffered(1))
    return pl.pallas_call(
        gated_kernel,
        grid=(steps,),
        out_shape=(
            jax.ShapeDtypeStruct((rows, ff), bf16),
            jax.ShapeDtypeStruct((rows, 2 * ff), bf16),
        ),
        in_specs=[
            row(width),
            pl.BlockSpec((tile, width), lambda i: (jnp.minimum(i, steps // 2 - 1), 0)),
            pl.BlockSpec((tile, width), lambda i: (jnp.maximum(i - steps // 2, 0), 0)),
            once(w_mlp),
            once(w_down),
        ],
        out_specs=(row(ff), row(2 * ff)),
        compiler_params=pltpu.CompilerParams(vmem_limit_bytes=VMEM_LIMIT),
        cost_estimate=pl.CostEstimate(
            flops=6 * rows * width * ff, bytes_accessed=40 * 2**20, transcendentals=rows * ff
        ),
        name="gated_unit",
    )(normed, cot_mine, cot_theirs, w_mlp, w_down)


def down_kernel(h_ref, w_ref, mine_ref, theirs_ref):
    width = w_ref.shape[1]
    tile = 512
    hidden = h_ref[...]

    def into(ref):
        def body(j, none):
            at = pl.ds(pl.multiple_of(j * tile, tile), tile)
            ref[:, at] = jnp.dot(hidden, w_ref[:, at], preferred_element_type=f32).astype(bf16)
            return none

        lax.fori_loop(0, width // tile, body, 0)

    first = pl.program_id(0) < pl.num_programs(0) // 2
    pl.when(first)(lambda: into(mine_ref))
    pl.when(jnp.logical_not(first))(lambda: into(theirs_ref))


def down_rows(hidden, w_down):
    rows, ff = hidden.shape
    width = w_down.shape[1]
    steps = 4
    tile = rows // steps
    part = jax.ShapeDtypeStruct((rows // 2, width), bf16)
    return pl.pallas_call(
        down_kernel,
        grid=(steps,),
        out_shape=(part, part),
        in_specs=[
            pl.BlockSpec((tile, ff), lambda i: (i, 0)),
            pl.BlockSpec((ff, width), lambda i: (0, 0), pipeline_mode=pl.Buffered(1)),
        ],
        out_specs=(
            pl.BlockSpec((tile, width), lambda i: (jnp.minimum(i, steps // 2 - 1), 0)),
            pl.BlockSpec((tile, width), lambda i: (jnp.maximum(i - steps // 2, 0), 0)),
        ),
        compiler_params=pltpu.CompilerParams(vmem_limit_bytes=VMEM_LIMIT),
        cost_estimate=cost(0.1),
        name="down_rows",
    )(hidden, w_down)


def split_kernel(moves, a_ref, b_ref, o_ref):
    for source, block, at, start, size in moves:
        ref = (a_ref, b_ref)[source]
        o_ref[block, :, at : at + size] = ref[:, start : start + size]


def join_kernel(moves, x_ref, a_ref, b_ref, g_ref, oa_ref, ob_ref, og_ref):
    for source, block, at, start, size in moves:
        ref = (oa_ref, ob_ref)[source]
        ref[:, start : start + size] = x_ref[block, :, at : at + size].astype(f32)
    total = jnp.sum(a_ref[...].astype(f32) * oa_ref[...], axis=1, keepdims=True) + jnp.sum(
        b_ref[...].astype(f32) * ob_ref[...], axis=1, keepdims=True
    )
    wide = jnp.broadcast_to(total / g_ref[...], (total.shape[0], LANES))
    og_ref[...] = wide.T[0:1]


def split_blocks(a, b, moves):
    rows, width = a.shape
    return pl.pallas_call(
        functools.partial(split_kernel, moves),
        out_shape=jax.ShapeDtypeStruct((NF, rows, 2 * width // NF), a.dtype),
        compiler_params=pltpu.CompilerParams(vmem_limit_bytes=VMEM_LIMIT),
        cost_estimate=cost(4),
        name="split_blocks",
    )(a, b)


def join_blocks(x, a, b, gain, moves):
    rows, width = a.shape
    out = jax.ShapeDtypeStruct((rows, width), f32)
    return pl.pallas_call(
        functools.partial(join_kernel, moves),
        out_shape=(out, out, jax.ShapeDtypeStruct((1, rows), f32)),
        compiler_params=pltpu.CompilerParams(vmem_limit_bytes=VMEM_LIMIT),
        cost_estimate=cost(5),
        name="join_blocks",
    )(x, a, b, gain)


def unpack_kernel(x_ref, out_ref, ga_ref, gx_ref, taps_ref, *row_refs):
    width = out_ref.shape[1]
    base = width + 2 * BLK
    out_ref[...] = x_ref[:, 0:width].astype(f32)
    ga_ref[...] = x_ref[:, width : width + BLK].astype(f32)
    gx_ref[...] = x_ref[:, width + BLK : base].astype(f32)
    last = base - base % LANES
    small = x_ref[:, last : last + LANES].astype(f32)
    taps_ref[...] = small[:, base - last : base - last + CONV]
    turned = small.T
    for i, ref in enumerate(row_refs):
        at = base - last + CONV + i
        ref[...] = turned[at : at + 1]


def unpack_sums(x, width):
    rows = x.shape[0]
    shape = lambda *dims: jax.ShapeDtypeStruct(dims, f32)
    return pl.pallas_call(
        unpack_kernel,
        out_shape=(shape(rows, width), shape(rows, BLK), shape(rows, BLK), shape(rows, CONV))
        + (shape(1, rows),) * 4,
        compiler_params=pltpu.CompilerParams(vmem_limit_bytes=VMEM_LIMIT),
        cost_estimate=cost(2),
        name="unpack_sums",
    )(x)


def pad_lanes(rows, width):
    have = rows.shape[-1]
    return jnp.pad(rows, ((0, 0), (0, width - have)))


def inverse_rms(rows):
    return lax.rsqrt(jnp.mean(rows * rows, axis=-1, keepdims=True) + norm_eps)


def norm_back(rows, scale, e):
    return scale * e - rows * (scale * scale * scale) * jnp.mean(e * rows, axis=-1, keepdims=True)


def on_device(
    tokens_in,
    segment_starts,
    cotangent,
    norm1_gain,
    rec_gate_weight,
    rec_in_weight,
    conv_weight,
    conv_bias,
    gate_a_weight,
    gate_a_bias,
    gate_x_weight,
    gate_x_bias,
    decay_rate,
    rec_out_weight,
    norm2_gain,
    mlp_gate_weight,
    mlp_up_weight,
    mlp_down_weight,
):
    count = lax.axis_size("z")
    z = lax.axis_index("z")
    spread = count // 2
    swap_axes = FEAT[len(FEAT) - (spread.bit_length() - 1) :]
    outer = NF // spread
    rows_tok, width = tokens_in.shape
    group_rows = NF * rows_tok
    chan_rows = conv_weight.shape[0]
    chans = chan_rows * count
    rows_w = rec_gate_weight.shape[0]
    ff_rows = mlp_down_weight.shape[0]
    ff = ff_rows * count
    chunk = 256

    chan_moves = [
        (
            source,
            k * spread + e,
            source * chans + zz * BLK,
            ((2 * e + zz) * outer + k) * BLK,
            BLK,
        )
        for source in range(2)
        for k in range(outer)
        for e in range(spread)
        for zz in range(2)
    ]
    ff_moves = [
        (source, f, source * ff + group * ff_rows, (group * NF + f) * ff_rows, ff_rows)
        for source in range(2)
        for f in range(NF)
        for group in range(count)
    ]
    place = [lax.axis_index(name) for name in FEAT]
    time = jnp.arange(NF, dtype=jnp.int32)
    bit = lambda value, here: jnp.where(value == here, 0, 1)
    order = (
        bit(time % 2, place[2]) * 4 + bit(time // 4, place[0]) * 2 + bit((time // 2) % 2, place[1])
    ).astype(jnp.int32)
    final = order[NF - 1] * rows_tok + rows_tok - 8

    pack = jnp.concatenate(
        [
            rec_out_weight,
            gate_a_weight,
            gate_x_weight,
            conv_weight,
            conv_bias[:, None],
            gate_a_bias[:, None],
            gate_x_bias[:, None],
            decay_rate[:, None],
        ],
        axis=1,
    )
    used = pack.shape[1]
    pack_width = -(-used // LANES) * LANES
    pack = pad_lanes(pack, pack_width)

    extra = jnp.concatenate(
        [
            pad_lanes(segment_starts.astype(bf16)[None], 2 * chans),
            pad_lanes(norm1_gain[None], 2 * chans),
            pad_lanes(norm2_gain[None], 2 * chans),
            jnp.zeros((13, 2 * chans), bf16),
        ],
        axis=0,
    )
    rec_send = jnp.concatenate(
        [
            split_blocks(rec_gate_weight, rec_in_weight, chan_moves),
            jnp.broadcast_to(extra[None], (NF, 16, 2 * chans)),
        ],
        axis=1,
    )
    pack_all = lax.all_gather(pack, "z", axis=0, tiled=True)
    (rec_got,) = exchange([rec_send], FEAT, 3)
    starts = rec_got[:, rows_w, :rows_tok].reshape(group_rows).astype(f32)

    plane_gains = jnp.stack(
        [
            rec_got[:, rows_w + 1, :rows_w].reshape(NF * rows_w),
            rec_got[:, rows_w + 2, :rows_w].reshape(NF * rows_w),
        ]
    ).astype(f32)
    gains = gather_groups(jnp.pad(plane_gains, ((0, 6), (0, 0))), count, 7)
    w_rec = lax.all_gather(
        rec_got[:, :rows_w].reshape(NF * rows_w, 2 * chans), "z", axis=0, tiled=True
    )
    mlp_send = split_blocks(mlp_gate_weight, mlp_up_weight, ff_moves)
    tokens_own, gains = hold(tokens_in, gains)
    tok_group, mlp_got = gather_exchange(tokens_own, mlp_send)
    tok_group, pack_all = hold(tok_group, pack_all)
    (pack_swap,) = exchange(
        [pack_all.reshape(spread, 2, chan_rows, pack_width)], swap_axes, 5
    )
    gain_one = gains[:, 0].reshape(1, width)
    gain_two = gains[:, 1].reshape(1, width)

    tok = tokens_in.astype(f32)
    tok_group = tok_group.astype(f32)
    normed = (tok_group * inverse_rms(tok_group) * gain_one).astype(bf16)

    w_mlp = lax.all_gather(mlp_got.reshape(NF * rows_w, 2 * ff), "z", axis=0, tiled=True)
    w_down = lax.all_gather(mlp_down_weight, "z", axis=0, tiled=True)

    mine = pack_swap.transpose(1, 0, 2, 3).reshape(chans, pack_width)
    w_out = mine[:, :width]
    small = mine[:, width + 2 * BLK : used].astype(f32).T

    unit = lax.broadcasted_iota(jnp.int32, (chans, chans), 0) // BLK
    same_block = unit == lax.broadcasted_iota(jnp.int32, (chans, chans), 1) // BLK

    def block_diag(w):
        return jnp.where(same_block, jnp.concatenate([w, w], axis=1), jnp.zeros((), w.dtype))

    wa = block_diag(mine[:, width : width + BLK])
    wx = block_diag(mine[:, width + BLK : width + 2 * BLK])

    open_one = 1.0 - starts
    ahead = jnp.concatenate([jnp.ones((TAIL,), f32), open_one])
    open_two = open_one * ahead[TAIL - 1 : TAIL - 1 + group_rows]
    open_three = open_two * ahead[TAIL - 2 : TAIL - 2 + group_rows]
    masks = jnp.stack([open_one, open_two, open_three], axis=1)
    end = open_one[group_rows - 2 :]
    later_open = jnp.concatenate(
        [jnp.zeros((8 - TAIL,), f32), (end[0] * end[1])[None], end[1:], jnp.ones((1,), f32)]
    )[:, None]

    rec_pre = jnp.dot(normed, w_rec, preferred_element_type=f32)
    rec_pre, cot_own = hold(rec_pre, cotangent)
    cot_x, cot_y = gather_near(cot_own)
    edge_rows = lax.dynamic_slice_in_dim(rec_pre, final, 8, 0)[:, chans:].astype(bf16)
    halo = lax.ppermute(
        edge_rows.astype(f32) * later_open, "z", [(i, i + 1) for i in range(count - 1)]
    )
    branch_in, conved, keep, prod, state_local, ends = forward_scan(
        order, rec_pre, halo, masks, small, wa, wx, chunk
    )
    ends, cot_x, cot_y = hold(ends, cot_x, cot_y)
    cot_top, cot_low = gather_diagonal(cot_x, cot_y)
    ends = gather_groups(ends, count, 2)
    state_in = jnp.zeros((1, chans), f32)
    for hop in range(count - 1):
        state_in = jnp.where(hop < z, ends[hop, 0:1] * state_in + ends[hop, 1:2], state_in)
    mixed = ((state_local + prod * state_in) * gelu_tanh(rec_pre[:, :chans])).astype(bf16)
    mixed_out = jnp.dot(mixed, w_out, preferred_element_type=f32).astype(bf16)
    mixed_out, cot_top, cot_low = hold(mixed_out, cot_top, cot_low)
    cot_chip = gather_chip(cotangent, cot_x, cot_y, cot_top, cot_low)
    cot_got = across(cot_chip, "c")
    middle = tok + scatter_feature(mixed_out)

    scale_two = inverse_rms(middle)
    normed_two = gather_feature((middle * scale_two * gain_two).astype(bf16))
    hidden, d_mlp = gated_unit(normed_two, cot_chip, cot_got, w_mlp, w_down)
    half_rows = group_rows // 2

    def back_rows(d, w):
        return lax.dot_general(d, w, contract_last, preferred_element_type=f32).astype(bf16)

    def over_rows(a, b_mine, b_theirs):
        return (
            lax.dot_general(a[:half_rows], b_mine, contract_first, preferred_element_type=f32)
            + lax.dot_general(a[half_rows:], b_theirs, contract_first, preferred_element_type=f32)
        ).astype(bf16)

    e_theirs = back_rows(d_mlp[half_rows:], w_mlp)
    d_mlp, e_theirs = hold(d_mlp, e_theirs)
    e_got = across(e_theirs, "c")
    e_mine = back_rows(d_mlp[:half_rows], w_mlp)
    e_keeps, e_x, e_y = scatter_near(e_mine, e_got)
    near_y, hidden = hold(e_keeps[0], hidden)
    e_keeps = (near_y,) + e_keeps[1:]
    down_part = over_rows(hidden, cot_chip, cot_got)
    down_part, hidden = hold(down_part, hidden)
    down_sum = lax.psum_scatter(down_part, "z", scatter_dimension=0, tiled=True)
    out_mine, out_theirs = down_rows(hidden, w_down)
    out_mine, out_theirs, e_x, e_y = hold(out_mine, out_theirs, e_x, e_y)
    e_two = gain_two * scatter_tail(e_keeps, e_x, e_y)
    d_middle = cotangent.astype(f32) + norm_back(middle, scale_two, e_two)
    d_own = d_middle.astype(bf16)
    d_x, d_y = gather_near(d_own)
    d_own, d_mlp, out_mine, out_theirs = hold(d_own, d_mlp, out_mine, out_theirs)
    out_got = across(out_theirs, "c")
    mlp_part = lax.dot_general(
        normed_two, d_mlp, contract_first, preferred_element_type=f32
    ).astype(bf16)
    out_keeps = scatter_keeps(out_mine, out_got)
    out_x, out_y = scatter_sends(out_mine, out_got)
    d_x, d_y, mlp_part, out_x, out_y, *out_keeps = hold(
        d_x, d_y, mlp_part, out_x, out_y, *out_keeps
    )
    mlp_sum = lax.psum_scatter(mlp_part, "z", scatter_dimension=0, tiled=True)
    d_rec = gather_tail(d_own, d_x, d_y)
    d_rec, down_sum, out_x, out_y = hold(d_rec, down_sum, out_x, out_y)
    out_x, out_y = across(out_x, "x"), across(out_y, "y")

    d_mixed = lax.dot_general(d_rec, w_out, contract_last, preferred_element_type=f32)
    adj_prod, adj_local, heads = adjoint_scan(order, d_mixed, rec_pre, keep, chunk)
    heads = gather_groups(heads, count, 2)
    heads, out_x, out_y = hold(heads, out_x, out_y)
    out_last = scatter_relay(out_keeps, out_x, out_y)
    adj_in = jnp.zeros((1, chans), f32)
    for hop in range(count - 1, 0, -1):
        adj_in = jnp.where(hop > z, heads[hop, 0:1] * adj_in + heads[hop, 1:2], adj_in)
    enter = jnp.concatenate([state_in, adj_in, jnp.zeros((6, chans), f32)])
    d_rec_pre, sums, edge, grad_a, grad_x = backward_scan(
        order, d_mixed, rec_pre, state_local, prod, adj_local, adj_prod, branch_in, halo, conved,
        masks, small, enter, wa, wx, chunk,
    )
    after = lax.ppermute(edge, "z", [(i + 1, i) for i in range(count - 1)]) * later_open
    edge, mixed = hold(edge, mixed)
    grad_out = lax.dot_general(mixed, d_rec, contract_first, preferred_element_type=f32).astype(
        bf16
    )
    after, grad_out = hold(after, grad_out)
    tail_sum = lax.dynamic_slice_in_dim(d_rec_pre, final, 8, 0).astype(f32) + jnp.pad(
        after, ((0, 0), (chans, 0))
    )
    d_rec_pre = lax.dynamic_update_slice_in_dim(d_rec_pre, tail_sum.astype(bf16), final, 0)
    rec_part = lax.dot_general(
        normed, d_rec_pre, contract_first, preferred_element_type=f32
    ).astype(bf16)
    rec_part, d_rec_pre, grad_a, grad_x, sums, *out_last = hold(
        rec_part, d_rec_pre, grad_a, grad_x, sums, *out_last
    )
    layer_out = (middle + scatter_sum(out_keeps, out_x, out_y, *out_last)).astype(bf16)
    rec_sum = lax.psum_scatter(rec_part, "z", scatter_dimension=0, tiled=True)
    fold = (
        lax.broadcasted_iota(jnp.int32, (chans, BLK), 0) % BLK
        == lax.broadcasted_iota(jnp.int32, (chans, BLK), 1)
    ).astype(bf16)

    def diagonal(w):
        kept = jnp.where(same_block, w, 0.0).astype(bf16)
        return jnp.dot(kept, fold, preferred_element_type=f32).astype(bf16)

    back_pack = jnp.concatenate(
        [
            grad_out,
            diagonal(grad_a),
            diagonal(grad_x),
            sums.T.astype(bf16),
        ],
        axis=1,
    )
    back_pack = pad_lanes(back_pack, pack_width)
    back_pack = back_pack.reshape(2, spread, chan_rows, pack_width).transpose(1, 0, 2, 3)
    (back_swap,) = exchange([back_pack], swap_axes, 5)
    back_swap = back_swap.reshape(count * chan_rows, pack_width)
    back_swap, mlp_sum, d_rec_pre = hold(back_swap, mlp_sum, d_rec_pre)
    pack_sum = lax.psum_scatter(back_swap, "z", scatter_dimension=0, tiled=True)
    one_sum, mlp_back = scatter_dot(d_rec_pre, w_rec, mlp_sum.reshape(NF, rows_w, 2 * ff))
    one_sum, rec_sum, down_sum = hold(one_sum, rec_sum, down_sum)
    (rec_back,) = exchange([rec_sum.reshape(NF, rows_w, 2 * chans)], FEAT, 10)
    rec_back, pack_sum = hold(rec_back, pack_sum)
    e_one = gain_one * one_sum
    grad_tokens = d_middle + norm_back(tok, inverse_rms(tok), e_one)
    grad_gate, grad_up, grad_gain_two = join_blocks(
        mlp_back, mlp_gate_weight, mlp_up_weight, norm2_gain.astype(f32)[:, None], ff_moves
    )
    grad_rec_gate, grad_rec_in, grad_gain_one = join_blocks(
        rec_back, rec_gate_weight, rec_in_weight, norm1_gain.astype(f32)[:, None], chan_moves
    )

    grad_out, grad_a, grad_x, grad_taps, *grad_rows = unpack_sums(pack_sum, width)
    grad_offset, grad_a_bias, grad_x_bias, grad_rate = (r.reshape(chan_rows) for r in grad_rows)
    return (
        layer_out,
        grad_tokens,
        grad_gain_one.reshape(rows_w),
        grad_rec_gate,
        grad_rec_in,
        grad_taps,
        grad_offset,
        grad_a,
        grad_a_bias,
        grad_x,
        grad_x_bias,
        grad_rate,
        grad_out,
        grad_gain_two.reshape(rows_w),
        grad_gate,
        grad_up,
        down_sum.astype(f32),
    )


def solution(mesh):
    wide, narrow = mesh.shape["wide"], mesh.shape["narrow"]
    groups = wide * narrow // NF
    grid = Mesh(mesh.devices.reshape((groups,) + (2,) * len(FEAT)), ("z",) + FEAT)
    flat = P(("z",) + FEAT)
    wide_rows = P(("z",) + FEAT, None)
    one, two = flat, wide_rows
    return jax.shard_map(
        on_device,
        mesh=grid,
        in_specs=(
            two, one, two, one, two, two, two, one, two, one, two, one, one, two, one, two, two, two,
        ),
        out_specs=(
            two, two, one, two, two, two, one, two, one, two, one, one, two, one, two, two, two,
        ),
        check_vma=False,
    )
```

```python
import functools

import jax
import jax.numpy as jnp
from jax import lax
from jax.experimental import pallas as pl
from jax.experimental.pallas import tpu as pltpu
from jax.sharding import Mesh
from jax.sharding import PartitionSpec as P

BLK = 160
CONV = 4
TAIL = CONV - 1
LANES = 128
FEAT = ("x", "y", "c")
NF = 8
OWN, ACROSS_Y, ACROSS_X, DIAGONAL = 0, 1, 2, 3

norm_eps = 1e-06
decay_scale = 8.0
push_shift = 0.05
f32 = jnp.float32
bf16 = jnp.bfloat16
MESH = pl.DeviceIdType.MESH
contract_last = (((1,), (1,)), ((), ()))
contract_first = (((0,), (0,)), ((), ()))
VMEM_LIMIT = 56 * 2**20


def cost(micros, flops=0):
    return pl.CostEstimate(
        flops=int(flops), bytes_accessed=int(micros * 3.0e6), transcendentals=0
    )


def hbm_spec():
    return pl.BlockSpec(memory_space=pl.ANY)


def vmem_spec():
    return pl.BlockSpec(memory_space=pltpu.VMEM)


def greet(peers):
    barrier = pltpu.get_barrier_semaphore()
    for device in peers:
        pl.semaphore_signal(barrier, inc=1, device_id=device, device_id_type=MESH)
    pl.semaphore_wait(barrier, len(peers))


def feature_place():
    return tuple(lax.axis_index(name) for name in FEAT)


def remote(src, dst, send_sem, recv_sem, device):
    return pltpu.make_async_remote_copy(
        src_ref=src,
        dst_ref=dst,
        send_sem=send_sem,
        recv_sem=recv_sem,
        device_id=device,
        device_id_type=MESH,
    )


def gather_kernel(*refs):
    if len(refs) == 5:
        x_ref, o_ref, local_sem, ssem, rsem = refs
        extra = ()
    else:
        x_ref, b_ref, o_ref, e_ref, local_sem, ssem, rsem, *sems = refs
        extra = exchange_parts(FEAT, b_ref, e_ref, *sems)
    x, y, c = feature_place()
    to_x, to_y, to_c = {"x": 1 - x}, {"y": 1 - y}, {"c": 1 - c}
    half = x_ref.shape[0] // 2
    top, low = pl.ds(0, half), pl.ds(half, half)
    greet(extra[0] if extra else (to_x, to_y, to_c))

    def copy(i, src, dst, device):
        return remote(src, dst, ssem.at[i], rsem.at[i], device)

    own = pltpu.make_async_copy(x_ref, o_ref.at[OWN], local_sem)
    x_top = copy(0, x_ref.at[top], o_ref.at[ACROSS_X, top], to_x)
    x_low = copy(1, x_ref.at[low], o_ref.at[ACROSS_X, low], to_x)
    y_low = copy(2, x_ref.at[low], o_ref.at[ACROSS_Y, low], to_y)
    y_top = copy(3, x_ref.at[top], o_ref.at[ACROSS_Y, top], to_y)
    c_own = copy(4, x_ref, o_ref.at[4 + OWN], to_c)
    y_fwd = copy(5, o_ref.at[ACROSS_X, top], o_ref.at[DIAGONAL, top], to_y)
    x_fwd = copy(6, o_ref.at[ACROSS_Y, low], o_ref.at[DIAGONAL, low], to_x)
    c_x = copy(7, o_ref.at[ACROSS_X], o_ref.at[4 + ACROSS_X], to_c)
    c_y = copy(8, o_ref.at[ACROSS_Y], o_ref.at[4 + ACROSS_Y], to_c)
    c_d = copy(9, o_ref.at[DIAGONAL], o_ref.at[4 + DIAGONAL], to_c)
    for one in (x_top, y_low, x_low, y_top, c_own, own):
        one.start()
    if extra:
        extra[1].start()
        for one in extra[2]:
            one.start()
    x_top.wait_recv()
    y_fwd.start()
    y_low.wait_recv()
    x_fwd.start()
    x_low.wait_recv()
    c_x.start()
    y_top.wait_recv()
    c_y.start()
    y_fwd.wait_recv()
    x_fwd.wait_recv()
    c_d.start()
    for one in (c_own, c_x, c_y, c_d):
        one.wait_recv()
    for one in (x_top, x_low, y_low, y_top, c_own, y_fwd, x_fwd, c_x, c_y, c_d):
        one.wait_send()
    own.wait()
    if extra:
        for one in extra[2]:
            one.wait()
        extra[1].wait()


def gather_feature(block):
    rows, width = block.shape
    out = pl.pallas_call(
        gather_kernel,
        out_shape=jax.ShapeDtypeStruct((NF, rows, width), block.dtype),
        in_specs=[vmem_spec()],
        out_specs=hbm_spec(),
        scratch_shapes=[
            pltpu.SemaphoreType.DMA,
            pltpu.SemaphoreType.DMA((10,)),
            pltpu.SemaphoreType.DMA((10,)),
        ],
        compiler_params=pltpu.CompilerParams(
            collective_id=0, has_side_effects=True, vmem_limit_bytes=VMEM_LIMIT
        ),
        cost_estimate=cost(40),
        name="gather_feature",
    )(block)
    return out.reshape(NF * rows, width)


def scatter_flow(
    p_theirs, o_ref, own, other, total, rx, ry, relay, rx_last, ry_last, ssem, rsem,
    peers, begin, stage, ready
):
    x, y, c = feature_place()
    to_x, to_y, to_c = {"x": 1 - x}, {"y": 1 - y}, {"c": 1 - c}
    rows, width = o_ref.shape
    half = rows // 2
    top, low = pl.ds(0, half), pl.ds(half, half)
    step = 16

    def copy(i, src, dst, device):
        return remote(src, dst, ssem.at[i], rsem.at[i], device)

    greet(peers or (to_x, to_y, to_c))
    begin()
    cross = [copy(r, p_theirs(r), other.at[r], to_c) for r in range(4)]

    def add_into(r):
        ready(r)
        cross[r].wait_recv()

        def body(i, none):
            at = pl.ds(pl.multiple_of(i * step, step), step)
            total[r, at] = (own[r, at].astype(f32) + other[r, at].astype(f32)).astype(total.dtype)
            return none

        lax.fori_loop(0, rows // step, body, 0)

    x_diag = copy(4, total.at[DIAGONAL, top], rx.at[1], to_x)
    y_diag = copy(5, total.at[DIAGONAL, low], ry.at[1], to_y)
    x_near = copy(6, total.at[ACROSS_X, top], rx.at[0], to_x)
    y_near = copy(7, total.at[ACROSS_Y, low], ry.at[0], to_y)
    y_last = copy(8, relay.at[0], ry_last, to_y)
    x_last = copy(9, relay.at[1], rx_last, to_x)

    stage(DIAGONAL, cross)
    stage(ACROSS_X, cross)
    add_into(DIAGONAL)
    x_diag.start()
    y_diag.start()
    stage(ACROSS_Y, cross)
    add_into(ACROSS_X)
    x_near.start()
    stage(OWN, cross)
    add_into(ACROSS_Y)
    y_near.start()
    ready(OWN)
    cross[OWN].wait_recv()

    def relay_add(slot, r, start, got):
        def body(i, none):
            at = pl.ds(pl.multiple_of(i * step, step), step)
            here = pl.ds(pl.multiple_of(start + i * step, step), step)
            relay[slot, at] = (total[r, here].astype(f32) + got[1, at].astype(f32)).astype(
                relay.dtype
            )
            return none

        lax.fori_loop(0, half // step, body, 0)

    x_diag.wait_recv()
    relay_add(0, ACROSS_Y, 0, rx)
    y_last.start()
    y_diag.wait_recv()
    relay_add(1, ACROSS_X, half, ry)
    x_last.start()

    def finish(start, near, last):
        def body(i, none):
            at = pl.ds(pl.multiple_of(i * step, step), step)
            here = pl.ds(pl.multiple_of(start + i * step, step), step)
            o_ref[here] = (own[OWN, here].astype(f32) + other[OWN, here].astype(f32)) + (
                near[0, at].astype(f32) + last[at].astype(f32)
            )
            return none

        lax.fori_loop(0, half // step, body, 0)

    x_near.wait_recv()
    y_last.wait_recv()
    finish(0, rx, ry_last)
    y_near.wait_recv()
    x_last.wait_recv()
    finish(half, ry, rx_last)
    for one in cross + [x_diag, y_diag, x_near, y_near, x_last, y_last]:
        one.wait_send()


def scatter_kernel(
    p_ref, o_ref, own, other, total, rx, ry, relay, rx_last, ry_last, lsem, ssem, rsem
):
    loads = [pltpu.make_async_copy(p_ref.at[r], own.at[r], lsem.at[r]) for r in range(4)]
    for r in (DIAGONAL, ACROSS_X, ACROSS_Y, OWN):
        loads[r].start()
    scatter_flow(
        lambda r: p_ref.at[4 + r], o_ref, own, other, total, rx, ry, relay, rx_last, ry_last,
        ssem, rsem, None, lambda: None, lambda r, cross: cross[r].start(),
        lambda r: loads[r].wait(),
    )


def scatter_dot_kernel(
    a_ref, w_ref, b_ref, o_ref, e_ref, theirs, own, other, total, rx, ry, relay, rx_last, ry_last,
    ssem, rsem, local_sem, xssem, xrsem
):
    peers, kept, copies = exchange_parts(FEAT, b_ref, e_ref, local_sem, xssem, xrsem)
    rows, width = o_ref.shape
    tile = 512

    def begin():
        kept.start()
        for one in copies:
            one.start()

    def dot_into(block, ref, r):
        rows_in = a_ref[pl.ds(block * rows, rows)]

        def body(j, none):
            at = pl.ds(pl.multiple_of(j * tile, tile), tile)
            ref[r, :, at] = lax.dot_general(
                rows_in, w_ref[at], contract_last, preferred_element_type=f32
            ).astype(ref.dtype)
            return none

        lax.fori_loop(0, width // tile, body, 0)

    def stage(r, cross):
        dot_into(4 + r, theirs, r)
        cross[r].start()
        dot_into(r, own, r)

    scatter_flow(
        lambda r: theirs.at[r], o_ref, own, other, total, rx, ry, relay, rx_last, ry_last,
        ssem, rsem, peers, begin, stage, lambda r: None,
    )
    for one in copies:
        one.wait()
    kept.wait()


def scatter_dot(rows_in, w, blocks):
    rows, width = rows_in.shape[0] // NF, w.shape[0]
    half = rows // 2
    kind = rows_in.dtype
    four = pltpu.VMEM((4, rows, width), kind)
    two = pltpu.VMEM((2, half, width), kind)
    one = pltpu.VMEM((half, width), kind)
    return pl.pallas_call(
        scatter_dot_kernel,
        out_shape=(
            jax.ShapeDtypeStruct((rows, width), f32),
            jax.ShapeDtypeStruct(blocks.shape, blocks.dtype),
        ),
        in_specs=[vmem_spec()] * 3,
        out_specs=(vmem_spec(), hbm_spec()),
        scratch_shapes=[four] * 4
        + [two] * 3
        + [one] * 2
        + [
            pltpu.SemaphoreType.DMA((10,)),
            pltpu.SemaphoreType.DMA((10,)),
            pltpu.SemaphoreType.DMA,
            pltpu.SemaphoreType.DMA((NF - 1,)),
            pltpu.SemaphoreType.DMA((NF - 1,)),
        ],
        compiler_params=pltpu.CompilerParams(
            collective_id=11, has_side_effects=True, vmem_limit_bytes=VMEM_LIMIT
        ),
        cost_estimate=cost(55),
        name="scatter_dot",
    )(rows_in, w, blocks)


def scatter_feature(partial):
    rows, width = partial.shape[0] // NF, partial.shape[1]
    half = rows // 2
    kind = partial.dtype
    return pl.pallas_call(
        scatter_kernel,
        out_shape=jax.ShapeDtypeStruct((rows, width), f32),
        in_specs=[hbm_spec()],
        out_specs=vmem_spec(),
        scratch_shapes=[
            pltpu.VMEM((4, rows, width), kind),
            pltpu.VMEM((4, rows, width), kind),
            pltpu.VMEM((4, rows, width), kind),
            pltpu.VMEM((2, half, width), kind),
            pltpu.VMEM((2, half, width), kind),
            pltpu.VMEM((2, half, width), kind),
            pltpu.VMEM((half, width), kind),
            pltpu.VMEM((half, width), kind),
            pltpu.SemaphoreType.DMA((4,)),
            pltpu.SemaphoreType.DMA((10,)),
            pltpu.SemaphoreType.DMA((10,)),
        ],
        compiler_params=pltpu.CompilerParams(
            collective_id=1, has_side_effects=True, vmem_limit_bytes=VMEM_LIMIT
        ),
        cost_estimate=cost(45),
        name="scatter_feature",
    )(partial.reshape(NF, rows, width))


def across(value, axis):
    return lax.ppermute(value, axis, [(0, 1), (1, 0)])


def hold(*values):
    return lax.optimization_barrier(values)


def gather_near(block):
    return across(block, "x"), across(block, "y")


def gather_diagonal(by_x, by_y):
    half = by_x.shape[0] // 2
    return across(by_x[:half], "y"), across(by_y[half:], "x")


def gather_chip(block, by_x, by_y, d_top, d_low):
    return jnp.concatenate([block, by_y, by_x, d_top, d_low])


def scatter_halves(mine, got):
    shape = (4, 2, mine.shape[0] // 8, mine.shape[1])
    return mine.reshape(shape), got.reshape(shape)


def add_low(a, b):
    return (a.astype(f32) + b.astype(f32)).astype(a.dtype)


def scatter_sends(mine, got):
    mine, got = scatter_halves(mine, got)
    by_x = add_low(mine[ACROSS_X:, 0], got[ACROSS_X:, 0])
    by_y = add_low(mine[ACROSS_Y::2, 1], got[ACROSS_Y::2, 1])
    return by_x, by_y


def scatter_keeps(mine, got):
    mine, got = scatter_halves(mine, got)
    near_y = add_low(mine[ACROSS_Y, 0], got[ACROSS_Y, 0])
    near_x = add_low(mine[ACROSS_X, 1], got[ACROSS_X, 1])
    return near_y, near_x, add_low(mine[OWN], got[OWN])


def scatter_near(mine, got):
    mine, got = hold(mine, got)
    by_x, by_y = scatter_sends(mine, got)
    by_x, by_y, mine, got = hold(by_x, by_y, mine, got)
    return scatter_keeps(mine, got), across(by_x, "x"), across(by_y, "y")


def scatter_relay(keeps, by_x, by_y):
    near_y, near_x, _ = keeps
    return across(add_low(near_y, by_x[1]), "y"), across(add_low(near_x, by_y[1]), "x")


def scatter_sum(keeps, by_x, by_y, y_last, x_last):
    own = keeps[2].astype(f32)
    upper = own[0] + by_x[0].astype(f32) + y_last.astype(f32)
    lower = own[1] + by_y[0].astype(f32) + x_last.astype(f32)
    return jnp.concatenate([upper, lower])


def gather_tail_kernel(x_ref, bx_ref, by_ref, o_ref, lsem, ssem, rsem):
    x, y, c = feature_place()
    to_x, to_y, to_c = {"x": 1 - x}, {"y": 1 - y}, {"c": 1 - c}
    half = x_ref.shape[0] // 2
    top, low = pl.ds(0, half), pl.ds(half, half)

    def copy(i, src, dst, device):
        return remote(src, dst, ssem.at[i], rsem.at[i], device)

    places = ((x_ref, OWN), (by_ref, ACROSS_Y), (bx_ref, ACROSS_X))
    local = [
        pltpu.make_async_copy(ref, o_ref.at[slot], lsem.at[i])
        for i, (ref, slot) in enumerate(places)
    ]
    greet((to_x, to_y, to_c))
    y_fwd = copy(0, bx_ref.at[top], o_ref.at[DIAGONAL, top], to_y)
    x_fwd = copy(1, by_ref.at[low], o_ref.at[DIAGONAL, low], to_x)
    cross = [
        copy(2 + i, ref, o_ref.at[4 + slot], to_c) for i, (ref, slot) in enumerate(places)
    ]
    last = copy(5, o_ref.at[DIAGONAL], o_ref.at[4 + DIAGONAL], to_c)
    for one in [y_fwd, x_fwd] + cross + local:
        one.start()
    y_fwd.wait_recv()
    x_fwd.wait_recv()
    last.start()
    for one in cross + [last]:
        one.wait_recv()
    for one in cross + [y_fwd, x_fwd, last]:
        one.wait_send()
    for one in local:
        one.wait()


def gather_tail(block, by_x, by_y):
    rows, width = block.shape
    out = pl.pallas_call(
        gather_tail_kernel,
        out_shape=jax.ShapeDtypeStruct((NF, rows, width), block.dtype),
        in_specs=[vmem_spec()] * 3,
        out_specs=hbm_spec(),
        scratch_shapes=[
            pltpu.SemaphoreType.DMA((3,)),
            pltpu.SemaphoreType.DMA((6,)),
            pltpu.SemaphoreType.DMA((6,)),
        ],
        compiler_params=pltpu.CompilerParams(
            collective_id=8, has_side_effects=True, vmem_limit_bytes=VMEM_LIMIT
        ),
        cost_estimate=cost(16),
        name="gather_tail",
    )(block, by_x, by_y)
    return out.reshape(NF * rows, width)


def scatter_tail_kernel(
    ny_ref, nx_ref, own_ref, bx_ref, by_ref, o_ref, near, own, bx, by, relay, last, lsem, ssem, rsem
):
    x, y, c = feature_place()
    to_x, to_y = {"x": 1 - x}, {"y": 1 - y}
    half = o_ref.shape[0] // 2
    step = 16

    def load(i, src, dst):
        one = pltpu.make_async_copy(src, dst, lsem.at[i])
        one.start()
        return one

    loads = [
        load(0, ny_ref, near.at[0]),
        load(1, bx_ref, bx),
        load(2, nx_ref, near.at[1]),
        load(3, by_ref, by),
        load(4, own_ref, own),
    ]
    greet((to_x, to_y))
    sends = [
        remote(relay.at[0], last.at[0], ssem.at[0], rsem.at[0], to_y),
        remote(relay.at[1], last.at[1], ssem.at[1], rsem.at[1], to_x),
    ]

    def tiles(body):
        def one(i, none):
            body(pl.ds(pl.multiple_of(i * step, step), step), i * step)
            return none

        lax.fori_loop(0, half // step, one, 0)

    for side, got in ((0, bx), (1, by)):
        loads[2 * side].wait()
        loads[2 * side + 1].wait()

        def add(at, _, side=side, got=got):
            relay[side, at] = (near[side, at].astype(f32) + got[1, at].astype(f32)).astype(
                relay.dtype
            )

        tiles(add)
        sends[side].start()
    loads[4].wait()
    for side, got in ((0, bx), (1, by)):

        def base(at, start, side=side, got=got):
            here = pl.ds(pl.multiple_of(side * half + start, step), step)
            o_ref[here] = own[side, at].astype(f32) + got[0, at].astype(f32)

        tiles(base)
    for side in range(2):
        sends[side].wait_recv()

        def finish(at, start, side=side):
            here = pl.ds(pl.multiple_of(side * half + start, step), step)
            o_ref[here] = o_ref[here] + last[side, at].astype(f32)

        tiles(finish)
    for one in sends:
        one.wait_send()


def scatter_tail(keeps, by_x, by_y):
    _, half, width = by_x.shape
    kind = by_x.dtype
    pair = pltpu.VMEM((2, half, width), kind)
    return pl.pallas_call(
        scatter_tail_kernel,
        out_shape=jax.ShapeDtypeStruct((2 * half, width), f32),
        in_specs=[hbm_spec()] * 5,
        out_specs=vmem_spec(),
        scratch_shapes=[pair] * 6
        + [
            pltpu.SemaphoreType.DMA((5,)),
            pltpu.SemaphoreType.DMA((2,)),
            pltpu.SemaphoreType.DMA((2,)),
        ],
        compiler_params=pltpu.CompilerParams(
            collective_id=9, has_side_effects=True, vmem_limit_bytes=VMEM_LIMIT
        ),
        cost_estimate=cost(16),
        name="scatter_tail",
    )(*keeps, by_x, by_y)


def exchange_parts(axes, x_ref, o_ref, local_sem, ssem, rsem):
    place = [lax.axis_index(name) for name in axes]
    count = 2 ** len(axes)

    def rank(coords):
        total = 0
        for one in coords:
            total = total * 2 + one
        return total

    mine = rank(place)
    own = pltpu.make_async_copy(x_ref.at[mine], o_ref.at[mine], local_sem)
    peers, copies = [], []
    for mask in range(count - 1, 0, -1):
        bits = [(mask // 2 ** (len(axes) - 1 - i)) % 2 for i in range(len(axes))]
        coords = [1 - p if bit else p for p, bit in zip(place, bits)]
        device = {name: q for name, q, bit in zip(axes, coords, bits) if bit}
        peers.append(device)
        copies.append(
            remote(
                x_ref.at[rank(coords)],
                o_ref.at[mine],
                ssem.at[mask - 1],
                rsem.at[mask - 1],
                device,
            )
        )
    return peers, own, copies


def exchange_kernel(axes, *refs):
    count = (len(refs) - 3) // 2
    sources, targets = refs[:count], refs[count : 2 * count]
    local_sem, ssem, rsem = refs[2 * count :]
    parts = [
        exchange_parts(axes, sources[i], targets[i], local_sem.at[i], ssem.at[i], rsem.at[i])
        for i in range(count)
    ]
    for _, own, _ in parts:
        own.start()
    greet(parts[0][0])
    for _, _, copies in parts:
        for one in copies:
            one.start()
    for _, own, copies in parts:
        for one in copies:
            one.wait()
        own.wait()


def exchange(arrays, axes, ident):
    peers = 2 ** len(axes) - 1
    count = len(arrays)
    return pl.pallas_call(
        functools.partial(exchange_kernel, axes),
        out_shape=tuple(jax.ShapeDtypeStruct(a.shape, a.dtype) for a in arrays),
        in_specs=[vmem_spec()] * count,
        out_specs=(hbm_spec(),) * count,
        scratch_shapes=[
            pltpu.SemaphoreType.DMA((count,)),
            pltpu.SemaphoreType.DMA((count, peers)),
            pltpu.SemaphoreType.DMA((count, peers)),
        ],
        compiler_params=pltpu.CompilerParams(
            collective_id=ident, has_side_effects=True, vmem_limit_bytes=VMEM_LIMIT
        ),
        cost_estimate=cost(15),
        name="exchange",
    )(*arrays)


def gather_exchange(block, blocks):
    rows, width = block.shape
    out, got = pl.pallas_call(
        gather_kernel,
        out_shape=(
            jax.ShapeDtypeStruct((NF, rows, width), block.dtype),
            jax.ShapeDtypeStruct(blocks.shape, blocks.dtype),
        ),
        in_specs=[vmem_spec()] * 2,
        out_specs=(hbm_spec(),) * 2,
        scratch_shapes=[
            pltpu.SemaphoreType.DMA,
            pltpu.SemaphoreType.DMA((10,)),
            pltpu.SemaphoreType.DMA((10,)),
            pltpu.SemaphoreType.DMA,
            pltpu.SemaphoreType.DMA((NF - 1,)),
            pltpu.SemaphoreType.DMA((NF - 1,)),
        ],
        compiler_params=pltpu.CompilerParams(
            collective_id=4, has_side_effects=True, vmem_limit_bytes=VMEM_LIMIT
        ),
        cost_estimate=cost(55),
        name="gather_exchange",
    )(block, blocks)
    return out.reshape(NF * rows, width), got


def groups_kernel(count, x_ref, o_ref, local_sem, ssem, rsem):
    z = lax.axis_index("z")
    own = pltpu.make_async_copy(x_ref, o_ref.at[z], local_sem)
    own.start()
    targets = [{"z": lax.rem(z + hop, count)} for hop in range(1, count)]
    greet(targets)
    copies = [
        remote(x_ref, o_ref.at[z], ssem.at[i], rsem.at[i], device)
        for i, device in enumerate(targets)
    ]
    for one in copies:
        one.start()
    for one in copies:
        one.wait()
    own.wait()


def gather_groups(block, count, ident):
    return pl.pallas_call(
        functools.partial(groups_kernel, count),
        out_shape=jax.ShapeDtypeStruct((count,) + block.shape, block.dtype),
        in_specs=[vmem_spec()],
        out_specs=vmem_spec(),
        scratch_shapes=[
            pltpu.SemaphoreType.DMA,
            pltpu.SemaphoreType.DMA((count - 1,)),
            pltpu.SemaphoreType.DMA((count - 1,)),
        ],
        compiler_params=pltpu.CompilerParams(collective_id=ident, has_side_effects=True),
        cost_estimate=cost(5),
        name="gather_groups",
    )(block)


def gelu_tanh(values):
    return jax.nn.gelu(values, approximate=True)


def sigmoid(v):
    return 0.5 + 0.5 * jnp.tanh(0.5 * v)


def gelu_pair(v):
    root = 0.7978845608028654
    cube = 0.044715
    square = v * v
    t = jnp.tanh(root * (v + cube * square * v))
    value = 0.5 * v * (1.0 + t)
    slope = 0.5 * (1.0 + t) + 0.5 * v * (1.0 - t * t) * root * (1.0 + 3.0 * cube * square)
    return value, slope


def tile_scan(keep, push, reverse):
    rows = lax.broadcasted_iota(jnp.int32, keep.shape, 0)
    count = keep.shape[0]
    hop = 1
    while hop < count:
        if reverse:
            inside = rows < count - hop
            shift = count - hop
        else:
            inside = rows >= hop
            shift = hop
        keep_near = jnp.where(inside, pltpu.roll(keep, shift, 0), 1.0)
        push_near = jnp.where(inside, pltpu.roll(push, shift, 0), 0.0)
        push = push + keep * push_near
        keep = keep * keep_near
        hop *= 2
    return keep, push


def conv_of(ext, masks, taps, offset, rows):
    value = offset + taps[0:1] * ext[pl.ds(8, rows)]
    for k in range(1, CONV):
        value = value + taps[k : k + 1] * ext[pl.ds(8 - k, rows)] * masks[:, k - 1 : k]
    return value


def forward_kernel(
    order_ref,
    pre_ref,
    halo_ref,
    mask_ref,
    small_ref,
    wa_ref,
    wx_ref,
    branch_ref,
    conved_ref,
    keep_ref,
    prod_ref,
    state_ref,
    ends_ref,
    ext,
    carry,
):
    rows, width = branch_ref.shape
    step = pl.program_id(0)
    branch = pre_ref[:, width : 2 * width].astype(bf16)
    branch_ref[...] = branch

    @pl.when(step == 0)
    def _():
        ext[pl.ds(0, 8)] = halo_ref[...]
        carry[0:1] = jnp.ones_like(carry[0:1])
        carry[1:2] = jnp.zeros_like(carry[1:2])

    @pl.when(step > 0)
    def _():
        ext[pl.ds(0, 8)] = ext[pl.ds(rows, 8)]

    ext[pl.ds(8, rows)] = branch.astype(f32)
    masks = mask_ref[...]
    conved = conv_of(ext, masks, small_ref, small_ref[4:5], rows).astype(bf16)
    conved_ref[...] = conved
    logit_a = jnp.dot(conved, wa_ref[...], preferred_element_type=f32) + small_ref[5:6]
    logit_x = jnp.dot(conved, wx_ref[...], preferred_element_type=f32) + small_ref[6:7]
    decay = jnp.exp(-decay_scale * sigmoid(logit_a) * small_ref[7:8])
    keep_ref[...] = decay * masks[:, 0:1]
    state_ref[...] = (
        jnp.sqrt(1.0 - decay * decay + push_shift) * sigmoid(logit_x) * conved.astype(f32)
    )

    def body(i, held):
        prod_in, state_in = held
        at = pl.ds(pl.multiple_of(i * 8, 8), 8)
        keep, push = tile_scan(keep_ref[at], state_ref[at], False)
        state = push + keep * state_in
        prod = keep * prod_in
        prod_ref[at] = prod
        state_ref[at] = state
        return prod[7:8], state[7:8]

    prod_out, state_out = lax.fori_loop(
        0, rows // 8, body, (carry[0:1], carry[1:2]), unroll=4
    )
    carry[0:1] = prod_out
    carry[1:2] = state_out
    ends_ref[0:1] = prod_out
    ends_ref[1:2] = state_out
    ends_ref[2:8] = jnp.zeros_like(ends_ref[2:8])


def forward_scan(order, rec_pre, halo, masks, small, wa, wx, chunk):
    rows, width = rec_pre.shape[0], rec_pre.shape[1] // 2
    tile = pl.BlockSpec((chunk, width), lambda i, order: (order[i], 0))
    whole = lambda a: pl.BlockSpec(a.shape, lambda i, order: (0, 0))
    full = jax.ShapeDtypeStruct((rows, width), f32)
    low = jax.ShapeDtypeStruct((rows, width), bf16)
    return pl.pallas_call(
        forward_kernel,
        out_shape=(
            low,
            low,
            full,
            full,
            full,
            jax.ShapeDtypeStruct((8, width), f32),
        ),
        grid_spec=pltpu.PrefetchScalarGridSpec(
            num_scalar_prefetch=1,
            grid=(rows // chunk,),
            in_specs=[
                pl.BlockSpec((chunk, 2 * width), lambda i, order: (order[i], 0)),
                whole(halo),
                pl.BlockSpec((chunk, masks.shape[1]), lambda i, order: (i, 0)),
                whole(small),
                whole(wa),
                whole(wx),
            ],
            out_specs=(tile,) * 5 + (pl.BlockSpec((8, width), lambda i, order: (0, 0)),),
            scratch_shapes=[pltpu.VMEM((chunk + 8, width), f32), pltpu.VMEM((8, width), f32)],
        ),
        compiler_params=pltpu.CompilerParams(vmem_limit_bytes=VMEM_LIMIT),
        cost_estimate=cost(15),
        name="forward_scan",
    )(order, rec_pre, halo, masks, small, wa, wx)


def adjoint_kernel(
    order_ref, d_ref, w_ref, pre_ref, keep_ref, d_mixed_ref, prod_ref, adj_ref, heads_ref,
    keep_next, carry
):
    rows = d_ref.shape[0]
    d_mixed = lax.dot_general(d_ref[...], w_ref[...], contract_last, preferred_element_type=f32)
    d_mixed_ref[...] = d_mixed
    step = pl.program_id(0)

    @pl.when(step == 0)
    def _():
        keep_next[pl.ds(rows, 8)] = jnp.ones_like(keep_next[pl.ds(rows, 8)])
        carry[0:1] = jnp.ones_like(carry[0:1])
        carry[1:2] = jnp.zeros_like(carry[1:2])

    @pl.when(step > 0)
    def _():
        keep_next[pl.ds(rows, 8)] = keep_next[pl.ds(0, 8)]

    keep_next[pl.ds(0, rows)] = keep_ref[...]
    prod_ref[...] = keep_next[pl.ds(1, rows)]
    adj_ref[...] = d_mixed * gelu_tanh(pre_ref[:, 0 : adj_ref.shape[1]])
    tiles = rows // 8

    def body(i, held):
        prod_in, adj_in = held
        at = pl.ds(pl.multiple_of((tiles - 1 - i) * 8, 8), 8)
        keep, push = tile_scan(prod_ref[at], adj_ref[at], True)
        adj = push + keep * adj_in
        prod = keep * prod_in
        prod_ref[at] = prod
        adj_ref[at] = adj
        return prod[0:1], adj[0:1]

    prod_out, adj_out = lax.fori_loop(
        0, tiles, body, (carry[0:1], carry[1:2]), unroll=4
    )
    carry[0:1] = prod_out
    carry[1:2] = adj_out
    heads_ref[0:1] = keep_ref[0:1] * prod_out
    heads_ref[1:2] = keep_ref[0:1] * adj_out
    heads_ref[2:8] = jnp.zeros_like(heads_ref[2:8])


def adjoint_scan(order, d_rec, w_out, rec_pre, keep, chunk):
    rows, width = keep.shape
    last = rows // chunk - 1
    tile = pl.BlockSpec((chunk, width), lambda i, order: (order[last - i], 0))
    full = jax.ShapeDtypeStruct((rows, width), f32)
    return pl.pallas_call(
        adjoint_kernel,
        out_shape=(full, full, full, jax.ShapeDtypeStruct((8, width), f32)),
        grid_spec=pltpu.PrefetchScalarGridSpec(
            num_scalar_prefetch=1,
            grid=(rows // chunk,),
            in_specs=[
                pl.BlockSpec((chunk, d_rec.shape[1]), lambda i, order: (order[last - i], 0)),
                pl.BlockSpec((width, d_rec.shape[1]), lambda i, order: (0, 0)),
                pl.BlockSpec((chunk, 2 * width), lambda i, order: (order[last - i], 0)),
                tile,
            ],
            out_specs=(tile, tile, tile, pl.BlockSpec((8, width), lambda i, order: (0, 0))),
            scratch_shapes=[pltpu.VMEM((chunk + 8, width), f32), pltpu.VMEM((8, width), f32)],
        ),
        compiler_params=pltpu.CompilerParams(vmem_limit_bytes=VMEM_LIMIT),
        cost_estimate=cost(12),
        name="adjoint_scan",
    )(order, d_rec, w_out, rec_pre, keep)


def backward_kernel(
    order_ref,
    d_mixed_ref,
    pre_ref,
    state_ref,
    prod_ref,
    state_before_ref,
    prod_before_ref,
    adj_ref,
    adj_prod_ref,
    branch_ref,
    branch_before_ref,
    halo_ref,
    conved_ref,
    mask_ref,
    small_ref,
    enter_ref,
    wa_ref,
    wx_ref,
    d_pre_ref,
    sums_ref,
    edge_ref,
    ga_ref,
    gx_ref,
    ext,
    state_ext,
    later,
):
    rows, width = d_mixed_ref.shape
    step = pl.program_id(0)
    steps = pl.num_programs(0)
    state_in = enter_ref[0:1]
    adj_in = enter_ref[1:2]

    @pl.when(step == 0)
    def _():
        sums_ref[...] = jnp.zeros_like(sums_ref)
        ga_ref[...] = jnp.zeros_like(ga_ref)
        gx_ref[...] = jnp.zeros_like(gx_ref)
        for k in range(TAIL):
            later[k, pl.ds(rows, 8)] = jnp.zeros((8, width), f32)

    @pl.when(step > 0)
    def _():
        for k in range(TAIL):
            later[k, pl.ds(rows, 8)] = later[k, pl.ds(0, 8)]

    first = step == steps - 1

    @pl.when(first)
    def _():
        ext[pl.ds(0, 8)] = halo_ref[...]
        state_ext[pl.ds(0, 8)] = jnp.broadcast_to(state_in, (8, width))

    @pl.when(jnp.logical_not(first))
    def _():
        ext[pl.ds(0, 8)] = branch_before_ref[...].astype(f32)[8:16]
        state_ext[pl.ds(0, 8)] = state_before_ref[...] + prod_before_ref[...] * state_in

    ext[pl.ds(8, rows)] = branch_ref[...].astype(f32)
    state = state_ref[...] + prod_ref[...] * state_in
    state_ext[pl.ds(8, rows)] = state
    _, slope = gelu_pair(pre_ref[:, 0:width])
    d_pre_ref[:, 0:width] = (d_mixed_ref[...] * state * slope).astype(bf16)
    adjoint = adj_ref[...] + adj_prod_ref[...] * adj_in
    state_prev = state_ext[pl.ds(7, rows)]
    masks = mask_ref[...]
    conved_low = conved_ref[...]
    conved = conved_low.astype(f32)
    rates = small_ref[7:8]
    gate_a = sigmoid(
        jnp.dot(conved_low, wa_ref[...], preferred_element_type=f32) + small_ref[5:6]
    )
    gate_x = sigmoid(
        jnp.dot(conved_low, wx_ref[...], preferred_element_type=f32) + small_ref[6:7]
    )
    decay = jnp.exp(-decay_scale * gate_a * rates)
    square = 1.0 - decay * decay + push_shift
    inverse = lax.rsqrt(square)
    root = square * inverse
    d_decay = adjoint * (state_prev * masks[:, 0:1] - gate_x * conved * decay * inverse)
    slope_a = -decay_scale * d_decay * decay * gate_a
    d_logit_a = (slope_a * rates * (1.0 - gate_a)).astype(bf16)
    through = adjoint * root * gate_x
    d_logit_x = (through * conved * (1.0 - gate_x)).astype(bf16)
    d_conved = (
        through
        + lax.dot_general(d_logit_a, wa_ref[...], contract_last, preferred_element_type=f32)
        + lax.dot_general(d_logit_x, wx_ref[...], contract_last, preferred_element_type=f32)
    )
    d_conved = d_conved.astype(bf16).astype(f32)
    ga_ref[...] += lax.dot_general(
        conved_low, d_logit_a, contract_first, preferred_element_type=f32
    )
    gx_ref[...] += lax.dot_general(
        conved_low, d_logit_x, contract_first, preferred_element_type=f32
    )

    def total(v):
        return jnp.sum(v, axis=0, keepdims=True)

    sums_ref[0:1] += total(d_conved * ext[pl.ds(8, rows)])
    for k in range(1, CONV):
        masked = d_conved * masks[:, k - 1 : k]
        later[k - 1, pl.ds(0, rows)] = masked
        sums_ref[k : k + 1] += total(masked * ext[pl.ds(8 - k, rows)])
    sums_ref[4:5] += total(d_conved)
    sums_ref[5:6] += total(d_logit_a.astype(f32))
    sums_ref[6:7] += total(d_logit_x.astype(f32))
    sums_ref[7:8] += total(slope_a)
    d_branch = small_ref[0:1] * d_conved
    for k in range(1, CONV):
        d_branch = d_branch + small_ref[k : k + 1] * later[k - 1, pl.ds(k, rows)]
    d_pre_ref[:, width : 2 * width] = d_branch.astype(bf16)

    @pl.when(first)
    def _():
        for back in range(1, CONV):
            value = jnp.zeros((1, width), f32)
            for k in range(back, CONV):
                value = value + small_ref[k : k + 1] * later[k - 1, pl.ds(k - back, 1)]
            edge_ref[8 - back : 9 - back] = value
        edge_ref[0 : 8 - TAIL] = jnp.zeros((8 - TAIL, width), f32)


def backward_scan(
    order, d_mixed, rec_pre, state, prod, adj, adj_prod, branch_in, halo, conved, masks, small,
    enter, wa, wx, chunk,
):
    rows, width = state.shape
    last = rows // chunk - 1
    tile = pl.BlockSpec((chunk, width), lambda i, order: (order[last - i], 0))

    def before(size):
        per = chunk // size
        return pl.BlockSpec(
            (size, width),
            lambda i, order: (order[jnp.maximum(last - i - 1, 0)] * per + per - 1, 0),
        )

    pinned = lambda shape: pl.BlockSpec(shape, lambda i, order: (0, 0))
    whole = lambda a: pinned(a.shape)
    return pl.pallas_call(
        backward_kernel,
        out_shape=(
            jax.ShapeDtypeStruct((rows, 2 * width), bf16),
            jax.ShapeDtypeStruct((8, width), f32),
            jax.ShapeDtypeStruct((8, width), f32),
            jax.ShapeDtypeStruct((width, width), f32),
            jax.ShapeDtypeStruct((width, width), f32),
        ),
        grid_spec=pltpu.PrefetchScalarGridSpec(
            num_scalar_prefetch=1,
            grid=(rows // chunk,),
            in_specs=[
                tile,
                pl.BlockSpec((chunk, 2 * width), lambda i, order: (order[last - i], 0)),
                tile,
                tile,
                before(8),
                before(8),
                tile,
                tile,
                tile,
                before(16),
                whole(halo),
                tile,
                pl.BlockSpec((chunk, masks.shape[1]), lambda i, order: (last - i, 0)),
                whole(small),
                whole(enter),
                whole(wa),
                whole(wx),
            ],
            out_specs=(
                pl.BlockSpec((chunk, 2 * width), lambda i, order: (order[last - i], 0)),
                pinned((8, width)),
                pinned((8, width)),
                pinned((width, width)),
                pinned((width, width)),
            ),
            scratch_shapes=[
                pltpu.VMEM((chunk + 8, width), f32),
                pltpu.VMEM((chunk + 8, width), f32),
                pltpu.VMEM((TAIL, chunk + 8, width), f32),
            ],
        ),
        compiler_params=pltpu.CompilerParams(vmem_limit_bytes=VMEM_LIMIT),
        cost_estimate=cost(21),
        name="backward_scan",
    )(
        order, d_mixed, rec_pre, state, prod, state, prod, adj, adj_prod, branch_in, branch_in,
        halo, conved, masks, small, enter, wa, wx,
    )


def gated_kernel(n_ref, mine_ref, theirs_ref, w_ref, down_ref, hidden_ref, d_ref):
    ff = down_ref.shape[0]
    tile = 256
    normed = n_ref[...]
    cot = lax.select(
        pl.program_id(0) < pl.num_programs(0) // 2, mine_ref[...], theirs_ref[...]
    )

    def body(j, none):
        at = pl.ds(pl.multiple_of(j * tile, tile), tile)
        up_at = pl.ds(pl.multiple_of(ff + j * tile, tile), tile)
        gate = jnp.dot(normed, w_ref[:, at], preferred_element_type=f32)
        up = jnp.dot(normed, w_ref[:, up_at], preferred_element_type=f32)
        d_hidden = lax.dot_general(cot, down_ref[at], contract_last, preferred_element_type=f32)
        act, slope = gelu_pair(gate)
        hidden_ref[:, at] = (act * up).astype(bf16)
        d_ref[:, at] = (d_hidden * up * slope).astype(bf16)
        d_ref[:, up_at] = (d_hidden * act).astype(bf16)
        return none

    lax.fori_loop(0, ff // tile, body, 0)


def gated_unit(normed, cot_mine, cot_theirs, w_mlp, w_down):
    rows, width = normed.shape
    ff = w_down.shape[0]
    steps = 4
    tile = rows // steps
    row = lambda size: pl.BlockSpec((tile, size), lambda i: (i, 0))
    once = lambda a: pl.BlockSpec(a.shape, lambda i: (0, 0), pipeline_mode=pl.Buffered(1))
    return pl.pallas_call(
        gated_kernel,
        grid=(steps,),
        out_shape=(
            jax.ShapeDtypeStruct((rows, ff), bf16),
            jax.ShapeDtypeStruct((rows, 2 * ff), bf16),
        ),
        in_specs=[
            row(width),
            pl.BlockSpec((tile, width), lambda i: (jnp.minimum(i, steps // 2 - 1), 0)),
            pl.BlockSpec((tile, width), lambda i: (jnp.maximum(i - steps // 2, 0), 0)),
            once(w_mlp),
            once(w_down),
        ],
        out_specs=(row(ff), row(2 * ff)),
        compiler_params=pltpu.CompilerParams(vmem_limit_bytes=VMEM_LIMIT),
        cost_estimate=pl.CostEstimate(
            flops=6 * rows * width * ff, bytes_accessed=40 * 2**20, transcendentals=rows * ff
        ),
        name="gated_unit",
    )(normed, cot_mine, cot_theirs, w_mlp, w_down)


def down_kernel(h_ref, w_ref, mine_ref, theirs_ref):
    width = w_ref.shape[1]
    tile = 512
    hidden = h_ref[...]

    def into(ref):
        def body(j, none):
            at = pl.ds(pl.multiple_of(j * tile, tile), tile)
            ref[:, at] = jnp.dot(hidden, w_ref[:, at], preferred_element_type=f32).astype(bf16)
            return none

        lax.fori_loop(0, width // tile, body, 0)

    first = pl.program_id(0) < pl.num_programs(0) // 2
    pl.when(first)(lambda: into(mine_ref))
    pl.when(jnp.logical_not(first))(lambda: into(theirs_ref))


def down_rows(hidden, w_down):
    rows, ff = hidden.shape
    width = w_down.shape[1]
    steps = 4
    tile = rows // steps
    part = jax.ShapeDtypeStruct((rows // 2, width), bf16)
    return pl.pallas_call(
        down_kernel,
        grid=(steps,),
        out_shape=(part, part),
        in_specs=[
            pl.BlockSpec((tile, ff), lambda i: (i, 0)),
            pl.BlockSpec((ff, width), lambda i: (0, 0), pipeline_mode=pl.Buffered(1)),
        ],
        out_specs=(
            pl.BlockSpec((tile, width), lambda i: (jnp.minimum(i, steps // 2 - 1), 0)),
            pl.BlockSpec((tile, width), lambda i: (jnp.maximum(i - steps // 2, 0), 0)),
        ),
        compiler_params=pltpu.CompilerParams(vmem_limit_bytes=VMEM_LIMIT),
        cost_estimate=cost(0.1),
        name="down_rows",
    )(hidden, w_down)


def split_kernel(moves, a_ref, b_ref, o_ref):
    for source, block, at, start, size in moves:
        ref = (a_ref, b_ref)[source]
        o_ref[block, :, at : at + size] = ref[:, start : start + size]


def join_kernel(moves, x_ref, a_ref, b_ref, g_ref, oa_ref, ob_ref, og_ref):
    for source, block, at, start, size in moves:
        ref = (oa_ref, ob_ref)[source]
        ref[:, start : start + size] = x_ref[block, :, at : at + size].astype(f32)
    total = jnp.sum(a_ref[...].astype(f32) * oa_ref[...], axis=1, keepdims=True) + jnp.sum(
        b_ref[...].astype(f32) * ob_ref[...], axis=1, keepdims=True
    )
    wide = jnp.broadcast_to(total / g_ref[...], (total.shape[0], LANES))
    og_ref[...] = wide.T[0:1]


def split_blocks(a, b, moves):
    rows, width = a.shape
    return pl.pallas_call(
        functools.partial(split_kernel, moves),
        out_shape=jax.ShapeDtypeStruct((NF, rows, 2 * width // NF), a.dtype),
        compiler_params=pltpu.CompilerParams(vmem_limit_bytes=VMEM_LIMIT),
        cost_estimate=cost(4),
        name="split_blocks",
    )(a, b)


def join_blocks(x, a, b, gain, moves):
    rows, width = a.shape
    out = jax.ShapeDtypeStruct((rows, width), f32)
    return pl.pallas_call(
        functools.partial(join_kernel, moves),
        out_shape=(out, out, jax.ShapeDtypeStruct((1, rows), f32)),
        compiler_params=pltpu.CompilerParams(vmem_limit_bytes=VMEM_LIMIT),
        cost_estimate=cost(5),
        name="join_blocks",
    )(x, a, b, gain)


def pack_kernel(out_ref, ga_ref, gx_ref, sums_ref, o_ref, small):
    spread, _, chan_rows, total = o_ref.shape
    chans, width = out_ref.shape
    extra = total - width
    row = lax.broadcasted_iota(jnp.int32, (chans, chans), 0)
    col = lax.broadcasted_iota(jnp.int32, (chans, chans), 1)
    same = (row < BLK) == (col < BLK)
    at = lax.broadcasted_iota(jnp.int32, (chans, extra), 0)
    at = jnp.where(at < BLK, at, at - BLK)
    to = lax.broadcasted_iota(jnp.int32, (chans, extra), 1)

    def placed(ref, start):
        kept = jnp.where(same, ref[...], 0.0).astype(bf16)
        spot = jnp.where(to == at + start, 1.0, 0.0).astype(bf16)
        return jnp.dot(kept, spot, preferred_element_type=f32)

    rows = jnp.concatenate([sums_ref[...], jnp.zeros_like(sums_ref)]).astype(bf16)
    spot = jnp.where(
        lax.broadcasted_iota(jnp.int32, (16, extra), 0) + 2 * BLK
        == lax.broadcasted_iota(jnp.int32, (16, extra), 1),
        1.0,
        0.0,
    ).astype(bf16)
    small[...] = (
        placed(ga_ref, 0)
        + placed(gx_ref, BLK)
        + lax.dot_general(rows, spot, contract_first, preferred_element_type=f32)
    )
    for unit in range(2):
        for part in range(spread):
            here = pl.ds(unit * BLK + part * chan_rows, chan_rows)
            o_ref[part, unit, :, 0:width] = out_ref[here].astype(bf16)
            o_ref[part, unit, :, width:total] = small[here].astype(bf16)


def pack_sums(grad_out, grad_a, grad_x, sums, spread, chan_rows, total):
    chans, width = grad_out.shape
    return pl.pallas_call(
        pack_kernel,
        out_shape=jax.ShapeDtypeStruct((spread, 2, chan_rows, total), bf16),
        scratch_shapes=[pltpu.VMEM((chans, total - width), f32)],
        compiler_params=pltpu.CompilerParams(vmem_limit_bytes=VMEM_LIMIT),
        cost_estimate=cost(3),
        name="pack_sums",
    )(grad_out, grad_a, grad_x, sums)


def unpack_kernel(x_ref, out_ref, ga_ref, gx_ref, taps_ref, *row_refs):
    width = out_ref.shape[1]
    base = width + 2 * BLK
    out_ref[...] = x_ref[:, 0:width].astype(f32)
    ga_ref[...] = x_ref[:, width : width + BLK].astype(f32)
    gx_ref[...] = x_ref[:, width + BLK : base].astype(f32)
    last = base - base % LANES
    small = x_ref[:, last : last + LANES].astype(f32)
    taps_ref[...] = small[:, base - last : base - last + CONV]
    turned = small.T
    for i, ref in enumerate(row_refs):
        at = base - last + CONV + i
        ref[...] = turned[at : at + 1]


def unpack_sums(x, width):
    rows = x.shape[0]
    shape = lambda *dims: jax.ShapeDtypeStruct(dims, f32)
    return pl.pallas_call(
        unpack_kernel,
        out_shape=(shape(rows, width), shape(rows, BLK), shape(rows, BLK), shape(rows, CONV))
        + (shape(1, rows),) * 4,
        compiler_params=pltpu.CompilerParams(vmem_limit_bytes=VMEM_LIMIT),
        cost_estimate=cost(2),
        name="unpack_sums",
    )(x)


def pad_lanes(rows, width):
    have = rows.shape[-1]
    return jnp.pad(rows, ((0, 0), (0, width - have)))


def inverse_rms(rows):
    return lax.rsqrt(jnp.mean(rows * rows, axis=-1, keepdims=True) + norm_eps)


def norm_back(rows, scale, e):
    return scale * e - rows * (scale * scale * scale) * jnp.mean(e * rows, axis=-1, keepdims=True)


def on_device(
    tokens_in,
    segment_starts,
    cotangent,
    norm1_gain,
    rec_gate_weight,
    rec_in_weight,
    conv_weight,
    conv_bias,
    gate_a_weight,
    gate_a_bias,
    gate_x_weight,
    gate_x_bias,
    decay_rate,
    rec_out_weight,
    norm2_gain,
    mlp_gate_weight,
    mlp_up_weight,
    mlp_down_weight,
):
    count = lax.axis_size("z")
    z = lax.axis_index("z")
    spread = count // 2
    swap_axes = FEAT[len(FEAT) - (spread.bit_length() - 1) :]
    outer = NF // spread
    rows_tok, width = tokens_in.shape
    group_rows = NF * rows_tok
    chan_rows = conv_weight.shape[0]
    chans = chan_rows * count
    rows_w = rec_gate_weight.shape[0]
    ff_rows = mlp_down_weight.shape[0]
    ff = ff_rows * count
    chunk = 256

    chan_moves = [
        (
            source,
            k * spread + e,
            source * chans + zz * BLK,
            ((2 * e + zz) * outer + k) * BLK,
            BLK,
        )
        for source in range(2)
        for k in range(outer)
        for e in range(spread)
        for zz in range(2)
    ]
    ff_moves = [
        (source, f, source * ff + group * ff_rows, (group * NF + f) * ff_rows, ff_rows)
        for source in range(2)
        for f in range(NF)
        for group in range(count)
    ]
    place = [lax.axis_index(name) for name in FEAT]
    time = jnp.arange(NF, dtype=jnp.int32)
    bit = lambda value, here: jnp.where(value == here, 0, 1)
    order = (
        bit(time % 2, place[2]) * 4 + bit(time // 4, place[0]) * 2 + bit((time // 2) % 2, place[1])
    ).astype(jnp.int32)
    final = order[NF - 1] * rows_tok + rows_tok - 8

    pack = jnp.concatenate(
        [
            rec_out_weight,
            gate_a_weight,
            gate_x_weight,
            conv_weight,
            conv_bias[:, None],
            gate_a_bias[:, None],
            gate_x_bias[:, None],
            decay_rate[:, None],
        ],
        axis=1,
    )
    used = pack.shape[1]
    pack_width = -(-used // LANES) * LANES
    pack = pad_lanes(pack, pack_width)

    extra = jnp.concatenate(
        [
            pad_lanes(segment_starts.astype(bf16)[None], 2 * chans),
            pad_lanes(norm1_gain[None], 2 * chans),
            pad_lanes(norm2_gain[None], 2 * chans),
            jnp.zeros((13, 2 * chans), bf16),
        ],
        axis=0,
    )
    rec_send = jnp.concatenate(
        [
            split_blocks(rec_gate_weight, rec_in_weight, chan_moves),
            jnp.broadcast_to(extra[None], (NF, 16, 2 * chans)),
        ],
        axis=1,
    )
    pack_all = lax.all_gather(pack, "z", axis=0, tiled=True)
    (rec_got,) = exchange([rec_send], FEAT, 3)
    starts = rec_got[:, rows_w, :rows_tok].reshape(group_rows).astype(f32)

    plane_gains = jnp.stack(
        [
            rec_got[:, rows_w + 1, :rows_w].reshape(NF * rows_w),
            rec_got[:, rows_w + 2, :rows_w].reshape(NF * rows_w),
        ]
    ).astype(f32)
    gains = gather_groups(jnp.pad(plane_gains, ((0, 6), (0, 0))), count, 7)
    w_rec = lax.all_gather(
        rec_got[:, :rows_w].reshape(NF * rows_w, 2 * chans), "z", axis=0, tiled=True
    )
    mlp_send = split_blocks(mlp_gate_weight, mlp_up_weight, ff_moves)
    tokens_own, gains = hold(tokens_in, gains)
    tok_group, mlp_got = gather_exchange(tokens_own, mlp_send)
    tok_group, pack_all = hold(tok_group, pack_all)
    (pack_swap,) = exchange(
        [pack_all.reshape(spread, 2, chan_rows, pack_width)], swap_axes, 5
    )
    gain_one = gains[:, 0].reshape(1, width)
    gain_two = gains[:, 1].reshape(1, width)

    tok = tokens_in.astype(f32)
    tok_group = tok_group.astype(f32)
    normed = (tok_group * inverse_rms(tok_group) * gain_one).astype(bf16)

    w_mlp = lax.all_gather(mlp_got.reshape(NF * rows_w, 2 * ff), "z", axis=0, tiled=True)
    w_down = lax.all_gather(mlp_down_weight, "z", axis=0, tiled=True)

    mine = pack_swap.transpose(1, 0, 2, 3).reshape(chans, pack_width)
    w_out = mine[:, :width]
    small = mine[:, width + 2 * BLK : used].astype(f32).T

    unit = lax.broadcasted_iota(jnp.int32, (chans, chans), 0) // BLK
    same_block = unit == lax.broadcasted_iota(jnp.int32, (chans, chans), 1) // BLK

    def block_diag(w):
        return jnp.where(same_block, jnp.concatenate([w, w], axis=1), jnp.zeros((), w.dtype))

    wa = block_diag(mine[:, width : width + BLK])
    wx = block_diag(mine[:, width + BLK : width + 2 * BLK])

    open_one = 1.0 - starts
    ahead = jnp.concatenate([jnp.ones((TAIL,), f32), open_one])
    open_two = open_one * ahead[TAIL - 1 : TAIL - 1 + group_rows]
    open_three = open_two * ahead[TAIL - 2 : TAIL - 2 + group_rows]
    masks = jnp.stack([open_one, open_two, open_three], axis=1)
    end = open_one[group_rows - 2 :]
    later_open = jnp.concatenate(
        [jnp.zeros((8 - TAIL,), f32), (end[0] * end[1])[None], end[1:], jnp.ones((1,), f32)]
    )[:, None]

    rec_pre = jnp.dot(normed, w_rec, preferred_element_type=f32)
    rec_pre, cot_own = hold(rec_pre, cotangent)
    cot_x, cot_y = gather_near(cot_own)
    edge_rows = lax.dynamic_slice_in_dim(rec_pre, final, 8, 0)[:, chans:].astype(bf16)
    halo = lax.ppermute(
        edge_rows.astype(f32) * later_open, "z", [(i, i + 1) for i in range(count - 1)]
    )
    branch_in, conved, keep, prod, state_local, ends = forward_scan(
        order, rec_pre, halo, masks, small, wa, wx, chunk
    )
    ends, cot_x, cot_y = hold(ends, cot_x, cot_y)
    cot_top, cot_low = gather_diagonal(cot_x, cot_y)
    ends = gather_groups(ends, count, 2)
    state_in = jnp.zeros((1, chans), f32)
    for hop in range(count - 1):
        state_in = jnp.where(hop < z, ends[hop, 0:1] * state_in + ends[hop, 1:2], state_in)
    mixed = ((state_local + prod * state_in) * gelu_tanh(rec_pre[:, :chans])).astype(bf16)
    mixed_out = jnp.dot(mixed, w_out, preferred_element_type=f32).astype(bf16)
    mixed_out, cot_top, cot_low = hold(mixed_out, cot_top, cot_low)
    cot_chip = gather_chip(cotangent, cot_x, cot_y, cot_top, cot_low)
    cot_got = across(cot_chip, "c")
    middle = tok + scatter_feature(mixed_out)

    scale_two = inverse_rms(middle)
    normed_two = gather_feature((middle * scale_two * gain_two).astype(bf16))
    hidden, d_mlp = gated_unit(normed_two, cot_chip, cot_got, w_mlp, w_down)
    half_rows = group_rows // 2

    def back_rows(d, w):
        return lax.dot_general(d, w, contract_last, preferred_element_type=f32).astype(bf16)

    def over_rows(a, b_mine, b_theirs):
        return (
            lax.dot_general(a[:half_rows], b_mine, contract_first, preferred_element_type=f32)
            + lax.dot_general(a[half_rows:], b_theirs, contract_first, preferred_element_type=f32)
        ).astype(bf16)

    e_theirs = back_rows(d_mlp[half_rows:], w_mlp)
    d_mlp, e_theirs = hold(d_mlp, e_theirs)
    e_got = across(e_theirs, "c")
    e_mine = back_rows(d_mlp[:half_rows], w_mlp)
    e_keeps, e_x, e_y = scatter_near(e_mine, e_got)
    near_y, hidden = hold(e_keeps[0], hidden)
    e_keeps = (near_y,) + e_keeps[1:]
    down_part = over_rows(hidden, cot_chip, cot_got)
    down_part, hidden = hold(down_part, hidden)
    down_sum = lax.psum_scatter(down_part, "z", scatter_dimension=0, tiled=True)
    out_mine, out_theirs = down_rows(hidden, w_down)
    out_mine, out_theirs, e_x, e_y = hold(out_mine, out_theirs, e_x, e_y)
    e_two = gain_two * scatter_tail(e_keeps, e_x, e_y)
    d_middle = cotangent.astype(f32) + norm_back(middle, scale_two, e_two)
    d_own = d_middle.astype(bf16)
    d_x, d_y = gather_near(d_own)
    d_own, d_mlp, out_mine, out_theirs = hold(d_own, d_mlp, out_mine, out_theirs)
    out_got = across(out_theirs, "c")
    mlp_part = lax.dot_general(
        normed_two, d_mlp, contract_first, preferred_element_type=f32
    ).astype(bf16)
    out_keeps = scatter_keeps(out_mine, out_got)
    out_x, out_y = scatter_sends(out_mine, out_got)
    d_x, d_y, mlp_part, out_x, out_y, *out_keeps = hold(
        d_x, d_y, mlp_part, out_x, out_y, *out_keeps
    )
    mlp_sum = lax.psum_scatter(mlp_part, "z", scatter_dimension=0, tiled=True)
    d_rec = gather_tail(d_own, d_x, d_y)
    d_rec, down_sum, out_x, out_y = hold(d_rec, down_sum, out_x, out_y)
    out_x, out_y = across(out_x, "x"), across(out_y, "y")

    d_mixed, adj_prod, adj_local, heads = adjoint_scan(
        order, d_rec, mine, rec_pre, keep, chunk
    )
    from_later = [
        lax.ppermute(heads, "z", [(i + hop, i) for i in range(count - hop)])
        for hop in range(count - 1, 0, -1)
    ]
    *from_later, out_x, out_y = hold(*from_later, out_x, out_y)
    out_last = scatter_relay(out_keeps, out_x, out_y)
    adj_in = jnp.zeros((1, chans), f32)
    for one in from_later:
        adj_in = one[0:1] * adj_in + one[1:2]
    enter = jnp.concatenate([state_in, adj_in, jnp.zeros((6, chans), f32)])
    d_rec_pre, sums, edge, grad_a, grad_x = backward_scan(
        order, d_mixed, rec_pre, state_local, prod, adj_local, adj_prod, branch_in, halo, conved,
        masks, small, enter, wa, wx, chunk,
    )
    after = lax.ppermute(edge, "z", [(i + 1, i) for i in range(count - 1)]) * later_open
    edge, mixed = hold(edge, mixed)
    grad_out = lax.dot_general(mixed, d_rec, contract_first, preferred_element_type=f32)
    after, grad_out = hold(after, grad_out)
    tail_sum = lax.dynamic_slice_in_dim(d_rec_pre, final, 8, 0).astype(f32) + jnp.pad(
        after, ((0, 0), (chans, 0))
    )
    d_rec_pre = lax.dynamic_update_slice_in_dim(d_rec_pre, tail_sum.astype(bf16), final, 0)
    rec_part = lax.dot_general(
        normed, d_rec_pre, contract_first, preferred_element_type=f32
    ).astype(bf16)
    rec_part, d_rec_pre, grad_a, grad_x, sums, *out_last = hold(
        rec_part, d_rec_pre, grad_a, grad_x, sums, *out_last
    )
    layer_out = (middle + scatter_sum(out_keeps, out_x, out_y, *out_last)).astype(bf16)
    rec_sum = lax.psum_scatter(rec_part, "z", scatter_dimension=0, tiled=True)
    back_pack = pack_sums(grad_out, grad_a, grad_x, sums, spread, chan_rows, pack_width)
    (back_swap,) = exchange([back_pack], swap_axes, 5)
    back_swap = back_swap.reshape(count * chan_rows, pack_width)
    grad_down = down_sum.astype(f32)
    back_swap, d_rec_pre, layer_out, grad_down = hold(back_swap, d_rec_pre, layer_out, grad_down)
    mlp_sum, d_rec_pre = hold(mlp_sum, d_rec_pre)
    pack_sum = lax.psum_scatter(back_swap, "z", scatter_dimension=0, tiled=True)
    one_sum, mlp_back = scatter_dot(d_rec_pre, w_rec, mlp_sum.reshape(NF, rows_w, 2 * ff))
    one_sum, rec_sum = hold(one_sum, rec_sum)
    (rec_back,) = exchange([rec_sum.reshape(NF, rows_w, 2 * chans)], FEAT, 10)
    e_one = gain_one * one_sum
    grad_tokens = d_middle + norm_back(tok, inverse_rms(tok), e_one)
    grad_gate, grad_up, grad_gain_two = join_blocks(
        mlp_back, mlp_gate_weight, mlp_up_weight, norm2_gain.astype(f32)[:, None], ff_moves
    )
    grad_rec_gate, grad_rec_in, grad_gain_one = join_blocks(
        rec_back, rec_gate_weight, rec_in_weight, norm1_gain.astype(f32)[:, None], chan_moves
    )

    pack_sum, grad_gain_one, grad_gain_two, grad_tokens = hold(
        pack_sum, grad_gain_one, grad_gain_two, grad_tokens
    )
    grad_out, grad_a, grad_x, grad_taps, *grad_rows = unpack_sums(pack_sum, width)
    grad_offset, grad_a_bias, grad_x_bias, grad_rate = (r.reshape(chan_rows) for r in grad_rows)
    return (
        layer_out,
        grad_tokens,
        grad_gain_one.reshape(rows_w),
        grad_rec_gate,
        grad_rec_in,
        grad_taps,
        grad_offset,
        grad_a,
        grad_a_bias,
        grad_x,
        grad_x_bias,
        grad_rate,
        grad_out,
        grad_gain_two.reshape(rows_w),
        grad_gate,
        grad_up,
        grad_down,
    )


def solution(mesh):
    wide, narrow = mesh.shape["wide"], mesh.shape["narrow"]
    groups = wide * narrow // NF
    grid = Mesh(mesh.devices.reshape((groups,) + (2,) * len(FEAT)), ("z",) + FEAT)
    flat = P(("z",) + FEAT)
    wide_rows = P(("z",) + FEAT, None)
    one, two = flat, wide_rows
    return jax.shard_map(
        on_device,
        mesh=grid,
        in_specs=(
            two, one, two, one, two, two, two, one, two, one, two, one, one, two, one, two, two, two,
        ),
        out_specs=(
            two, two, one, two, two, two, one, two, one, two, one, one, two, one, two, two, two,
        ),
        check_vma=False,
    )
```

```python
import functools

import jax
import jax.numpy as jnp
from jax import lax
from jax.experimental import pallas as pl
from jax.experimental.pallas import tpu as pltpu
from jax.sharding import Mesh
from jax.sharding import PartitionSpec as P

BLK = 160
CONV = 4
TAIL = CONV - 1
LANES = 128
FEAT = ("x", "y", "c")
NF = 8
OWN, ACROSS_Y, ACROSS_X, DIAGONAL = 0, 1, 2, 3

norm_eps = 1e-06
decay_scale = 8.0
push_shift = 0.05
f32 = jnp.float32
bf16 = jnp.bfloat16
MESH = pl.DeviceIdType.MESH
contract_last = (((1,), (1,)), ((), ()))
contract_first = (((0,), (0,)), ((), ()))
VMEM_LIMIT = 56 * 2**20


def cost(micros, flops=0):
    return pl.CostEstimate(
        flops=int(flops), bytes_accessed=int(micros * 3.0e6), transcendentals=0
    )


def hbm_spec():
    return pl.BlockSpec(memory_space=pl.ANY)


def vmem_spec():
    return pl.BlockSpec(memory_space=pltpu.VMEM)


def greet(peers):
    barrier = pltpu.get_barrier_semaphore()
    for device in peers:
        pl.semaphore_signal(barrier, inc=1, device_id=device, device_id_type=MESH)
    pl.semaphore_wait(barrier, len(peers))


def feature_place():
    return tuple(lax.axis_index(name) for name in FEAT)


def remote(src, dst, send_sem, recv_sem, device):
    return pltpu.make_async_remote_copy(
        src_ref=src,
        dst_ref=dst,
        send_sem=send_sem,
        recv_sem=recv_sem,
        device_id=device,
        device_id_type=MESH,
    )


def gather_kernel(*refs):
    if len(refs) == 5:
        x_ref, o_ref, local_sem, ssem, rsem = refs
        extra = ()
    else:
        x_ref, b_ref, s_ref, t_ref, o_ref, e_ref, so_ref, to_ref = refs[:8]
        local_sem, ssem, rsem = refs[8:11]
        peers, kept, copies = exchange_parts(FEAT, b_ref, e_ref, *refs[11:14])
        others, own_small, small = groups_parts((s_ref, t_ref), (so_ref, to_ref), *refs[14:])
        extra = (peers + others, [kept] + own_small, copies + small)
    x, y, c = feature_place()
    to_x, to_y, to_c = {"x": 1 - x}, {"y": 1 - y}, {"c": 1 - c}
    half = x_ref.shape[0] // 2
    top, low = pl.ds(0, half), pl.ds(half, half)
    greet(extra[0] if extra else (to_x, to_y, to_c))

    def copy(i, src, dst, device):
        return remote(src, dst, ssem.at[i], rsem.at[i], device)

    own = pltpu.make_async_copy(x_ref, o_ref.at[OWN], local_sem)
    x_top = copy(0, x_ref.at[top], o_ref.at[ACROSS_X, top], to_x)
    x_low = copy(1, x_ref.at[low], o_ref.at[ACROSS_X, low], to_x)
    y_low = copy(2, x_ref.at[low], o_ref.at[ACROSS_Y, low], to_y)
    y_top = copy(3, x_ref.at[top], o_ref.at[ACROSS_Y, top], to_y)
    c_own = copy(4, x_ref, o_ref.at[4 + OWN], to_c)
    y_fwd = copy(5, o_ref.at[ACROSS_X, top], o_ref.at[DIAGONAL, top], to_y)
    x_fwd = copy(6, o_ref.at[ACROSS_Y, low], o_ref.at[DIAGONAL, low], to_x)
    c_x = copy(7, o_ref.at[ACROSS_X], o_ref.at[4 + ACROSS_X], to_c)
    c_y = copy(8, o_ref.at[ACROSS_Y], o_ref.at[4 + ACROSS_Y], to_c)
    c_d = copy(9, o_ref.at[DIAGONAL], o_ref.at[4 + DIAGONAL], to_c)
    for one in (x_top, y_low, x_low, y_top, c_own, own):
        one.start()
    if extra:
        for one in extra[1] + extra[2]:
            one.start()
    x_top.wait_recv()
    y_fwd.start()
    y_low.wait_recv()
    x_fwd.start()
    x_low.wait_recv()
    c_x.start()
    y_top.wait_recv()
    c_y.start()
    y_fwd.wait_recv()
    x_fwd.wait_recv()
    c_d.start()
    for one in (c_own, c_x, c_y, c_d):
        one.wait_recv()
    for one in (x_top, x_low, y_low, y_top, c_own, y_fwd, x_fwd, c_x, c_y, c_d):
        one.wait_send()
    own.wait()
    if extra:
        for one in extra[2] + extra[1]:
            one.wait()


def gather_feature(block):
    rows, width = block.shape
    out = pl.pallas_call(
        gather_kernel,
        out_shape=jax.ShapeDtypeStruct((NF, rows, width), block.dtype),
        in_specs=[vmem_spec()],
        out_specs=hbm_spec(),
        scratch_shapes=[
            pltpu.SemaphoreType.DMA,
            pltpu.SemaphoreType.DMA((10,)),
            pltpu.SemaphoreType.DMA((10,)),
        ],
        compiler_params=pltpu.CompilerParams(
            collective_id=0, has_side_effects=True, vmem_limit_bytes=VMEM_LIMIT
        ),
        cost_estimate=cost(40),
        name="gather_feature",
    )(block)
    return out.reshape(NF * rows, width)


def scatter_flow(
    p_theirs, o_ref, own, other, total, rx, ry, relay, rx_last, ry_last, ssem, rsem,
    peers, begin, stage, ready
):
    x, y, c = feature_place()
    to_x, to_y, to_c = {"x": 1 - x}, {"y": 1 - y}, {"c": 1 - c}
    rows, width = o_ref.shape
    half = rows // 2
    top, low = pl.ds(0, half), pl.ds(half, half)
    step = 16

    def copy(i, src, dst, device):
        return remote(src, dst, ssem.at[i], rsem.at[i], device)

    greet(peers or (to_x, to_y, to_c))
    begin()
    cross = [copy(r, p_theirs(r), other.at[r], to_c) for r in range(4)]

    def add_into(r):
        ready(r)
        cross[r].wait_recv()

        def body(i, none):
            at = pl.ds(pl.multiple_of(i * step, step), step)
            total[r, at] = (own[r, at].astype(f32) + other[r, at].astype(f32)).astype(total.dtype)
            return none

        lax.fori_loop(0, rows // step, body, 0)

    x_diag = copy(4, total.at[DIAGONAL, top], rx.at[1], to_x)
    y_diag = copy(5, total.at[DIAGONAL, low], ry.at[1], to_y)
    x_near = copy(6, total.at[ACROSS_X, top], rx.at[0], to_x)
    y_near = copy(7, total.at[ACROSS_Y, low], ry.at[0], to_y)
    y_last = copy(8, relay.at[0], ry_last, to_y)
    x_last = copy(9, relay.at[1], rx_last, to_x)

    stage(DIAGONAL, cross)
    stage(ACROSS_X, cross)
    add_into(DIAGONAL)
    x_diag.start()
    y_diag.start()
    stage(ACROSS_Y, cross)
    add_into(ACROSS_X)
    x_near.start()
    stage(OWN, cross)
    add_into(ACROSS_Y)
    y_near.start()
    ready(OWN)
    cross[OWN].wait_recv()

    def relay_add(slot, r, start, got):
        def body(i, none):
            at = pl.ds(pl.multiple_of(i * step, step), step)
            here = pl.ds(pl.multiple_of(start + i * step, step), step)
            relay[slot, at] = (total[r, here].astype(f32) + got[1, at].astype(f32)).astype(
                relay.dtype
            )
            return none

        lax.fori_loop(0, half // step, body, 0)

    x_diag.wait_recv()
    relay_add(0, ACROSS_Y, 0, rx)
    y_last.start()
    y_diag.wait_recv()
    relay_add(1, ACROSS_X, half, ry)
    x_last.start()

    def finish(start, near, last):
        def body(i, none):
            at = pl.ds(pl.multiple_of(i * step, step), step)
            here = pl.ds(pl.multiple_of(start + i * step, step), step)
            o_ref[here] = (own[OWN, here].astype(f32) + other[OWN, here].astype(f32)) + (
                near[0, at].astype(f32) + last[at].astype(f32)
            )
            return none

        lax.fori_loop(0, half // step, body, 0)

    x_near.wait_recv()
    y_last.wait_recv()
    finish(0, rx, ry_last)
    y_near.wait_recv()
    x_last.wait_recv()
    finish(half, ry, rx_last)
    for one in cross + [x_diag, y_diag, x_near, y_near, x_last, y_last]:
        one.wait_send()


def scatter_kernel(
    p_ref, o_ref, own, other, total, rx, ry, relay, rx_last, ry_last, lsem, ssem, rsem
):
    loads = [pltpu.make_async_copy(p_ref.at[r], own.at[r], lsem.at[r]) for r in range(4)]
    for r in (DIAGONAL, ACROSS_X, ACROSS_Y, OWN):
        loads[r].start()
    scatter_flow(
        lambda r: p_ref.at[4 + r], o_ref, own, other, total, rx, ry, relay, rx_last, ry_last,
        ssem, rsem, None, lambda: None, lambda r, cross: cross[r].start(),
        lambda r: loads[r].wait(),
    )


def scatter_dot_kernel(
    a_ref, w_ref, b_ref, o_ref, e_ref, theirs, own, other, total, rx, ry, relay, rx_last, ry_last,
    ssem, rsem, local_sem, xssem, xrsem
):
    peers, kept, copies = exchange_parts(FEAT, b_ref, e_ref, local_sem, xssem, xrsem)
    rows, width = o_ref.shape
    tile = 512

    def begin():
        kept.start()
        for one in copies:
            one.start()

    def dot_into(block, ref, r):
        rows_in = a_ref[pl.ds(block * rows, rows)]

        def body(j, none):
            at = pl.ds(pl.multiple_of(j * tile, tile), tile)
            ref[r, :, at] = lax.dot_general(
                rows_in, w_ref[at], contract_last, preferred_element_type=f32
            ).astype(ref.dtype)
            return none

        lax.fori_loop(0, width // tile, body, 0)

    def stage(r, cross):
        dot_into(4 + r, theirs, r)
        cross[r].start()
        dot_into(r, own, r)

    scatter_flow(
        lambda r: theirs.at[r], o_ref, own, other, total, rx, ry, relay, rx_last, ry_last,
        ssem, rsem, peers, begin, stage, lambda r: None,
    )
    for one in copies:
        one.wait()
    kept.wait()


def scatter_dot(rows_in, w, blocks):
    rows, width = rows_in.shape[0] // NF, w.shape[0]
    half = rows // 2
    kind = rows_in.dtype
    four = pltpu.VMEM((4, rows, width), kind)
    two = pltpu.VMEM((2, half, width), kind)
    one = pltpu.VMEM((half, width), kind)
    return pl.pallas_call(
        scatter_dot_kernel,
        out_shape=(
            jax.ShapeDtypeStruct((rows, width), f32),
            jax.ShapeDtypeStruct(blocks.shape, blocks.dtype),
        ),
        in_specs=[vmem_spec()] * 3,
        out_specs=(vmem_spec(), hbm_spec()),
        scratch_shapes=[four] * 4
        + [two] * 3
        + [one] * 2
        + [
            pltpu.SemaphoreType.DMA((10,)),
            pltpu.SemaphoreType.DMA((10,)),
            pltpu.SemaphoreType.DMA,
            pltpu.SemaphoreType.DMA((NF - 1,)),
            pltpu.SemaphoreType.DMA((NF - 1,)),
        ],
        compiler_params=pltpu.CompilerParams(
            collective_id=11, has_side_effects=True, vmem_limit_bytes=VMEM_LIMIT
        ),
        cost_estimate=cost(55),
        name="scatter_dot",
    )(rows_in, w, blocks)


def scatter_feature(partial):
    rows, width = partial.shape[0] // NF, partial.shape[1]
    half = rows // 2
    kind = partial.dtype
    return pl.pallas_call(
        scatter_kernel,
        out_shape=jax.ShapeDtypeStruct((rows, width), f32),
        in_specs=[hbm_spec()],
        out_specs=vmem_spec(),
        scratch_shapes=[
            pltpu.VMEM((4, rows, width), kind),
            pltpu.VMEM((4, rows, width), kind),
            pltpu.VMEM((4, rows, width), kind),
            pltpu.VMEM((2, half, width), kind),
            pltpu.VMEM((2, half, width), kind),
            pltpu.VMEM((2, half, width), kind),
            pltpu.VMEM((half, width), kind),
            pltpu.VMEM((half, width), kind),
            pltpu.SemaphoreType.DMA((4,)),
            pltpu.SemaphoreType.DMA((10,)),
            pltpu.SemaphoreType.DMA((10,)),
        ],
        compiler_params=pltpu.CompilerParams(
            collective_id=1, has_side_effects=True, vmem_limit_bytes=VMEM_LIMIT
        ),
        cost_estimate=cost(45),
        name="scatter_feature",
    )(partial.reshape(NF, rows, width))


def across(value, axis):
    return lax.ppermute(value, axis, [(0, 1), (1, 0)])


def hold(*values):
    return lax.optimization_barrier(values)


def gather_near(block):
    return across(block, "x"), across(block, "y")


def gather_diagonal(by_x, by_y):
    half = by_x.shape[0] // 2
    return across(by_x[:half], "y"), across(by_y[half:], "x")


def gather_chip(block, by_x, by_y, d_top, d_low):
    return jnp.concatenate([block, by_y, by_x, d_top, d_low])


def scatter_halves(mine, got):
    shape = (4, 2, mine.shape[0] // 8, mine.shape[1])
    return mine.reshape(shape), got.reshape(shape)


def add_low(a, b):
    return (a.astype(f32) + b.astype(f32)).astype(a.dtype)


def scatter_sends(mine, got):
    mine, got = scatter_halves(mine, got)
    by_x = add_low(mine[ACROSS_X:, 0], got[ACROSS_X:, 0])
    by_y = add_low(mine[ACROSS_Y::2, 1], got[ACROSS_Y::2, 1])
    return by_x, by_y


def scatter_keeps(mine, got):
    mine, got = scatter_halves(mine, got)
    near_y = add_low(mine[ACROSS_Y, 0], got[ACROSS_Y, 0])
    near_x = add_low(mine[ACROSS_X, 1], got[ACROSS_X, 1])
    return near_y, near_x, add_low(mine[OWN], got[OWN])


def scatter_near(mine, got):
    mine, got = hold(mine, got)
    by_x, by_y = scatter_sends(mine, got)
    by_x, by_y, mine, got = hold(by_x, by_y, mine, got)
    return scatter_keeps(mine, got), across(by_x, "x"), across(by_y, "y")


def scatter_relay(keeps, by_x, by_y):
    near_y, near_x, _ = keeps
    return across(add_low(near_y, by_x[1]), "y"), across(add_low(near_x, by_y[1]), "x")


def scatter_sum(keeps, by_x, by_y, y_last, x_last):
    own = keeps[2].astype(f32)
    upper = own[0] + by_x[0].astype(f32) + y_last.astype(f32)
    lower = own[1] + by_y[0].astype(f32) + x_last.astype(f32)
    return jnp.concatenate([upper, lower])


def gather_tail_kernel(x_ref, bx_ref, by_ref, o_ref, lsem, ssem, rsem):
    x, y, c = feature_place()
    to_x, to_y, to_c = {"x": 1 - x}, {"y": 1 - y}, {"c": 1 - c}
    half = x_ref.shape[0] // 2
    top, low = pl.ds(0, half), pl.ds(half, half)

    def copy(i, src, dst, device):
        return remote(src, dst, ssem.at[i], rsem.at[i], device)

    places = ((x_ref, OWN), (by_ref, ACROSS_Y), (bx_ref, ACROSS_X))
    local = [
        pltpu.make_async_copy(ref, o_ref.at[slot], lsem.at[i])
        for i, (ref, slot) in enumerate(places)
    ]
    greet((to_x, to_y, to_c))
    y_fwd = copy(0, bx_ref.at[top], o_ref.at[DIAGONAL, top], to_y)
    x_fwd = copy(1, by_ref.at[low], o_ref.at[DIAGONAL, low], to_x)
    cross = [
        copy(2 + i, ref, o_ref.at[4 + slot], to_c) for i, (ref, slot) in enumerate(places)
    ]
    last = copy(5, o_ref.at[DIAGONAL], o_ref.at[4 + DIAGONAL], to_c)
    for one in [y_fwd, x_fwd] + cross + local:
        one.start()
    y_fwd.wait_recv()
    x_fwd.wait_recv()
    last.start()
    for one in cross + [last]:
        one.wait_recv()
    for one in cross + [y_fwd, x_fwd, last]:
        one.wait_send()
    for one in local:
        one.wait()


def gather_tail(block, by_x, by_y):
    rows, width = block.shape
    out = pl.pallas_call(
        gather_tail_kernel,
        out_shape=jax.ShapeDtypeStruct((NF, rows, width), block.dtype),
        in_specs=[vmem_spec()] * 3,
        out_specs=hbm_spec(),
        scratch_shapes=[
            pltpu.SemaphoreType.DMA((3,)),
            pltpu.SemaphoreType.DMA((6,)),
            pltpu.SemaphoreType.DMA((6,)),
        ],
        compiler_params=pltpu.CompilerParams(
            collective_id=8, has_side_effects=True, vmem_limit_bytes=VMEM_LIMIT
        ),
        cost_estimate=cost(16),
        name="gather_tail",
    )(block, by_x, by_y)
    return out.reshape(NF * rows, width)


def scatter_tail_kernel(
    ny_ref, nx_ref, own_ref, bx_ref, by_ref, o_ref, near, own, bx, by, relay, last, lsem, ssem, rsem
):
    x, y, c = feature_place()
    to_x, to_y = {"x": 1 - x}, {"y": 1 - y}
    half = o_ref.shape[0] // 2
    step = 16

    def load(i, src, dst):
        one = pltpu.make_async_copy(src, dst, lsem.at[i])
        one.start()
        return one

    loads = [
        load(0, ny_ref, near.at[0]),
        load(1, bx_ref, bx),
        load(2, nx_ref, near.at[1]),
        load(3, by_ref, by),
        load(4, own_ref, own),
    ]
    greet((to_x, to_y))
    sends = [
        remote(relay.at[0], last.at[0], ssem.at[0], rsem.at[0], to_y),
        remote(relay.at[1], last.at[1], ssem.at[1], rsem.at[1], to_x),
    ]

    def tiles(body):
        def one(i, none):
            body(pl.ds(pl.multiple_of(i * step, step), step), i * step)
            return none

        lax.fori_loop(0, half // step, one, 0)

    for side, got in ((0, bx), (1, by)):
        loads[2 * side].wait()
        loads[2 * side + 1].wait()

        def add(at, _, side=side, got=got):
            relay[side, at] = (near[side, at].astype(f32) + got[1, at].astype(f32)).astype(
                relay.dtype
            )

        tiles(add)
        sends[side].start()
    loads[4].wait()
    for side, got in ((0, bx), (1, by)):

        def base(at, start, side=side, got=got):
            here = pl.ds(pl.multiple_of(side * half + start, step), step)
            o_ref[here] = own[side, at].astype(f32) + got[0, at].astype(f32)

        tiles(base)
    for side in range(2):
        sends[side].wait_recv()

        def finish(at, start, side=side):
            here = pl.ds(pl.multiple_of(side * half + start, step), step)
            o_ref[here] = o_ref[here] + last[side, at].astype(f32)

        tiles(finish)
    for one in sends:
        one.wait_send()


def scatter_tail(keeps, by_x, by_y):
    _, half, width = by_x.shape
    kind = by_x.dtype
    pair = pltpu.VMEM((2, half, width), kind)
    return pl.pallas_call(
        scatter_tail_kernel,
        out_shape=jax.ShapeDtypeStruct((2 * half, width), f32),
        in_specs=[hbm_spec()] * 5,
        out_specs=vmem_spec(),
        scratch_shapes=[pair] * 6
        + [
            pltpu.SemaphoreType.DMA((5,)),
            pltpu.SemaphoreType.DMA((2,)),
            pltpu.SemaphoreType.DMA((2,)),
        ],
        compiler_params=pltpu.CompilerParams(
            collective_id=9, has_side_effects=True, vmem_limit_bytes=VMEM_LIMIT
        ),
        cost_estimate=cost(16),
        name="scatter_tail",
    )(*keeps, by_x, by_y)


def exchange_parts(axes, x_ref, o_ref, local_sem, ssem, rsem):
    place = [lax.axis_index(name) for name in axes]
    count = 2 ** len(axes)

    def rank(coords):
        total = 0
        for one in coords:
            total = total * 2 + one
        return total

    mine = rank(place)
    own = pltpu.make_async_copy(x_ref.at[mine], o_ref.at[mine], local_sem)
    peers, copies = [], []
    for mask in range(count - 1, 0, -1):
        bits = [(mask // 2 ** (len(axes) - 1 - i)) % 2 for i in range(len(axes))]
        coords = [1 - p if bit else p for p, bit in zip(place, bits)]
        device = {name: q for name, q, bit in zip(axes, coords, bits) if bit}
        peers.append(device)
        copies.append(
            remote(
                x_ref.at[rank(coords)],
                o_ref.at[mine],
                ssem.at[mask - 1],
                rsem.at[mask - 1],
                device,
            )
        )
    return peers, own, copies


def exchange_kernel(axes, *refs):
    count = (len(refs) - 3) // 2
    sources, targets = refs[:count], refs[count : 2 * count]
    local_sem, ssem, rsem = refs[2 * count :]
    parts = [
        exchange_parts(axes, sources[i], targets[i], local_sem.at[i], ssem.at[i], rsem.at[i])
        for i in range(count)
    ]
    for _, own, _ in parts:
        own.start()
    greet(parts[0][0])
    for _, _, copies in parts:
        for one in copies:
            one.start()
    for _, own, copies in parts:
        for one in copies:
            one.wait()
        own.wait()


def exchange(arrays, axes, ident):
    peers = 2 ** len(axes) - 1
    count = len(arrays)
    return pl.pallas_call(
        functools.partial(exchange_kernel, axes),
        out_shape=tuple(jax.ShapeDtypeStruct(a.shape, a.dtype) for a in arrays),
        in_specs=[vmem_spec()] * count,
        out_specs=(hbm_spec(),) * count,
        scratch_shapes=[
            pltpu.SemaphoreType.DMA((count,)),
            pltpu.SemaphoreType.DMA((count, peers)),
            pltpu.SemaphoreType.DMA((count, peers)),
        ],
        compiler_params=pltpu.CompilerParams(
            collective_id=ident, has_side_effects=True, vmem_limit_bytes=VMEM_LIMIT
        ),
        cost_estimate=cost(15),
        name="exchange",
    )(*arrays)


def gather_exchange(block, blocks, smalls, count):
    rows, width = block.shape
    out, got, *small = pl.pallas_call(
        gather_kernel,
        out_shape=(
            jax.ShapeDtypeStruct((NF, rows, width), block.dtype),
            jax.ShapeDtypeStruct(blocks.shape, blocks.dtype),
        )
        + tuple(jax.ShapeDtypeStruct((count,) + a.shape, a.dtype) for a in smalls),
        in_specs=[vmem_spec()] * 4,
        out_specs=(hbm_spec(),) * 2 + (vmem_spec(),) * 2,
        scratch_shapes=[
            pltpu.SemaphoreType.DMA,
            pltpu.SemaphoreType.DMA((10,)),
            pltpu.SemaphoreType.DMA((10,)),
            pltpu.SemaphoreType.DMA,
            pltpu.SemaphoreType.DMA((NF - 1,)),
            pltpu.SemaphoreType.DMA((NF - 1,)),
            pltpu.SemaphoreType.DMA((2,)),
            pltpu.SemaphoreType.DMA((2, count - 1)),
            pltpu.SemaphoreType.DMA((2, count - 1)),
        ],
        compiler_params=pltpu.CompilerParams(
            collective_id=4, has_side_effects=True, vmem_limit_bytes=VMEM_LIMIT
        ),
        cost_estimate=cost(55),
        name="gather_exchange",
    )(block, blocks, *smalls)
    return out.reshape(NF * rows, width), got, *small


def groups_parts(sources, targets, local_sem, ssem, rsem):
    count = targets[0].shape[0]
    z = lax.axis_index("z")
    many = range(len(sources))
    own = [pltpu.make_async_copy(sources[k], targets[k].at[z], local_sem.at[k]) for k in many]
    peers = [{"z": lax.rem(z + hop, count)} for hop in range(1, count)]
    copies = [
        remote(sources[k], targets[k].at[z], ssem.at[k, i], rsem.at[k, i], device)
        for k in many
        for i, device in enumerate(peers)
    ]
    return peers, own, copies


def groups_kernel(*refs):
    many = (len(refs) - 3) // 2
    peers, own, copies = groups_parts(refs[:many], refs[many : 2 * many], *refs[2 * many :])
    for one in own:
        one.start()
    greet(peers)
    for one in copies:
        one.start()
    for one in copies + own:
        one.wait()


def gather_groups(blocks, count, ident):
    many = len(blocks)
    return pl.pallas_call(
        groups_kernel,
        out_shape=tuple(jax.ShapeDtypeStruct((count,) + b.shape, b.dtype) for b in blocks),
        in_specs=[vmem_spec()] * many,
        out_specs=(vmem_spec(),) * many,
        scratch_shapes=[
            pltpu.SemaphoreType.DMA((many,)),
            pltpu.SemaphoreType.DMA((many, count - 1)),
            pltpu.SemaphoreType.DMA((many, count - 1)),
        ],
        compiler_params=pltpu.CompilerParams(collective_id=ident, has_side_effects=True),
        cost_estimate=cost(5),
        name="gather_groups",
    )(*blocks)


def gelu_tanh(values):
    return jax.nn.gelu(values, approximate=True)


def sigmoid(v):
    return 0.5 + 0.5 * jnp.tanh(0.5 * v)


def gelu_pair(v):
    root = 0.7978845608028654
    cube = 0.044715
    square = v * v
    t = jnp.tanh(root * (v + cube * square * v))
    value = 0.5 * v * (1.0 + t)
    slope = 0.5 * (1.0 + t) + 0.5 * v * (1.0 - t * t) * root * (1.0 + 3.0 * cube * square)
    return value, slope


def tile_scan(keep, push, reverse):
    rows = lax.broadcasted_iota(jnp.int32, keep.shape, 0)
    count = keep.shape[0]
    hop = 1
    while hop < count:
        if reverse:
            inside = rows < count - hop
            shift = count - hop
        else:
            inside = rows >= hop
            shift = hop
        keep_near = jnp.where(inside, pltpu.roll(keep, shift, 0), 1.0)
        push_near = jnp.where(inside, pltpu.roll(push, shift, 0), 0.0)
        push = push + keep * push_near
        keep = keep * keep_near
        hop *= 2
    return keep, push


def conv_of(ext, masks, taps, offset, rows):
    value = offset + taps[0:1] * ext[pl.ds(8, rows)]
    for k in range(1, CONV):
        value = value + taps[k : k + 1] * ext[pl.ds(8 - k, rows)] * masks[:, k - 1 : k]
    return value


def forward_kernel(
    order_ref,
    pre_ref,
    halo_ref,
    mask_ref,
    small_ref,
    wa_ref,
    wx_ref,
    branch_ref,
    conved_ref,
    keep_ref,
    prod_ref,
    state_ref,
    ends_ref,
    ext,
    carry,
):
    rows, width = branch_ref.shape
    step = pl.program_id(0)
    branch = pre_ref[:, width : 2 * width].astype(bf16)
    branch_ref[...] = branch

    @pl.when(step == 0)
    def _():
        ext[pl.ds(0, 8)] = halo_ref[...]
        carry[0:1] = jnp.ones_like(carry[0:1])
        carry[1:2] = jnp.zeros_like(carry[1:2])

    @pl.when(step > 0)
    def _():
        ext[pl.ds(0, 8)] = ext[pl.ds(rows, 8)]

    ext[pl.ds(8, rows)] = branch.astype(f32)
    masks = mask_ref[...]
    conved = conv_of(ext, masks, small_ref, small_ref[4:5], rows).astype(bf16)
    conved_ref[...] = conved
    logit_a = jnp.dot(conved, wa_ref[...], preferred_element_type=f32) + small_ref[5:6]
    logit_x = jnp.dot(conved, wx_ref[...], preferred_element_type=f32) + small_ref[6:7]
    decay = jnp.exp(-decay_scale * sigmoid(logit_a) * small_ref[7:8])
    keep_ref[...] = decay * masks[:, 0:1]
    state_ref[...] = (
        jnp.sqrt(1.0 - decay * decay + push_shift) * sigmoid(logit_x) * conved.astype(f32)
    )

    def body(i, held):
        prod_in, state_in = held
        at = pl.ds(pl.multiple_of(i * 8, 8), 8)
        keep, push = tile_scan(keep_ref[at], state_ref[at], False)
        state = push + keep * state_in
        prod = keep * prod_in
        prod_ref[at] = prod
        state_ref[at] = state
        return prod[7:8], state[7:8]

    prod_out, state_out = lax.fori_loop(
        0, rows // 8, body, (carry[0:1], carry[1:2]), unroll=4
    )
    carry[0:1] = prod_out
    carry[1:2] = state_out
    ends_ref[0:1] = prod_out
    ends_ref[1:2] = state_out
    ends_ref[2:8] = jnp.zeros_like(ends_ref[2:8])


def forward_scan(order, rec_pre, halo, masks, small, wa, wx, chunk):
    rows, width = rec_pre.shape[0], rec_pre.shape[1] // 2
    tile = pl.BlockSpec((chunk, width), lambda i, order: (order[i], 0))
    whole = lambda a: pl.BlockSpec(a.shape, lambda i, order: (0, 0))
    full = jax.ShapeDtypeStruct((rows, width), f32)
    low = jax.ShapeDtypeStruct((rows, width), bf16)
    return pl.pallas_call(
        forward_kernel,
        out_shape=(
            low,
            low,
            full,
            full,
            full,
            jax.ShapeDtypeStruct((8, width), f32),
        ),
        grid_spec=pltpu.PrefetchScalarGridSpec(
            num_scalar_prefetch=1,
            grid=(rows // chunk,),
            in_specs=[
                pl.BlockSpec((chunk, 2 * width), lambda i, order: (order[i], 0)),
                whole(halo),
                pl.BlockSpec((chunk, masks.shape[1]), lambda i, order: (i, 0)),
                whole(small),
                whole(wa),
                whole(wx),
            ],
            out_specs=(tile,) * 5 + (pl.BlockSpec((8, width), lambda i, order: (0, 0)),),
            scratch_shapes=[pltpu.VMEM((chunk + 8, width), f32), pltpu.VMEM((8, width), f32)],
        ),
        compiler_params=pltpu.CompilerParams(vmem_limit_bytes=VMEM_LIMIT),
        cost_estimate=cost(15),
        name="forward_scan",
    )(order, rec_pre, halo, masks, small, wa, wx)


def adjoint_kernel(
    order_ref, d_ref, w_ref, pre_ref, keep_ref, d_mixed_ref, prod_ref, adj_ref, heads_ref,
    keep_next, carry
):
    rows = d_ref.shape[0]
    d_mixed = lax.dot_general(d_ref[...], w_ref[...], contract_last, preferred_element_type=f32)
    d_mixed_ref[...] = d_mixed
    step = pl.program_id(0)

    @pl.when(step == 0)
    def _():
        keep_next[pl.ds(rows, 8)] = jnp.ones_like(keep_next[pl.ds(rows, 8)])
        carry[0:1] = jnp.ones_like(carry[0:1])
        carry[1:2] = jnp.zeros_like(carry[1:2])

    @pl.when(step > 0)
    def _():
        keep_next[pl.ds(rows, 8)] = keep_next[pl.ds(0, 8)]

    keep_next[pl.ds(0, rows)] = keep_ref[...]
    prod_ref[...] = keep_next[pl.ds(1, rows)]
    adj_ref[...] = d_mixed * gelu_tanh(pre_ref[:, 0 : adj_ref.shape[1]])
    tiles = rows // 8

    def body(i, held):
        prod_in, adj_in = held
        at = pl.ds(pl.multiple_of((tiles - 1 - i) * 8, 8), 8)
        keep, push = tile_scan(prod_ref[at], adj_ref[at], True)
        adj = push + keep * adj_in
        prod = keep * prod_in
        prod_ref[at] = prod
        adj_ref[at] = adj
        return prod[0:1], adj[0:1]

    prod_out, adj_out = lax.fori_loop(
        0, tiles, body, (carry[0:1], carry[1:2]), unroll=4
    )
    carry[0:1] = prod_out
    carry[1:2] = adj_out
    heads_ref[0:1] = keep_ref[0:1] * prod_out
    heads_ref[1:2] = keep_ref[0:1] * adj_out
    heads_ref[2:8] = jnp.zeros_like(heads_ref[2:8])


def adjoint_scan(order, d_rec, w_out, rec_pre, keep, chunk):
    rows, width = keep.shape
    last = rows // chunk - 1
    tile = pl.BlockSpec((chunk, width), lambda i, order: (order[last - i], 0))
    full = jax.ShapeDtypeStruct((rows, width), f32)
    return pl.pallas_call(
        adjoint_kernel,
        out_shape=(full, full, full, jax.ShapeDtypeStruct((8, width), f32)),
        grid_spec=pltpu.PrefetchScalarGridSpec(
            num_scalar_prefetch=1,
            grid=(rows // chunk,),
            in_specs=[
                pl.BlockSpec((chunk, d_rec.shape[1]), lambda i, order: (order[last - i], 0)),
                pl.BlockSpec((width, d_rec.shape[1]), lambda i, order: (0, 0)),
                pl.BlockSpec((chunk, 2 * width), lambda i, order: (order[last - i], 0)),
                tile,
            ],
            out_specs=(tile, tile, tile, pl.BlockSpec((8, width), lambda i, order: (0, 0))),
            scratch_shapes=[pltpu.VMEM((chunk + 8, width), f32), pltpu.VMEM((8, width), f32)],
        ),
        compiler_params=pltpu.CompilerParams(vmem_limit_bytes=VMEM_LIMIT),
        cost_estimate=cost(12),
        name="adjoint_scan",
    )(order, d_rec, w_out, rec_pre, keep)


def backward_kernel(
    order_ref,
    d_mixed_ref,
    pre_ref,
    state_ref,
    prod_ref,
    state_before_ref,
    prod_before_ref,
    adj_ref,
    adj_prod_ref,
    branch_ref,
    branch_before_ref,
    halo_ref,
    conved_ref,
    mask_ref,
    small_ref,
    enter_ref,
    wa_ref,
    wx_ref,
    d_pre_ref,
    sums_ref,
    edge_ref,
    ga_ref,
    gx_ref,
    ext,
    state_ext,
    later,
):
    rows, width = d_mixed_ref.shape
    step = pl.program_id(0)
    steps = pl.num_programs(0)
    state_in = enter_ref[0:1]
    adj_in = enter_ref[1:2]

    @pl.when(step == 0)
    def _():
        sums_ref[...] = jnp.zeros_like(sums_ref)
        ga_ref[...] = jnp.zeros_like(ga_ref)
        gx_ref[...] = jnp.zeros_like(gx_ref)
        for k in range(TAIL):
            later[k, pl.ds(rows, 8)] = jnp.zeros((8, width), f32)

    @pl.when(step > 0)
    def _():
        for k in range(TAIL):
            later[k, pl.ds(rows, 8)] = later[k, pl.ds(0, 8)]

    first = step == steps - 1

    @pl.when(first)
    def _():
        ext[pl.ds(0, 8)] = halo_ref[...]
        state_ext[pl.ds(0, 8)] = jnp.broadcast_to(state_in, (8, width))

    @pl.when(jnp.logical_not(first))
    def _():
        ext[pl.ds(0, 8)] = branch_before_ref[...].astype(f32)[8:16]
        state_ext[pl.ds(0, 8)] = state_before_ref[...] + prod_before_ref[...] * state_in

    ext[pl.ds(8, rows)] = branch_ref[...].astype(f32)
    state = state_ref[...] + prod_ref[...] * state_in
    state_ext[pl.ds(8, rows)] = state
    _, slope = gelu_pair(pre_ref[:, 0:width])
    d_pre_ref[:, 0:width] = (d_mixed_ref[...] * state * slope).astype(bf16)
    adjoint = adj_ref[...] + adj_prod_ref[...] * adj_in
    state_prev = state_ext[pl.ds(7, rows)]
    masks = mask_ref[...]
    conved_low = conved_ref[...]
    conved = conved_low.astype(f32)
    rates = small_ref[7:8]
    gate_a = sigmoid(
        jnp.dot(conved_low, wa_ref[...], preferred_element_type=f32) + small_ref[5:6]
    )
    gate_x = sigmoid(
        jnp.dot(conved_low, wx_ref[...], preferred_element_type=f32) + small_ref[6:7]
    )
    decay = jnp.exp(-decay_scale * gate_a * rates)
    square = 1.0 - decay * decay + push_shift
    inverse = lax.rsqrt(square)
    root = square * inverse
    d_decay = adjoint * (state_prev * masks[:, 0:1] - gate_x * conved * decay * inverse)
    slope_a = -decay_scale * d_decay * decay * gate_a
    d_logit_a = (slope_a * rates * (1.0 - gate_a)).astype(bf16)
    through = adjoint * root * gate_x
    d_logit_x = (through * conved * (1.0 - gate_x)).astype(bf16)
    d_conved = (
        through
        + lax.dot_general(d_logit_a, wa_ref[...], contract_last, preferred_element_type=f32)
        + lax.dot_general(d_logit_x, wx_ref[...], contract_last, preferred_element_type=f32)
    )
    d_conved = d_conved.astype(bf16).astype(f32)
    ga_ref[...] += lax.dot_general(
        conved_low, d_logit_a, contract_first, preferred_element_type=f32
    )
    gx_ref[...] += lax.dot_general(
        conved_low, d_logit_x, contract_first, preferred_element_type=f32
    )

    def total(v):
        return jnp.sum(v, axis=0, keepdims=True)

    sums_ref[0:1] += total(d_conved * ext[pl.ds(8, rows)])
    for k in range(1, CONV):
        masked = d_conved * masks[:, k - 1 : k]
        later[k - 1, pl.ds(0, rows)] = masked
        sums_ref[k : k + 1] += total(masked * ext[pl.ds(8 - k, rows)])
    sums_ref[4:5] += total(d_conved)
    sums_ref[5:6] += total(d_logit_a.astype(f32))
    sums_ref[6:7] += total(d_logit_x.astype(f32))
    sums_ref[7:8] += total(slope_a)
    d_branch = small_ref[0:1] * d_conved
    for k in range(1, CONV):
        d_branch = d_branch + small_ref[k : k + 1] * later[k - 1, pl.ds(k, rows)]
    d_pre_ref[:, width : 2 * width] = d_branch.astype(bf16)

    @pl.when(first)
    def _():
        for back in range(1, CONV):
            value = jnp.zeros((1, width), f32)
            for k in range(back, CONV):
                value = value + small_ref[k : k + 1] * later[k - 1, pl.ds(k - back, 1)]
            edge_ref[8 - back : 9 - back] = value
        edge_ref[0 : 8 - TAIL] = jnp.zeros((8 - TAIL, width), f32)


def backward_scan(
    order, d_mixed, rec_pre, state, prod, adj, adj_prod, branch_in, halo, conved, masks, small,
    enter, wa, wx, chunk,
):
    rows, width = state.shape
    last = rows // chunk - 1
    tile = pl.BlockSpec((chunk, width), lambda i, order: (order[last - i], 0))

    def before(size):
        per = chunk // size
        return pl.BlockSpec(
            (size, width),
            lambda i, order: (order[jnp.maximum(last - i - 1, 0)] * per + per - 1, 0),
        )

    pinned = lambda shape: pl.BlockSpec(shape, lambda i, order: (0, 0))
    whole = lambda a: pinned(a.shape)
    return pl.pallas_call(
        backward_kernel,
        out_shape=(
            jax.ShapeDtypeStruct((rows, 2 * width), bf16),
            jax.ShapeDtypeStruct((8, width), f32),
            jax.ShapeDtypeStruct((8, width), f32),
            jax.ShapeDtypeStruct((width, width), f32),
            jax.ShapeDtypeStruct((width, width), f32),
        ),
        grid_spec=pltpu.PrefetchScalarGridSpec(
            num_scalar_prefetch=1,
            grid=(rows // chunk,),
            in_specs=[
                tile,
                pl.BlockSpec((chunk, 2 * width), lambda i, order: (order[last - i], 0)),
                tile,
                tile,
                before(8),
                before(8),
                tile,
                tile,
                tile,
                before(16),
                whole(halo),
                tile,
                pl.BlockSpec((chunk, masks.shape[1]), lambda i, order: (last - i, 0)),
                whole(small),
                whole(enter),
                whole(wa),
                whole(wx),
            ],
            out_specs=(
                pl.BlockSpec((chunk, 2 * width), lambda i, order: (order[last - i], 0)),
                pinned((8, width)),
                pinned((8, width)),
                pinned((width, width)),
                pinned((width, width)),
            ),
            scratch_shapes=[
                pltpu.VMEM((chunk + 8, width), f32),
                pltpu.VMEM((chunk + 8, width), f32),
                pltpu.VMEM((TAIL, chunk + 8, width), f32),
            ],
        ),
        compiler_params=pltpu.CompilerParams(vmem_limit_bytes=VMEM_LIMIT),
        cost_estimate=cost(21),
        name="backward_scan",
    )(
        order, d_mixed, rec_pre, state, prod, state, prod, adj, adj_prod, branch_in, branch_in,
        halo, conved, masks, small, enter, wa, wx,
    )


def gated_kernel(n_ref, mine_ref, theirs_ref, w_ref, down_ref, hidden_ref, d_ref):
    ff = down_ref.shape[0]
    tile = 256
    normed = n_ref[...]
    cot = lax.select(
        pl.program_id(0) < pl.num_programs(0) // 2, mine_ref[...], theirs_ref[...]
    )

    def body(j, none):
        at = pl.ds(pl.multiple_of(j * tile, tile), tile)
        up_at = pl.ds(pl.multiple_of(ff + j * tile, tile), tile)
        gate = jnp.dot(normed, w_ref[:, at], preferred_element_type=f32)
        up = jnp.dot(normed, w_ref[:, up_at], preferred_element_type=f32)
        d_hidden = lax.dot_general(cot, down_ref[at], contract_last, preferred_element_type=f32)
        act, slope = gelu_pair(gate)
        hidden_ref[:, at] = (act * up).astype(bf16)
        d_ref[:, at] = (d_hidden * up * slope).astype(bf16)
        d_ref[:, up_at] = (d_hidden * act).astype(bf16)
        return none

    lax.fori_loop(0, ff // tile, body, 0)


def gated_unit(normed, cot_mine, cot_theirs, w_mlp, w_down):
    rows, width = normed.shape
    ff = w_down.shape[0]
    steps = 4
    tile = rows // steps
    row = lambda size: pl.BlockSpec((tile, size), lambda i: (i, 0))
    once = lambda a: pl.BlockSpec(a.shape, lambda i: (0, 0), pipeline_mode=pl.Buffered(1))
    return pl.pallas_call(
        gated_kernel,
        grid=(steps,),
        out_shape=(
            jax.ShapeDtypeStruct((rows, ff), bf16),
            jax.ShapeDtypeStruct((rows, 2 * ff), bf16),
        ),
        in_specs=[
            row(width),
            pl.BlockSpec((tile, width), lambda i: (jnp.minimum(i, steps // 2 - 1), 0)),
            pl.BlockSpec((tile, width), lambda i: (jnp.maximum(i - steps // 2, 0), 0)),
            once(w_mlp),
            once(w_down),
        ],
        out_specs=(row(ff), row(2 * ff)),
        compiler_params=pltpu.CompilerParams(vmem_limit_bytes=VMEM_LIMIT),
        cost_estimate=pl.CostEstimate(
            flops=6 * rows * width * ff, bytes_accessed=40 * 2**20, transcendentals=rows * ff
        ),
        name="gated_unit",
    )(normed, cot_mine, cot_theirs, w_mlp, w_down)


def down_kernel(h_ref, w_ref, mine_ref, theirs_ref):
    width = w_ref.shape[1]
    tile = 512
    hidden = h_ref[...]

    def into(ref):
        def body(j, none):
            at = pl.ds(pl.multiple_of(j * tile, tile), tile)
            ref[:, at] = jnp.dot(hidden, w_ref[:, at], preferred_element_type=f32).astype(bf16)
            return none

        lax.fori_loop(0, width // tile, body, 0)

    first = pl.program_id(0) < pl.num_programs(0) // 2
    pl.when(first)(lambda: into(mine_ref))
    pl.when(jnp.logical_not(first))(lambda: into(theirs_ref))


def down_rows(hidden, w_down):
    rows, ff = hidden.shape
    width = w_down.shape[1]
    steps = 4
    tile = rows // steps
    part = jax.ShapeDtypeStruct((rows // 2, width), bf16)
    return pl.pallas_call(
        down_kernel,
        grid=(steps,),
        out_shape=(part, part),
        in_specs=[
            pl.BlockSpec((tile, ff), lambda i: (i, 0)),
            pl.BlockSpec((ff, width), lambda i: (0, 0), pipeline_mode=pl.Buffered(1)),
        ],
        out_specs=(
            pl.BlockSpec((tile, width), lambda i: (jnp.minimum(i, steps // 2 - 1), 0)),
            pl.BlockSpec((tile, width), lambda i: (jnp.maximum(i - steps // 2, 0), 0)),
        ),
        compiler_params=pltpu.CompilerParams(vmem_limit_bytes=VMEM_LIMIT),
        cost_estimate=cost(0.1),
        name="down_rows",
    )(hidden, w_down)


def split_kernel(moves, a_ref, b_ref, o_ref):
    for source, block, at, start, size in moves:
        ref = (a_ref, b_ref)[source]
        o_ref[block, :, at : at + size] = ref[:, start : start + size]


def join_kernel(moves, x_ref, a_ref, b_ref, g_ref, oa_ref, ob_ref, og_ref):
    for source, block, at, start, size in moves:
        ref = (oa_ref, ob_ref)[source]
        ref[:, start : start + size] = x_ref[block, :, at : at + size].astype(f32)
    total = jnp.sum(a_ref[...].astype(f32) * oa_ref[...], axis=1, keepdims=True) + jnp.sum(
        b_ref[...].astype(f32) * ob_ref[...], axis=1, keepdims=True
    )
    wide = jnp.broadcast_to(total / g_ref[...], (total.shape[0], LANES))
    og_ref[...] = wide.T[0:1]


def split_blocks(a, b, moves):
    rows, width = a.shape
    return pl.pallas_call(
        functools.partial(split_kernel, moves),
        out_shape=jax.ShapeDtypeStruct((NF, rows, 2 * width // NF), a.dtype),
        compiler_params=pltpu.CompilerParams(vmem_limit_bytes=VMEM_LIMIT),
        cost_estimate=cost(4),
        name="split_blocks",
    )(a, b)


def join_blocks(x, a, b, gain, moves):
    rows, width = a.shape
    out = jax.ShapeDtypeStruct((rows, width), f32)
    return pl.pallas_call(
        functools.partial(join_kernel, moves),
        out_shape=(out, out, jax.ShapeDtypeStruct((1, rows), f32)),
        compiler_params=pltpu.CompilerParams(vmem_limit_bytes=VMEM_LIMIT),
        cost_estimate=cost(5),
        name="join_blocks",
    )(x, a, b, gain)


def pack_kernel(out_ref, ga_ref, gx_ref, sums_ref, o_ref, small):
    spread, _, chan_rows, total = o_ref.shape
    chans, width = out_ref.shape
    extra = total - width
    row = lax.broadcasted_iota(jnp.int32, (chans, chans), 0)
    col = lax.broadcasted_iota(jnp.int32, (chans, chans), 1)
    same = (row < BLK) == (col < BLK)
    at = lax.broadcasted_iota(jnp.int32, (chans, extra), 0)
    at = jnp.where(at < BLK, at, at - BLK)
    to = lax.broadcasted_iota(jnp.int32, (chans, extra), 1)

    def placed(ref, start):
        kept = jnp.where(same, ref[...], 0.0).astype(bf16)
        spot = jnp.where(to == at + start, 1.0, 0.0).astype(bf16)
        return jnp.dot(kept, spot, preferred_element_type=f32)

    rows = jnp.concatenate([sums_ref[...], jnp.zeros_like(sums_ref)]).astype(bf16)
    spot = jnp.where(
        lax.broadcasted_iota(jnp.int32, (16, extra), 0) + 2 * BLK
        == lax.broadcasted_iota(jnp.int32, (16, extra), 1),
        1.0,
        0.0,
    ).astype(bf16)
    small[...] = (
        placed(ga_ref, 0)
        + placed(gx_ref, BLK)
        + lax.dot_general(rows, spot, contract_first, preferred_element_type=f32)
    )
    for unit in range(2):
        for part in range(spread):
            here = pl.ds(unit * BLK + part * chan_rows, chan_rows)
            o_ref[part, unit, :, 0:width] = out_ref[here].astype(bf16)
            o_ref[part, unit, :, width:total] = small[here].astype(bf16)


def pack_sums(grad_out, grad_a, grad_x, sums, spread, chan_rows, total):
    chans, width = grad_out.shape
    return pl.pallas_call(
        pack_kernel,
        out_shape=jax.ShapeDtypeStruct((spread, 2, chan_rows, total), bf16),
        scratch_shapes=[pltpu.VMEM((chans, total - width), f32)],
        compiler_params=pltpu.CompilerParams(vmem_limit_bytes=VMEM_LIMIT),
        cost_estimate=cost(3),
        name="pack_sums",
    )(grad_out, grad_a, grad_x, sums)


def unpack_kernel(x_ref, out_ref, ga_ref, gx_ref, taps_ref, *row_refs):
    width = out_ref.shape[1]
    base = width + 2 * BLK
    out_ref[...] = x_ref[:, 0:width].astype(f32)
    ga_ref[...] = x_ref[:, width : width + BLK].astype(f32)
    gx_ref[...] = x_ref[:, width + BLK : base].astype(f32)
    last = base - base % LANES
    small = x_ref[:, last : last + LANES].astype(f32)
    taps_ref[...] = small[:, base - last : base - last + CONV]
    turned = small.T
    for i, ref in enumerate(row_refs):
        at = base - last + CONV + i
        ref[...] = turned[at : at + 1]


def unpack_sums(x, width):
    rows = x.shape[0]
    shape = lambda *dims: jax.ShapeDtypeStruct(dims, f32)
    return pl.pallas_call(
        unpack_kernel,
        out_shape=(shape(rows, width), shape(rows, BLK), shape(rows, BLK), shape(rows, CONV))
        + (shape(1, rows),) * 4,
        compiler_params=pltpu.CompilerParams(vmem_limit_bytes=VMEM_LIMIT),
        cost_estimate=cost(2),
        name="unpack_sums",
    )(x)


def pad_lanes(rows, width):
    have = rows.shape[-1]
    return jnp.pad(rows, ((0, 0), (0, width - have)))


def inverse_rms(rows):
    return lax.rsqrt(jnp.mean(rows * rows, axis=-1, keepdims=True) + norm_eps)


def norm_back(rows, scale, e):
    return scale * e - rows * (scale * scale * scale) * jnp.mean(e * rows, axis=-1, keepdims=True)


def on_device(
    tokens_in,
    segment_starts,
    cotangent,
    norm1_gain,
    rec_gate_weight,
    rec_in_weight,
    conv_weight,
    conv_bias,
    gate_a_weight,
    gate_a_bias,
    gate_x_weight,
    gate_x_bias,
    decay_rate,
    rec_out_weight,
    norm2_gain,
    mlp_gate_weight,
    mlp_up_weight,
    mlp_down_weight,
):
    count = lax.axis_size("z")
    z = lax.axis_index("z")
    spread = count // 2
    swap_axes = FEAT[len(FEAT) - (spread.bit_length() - 1) :]
    outer = NF // spread
    rows_tok, width = tokens_in.shape
    group_rows = NF * rows_tok
    chan_rows = conv_weight.shape[0]
    chans = chan_rows * count
    rows_w = rec_gate_weight.shape[0]
    ff_rows = mlp_down_weight.shape[0]
    ff = ff_rows * count
    chunk = 256

    chan_moves = [
        (
            source,
            k * spread + e,
            source * chans + zz * BLK,
            ((2 * e + zz) * outer + k) * BLK,
            BLK,
        )
        for source in range(2)
        for k in range(outer)
        for e in range(spread)
        for zz in range(2)
    ]
    ff_moves = [
        (source, f, source * ff + group * ff_rows, (group * NF + f) * ff_rows, ff_rows)
        for source in range(2)
        for f in range(NF)
        for group in range(count)
    ]
    place = [lax.axis_index(name) for name in FEAT]
    time = jnp.arange(NF, dtype=jnp.int32)
    bit = lambda value, here: jnp.where(value == here, 0, 1)
    order = (
        bit(time % 2, place[2]) * 4 + bit(time // 4, place[0]) * 2 + bit((time // 2) % 2, place[1])
    ).astype(jnp.int32)
    final = order[NF - 1] * rows_tok + rows_tok - 8

    pack = jnp.concatenate(
        [
            gate_a_weight,
            gate_x_weight,
            conv_weight,
            conv_bias[:, None],
            gate_a_bias[:, None],
            gate_x_bias[:, None],
            decay_rate[:, None],
        ],
        axis=1,
    )
    used = pack.shape[1]
    extra_width = -(-used // LANES) * LANES
    pack_width = width + extra_width
    pack = pad_lanes(pack, extra_width)

    extra = jnp.concatenate(
        [
            pad_lanes(segment_starts.astype(bf16)[None], 2 * chans),
            pad_lanes(norm1_gain[None], 2 * chans),
            pad_lanes(norm2_gain[None], 2 * chans),
            jnp.zeros((13, 2 * chans), bf16),
        ],
        axis=0,
    )
    rec_send = jnp.concatenate(
        [
            split_blocks(rec_gate_weight, rec_in_weight, chan_moves),
            jnp.broadcast_to(extra[None], (NF, 16, 2 * chans)),
        ],
        axis=1,
    )
    out_all = lax.all_gather(rec_out_weight, "z", axis=0, tiled=True)
    (rec_got,) = exchange([rec_send], FEAT, 3)
    starts = rec_got[:, rows_w, :rows_tok].reshape(group_rows).astype(f32)

    plane_gains = jnp.stack(
        [
            rec_got[:, rows_w + 1, :rows_w].reshape(NF * rows_w),
            rec_got[:, rows_w + 2, :rows_w].reshape(NF * rows_w),
        ]
    ).astype(f32)
    rec_mine = rec_got[:, :rows_w].reshape(NF * rows_w, 2 * chans)
    w_rec = lax.all_gather(rec_mine, "z", axis=0, tiled=True)
    mlp_send = split_blocks(mlp_gate_weight, mlp_up_weight, ff_moves)
    tok_group, mlp_got, gains, pack_all = gather_exchange(
        tokens_in, mlp_send, [jnp.pad(plane_gains, ((0, 6), (0, 0))), pack], count
    )
    tok_group, pack_all, out_all = hold(tok_group, pack_all, out_all)
    out_swap, pack_swap = exchange(
        [
            out_all.reshape(spread, 2, chan_rows, width),
            pack_all.reshape(spread, 2, chan_rows, extra_width),
        ],
        swap_axes,
        12,
    )
    gain_one = gains[:, 0].reshape(1, width)
    gain_two = gains[:, 1].reshape(1, width)

    tok = tokens_in.astype(f32)
    tok_group = tok_group.astype(f32)
    normed = (tok_group * inverse_rms(tok_group) * gain_one).astype(bf16)

    w_mlp = lax.all_gather(mlp_got.reshape(NF * rows_w, 2 * ff), "z", axis=0, tiled=True)
    w_down = lax.all_gather(mlp_down_weight, "z", axis=0, tiled=True)

    w_out = out_swap.transpose(1, 0, 2, 3).reshape(chans, width)
    mine = pack_swap.transpose(1, 0, 2, 3).reshape(chans, extra_width)
    small = mine[:, 2 * BLK : used].astype(f32).T

    unit = lax.broadcasted_iota(jnp.int32, (chans, chans), 0) // BLK
    same_block = unit == lax.broadcasted_iota(jnp.int32, (chans, chans), 1) // BLK

    def block_diag(w):
        return jnp.where(same_block, jnp.concatenate([w, w], axis=1), jnp.zeros((), w.dtype))

    wa = block_diag(mine[:, :BLK])
    wx = block_diag(mine[:, BLK : 2 * BLK])

    open_one = 1.0 - starts
    ahead = jnp.concatenate([jnp.ones((TAIL,), f32), open_one])
    open_two = open_one * ahead[TAIL - 1 : TAIL - 1 + group_rows]
    open_three = open_two * ahead[TAIL - 2 : TAIL - 2 + group_rows]
    masks = jnp.stack([open_one, open_two, open_three], axis=1)
    end = open_one[group_rows - 2 :]
    later_open = jnp.concatenate(
        [jnp.zeros((8 - TAIL,), f32), (end[0] * end[1])[None], end[1:], jnp.ones((1,), f32)]
    )[:, None]

    rec_pre = jnp.dot(normed, w_rec, preferred_element_type=f32)
    rec_pre, cot_own = hold(rec_pre, cotangent)
    cot_x, cot_y = gather_near(cot_own)
    edge_rows = lax.dynamic_slice_in_dim(rec_pre, final, 8, 0)[:, chans:].astype(bf16)
    halo = lax.ppermute(
        edge_rows.astype(f32) * later_open, "z", [(i, i + 1) for i in range(count - 1)]
    )
    branch_in, conved, keep, prod, state_local, ends = forward_scan(
        order, rec_pre, halo, masks, small, wa, wx, chunk
    )
    ends, cot_x, cot_y = hold(ends, cot_x, cot_y)
    cot_top, cot_low = gather_diagonal(cot_x, cot_y)
    (ends,) = gather_groups([ends], count, 2)
    state_in = jnp.zeros((1, chans), f32)
    for hop in range(count - 1):
        state_in = jnp.where(hop < z, ends[hop, 0:1] * state_in + ends[hop, 1:2], state_in)
    mixed = ((state_local + prod * state_in) * gelu_tanh(rec_pre[:, :chans])).astype(bf16)
    mixed_out = jnp.dot(mixed, w_out, preferred_element_type=f32).astype(bf16)
    mixed_out, cot_top, cot_low = hold(mixed_out, cot_top, cot_low)
    cot_chip = gather_chip(cotangent, cot_x, cot_y, cot_top, cot_low)
    cot_got = across(cot_chip, "c")
    middle = tok + scatter_feature(mixed_out)

    scale_two = inverse_rms(middle)
    normed_two = gather_feature((middle * scale_two * gain_two).astype(bf16))
    hidden, d_mlp = gated_unit(normed_two, cot_chip, cot_got, w_mlp, w_down)
    half_rows = group_rows // 2

    def back_rows(d, w):
        return lax.dot_general(d, w, contract_last, preferred_element_type=f32).astype(bf16)

    def over_rows(a, b_mine, b_theirs):
        return (
            lax.dot_general(a[:half_rows], b_mine, contract_first, preferred_element_type=f32)
            + lax.dot_general(a[half_rows:], b_theirs, contract_first, preferred_element_type=f32)
        ).astype(bf16)

    e_theirs = back_rows(d_mlp[half_rows:], w_mlp)
    d_mlp, e_theirs = hold(d_mlp, e_theirs)
    e_got = across(e_theirs, "c")
    e_mine = back_rows(d_mlp[:half_rows], w_mlp)
    e_keeps, e_x, e_y = scatter_near(e_mine, e_got)
    near_y, hidden = hold(e_keeps[0], hidden)
    e_keeps = (near_y,) + e_keeps[1:]
    down_part = over_rows(hidden, cot_chip, cot_got)
    down_part, hidden = hold(down_part, hidden)
    down_sum = lax.psum_scatter(down_part, "z", scatter_dimension=0, tiled=True)
    out_mine, out_theirs = down_rows(hidden, w_down)
    out_mine, out_theirs, e_x, e_y = hold(out_mine, out_theirs, e_x, e_y)
    e_two = gain_two * scatter_tail(e_keeps, e_x, e_y)
    d_middle = cotangent.astype(f32) + norm_back(middle, scale_two, e_two)
    d_own = d_middle.astype(bf16)
    d_x, d_y = gather_near(d_own)
    d_own, d_mlp, out_mine, out_theirs = hold(d_own, d_mlp, out_mine, out_theirs)
    out_got = across(out_theirs, "c")
    mlp_part = lax.dot_general(
        normed_two, d_mlp, contract_first, preferred_element_type=f32
    ).astype(bf16)
    out_keeps = scatter_keeps(out_mine, out_got)
    out_x, out_y = scatter_sends(out_mine, out_got)
    d_x, d_y, mlp_part, out_x, out_y, *out_keeps = hold(
        d_x, d_y, mlp_part, out_x, out_y, *out_keeps
    )
    mlp_sum = lax.psum_scatter(mlp_part, "z", scatter_dimension=0, tiled=True)
    d_rec = gather_tail(d_own, d_x, d_y)
    d_rec, down_sum, out_x, out_y = hold(d_rec, down_sum, out_x, out_y)
    out_x, out_y = across(out_x, "x"), across(out_y, "y")

    d_mixed, adj_prod, adj_local, heads = adjoint_scan(
        order, d_rec, w_out, rec_pre, keep, chunk
    )
    from_later = [
        lax.ppermute(heads, "z", [(i + hop, i) for i in range(count - hop)])
        for hop in range(count - 1, 0, -1)
    ]
    *from_later, out_x, out_y = hold(*from_later, out_x, out_y)
    out_last = scatter_relay(out_keeps, out_x, out_y)
    adj_in = jnp.zeros((1, chans), f32)
    for one in from_later:
        adj_in = one[0:1] * adj_in + one[1:2]
    enter = jnp.concatenate([state_in, adj_in, jnp.zeros((6, chans), f32)])
    d_rec_pre, sums, edge, grad_a, grad_x = backward_scan(
        order, d_mixed, rec_pre, state_local, prod, adj_local, adj_prod, branch_in, halo, conved,
        masks, small, enter, wa, wx, chunk,
    )
    after = lax.ppermute(edge, "z", [(i + 1, i) for i in range(count - 1)]) * later_open
    edge, mixed = hold(edge, mixed)
    grad_out = lax.dot_general(mixed, d_rec, contract_first, preferred_element_type=f32)
    after, grad_out = hold(after, grad_out)
    tail_sum = lax.dynamic_slice_in_dim(d_rec_pre, final, 8, 0).astype(f32) + jnp.pad(
        after, ((0, 0), (chans, 0))
    )
    d_rec_pre = lax.dynamic_update_slice_in_dim(d_rec_pre, tail_sum.astype(bf16), final, 0)
    rec_part = lax.dot_general(
        normed, d_rec_pre, contract_first, preferred_element_type=f32
    ).astype(bf16)
    rec_part, d_rec_pre, grad_a, grad_x, sums, *out_last = hold(
        rec_part, d_rec_pre, grad_a, grad_x, sums, *out_last
    )
    layer_out = (middle + scatter_sum(out_keeps, out_x, out_y, *out_last)).astype(bf16)
    rec_sum = lax.psum_scatter(rec_part, "z", scatter_dimension=0, tiled=True)
    back_pack = pack_sums(grad_out, grad_a, grad_x, sums, spread, chan_rows, pack_width)
    (back_swap,) = exchange([back_pack], swap_axes, 5)
    back_swap = back_swap.reshape(count * chan_rows, pack_width)
    grad_down = down_sum.astype(f32)
    back_swap, d_rec_pre, layer_out, grad_down = hold(back_swap, d_rec_pre, layer_out, grad_down)
    mlp_sum, d_rec_pre = hold(mlp_sum, d_rec_pre)
    pack_sum = lax.psum_scatter(back_swap, "z", scatter_dimension=0, tiled=True)
    one_sum, mlp_back = scatter_dot(d_rec_pre, w_rec, mlp_sum.reshape(NF, rows_w, 2 * ff))
    one_sum, rec_sum = hold(one_sum, rec_sum)
    (rec_back,) = exchange([rec_sum.reshape(NF, rows_w, 2 * chans)], FEAT, 10)
    e_one = gain_one * one_sum
    grad_tokens = d_middle + norm_back(tok, inverse_rms(tok), e_one)
    grad_gate, grad_up, grad_gain_two = join_blocks(
        mlp_back, mlp_gate_weight, mlp_up_weight, norm2_gain.astype(f32)[:, None], ff_moves
    )
    grad_rec_gate, grad_rec_in, grad_gain_one = join_blocks(
        rec_back, rec_gate_weight, rec_in_weight, norm1_gain.astype(f32)[:, None], chan_moves
    )

    pack_sum, grad_gain_one, grad_gain_two, grad_tokens = hold(
        pack_sum, grad_gain_one, grad_gain_two, grad_tokens
    )
    grad_out, grad_a, grad_x, grad_taps, *grad_rows = unpack_sums(pack_sum, width)
    grad_offset, grad_a_bias, grad_x_bias, grad_rate = (r.reshape(chan_rows) for r in grad_rows)
    return (
        layer_out,
        grad_tokens,
        grad_gain_one.reshape(rows_w),
        grad_rec_gate,
        grad_rec_in,
        grad_taps,
        grad_offset,
        grad_a,
        grad_a_bias,
        grad_x,
        grad_x_bias,
        grad_rate,
        grad_out,
        grad_gain_two.reshape(rows_w),
        grad_gate,
        grad_up,
        grad_down,
    )


def solution(mesh):
    wide, narrow = mesh.shape["wide"], mesh.shape["narrow"]
    groups = wide * narrow // NF
    grid = Mesh(mesh.devices.reshape((groups,) + (2,) * len(FEAT)), ("z",) + FEAT)
    flat = P(("z",) + FEAT)
    wide_rows = P(("z",) + FEAT, None)
    one, two = flat, wide_rows
    return jax.shard_map(
        on_device,
        mesh=grid,
        in_specs=(
            two, one, two, one, two, two, two, one, two, one, two, one, one, two, one, two, two, two,
        ),
        out_specs=(
            two, two, one, two, two, two, one, two, one, two, one, one, two, one, two, two, two,
        ),
        check_vma=False,
    )
```

```python
import functools

import jax
import jax.numpy as jnp
from jax import lax
from jax.experimental import pallas as pl
from jax.experimental.pallas import tpu as pltpu
from jax.sharding import Mesh
from jax.sharding import PartitionSpec as P

BLK = 160
CONV = 4
TAIL = CONV - 1
LANES = 128
FEAT = ("x", "y", "c")
NF = 8
OWN, ACROSS_Y, ACROSS_X, DIAGONAL = 0, 1, 2, 3

norm_eps = 1e-06
decay_scale = 8.0
push_shift = 0.05
f32 = jnp.float32
bf16 = jnp.bfloat16
MESH = pl.DeviceIdType.MESH
contract_last = (((1,), (1,)), ((), ()))
contract_first = (((0,), (0,)), ((), ()))
VMEM_LIMIT = 56 * 2**20


def cost(micros, flops=0):
    return pl.CostEstimate(
        flops=int(flops), bytes_accessed=int(micros * 3.0e6), transcendentals=0
    )


def hbm_spec():
    return pl.BlockSpec(memory_space=pl.ANY)


def vmem_spec():
    return pl.BlockSpec(memory_space=pltpu.VMEM)


def greet(peers):
    barrier = pltpu.get_barrier_semaphore()
    for device in peers:
        pl.semaphore_signal(barrier, inc=1, device_id=device, device_id_type=MESH)
    pl.semaphore_wait(barrier, len(peers))


def feature_place():
    return tuple(lax.axis_index(name) for name in FEAT)


def remote(src, dst, send_sem, recv_sem, device):
    return pltpu.make_async_remote_copy(
        src_ref=src,
        dst_ref=dst,
        send_sem=send_sem,
        recv_sem=recv_sem,
        device_id=device,
        device_id_type=MESH,
    )


def gather_kernel(*refs):
    if len(refs) == 5:
        x_ref, o_ref, local_sem, ssem, rsem = refs
        extra = ()
    else:
        x_ref, b_ref, s_ref, t_ref, o_ref, e_ref, so_ref, to_ref = refs[:8]
        local_sem, ssem, rsem = refs[8:11]
        peers, kept, copies = exchange_parts(FEAT, b_ref, e_ref, *refs[11:14])
        others, own_small, small = groups_parts((s_ref, t_ref), (so_ref, to_ref), *refs[14:])
        extra = (peers + others, [kept] + own_small, copies + small)
    x, y, c = feature_place()
    to_x, to_y, to_c = {"x": 1 - x}, {"y": 1 - y}, {"c": 1 - c}
    half = x_ref.shape[0] // 2
    top, low = pl.ds(0, half), pl.ds(half, half)
    greet(extra[0] if extra else (to_x, to_y, to_c))

    def copy(i, src, dst, device):
        return remote(src, dst, ssem.at[i], rsem.at[i], device)

    own = pltpu.make_async_copy(x_ref, o_ref.at[OWN], local_sem)
    x_top = copy(0, x_ref.at[top], o_ref.at[ACROSS_X, top], to_x)
    x_low = copy(1, x_ref.at[low], o_ref.at[ACROSS_X, low], to_x)
    y_low = copy(2, x_ref.at[low], o_ref.at[ACROSS_Y, low], to_y)
    y_top = copy(3, x_ref.at[top], o_ref.at[ACROSS_Y, top], to_y)
    c_own = copy(4, x_ref, o_ref.at[4 + OWN], to_c)
    y_fwd = copy(5, o_ref.at[ACROSS_X, top], o_ref.at[DIAGONAL, top], to_y)
    x_fwd = copy(6, o_ref.at[ACROSS_Y, low], o_ref.at[DIAGONAL, low], to_x)
    c_x = copy(7, o_ref.at[ACROSS_X], o_ref.at[4 + ACROSS_X], to_c)
    c_y = copy(8, o_ref.at[ACROSS_Y], o_ref.at[4 + ACROSS_Y], to_c)
    c_d = copy(9, o_ref.at[DIAGONAL], o_ref.at[4 + DIAGONAL], to_c)
    for one in (x_top, y_low, x_low, y_top, c_own, own):
        one.start()
    if extra:
        for one in extra[1] + extra[2]:
            one.start()
    x_top.wait_recv()
    y_fwd.start()
    y_low.wait_recv()
    x_fwd.start()
    x_low.wait_recv()
    c_x.start()
    y_top.wait_recv()
    c_y.start()
    y_fwd.wait_recv()
    x_fwd.wait_recv()
    c_d.start()
    for one in (c_own, c_x, c_y, c_d):
        one.wait_recv()
    for one in (x_top, x_low, y_low, y_top, c_own, y_fwd, x_fwd, c_x, c_y, c_d):
        one.wait_send()
    own.wait()
    if extra:
        for one in extra[2] + extra[1]:
            one.wait()


def gather_feature(block):
    rows, width = block.shape
    out = pl.pallas_call(
        gather_kernel,
        out_shape=jax.ShapeDtypeStruct((NF, rows, width), block.dtype),
        in_specs=[vmem_spec()],
        out_specs=hbm_spec(),
        scratch_shapes=[
            pltpu.SemaphoreType.DMA,
            pltpu.SemaphoreType.DMA((10,)),
            pltpu.SemaphoreType.DMA((10,)),
        ],
        compiler_params=pltpu.CompilerParams(
            collective_id=0, has_side_effects=True, vmem_limit_bytes=VMEM_LIMIT
        ),
        cost_estimate=cost(40),
        name="gather_feature",
    )(block)
    return out.reshape(NF * rows, width)


def scatter_flow(
    p_theirs, o_ref, own, other, total, rx, ry, relay, rx_last, ry_last, ssem, rsem,
    peers, begin, stage, ready
):
    x, y, c = feature_place()
    to_x, to_y, to_c = {"x": 1 - x}, {"y": 1 - y}, {"c": 1 - c}
    rows, width = o_ref.shape
    half = rows // 2
    top, low = pl.ds(0, half), pl.ds(half, half)
    step = 16

    def copy(i, src, dst, device):
        return remote(src, dst, ssem.at[i], rsem.at[i], device)

    greet(peers or (to_x, to_y, to_c))
    begin()
    cross = [copy(r, p_theirs(r), other.at[r], to_c) for r in range(4)]

    def add_into(r):
        ready(r)
        cross[r].wait_recv()

        def body(i, none):
            at = pl.ds(pl.multiple_of(i * step, step), step)
            total[r, at] = (own[r, at].astype(f32) + other[r, at].astype(f32)).astype(total.dtype)
            return none

        lax.fori_loop(0, rows // step, body, 0)

    x_diag = copy(4, total.at[DIAGONAL, top], rx.at[1], to_x)
    y_diag = copy(5, total.at[DIAGONAL, low], ry.at[1], to_y)
    x_near = copy(6, total.at[ACROSS_X, top], rx.at[0], to_x)
    y_near = copy(7, total.at[ACROSS_Y, low], ry.at[0], to_y)
    y_last = copy(8, relay.at[0], ry_last, to_y)
    x_last = copy(9, relay.at[1], rx_last, to_x)

    stage(DIAGONAL, cross)
    stage(ACROSS_X, cross)
    add_into(DIAGONAL)
    x_diag.start()
    y_diag.start()
    stage(ACROSS_Y, cross)
    add_into(ACROSS_X)
    x_near.start()
    stage(OWN, cross)
    add_into(ACROSS_Y)
    y_near.start()
    ready(OWN)
    cross[OWN].wait_recv()

    def relay_add(slot, r, start, got):
        def body(i, none):
            at = pl.ds(pl.multiple_of(i * step, step), step)
            here = pl.ds(pl.multiple_of(start + i * step, step), step)
            relay[slot, at] = (total[r, here].astype(f32) + got[1, at].astype(f32)).astype(
                relay.dtype
            )
            return none

        lax.fori_loop(0, half // step, body, 0)

    x_diag.wait_recv()
    relay_add(0, ACROSS_Y, 0, rx)
    y_last.start()
    y_diag.wait_recv()
    relay_add(1, ACROSS_X, half, ry)
    x_last.start()

    def finish(start, near, last):
        def body(i, none):
            at = pl.ds(pl.multiple_of(i * step, step), step)
            here = pl.ds(pl.multiple_of(start + i * step, step), step)
            o_ref[here] = (own[OWN, here].astype(f32) + other[OWN, here].astype(f32)) + (
                near[0, at].astype(f32) + last[at].astype(f32)
            )
            return none

        lax.fori_loop(0, half // step, body, 0)

    x_near.wait_recv()
    y_last.wait_recv()
    finish(0, rx, ry_last)
    y_near.wait_recv()
    x_last.wait_recv()
    finish(half, ry, rx_last)
    for one in cross + [x_diag, y_diag, x_near, y_near, x_last, y_last]:
        one.wait_send()


def scatter_kernel(
    p_ref, o_ref, own, other, total, rx, ry, relay, rx_last, ry_last, lsem, ssem, rsem
):
    loads = [pltpu.make_async_copy(p_ref.at[r], own.at[r], lsem.at[r]) for r in range(4)]
    for r in (DIAGONAL, ACROSS_X, ACROSS_Y, OWN):
        loads[r].start()
    scatter_flow(
        lambda r: p_ref.at[4 + r], o_ref, own, other, total, rx, ry, relay, rx_last, ry_last,
        ssem, rsem, None, lambda: None, lambda r, cross: cross[r].start(),
        lambda r: loads[r].wait(),
    )


def scatter_dot_kernel(
    a_ref, w_ref, b_ref, o_ref, e_ref, theirs, own, other, total, rx, ry, relay, rx_last, ry_last,
    ssem, rsem, local_sem, xssem, xrsem
):
    peers, kept, copies = exchange_parts(FEAT, b_ref, e_ref, local_sem, xssem, xrsem)
    rows, width = o_ref.shape
    tile = 512

    def begin():
        kept.start()
        for one in copies:
            one.start()

    def dot_into(block, ref, r):
        rows_in = a_ref[pl.ds(block * rows, rows)]

        def body(j, none):
            at = pl.ds(pl.multiple_of(j * tile, tile), tile)
            ref[r, :, at] = lax.dot_general(
                rows_in, w_ref[at], contract_last, preferred_element_type=f32
            ).astype(ref.dtype)
            return none

        lax.fori_loop(0, width // tile, body, 0)

    def stage(r, cross):
        dot_into(4 + r, theirs, r)
        cross[r].start()
        dot_into(r, own, r)

    scatter_flow(
        lambda r: theirs.at[r], o_ref, own, other, total, rx, ry, relay, rx_last, ry_last,
        ssem, rsem, peers, begin, stage, lambda r: None,
    )
    for one in copies:
        one.wait()
    kept.wait()


def scatter_dot(rows_in, w, blocks):
    rows, width = rows_in.shape[0] // NF, w.shape[0]
    half = rows // 2
    kind = rows_in.dtype
    four = pltpu.VMEM((4, rows, width), kind)
    two = pltpu.VMEM((2, half, width), kind)
    one = pltpu.VMEM((half, width), kind)
    return pl.pallas_call(
        scatter_dot_kernel,
        out_shape=(
            jax.ShapeDtypeStruct((rows, width), f32),
            jax.ShapeDtypeStruct(blocks.shape, blocks.dtype),
        ),
        in_specs=[vmem_spec()] * 3,
        out_specs=(vmem_spec(), hbm_spec()),
        scratch_shapes=[four] * 4
        + [two] * 3
        + [one] * 2
        + [
            pltpu.SemaphoreType.DMA((10,)),
            pltpu.SemaphoreType.DMA((10,)),
            pltpu.SemaphoreType.DMA,
            pltpu.SemaphoreType.DMA((NF - 1,)),
            pltpu.SemaphoreType.DMA((NF - 1,)),
        ],
        compiler_params=pltpu.CompilerParams(
            collective_id=11, has_side_effects=True, vmem_limit_bytes=VMEM_LIMIT
        ),
        cost_estimate=cost(55),
        name="scatter_dot",
    )(rows_in, w, blocks)


def scatter_feature(partial):
    rows, width = partial.shape[0] // NF, partial.shape[1]
    half = rows // 2
    kind = partial.dtype
    return pl.pallas_call(
        scatter_kernel,
        out_shape=jax.ShapeDtypeStruct((rows, width), f32),
        in_specs=[hbm_spec()],
        out_specs=vmem_spec(),
        scratch_shapes=[
            pltpu.VMEM((4, rows, width), kind),
            pltpu.VMEM((4, rows, width), kind),
            pltpu.VMEM((4, rows, width), kind),
            pltpu.VMEM((2, half, width), kind),
            pltpu.VMEM((2, half, width), kind),
            pltpu.VMEM((2, half, width), kind),
            pltpu.VMEM((half, width), kind),
            pltpu.VMEM((half, width), kind),
            pltpu.SemaphoreType.DMA((4,)),
            pltpu.SemaphoreType.DMA((10,)),
            pltpu.SemaphoreType.DMA((10,)),
        ],
        compiler_params=pltpu.CompilerParams(
            collective_id=1, has_side_effects=True, vmem_limit_bytes=VMEM_LIMIT
        ),
        cost_estimate=cost(45),
        name="scatter_feature",
    )(partial.reshape(NF, rows, width))


def across(value, axis):
    return lax.ppermute(value, axis, [(0, 1), (1, 0)])


def hold(*values):
    return lax.optimization_barrier(values)


def gather_near(block):
    return across(block, "x"), across(block, "y")


def gather_diagonal(by_x, by_y):
    half = by_x.shape[0] // 2
    return across(by_x[:half], "y"), across(by_y[half:], "x")


def gather_chip(block, by_x, by_y, d_top, d_low):
    return jnp.concatenate([block, by_y, by_x, d_top, d_low])


def scatter_halves(mine, got):
    shape = (4, 2, mine.shape[0] // 8, mine.shape[1])
    return mine.reshape(shape), got.reshape(shape)


def add_low(a, b):
    return (a.astype(f32) + b.astype(f32)).astype(a.dtype)


def scatter_sends(mine, got):
    mine, got = scatter_halves(mine, got)
    by_x = add_low(mine[ACROSS_X:, 0], got[ACROSS_X:, 0])
    by_y = add_low(mine[ACROSS_Y::2, 1], got[ACROSS_Y::2, 1])
    return by_x, by_y


def scatter_keeps(mine, got):
    mine, got = scatter_halves(mine, got)
    near_y = add_low(mine[ACROSS_Y, 0], got[ACROSS_Y, 0])
    near_x = add_low(mine[ACROSS_X, 1], got[ACROSS_X, 1])
    return near_y, near_x, add_low(mine[OWN], got[OWN])


def scatter_near(mine, got):
    mine, got = hold(mine, got)
    by_x, by_y = scatter_sends(mine, got)
    by_x, by_y, mine, got = hold(by_x, by_y, mine, got)
    return scatter_keeps(mine, got), across(by_x, "x"), across(by_y, "y")


def scatter_relay(mine, got, by_x, by_y):
    mine, got = scatter_halves(mine, got)

    def joined(chip, side, arrived):
        near = mine[chip, side].astype(f32) + got[chip, side].astype(f32)
        return (near + arrived[1].astype(f32)).astype(arrived.dtype)

    return across(joined(ACROSS_Y, 0, by_x), "y"), across(joined(ACROSS_X, 1, by_y), "x")


def scatter_sum(mine, got, by_x, by_y, y_last, x_last):
    mine, got = scatter_halves(mine, got)
    own = mine[OWN].astype(f32) + got[OWN].astype(f32)
    upper = own[0] + by_x[0].astype(f32) + y_last.astype(f32)
    lower = own[1] + by_y[0].astype(f32) + x_last.astype(f32)
    return jnp.concatenate([upper, lower])


def gather_tail_kernel(x_ref, bx_ref, by_ref, o_ref, lsem, ssem, rsem):
    x, y, c = feature_place()
    to_x, to_y, to_c = {"x": 1 - x}, {"y": 1 - y}, {"c": 1 - c}
    half = x_ref.shape[0] // 2
    top, low = pl.ds(0, half), pl.ds(half, half)

    def copy(i, src, dst, device):
        return remote(src, dst, ssem.at[i], rsem.at[i], device)

    places = ((x_ref, OWN), (by_ref, ACROSS_Y), (bx_ref, ACROSS_X))
    local = [
        pltpu.make_async_copy(ref, o_ref.at[slot], lsem.at[i])
        for i, (ref, slot) in enumerate(places)
    ]
    greet((to_x, to_y, to_c))
    y_fwd = copy(0, bx_ref.at[top], o_ref.at[DIAGONAL, top], to_y)
    x_fwd = copy(1, by_ref.at[low], o_ref.at[DIAGONAL, low], to_x)
    cross = [
        copy(2 + i, ref, o_ref.at[4 + slot], to_c) for i, (ref, slot) in enumerate(places)
    ]
    last = copy(5, o_ref.at[DIAGONAL], o_ref.at[4 + DIAGONAL], to_c)
    for one in [y_fwd, x_fwd] + cross + local:
        one.start()
    y_fwd.wait_recv()
    x_fwd.wait_recv()
    last.start()
    for one in cross + [last]:
        one.wait_recv()
    for one in cross + [y_fwd, x_fwd, last]:
        one.wait_send()
    for one in local:
        one.wait()


def gather_tail(block, by_x, by_y):
    rows, width = block.shape
    out = pl.pallas_call(
        gather_tail_kernel,
        out_shape=jax.ShapeDtypeStruct((NF, rows, width), block.dtype),
        in_specs=[vmem_spec()] * 3,
        out_specs=hbm_spec(),
        scratch_shapes=[
            pltpu.SemaphoreType.DMA((3,)),
            pltpu.SemaphoreType.DMA((6,)),
            pltpu.SemaphoreType.DMA((6,)),
        ],
        compiler_params=pltpu.CompilerParams(
            collective_id=8, has_side_effects=True, vmem_limit_bytes=VMEM_LIMIT
        ),
        cost_estimate=cost(16),
        name="gather_tail",
    )(block, by_x, by_y)
    return out.reshape(NF * rows, width)


def scatter_tail_kernel(
    ny_ref, nx_ref, own_ref, bx_ref, by_ref, o_ref, near, own, bx, by, relay, last, lsem, ssem, rsem
):
    x, y, c = feature_place()
    to_x, to_y = {"x": 1 - x}, {"y": 1 - y}
    half = o_ref.shape[0] // 2
    step = 16

    def load(i, src, dst):
        one = pltpu.make_async_copy(src, dst, lsem.at[i])
        one.start()
        return one

    loads = [
        load(0, ny_ref, near.at[0]),
        load(1, bx_ref, bx),
        load(2, nx_ref, near.at[1]),
        load(3, by_ref, by),
        load(4, own_ref, own),
    ]
    greet((to_x, to_y))
    sends = [
        remote(relay.at[0], last.at[0], ssem.at[0], rsem.at[0], to_y),
        remote(relay.at[1], last.at[1], ssem.at[1], rsem.at[1], to_x),
    ]

    def tiles(body):
        def one(i, none):
            body(pl.ds(pl.multiple_of(i * step, step), step), i * step)
            return none

        lax.fori_loop(0, half // step, one, 0)

    for side, got in ((0, bx), (1, by)):
        loads[2 * side].wait()
        loads[2 * side + 1].wait()

        def add(at, _, side=side, got=got):
            relay[side, at] = (near[side, at].astype(f32) + got[1, at].astype(f32)).astype(
                relay.dtype
            )

        tiles(add)
        sends[side].start()
    loads[4].wait()
    for side, got in ((0, bx), (1, by)):

        def base(at, start, side=side, got=got):
            here = pl.ds(pl.multiple_of(side * half + start, step), step)
            o_ref[here] = own[side, at].astype(f32) + got[0, at].astype(f32)

        tiles(base)
    for side in range(2):
        sends[side].wait_recv()

        def finish(at, start, side=side):
            here = pl.ds(pl.multiple_of(side * half + start, step), step)
            o_ref[here] = o_ref[here] + last[side, at].astype(f32)

        tiles(finish)
    for one in sends:
        one.wait_send()


def scatter_tail(keeps, by_x, by_y):
    _, half, width = by_x.shape
    kind = by_x.dtype
    pair = pltpu.VMEM((2, half, width), kind)
    return pl.pallas_call(
        scatter_tail_kernel,
        out_shape=jax.ShapeDtypeStruct((2 * half, width), f32),
        in_specs=[hbm_spec()] * 5,
        out_specs=vmem_spec(),
        scratch_shapes=[pair] * 6
        + [
            pltpu.SemaphoreType.DMA((5,)),
            pltpu.SemaphoreType.DMA((2,)),
            pltpu.SemaphoreType.DMA((2,)),
        ],
        compiler_params=pltpu.CompilerParams(
            collective_id=9, has_side_effects=True, vmem_limit_bytes=VMEM_LIMIT
        ),
        cost_estimate=cost(16),
        name="scatter_tail",
    )(*keeps, by_x, by_y)


def exchange_parts(axes, x_ref, o_ref, local_sem, ssem, rsem):
    place = [lax.axis_index(name) for name in axes]
    count = 2 ** len(axes)

    def rank(coords):
        total = 0
        for one in coords:
            total = total * 2 + one
        return total

    mine = rank(place)
    own = pltpu.make_async_copy(x_ref.at[mine], o_ref.at[mine], local_sem)
    peers, copies = [], []
    for mask in range(count - 1, 0, -1):
        bits = [(mask // 2 ** (len(axes) - 1 - i)) % 2 for i in range(len(axes))]
        coords = [1 - p if bit else p for p, bit in zip(place, bits)]
        device = {name: q for name, q, bit in zip(axes, coords, bits) if bit}
        peers.append(device)
        copies.append(
            remote(
                x_ref.at[rank(coords)],
                o_ref.at[mine],
                ssem.at[mask - 1],
                rsem.at[mask - 1],
                device,
            )
        )
    return peers, own, copies


def exchange_kernel(axes, *refs):
    count = (len(refs) - 3) // 2
    sources, targets = refs[:count], refs[count : 2 * count]
    local_sem, ssem, rsem = refs[2 * count :]
    parts = [
        exchange_parts(axes, sources[i], targets[i], local_sem.at[i], ssem.at[i], rsem.at[i])
        for i in range(count)
    ]
    for _, own, _ in parts:
        own.start()
    greet(parts[0][0])
    for _, _, copies in parts:
        for one in copies:
            one.start()
    for _, own, copies in parts:
        for one in copies:
            one.wait()
        own.wait()


def exchange(arrays, axes, ident):
    peers = 2 ** len(axes) - 1
    count = len(arrays)
    return pl.pallas_call(
        functools.partial(exchange_kernel, axes),
        out_shape=tuple(jax.ShapeDtypeStruct(a.shape, a.dtype) for a in arrays),
        in_specs=[vmem_spec()] * count,
        out_specs=(hbm_spec(),) * count,
        scratch_shapes=[
            pltpu.SemaphoreType.DMA((count,)),
            pltpu.SemaphoreType.DMA((count, peers)),
            pltpu.SemaphoreType.DMA((count, peers)),
        ],
        compiler_params=pltpu.CompilerParams(
            collective_id=ident, has_side_effects=True, vmem_limit_bytes=VMEM_LIMIT
        ),
        cost_estimate=cost(15),
        name="exchange",
    )(*arrays)


def gather_exchange(block, blocks, smalls, count):
    rows, width = block.shape
    out, got, *small = pl.pallas_call(
        gather_kernel,
        out_shape=(
            jax.ShapeDtypeStruct((NF, rows, width), block.dtype),
            jax.ShapeDtypeStruct(blocks.shape, blocks.dtype),
        )
        + tuple(jax.ShapeDtypeStruct((count,) + a.shape, a.dtype) for a in smalls),
        in_specs=[vmem_spec()] * 4,
        out_specs=(hbm_spec(),) * 2 + (vmem_spec(),) * 2,
        scratch_shapes=[
            pltpu.SemaphoreType.DMA,
            pltpu.SemaphoreType.DMA((10,)),
            pltpu.SemaphoreType.DMA((10,)),
            pltpu.SemaphoreType.DMA,
            pltpu.SemaphoreType.DMA((NF - 1,)),
            pltpu.SemaphoreType.DMA((NF - 1,)),
            pltpu.SemaphoreType.DMA((2,)),
            pltpu.SemaphoreType.DMA((2, count - 1)),
            pltpu.SemaphoreType.DMA((2, count - 1)),
        ],
        compiler_params=pltpu.CompilerParams(
            collective_id=4, has_side_effects=True, vmem_limit_bytes=VMEM_LIMIT
        ),
        cost_estimate=cost(55),
        name="gather_exchange",
    )(block, blocks, *smalls)
    return out.reshape(NF * rows, width), got, *small


def groups_parts(sources, targets, local_sem, ssem, rsem):
    count = targets[0].shape[0]
    z = lax.axis_index("z")
    many = range(len(sources))
    own = [pltpu.make_async_copy(sources[k], targets[k].at[z], local_sem.at[k]) for k in many]
    peers = [{"z": lax.rem(z + hop, count)} for hop in range(1, count)]
    copies = [
        remote(sources[k], targets[k].at[z], ssem.at[k, i], rsem.at[k, i], device)
        for k in many
        for i, device in enumerate(peers)
    ]
    return peers, own, copies


def groups_kernel(*refs):
    many = (len(refs) - 3) // 2
    peers, own, copies = groups_parts(refs[:many], refs[many : 2 * many], *refs[2 * many :])
    for one in own:
        one.start()
    greet(peers)
    for one in copies:
        one.start()
    for one in copies + own:
        one.wait()


def gather_groups(blocks, count, ident):
    many = len(blocks)
    return pl.pallas_call(
        groups_kernel,
        out_shape=tuple(jax.ShapeDtypeStruct((count,) + b.shape, b.dtype) for b in blocks),
        in_specs=[vmem_spec()] * many,
        out_specs=(vmem_spec(),) * many,
        scratch_shapes=[
            pltpu.SemaphoreType.DMA((many,)),
            pltpu.SemaphoreType.DMA((many, count - 1)),
            pltpu.SemaphoreType.DMA((many, count - 1)),
        ],
        compiler_params=pltpu.CompilerParams(collective_id=ident, has_side_effects=True),
        cost_estimate=cost(5),
        name="gather_groups",
    )(*blocks)


def gelu_tanh(values):
    return jax.nn.gelu(values, approximate=True)


def sigmoid(v):
    return 0.5 + 0.5 * jnp.tanh(0.5 * v)


def gelu_pair(v):
    root = 0.7978845608028654
    cube = 0.044715
    square = v * v
    t = jnp.tanh(root * (v + cube * square * v))
    value = 0.5 * v * (1.0 + t)
    slope = 0.5 * (1.0 + t) + 0.5 * v * (1.0 - t * t) * root * (1.0 + 3.0 * cube * square)
    return value, slope


def tile_scan(keep, push, reverse):
    rows = lax.broadcasted_iota(jnp.int32, keep.shape, 0)
    count = keep.shape[0]
    hop = 1
    while hop < count:
        if reverse:
            inside = rows < count - hop
            shift = count - hop
        else:
            inside = rows >= hop
            shift = hop
        keep_near = jnp.where(inside, pltpu.roll(keep, shift, 0), 1.0)
        push_near = jnp.where(inside, pltpu.roll(push, shift, 0), 0.0)
        push = push + keep * push_near
        keep = keep * keep_near
        hop *= 2
    return keep, push


def conv_of(ext, masks, taps, offset, rows):
    value = offset + taps[0:1] * ext[pl.ds(8, rows)]
    for k in range(1, CONV):
        value = value + taps[k : k + 1] * ext[pl.ds(8 - k, rows)] * masks[:, k - 1 : k]
    return value


def forward_kernel(
    order_ref,
    pre_ref,
    halo_ref,
    mask_ref,
    small_ref,
    wa_ref,
    wx_ref,
    branch_ref,
    conved_ref,
    keep_ref,
    prod_ref,
    state_ref,
    ends_ref,
    ext,
    carry,
):
    rows, width = branch_ref.shape
    step = pl.program_id(0)
    branch = pre_ref[:, width : 2 * width].astype(bf16)
    branch_ref[...] = branch

    @pl.when(step == 0)
    def _():
        ext[pl.ds(0, 8)] = halo_ref[...]
        carry[0:1] = jnp.ones_like(carry[0:1])
        carry[1:2] = jnp.zeros_like(carry[1:2])

    @pl.when(step > 0)
    def _():
        ext[pl.ds(0, 8)] = ext[pl.ds(rows, 8)]

    ext[pl.ds(8, rows)] = branch.astype(f32)
    masks = mask_ref[...]
    conved = conv_of(ext, masks, small_ref, small_ref[4:5], rows).astype(bf16)
    conved_ref[...] = conved
    logit_a = jnp.dot(conved, wa_ref[...], preferred_element_type=f32) + small_ref[5:6]
    logit_x = jnp.dot(conved, wx_ref[...], preferred_element_type=f32) + small_ref[6:7]
    decay = jnp.exp(-decay_scale * sigmoid(logit_a) * small_ref[7:8])
    keep_ref[...] = decay * masks[:, 0:1]
    state_ref[...] = (
        jnp.sqrt(1.0 - decay * decay + push_shift) * sigmoid(logit_x) * conved.astype(f32)
    )

    def body(i, held):
        prod_in, state_in = held
        at = pl.ds(pl.multiple_of(i * 8, 8), 8)
        keep, push = tile_scan(keep_ref[at], state_ref[at], False)
        state = push + keep * state_in
        prod = keep * prod_in
        prod_ref[at] = prod
        state_ref[at] = state
        return prod[7:8], state[7:8]

    prod_out, state_out = lax.fori_loop(
        0, rows // 8, body, (carry[0:1], carry[1:2]), unroll=4
    )
    carry[0:1] = prod_out
    carry[1:2] = state_out
    ends_ref[0:1] = prod_out
    ends_ref[1:2] = state_out
    ends_ref[2:8] = jnp.zeros_like(ends_ref[2:8])


def forward_scan(order, rec_pre, halo, masks, small, wa, wx, chunk):
    rows, width = rec_pre.shape[0], rec_pre.shape[1] // 2
    tile = pl.BlockSpec((chunk, width), lambda i, order: (order[i], 0))
    whole = lambda a: pl.BlockSpec(a.shape, lambda i, order: (0, 0))
    full = jax.ShapeDtypeStruct((rows, width), f32)
    low = jax.ShapeDtypeStruct((rows, width), bf16)
    return pl.pallas_call(
        forward_kernel,
        out_shape=(
            low,
            low,
            full,
            full,
            full,
            jax.ShapeDtypeStruct((8, width), f32),
        ),
        grid_spec=pltpu.PrefetchScalarGridSpec(
            num_scalar_prefetch=1,
            grid=(rows // chunk,),
            in_specs=[
                pl.BlockSpec((chunk, 2 * width), lambda i, order: (order[i], 0)),
                whole(halo),
                pl.BlockSpec((chunk, masks.shape[1]), lambda i, order: (i, 0)),
                whole(small),
                whole(wa),
                whole(wx),
            ],
            out_specs=(tile,) * 5 + (pl.BlockSpec((8, width), lambda i, order: (0, 0)),),
            scratch_shapes=[pltpu.VMEM((chunk + 8, width), f32), pltpu.VMEM((8, width), f32)],
        ),
        compiler_params=pltpu.CompilerParams(vmem_limit_bytes=VMEM_LIMIT),
        cost_estimate=cost(15),
        name="forward_scan",
    )(order, rec_pre, halo, masks, small, wa, wx)


def adjoint_kernel(
    order_ref, d_ref, w_ref, pre_ref, keep_ref, d_mixed_ref, prod_ref, adj_ref, heads_ref,
    keep_next, carry
):
    rows = d_ref.shape[0]
    d_mixed = lax.dot_general(d_ref[...], w_ref[...], contract_last, preferred_element_type=f32)
    d_mixed_ref[...] = d_mixed
    step = pl.program_id(0)

    @pl.when(step == 0)
    def _():
        keep_next[pl.ds(rows, 8)] = jnp.ones_like(keep_next[pl.ds(rows, 8)])
        carry[0:1] = jnp.ones_like(carry[0:1])
        carry[1:2] = jnp.zeros_like(carry[1:2])

    @pl.when(step > 0)
    def _():
        keep_next[pl.ds(rows, 8)] = keep_next[pl.ds(0, 8)]

    keep_next[pl.ds(0, rows)] = keep_ref[...]
    prod_ref[...] = keep_next[pl.ds(1, rows)]
    adj_ref[...] = d_mixed * gelu_tanh(pre_ref[:, 0 : adj_ref.shape[1]])
    tiles = rows // 8

    def body(i, held):
        prod_in, adj_in = held
        at = pl.ds(pl.multiple_of((tiles - 1 - i) * 8, 8), 8)
        keep, push = tile_scan(prod_ref[at], adj_ref[at], True)
        adj = push + keep * adj_in
        prod = keep * prod_in
        prod_ref[at] = prod
        adj_ref[at] = adj
        return prod[0:1], adj[0:1]

    prod_out, adj_out = lax.fori_loop(
        0, tiles, body, (carry[0:1], carry[1:2]), unroll=4
    )
    carry[0:1] = prod_out
    carry[1:2] = adj_out
    heads_ref[0:1] = keep_ref[0:1] * prod_out
    heads_ref[1:2] = keep_ref[0:1] * adj_out
    heads_ref[2:8] = jnp.zeros_like(heads_ref[2:8])


def adjoint_scan(order, d_rec, w_out, rec_pre, keep, chunk):
    rows, width = keep.shape
    last = rows // chunk - 1
    tile = pl.BlockSpec((chunk, width), lambda i, order: (order[last - i], 0))
    full = jax.ShapeDtypeStruct((rows, width), f32)
    return pl.pallas_call(
        adjoint_kernel,
        out_shape=(full, full, full, jax.ShapeDtypeStruct((8, width), f32)),
        grid_spec=pltpu.PrefetchScalarGridSpec(
            num_scalar_prefetch=1,
            grid=(rows // chunk,),
            in_specs=[
                pl.BlockSpec((chunk, d_rec.shape[1]), lambda i, order: (order[last - i], 0)),
                pl.BlockSpec((width, d_rec.shape[1]), lambda i, order: (0, 0)),
                pl.BlockSpec((chunk, 2 * width), lambda i, order: (order[last - i], 0)),
                tile,
            ],
            out_specs=(tile, tile, tile, pl.BlockSpec((8, width), lambda i, order: (0, 0))),
            scratch_shapes=[pltpu.VMEM((chunk + 8, width), f32), pltpu.VMEM((8, width), f32)],
        ),
        compiler_params=pltpu.CompilerParams(vmem_limit_bytes=VMEM_LIMIT),
        cost_estimate=cost(12),
        name="adjoint_scan",
    )(order, d_rec, w_out, rec_pre, keep)


def backward_kernel(
    order_ref,
    d_mixed_ref,
    pre_ref,
    state_ref,
    prod_ref,
    state_before_ref,
    prod_before_ref,
    adj_ref,
    adj_prod_ref,
    branch_ref,
    branch_before_ref,
    halo_ref,
    conved_ref,
    mask_ref,
    small_ref,
    enter_ref,
    wa_ref,
    wx_ref,
    d_pre_ref,
    sums_ref,
    edge_ref,
    ga_ref,
    gx_ref,
    ext,
    state_ext,
    later,
):
    rows, width = d_mixed_ref.shape
    step = pl.program_id(0)
    steps = pl.num_programs(0)
    state_in = enter_ref[0:1]
    adj_in = enter_ref[1:2]

    @pl.when(step == 0)
    def _():
        sums_ref[...] = jnp.zeros_like(sums_ref)
        ga_ref[...] = jnp.zeros_like(ga_ref)
        gx_ref[...] = jnp.zeros_like(gx_ref)
        for k in range(TAIL):
            later[k, pl.ds(rows, 8)] = jnp.zeros((8, width), f32)

    @pl.when(step > 0)
    def _():
        for k in range(TAIL):
            later[k, pl.ds(rows, 8)] = later[k, pl.ds(0, 8)]

    first = step == steps - 1

    @pl.when(first)
    def _():
        ext[pl.ds(0, 8)] = halo_ref[...]
        state_ext[pl.ds(0, 8)] = jnp.broadcast_to(state_in, (8, width))

    @pl.when(jnp.logical_not(first))
    def _():
        ext[pl.ds(0, 8)] = branch_before_ref[...].astype(f32)[8:16]
        state_ext[pl.ds(0, 8)] = state_before_ref[...] + prod_before_ref[...] * state_in

    ext[pl.ds(8, rows)] = branch_ref[...].astype(f32)
    state = state_ref[...] + prod_ref[...] * state_in
    state_ext[pl.ds(8, rows)] = state
    _, slope = gelu_pair(pre_ref[:, 0:width])
    d_pre_ref[:, 0:width] = (d_mixed_ref[...] * state * slope).astype(bf16)
    adjoint = adj_ref[...] + adj_prod_ref[...] * adj_in
    state_prev = state_ext[pl.ds(7, rows)]
    masks = mask_ref[...]
    conved_low = conved_ref[...]
    conved = conved_low.astype(f32)
    rates = small_ref[7:8]
    gate_a = sigmoid(
        jnp.dot(conved_low, wa_ref[...], preferred_element_type=f32) + small_ref[5:6]
    )
    gate_x = sigmoid(
        jnp.dot(conved_low, wx_ref[...], preferred_element_type=f32) + small_ref[6:7]
    )
    decay = jnp.exp(-decay_scale * gate_a * rates)
    square = 1.0 - decay * decay + push_shift
    inverse = lax.rsqrt(square)
    root = square * inverse
    d_decay = adjoint * (state_prev * masks[:, 0:1] - gate_x * conved * decay * inverse)
    slope_a = -decay_scale * d_decay * decay * gate_a
    d_logit_a = (slope_a * rates * (1.0 - gate_a)).astype(bf16)
    through = adjoint * root * gate_x
    d_logit_x = (through * conved * (1.0 - gate_x)).astype(bf16)
    d_conved = (
        through
        + lax.dot_general(d_logit_a, wa_ref[...], contract_last, preferred_element_type=f32)
        + lax.dot_general(d_logit_x, wx_ref[...], contract_last, preferred_element_type=f32)
    )
    d_conved = d_conved.astype(bf16).astype(f32)
    ga_ref[...] += lax.dot_general(
        conved_low, d_logit_a, contract_first, preferred_element_type=f32
    )
    gx_ref[...] += lax.dot_general(
        conved_low, d_logit_x, contract_first, preferred_element_type=f32
    )

    def total(v):
        return jnp.sum(v, axis=0, keepdims=True)

    sums_ref[0:1] += total(d_conved * ext[pl.ds(8, rows)])
    for k in range(1, CONV):
        masked = d_conved * masks[:, k - 1 : k]
        later[k - 1, pl.ds(0, rows)] = masked
        sums_ref[k : k + 1] += total(masked * ext[pl.ds(8 - k, rows)])
    sums_ref[4:5] += total(d_conved)
    sums_ref[5:6] += total(d_logit_a.astype(f32))
    sums_ref[6:7] += total(d_logit_x.astype(f32))
    sums_ref[7:8] += total(slope_a)
    d_branch = small_ref[0:1] * d_conved
    for k in range(1, CONV):
        d_branch = d_branch + small_ref[k : k + 1] * later[k - 1, pl.ds(k, rows)]
    d_pre_ref[:, width : 2 * width] = d_branch.astype(bf16)

    @pl.when(first)
    def _():
        for back in range(1, CONV):
            value = jnp.zeros((1, width), f32)
            for k in range(back, CONV):
                value = value + small_ref[k : k + 1] * later[k - 1, pl.ds(k - back, 1)]
            edge_ref[8 - back : 9 - back] = value
        edge_ref[0 : 8 - TAIL] = jnp.zeros((8 - TAIL, width), f32)


def backward_scan(
    order, d_mixed, rec_pre, state, prod, adj, adj_prod, branch_in, halo, conved, masks, small,
    enter, wa, wx, chunk,
):
    rows, width = state.shape
    last = rows // chunk - 1
    tile = pl.BlockSpec((chunk, width), lambda i, order: (order[last - i], 0))

    def before(size):
        per = chunk // size
        return pl.BlockSpec(
            (size, width),
            lambda i, order: (order[jnp.maximum(last - i - 1, 0)] * per + per - 1, 0),
        )

    pinned = lambda shape: pl.BlockSpec(shape, lambda i, order: (0, 0))
    whole = lambda a: pinned(a.shape)
    return pl.pallas_call(
        backward_kernel,
        out_shape=(
            jax.ShapeDtypeStruct((rows, 2 * width), bf16),
            jax.ShapeDtypeStruct((8, width), f32),
            jax.ShapeDtypeStruct((8, width), f32),
            jax.ShapeDtypeStruct((width, width), f32),
            jax.ShapeDtypeStruct((width, width), f32),
        ),
        grid_spec=pltpu.PrefetchScalarGridSpec(
            num_scalar_prefetch=1,
            grid=(rows // chunk,),
            in_specs=[
                tile,
                pl.BlockSpec((chunk, 2 * width), lambda i, order: (order[last - i], 0)),
                tile,
                tile,
                before(8),
                before(8),
                tile,
                tile,
                tile,
                before(16),
                whole(halo),
                tile,
                pl.BlockSpec((chunk, masks.shape[1]), lambda i, order: (last - i, 0)),
                whole(small),
                whole(enter),
                whole(wa),
                whole(wx),
            ],
            out_specs=(
                pl.BlockSpec((chunk, 2 * width), lambda i, order: (order[last - i], 0)),
                pinned((8, width)),
                pinned((8, width)),
                pinned((width, width)),
                pinned((width, width)),
            ),
            scratch_shapes=[
                pltpu.VMEM((chunk + 8, width), f32),
                pltpu.VMEM((chunk + 8, width), f32),
                pltpu.VMEM((TAIL, chunk + 8, width), f32),
            ],
        ),
        compiler_params=pltpu.CompilerParams(vmem_limit_bytes=VMEM_LIMIT),
        cost_estimate=cost(21),
        name="backward_scan",
    )(
        order, d_mixed, rec_pre, state, prod, state, prod, adj, adj_prod, branch_in, branch_in,
        halo, conved, masks, small, enter, wa, wx,
    )


def gated_kernel(n_ref, mine_ref, theirs_ref, w_ref, down_ref, hidden_ref, d_ref):
    ff = down_ref.shape[0]
    tile = 256
    normed = n_ref[...]
    cot = lax.select(
        pl.program_id(0) < pl.num_programs(0) // 2, mine_ref[...], theirs_ref[...]
    )

    def body(j, none):
        at = pl.ds(pl.multiple_of(j * tile, tile), tile)
        up_at = pl.ds(pl.multiple_of(ff + j * tile, tile), tile)
        gate = jnp.dot(normed, w_ref[:, at], preferred_element_type=f32)
        up = jnp.dot(normed, w_ref[:, up_at], preferred_element_type=f32)
        d_hidden = lax.dot_general(cot, down_ref[at], contract_last, preferred_element_type=f32)
        act, slope = gelu_pair(gate)
        hidden_ref[:, at] = (act * up).astype(bf16)
        d_ref[:, at] = (d_hidden * up * slope).astype(bf16)
        d_ref[:, up_at] = (d_hidden * act).astype(bf16)
        return none

    lax.fori_loop(0, ff // tile, body, 0)


def gated_unit(normed, cot_mine, cot_theirs, w_mlp, w_down):
    rows, width = normed.shape
    ff = w_down.shape[0]
    steps = 4
    tile = rows // steps
    row = lambda size: pl.BlockSpec((tile, size), lambda i: (i, 0))
    once = lambda a: pl.BlockSpec(a.shape, lambda i: (0, 0), pipeline_mode=pl.Buffered(1))
    return pl.pallas_call(
        gated_kernel,
        grid=(steps,),
        out_shape=(
            jax.ShapeDtypeStruct((rows, ff), bf16),
            jax.ShapeDtypeStruct((rows, 2 * ff), bf16),
        ),
        in_specs=[
            row(width),
            pl.BlockSpec((tile, width), lambda i: (jnp.minimum(i, steps // 2 - 1), 0)),
            pl.BlockSpec((tile, width), lambda i: (jnp.maximum(i - steps // 2, 0), 0)),
            once(w_mlp),
            once(w_down),
        ],
        out_specs=(row(ff), row(2 * ff)),
        compiler_params=pltpu.CompilerParams(vmem_limit_bytes=VMEM_LIMIT),
        cost_estimate=pl.CostEstimate(
            flops=6 * rows * width * ff, bytes_accessed=40 * 2**20, transcendentals=rows * ff
        ),
        name="gated_unit",
    )(normed, cot_mine, cot_theirs, w_mlp, w_down)


def down_kernel(h_ref, w_ref, mine_ref, theirs_ref):
    width = w_ref.shape[1]
    tile = 512
    hidden = h_ref[...]

    def into(ref):
        def body(j, none):
            at = pl.ds(pl.multiple_of(j * tile, tile), tile)
            ref[:, at] = jnp.dot(hidden, w_ref[:, at], preferred_element_type=f32).astype(bf16)
            return none

        lax.fori_loop(0, width // tile, body, 0)

    first = pl.program_id(0) < pl.num_programs(0) // 2
    pl.when(first)(lambda: into(mine_ref))
    pl.when(jnp.logical_not(first))(lambda: into(theirs_ref))


def down_rows(hidden, w_down):
    rows, ff = hidden.shape
    width = w_down.shape[1]
    steps = 4
    tile = rows // steps
    part = jax.ShapeDtypeStruct((rows // 2, width), bf16)
    return pl.pallas_call(
        down_kernel,
        grid=(steps,),
        out_shape=(part, part),
        in_specs=[
            pl.BlockSpec((tile, ff), lambda i: (i, 0)),
            pl.BlockSpec((ff, width), lambda i: (0, 0), pipeline_mode=pl.Buffered(1)),
        ],
        out_specs=(
            pl.BlockSpec((tile, width), lambda i: (jnp.minimum(i, steps // 2 - 1), 0)),
            pl.BlockSpec((tile, width), lambda i: (jnp.maximum(i - steps // 2, 0), 0)),
        ),
        compiler_params=pltpu.CompilerParams(vmem_limit_bytes=VMEM_LIMIT),
        cost_estimate=cost(0.1),
        name="down_rows",
    )(hidden, w_down)


def split_kernel(moves, a_ref, b_ref, o_ref):
    for source, block, at, start, size in moves:
        ref = (a_ref, b_ref)[source]
        o_ref[block, :, at : at + size] = ref[:, start : start + size]


def join_kernel(moves, x_ref, a_ref, b_ref, g_ref, oa_ref, ob_ref, og_ref):
    for source, block, at, start, size in moves:
        ref = (oa_ref, ob_ref)[source]
        ref[:, start : start + size] = x_ref[block, :, at : at + size].astype(f32)
    total = jnp.sum(a_ref[...].astype(f32) * oa_ref[...], axis=1, keepdims=True) + jnp.sum(
        b_ref[...].astype(f32) * ob_ref[...], axis=1, keepdims=True
    )
    wide = jnp.broadcast_to(total / g_ref[...], (total.shape[0], LANES))
    og_ref[...] = wide.T[0:1]


def split_blocks(a, b, moves):
    rows, width = a.shape
    return pl.pallas_call(
        functools.partial(split_kernel, moves),
        out_shape=jax.ShapeDtypeStruct((NF, rows, 2 * width // NF), a.dtype),
        compiler_params=pltpu.CompilerParams(vmem_limit_bytes=VMEM_LIMIT),
        cost_estimate=cost(4),
        name="split_blocks",
    )(a, b)


def join_blocks(x, a, b, gain, moves):
    rows, width = a.shape
    out = jax.ShapeDtypeStruct((rows, width), f32)
    return pl.pallas_call(
        functools.partial(join_kernel, moves),
        out_shape=(out, out, jax.ShapeDtypeStruct((1, rows), f32)),
        compiler_params=pltpu.CompilerParams(vmem_limit_bytes=VMEM_LIMIT),
        cost_estimate=cost(5),
        name="join_blocks",
    )(x, a, b, gain)


def pack_kernel(out_ref, ga_ref, gx_ref, sums_ref, o_ref, small):
    spread, _, chan_rows, total = o_ref.shape
    chans, width = out_ref.shape
    extra = total - width
    row = lax.broadcasted_iota(jnp.int32, (chans, chans), 0)
    col = lax.broadcasted_iota(jnp.int32, (chans, chans), 1)
    same = (row < BLK) == (col < BLK)
    at = lax.broadcasted_iota(jnp.int32, (chans, extra), 0)
    at = jnp.where(at < BLK, at, at - BLK)
    to = lax.broadcasted_iota(jnp.int32, (chans, extra), 1)

    def placed(ref, start):
        kept = jnp.where(same, ref[...], 0.0).astype(bf16)
        spot = jnp.where(to == at + start, 1.0, 0.0).astype(bf16)
        return jnp.dot(kept, spot, preferred_element_type=f32)

    rows = jnp.concatenate([sums_ref[...], jnp.zeros_like(sums_ref)]).astype(bf16)
    spot = jnp.where(
        lax.broadcasted_iota(jnp.int32, (16, extra), 0) + 2 * BLK
        == lax.broadcasted_iota(jnp.int32, (16, extra), 1),
        1.0,
        0.0,
    ).astype(bf16)
    small[...] = (
        placed(ga_ref, 0)
        + placed(gx_ref, BLK)
        + lax.dot_general(rows, spot, contract_first, preferred_element_type=f32)
    )
    for unit in range(2):
        for part in range(spread):
            here = pl.ds(unit * BLK + part * chan_rows, chan_rows)
            o_ref[part, unit, :, 0:width] = out_ref[here].astype(bf16)
            o_ref[part, unit, :, width:total] = small[here].astype(bf16)


def pack_sums(grad_out, grad_a, grad_x, sums, spread, chan_rows, total):
    chans, width = grad_out.shape
    return pl.pallas_call(
        pack_kernel,
        out_shape=jax.ShapeDtypeStruct((spread, 2, chan_rows, total), bf16),
        scratch_shapes=[pltpu.VMEM((chans, total - width), f32)],
        compiler_params=pltpu.CompilerParams(vmem_limit_bytes=VMEM_LIMIT),
        cost_estimate=cost(3),
        name="pack_sums",
    )(grad_out, grad_a, grad_x, sums)


def unpack_kernel(x_ref, out_ref, ga_ref, gx_ref, taps_ref, *row_refs):
    width = out_ref.shape[1]
    base = width + 2 * BLK
    out_ref[...] = x_ref[:, 0:width].astype(f32)
    ga_ref[...] = x_ref[:, width : width + BLK].astype(f32)
    gx_ref[...] = x_ref[:, width + BLK : base].astype(f32)
    last = base - base % LANES
    small = x_ref[:, last : last + LANES].astype(f32)
    taps_ref[...] = small[:, base - last : base - last + CONV]
    turned = small.T
    for i, ref in enumerate(row_refs):
        at = base - last + CONV + i
        ref[...] = turned[at : at + 1]


def unpack_sums(x, width):
    rows = x.shape[0]
    shape = lambda *dims: jax.ShapeDtypeStruct(dims, f32)
    return pl.pallas_call(
        unpack_kernel,
        out_shape=(shape(rows, width), shape(rows, BLK), shape(rows, BLK), shape(rows, CONV))
        + (shape(1, rows),) * 4,
        compiler_params=pltpu.CompilerParams(vmem_limit_bytes=VMEM_LIMIT),
        cost_estimate=cost(2),
        name="unpack_sums",
    )(x)


def pad_lanes(rows, width):
    have = rows.shape[-1]
    return jnp.pad(rows, ((0, 0), (0, width - have)))


def inverse_rms(rows):
    return lax.rsqrt(jnp.mean(rows * rows, axis=-1, keepdims=True) + norm_eps)


def norm_back(rows, scale, e):
    return scale * e - rows * (scale * scale * scale) * jnp.mean(e * rows, axis=-1, keepdims=True)


def on_device(
    tokens_in,
    segment_starts,
    cotangent,
    norm1_gain,
    rec_gate_weight,
    rec_in_weight,
    conv_weight,
    conv_bias,
    gate_a_weight,
    gate_a_bias,
    gate_x_weight,
    gate_x_bias,
    decay_rate,
    rec_out_weight,
    norm2_gain,
    mlp_gate_weight,
    mlp_up_weight,
    mlp_down_weight,
):
    count = lax.axis_size("z")
    z = lax.axis_index("z")
    spread = count // 2
    swap_axes = FEAT[len(FEAT) - (spread.bit_length() - 1) :]
    outer = NF // spread
    rows_tok, width = tokens_in.shape
    group_rows = NF * rows_tok
    chan_rows = conv_weight.shape[0]
    chans = chan_rows * count
    rows_w = rec_gate_weight.shape[0]
    ff_rows = mlp_down_weight.shape[0]
    ff = ff_rows * count
    chunk = 256

    chan_moves = [
        (
            source,
            k * spread + e,
            source * chans + zz * BLK,
            ((2 * e + zz) * outer + k) * BLK,
            BLK,
        )
        for source in range(2)
        for k in range(outer)
        for e in range(spread)
        for zz in range(2)
    ]
    ff_moves = [
        (source, f, source * ff + group * ff_rows, (group * NF + f) * ff_rows, ff_rows)
        for source in range(2)
        for f in range(NF)
        for group in range(count)
    ]
    place = [lax.axis_index(name) for name in FEAT]
    time = jnp.arange(NF, dtype=jnp.int32)
    bit = lambda value, here: jnp.where(value == here, 0, 1)
    order = (
        bit(time % 2, place[2]) * 4 + bit(time // 4, place[0]) * 2 + bit((time // 2) % 2, place[1])
    ).astype(jnp.int32)
    final = order[NF - 1] * rows_tok + rows_tok - 8

    pack = jnp.concatenate(
        [
            gate_a_weight,
            gate_x_weight,
            conv_weight,
            conv_bias[:, None],
            gate_a_bias[:, None],
            gate_x_bias[:, None],
            decay_rate[:, None],
        ],
        axis=1,
    )
    used = pack.shape[1]
    extra_width = -(-used // LANES) * LANES
    pack_width = width + extra_width
    pack = pad_lanes(pack, extra_width)

    extra = jnp.concatenate(
        [
            pad_lanes(segment_starts.astype(bf16)[None], 2 * chans),
            pad_lanes(norm1_gain[None], 2 * chans),
            pad_lanes(norm2_gain[None], 2 * chans),
            jnp.zeros((13, 2 * chans), bf16),
        ],
        axis=0,
    )
    rec_send = jnp.concatenate(
        [
            split_blocks(rec_gate_weight, rec_in_weight, chan_moves),
            jnp.broadcast_to(extra[None], (NF, 16, 2 * chans)),
        ],
        axis=1,
    )
    out_all = lax.all_gather(rec_out_weight, "z", axis=0, tiled=True)
    (rec_got,) = exchange([rec_send], FEAT, 3)
    starts = rec_got[:, rows_w, :rows_tok].reshape(group_rows).astype(f32)

    plane_gains = jnp.stack(
        [
            rec_got[:, rows_w + 1, :rows_w].reshape(NF * rows_w),
            rec_got[:, rows_w + 2, :rows_w].reshape(NF * rows_w),
        ]
    ).astype(f32)
    rec_mine = rec_got[:, :rows_w].reshape(NF * rows_w, 2 * chans)
    w_rec = lax.all_gather(rec_mine, "z", axis=0, tiled=True)
    mlp_send = split_blocks(mlp_gate_weight, mlp_up_weight, ff_moves)
    tok_group, mlp_got, gains, pack_all = gather_exchange(
        tokens_in, mlp_send, [jnp.pad(plane_gains, ((0, 6), (0, 0))), pack], count
    )
    tok_group, pack_all, out_all = hold(tok_group, pack_all, out_all)
    out_swap, pack_swap = exchange(
        [
            out_all.reshape(spread, 2, chan_rows, width),
            pack_all.reshape(spread, 2, chan_rows, extra_width),
        ],
        swap_axes,
        12,
    )
    gain_one = gains[:, 0].reshape(1, width)
    gain_two = gains[:, 1].reshape(1, width)

    tok = tokens_in.astype(f32)
    tok_group = tok_group.astype(f32)
    normed = (tok_group * inverse_rms(tok_group) * gain_one).astype(bf16)

    w_mlp = lax.all_gather(mlp_got.reshape(NF * rows_w, 2 * ff), "z", axis=0, tiled=True)
    w_down = lax.all_gather(mlp_down_weight, "z", axis=0, tiled=True)

    w_out = out_swap.transpose(1, 0, 2, 3).reshape(chans, width)
    mine = pack_swap.transpose(1, 0, 2, 3).reshape(chans, extra_width)
    small = mine[:, 2 * BLK : used].astype(f32).T

    unit = lax.broadcasted_iota(jnp.int32, (chans, chans), 0) // BLK
    same_block = unit == lax.broadcasted_iota(jnp.int32, (chans, chans), 1) // BLK

    def block_diag(w):
        return jnp.where(same_block, jnp.concatenate([w, w], axis=1), jnp.zeros((), w.dtype))

    wa = block_diag(mine[:, :BLK])
    wx = block_diag(mine[:, BLK : 2 * BLK])

    open_one = 1.0 - starts
    ahead = jnp.concatenate([jnp.ones((TAIL,), f32), open_one])
    open_two = open_one * ahead[TAIL - 1 : TAIL - 1 + group_rows]
    open_three = open_two * ahead[TAIL - 2 : TAIL - 2 + group_rows]
    masks = jnp.stack([open_one, open_two, open_three], axis=1)
    end = open_one[group_rows - 2 :]
    later_open = jnp.concatenate(
        [jnp.zeros((8 - TAIL,), f32), (end[0] * end[1])[None], end[1:], jnp.ones((1,), f32)]
    )[:, None]

    rec_pre = jnp.dot(normed, w_rec, preferred_element_type=f32)
    rec_pre, cot_own = hold(rec_pre, cotangent)
    cot_x, cot_y = gather_near(cot_own)
    edge_rows = lax.dynamic_slice_in_dim(rec_pre, final, 8, 0)[:, chans:].astype(bf16)
    halo = lax.ppermute(
        edge_rows.astype(f32) * later_open, "z", [(i, i + 1) for i in range(count - 1)]
    )
    branch_in, conved, keep, prod, state_local, ends = forward_scan(
        order, rec_pre, halo, masks, small, wa, wx, chunk
    )
    ends, cot_x, cot_y = hold(ends, cot_x, cot_y)
    cot_top, cot_low = gather_diagonal(cot_x, cot_y)
    (ends,) = gather_groups([ends], count, 2)
    state_in = jnp.zeros((1, chans), f32)
    for hop in range(count - 1):
        state_in = jnp.where(hop < z, ends[hop, 0:1] * state_in + ends[hop, 1:2], state_in)
    mixed = ((state_local + prod * state_in) * gelu_tanh(rec_pre[:, :chans])).astype(bf16)
    mixed_out = jnp.dot(mixed, w_out, preferred_element_type=f32).astype(bf16)
    mixed_out, cot_top, cot_low = hold(mixed_out, cot_top, cot_low)
    cot_chip = gather_chip(cotangent, cot_x, cot_y, cot_top, cot_low)
    cot_got = across(cot_chip, "c")
    middle = tok + scatter_feature(mixed_out)

    scale_two = inverse_rms(middle)
    normed_two = gather_feature((middle * scale_two * gain_two).astype(bf16))
    hidden, d_mlp = gated_unit(normed_two, cot_chip, cot_got, w_mlp, w_down)
    half_rows = group_rows // 2

    def back_rows(d, w):
        return lax.dot_general(d, w, contract_last, preferred_element_type=f32).astype(bf16)

    def over_rows(a, b_mine, b_theirs):
        return (
            lax.dot_general(a[:half_rows], b_mine, contract_first, preferred_element_type=f32)
            + lax.dot_general(a[half_rows:], b_theirs, contract_first, preferred_element_type=f32)
        ).astype(bf16)

    e_theirs = back_rows(d_mlp[half_rows:], w_mlp)
    d_mlp, e_theirs = hold(d_mlp, e_theirs)
    e_got = across(e_theirs, "c")
    e_mine = back_rows(d_mlp[:half_rows], w_mlp)
    e_keeps, e_x, e_y = scatter_near(e_mine, e_got)
    near_y, hidden = hold(e_keeps[0], hidden)
    e_keeps = (near_y,) + e_keeps[1:]
    down_part = over_rows(hidden, cot_chip, cot_got)
    down_part, hidden = hold(down_part, hidden)
    down_sum = lax.psum_scatter(down_part, "z", scatter_dimension=0, tiled=True)
    out_mine, out_theirs = down_rows(hidden, w_down)
    out_mine, out_theirs, e_x, e_y = hold(out_mine, out_theirs, e_x, e_y)
    e_two = gain_two * scatter_tail(e_keeps, e_x, e_y)
    d_middle = cotangent.astype(f32) + norm_back(middle, scale_two, e_two)
    d_own = d_middle.astype(bf16)
    d_x, d_y = gather_near(d_own)
    d_own, d_mlp, out_mine, out_theirs = hold(d_own, d_mlp, out_mine, out_theirs)
    out_got = across(out_theirs, "c")
    mlp_part = lax.dot_general(
        normed_two, d_mlp, contract_first, preferred_element_type=f32
    ).astype(bf16)
    out_x, out_y = scatter_sends(out_mine, out_got)
    d_x, d_y, mlp_part, out_x, out_y = hold(d_x, d_y, mlp_part, out_x, out_y)
    mlp_sum = lax.psum_scatter(mlp_part, "z", scatter_dimension=0, tiled=True)
    d_rec = gather_tail(d_own, d_x, d_y)
    d_rec, down_sum, out_x, out_y = hold(d_rec, down_sum, out_x, out_y)
    out_x, out_y = across(out_x, "x"), across(out_y, "y")

    d_mixed, adj_prod, adj_local, heads = adjoint_scan(
        order, d_rec, w_out, rec_pre, keep, chunk
    )
    from_later = [
        lax.ppermute(heads, "z", [(i + hop, i) for i in range(count - hop)])
        for hop in range(count - 1, 0, -1)
    ]
    *from_later, out_x, out_y = hold(*from_later, out_x, out_y)
    out_last = scatter_relay(out_mine, out_got, out_x, out_y)
    adj_in = jnp.zeros((1, chans), f32)
    for one in from_later:
        adj_in = one[0:1] * adj_in + one[1:2]
    enter = jnp.concatenate([state_in, adj_in, jnp.zeros((6, chans), f32)])
    d_rec_pre, sums, edge, grad_a, grad_x = backward_scan(
        order, d_mixed, rec_pre, state_local, prod, adj_local, adj_prod, branch_in, halo, conved,
        masks, small, enter, wa, wx, chunk,
    )
    after = lax.ppermute(edge, "z", [(i + 1, i) for i in range(count - 1)]) * later_open
    edge, mixed = hold(edge, mixed)
    grad_out = lax.dot_general(mixed, d_rec, contract_first, preferred_element_type=f32)
    after, grad_out = hold(after, grad_out)
    tail_sum = lax.dynamic_slice_in_dim(d_rec_pre, final, 8, 0).astype(f32) + jnp.pad(
        after, ((0, 0), (chans, 0))
    )
    d_rec_pre = lax.dynamic_update_slice_in_dim(d_rec_pre, tail_sum.astype(bf16), final, 0)
    rec_part = lax.dot_general(
        normed, d_rec_pre, contract_first, preferred_element_type=f32
    ).astype(bf16)
    rec_part, d_rec_pre, grad_a, grad_x, sums, *out_last = hold(
        rec_part, d_rec_pre, grad_a, grad_x, sums, *out_last
    )
    layer_out = (middle + scatter_sum(out_mine, out_got, out_x, out_y, *out_last)).astype(bf16)
    rec_sum = lax.psum_scatter(rec_part, "z", scatter_dimension=0, tiled=True)
    back_pack = pack_sums(grad_out, grad_a, grad_x, sums, spread, chan_rows, pack_width)
    (back_swap,) = exchange([back_pack], swap_axes, 5)
    back_swap = back_swap.reshape(count * chan_rows, pack_width)
    grad_down = down_sum.astype(f32)
    back_swap, d_rec_pre, layer_out, grad_down = hold(back_swap, d_rec_pre, layer_out, grad_down)
    mlp_sum, d_rec_pre = hold(mlp_sum, d_rec_pre)
    pack_sum = lax.psum_scatter(back_swap, "z", scatter_dimension=0, tiled=True)
    one_sum, mlp_back = scatter_dot(d_rec_pre, w_rec, mlp_sum.reshape(NF, rows_w, 2 * ff))
    one_sum, rec_sum = hold(one_sum, rec_sum)
    (rec_back,) = exchange([rec_sum.reshape(NF, rows_w, 2 * chans)], FEAT, 10)
    e_one = gain_one * one_sum
    grad_tokens = d_middle + norm_back(tok, inverse_rms(tok), e_one)
    grad_gate, grad_up, grad_gain_two = join_blocks(
        mlp_back, mlp_gate_weight, mlp_up_weight, norm2_gain.astype(f32)[:, None], ff_moves
    )
    grad_rec_gate, grad_rec_in, grad_gain_one = join_blocks(
        rec_back, rec_gate_weight, rec_in_weight, norm1_gain.astype(f32)[:, None], chan_moves
    )

    pack_sum, grad_gain_one, grad_gain_two, grad_tokens = hold(
        pack_sum, grad_gain_one, grad_gain_two, grad_tokens
    )
    grad_out, grad_a, grad_x, grad_taps, *grad_rows = unpack_sums(pack_sum, width)
    grad_offset, grad_a_bias, grad_x_bias, grad_rate = (r.reshape(chan_rows) for r in grad_rows)
    return (
        layer_out,
        grad_tokens,
        grad_gain_one.reshape(rows_w),
        grad_rec_gate,
        grad_rec_in,
        grad_taps,
        grad_offset,
        grad_a,
        grad_a_bias,
        grad_x,
        grad_x_bias,
        grad_rate,
        grad_out,
        grad_gain_two.reshape(rows_w),
        grad_gate,
        grad_up,
        grad_down,
    )


def solution(mesh):
    wide, narrow = mesh.shape["wide"], mesh.shape["narrow"]
    groups = wide * narrow // NF
    grid = Mesh(mesh.devices.reshape((groups,) + (2,) * len(FEAT)), ("z",) + FEAT)
    flat = P(("z",) + FEAT)
    wide_rows = P(("z",) + FEAT, None)
    one, two = flat, wide_rows
    return jax.shard_map(
        on_device,
        mesh=grid,
        in_specs=(
            two, one, two, one, two, two, two, one, two, one, two, one, one, two, one, two, two, two,
        ),
        out_specs=(
            two, two, one, two, two, two, one, two, one, two, one, one, two, one, two, two, two,
        ),
        check_vma=False,
    )
```

```python
import functools

import jax
import jax.numpy as jnp
from jax import lax
from jax.experimental import pallas as pl
from jax.experimental.pallas import tpu as pltpu
from jax.sharding import Mesh
from jax.sharding import PartitionSpec as P

BLK = 160
CONV = 4
TAIL = CONV - 1
LANES = 128
FEAT = ("x", "y", "c")
NF = 8
OWN, ACROSS_Y, ACROSS_X, DIAGONAL = 0, 1, 2, 3

norm_eps = 1e-06
decay_scale = 8.0
push_shift = 0.05
f32 = jnp.float32
bf16 = jnp.bfloat16
MESH = pl.DeviceIdType.MESH
contract_last = (((1,), (1,)), ((), ()))
contract_first = (((0,), (0,)), ((), ()))
VMEM_LIMIT = 56 * 2**20


def cost(micros, flops=0):
    return pl.CostEstimate(
        flops=int(flops), bytes_accessed=int(micros * 3.0e6), transcendentals=0
    )


def hbm_spec():
    return pl.BlockSpec(memory_space=pl.ANY)


def vmem_spec():
    return pl.BlockSpec(memory_space=pltpu.VMEM)


def greet(peers):
    barrier = pltpu.get_barrier_semaphore()
    for device in peers:
        pl.semaphore_signal(barrier, inc=1, device_id=device, device_id_type=MESH)
    pl.semaphore_wait(barrier, len(peers))


def feature_place():
    return tuple(lax.axis_index(name) for name in FEAT)


def remote(src, dst, send_sem, recv_sem, device):
    return pltpu.make_async_remote_copy(
        src_ref=src,
        dst_ref=dst,
        send_sem=send_sem,
        recv_sem=recv_sem,
        device_id=device,
        device_id_type=MESH,
    )


def gather_kernel(*refs):
    if len(refs) == 5:
        x_ref, o_ref, local_sem, ssem, rsem = refs
        extra = ()
    else:
        x_ref, b_ref, s_ref, t_ref, o_ref, e_ref, so_ref, to_ref = refs[:8]
        local_sem, ssem, rsem = refs[8:11]
        peers, kept, copies = exchange_parts(FEAT, b_ref, e_ref, *refs[11:14])
        others, own_small, small = groups_parts((s_ref, t_ref), (so_ref, to_ref), *refs[14:])
        extra = (peers + others, [kept] + own_small, copies + small)
    x, y, c = feature_place()
    to_x, to_y, to_c = {"x": 1 - x}, {"y": 1 - y}, {"c": 1 - c}
    half = x_ref.shape[0] // 2
    top, low = pl.ds(0, half), pl.ds(half, half)
    greet(extra[0] if extra else (to_x, to_y, to_c))

    def copy(i, src, dst, device):
        return remote(src, dst, ssem.at[i], rsem.at[i], device)

    own = pltpu.make_async_copy(x_ref, o_ref.at[OWN], local_sem)
    x_top = copy(0, x_ref.at[top], o_ref.at[ACROSS_X, top], to_x)
    x_low = copy(1, x_ref.at[low], o_ref.at[ACROSS_X, low], to_x)
    y_low = copy(2, x_ref.at[low], o_ref.at[ACROSS_Y, low], to_y)
    y_top = copy(3, x_ref.at[top], o_ref.at[ACROSS_Y, top], to_y)
    c_own = copy(4, x_ref, o_ref.at[4 + OWN], to_c)
    y_fwd = copy(5, o_ref.at[ACROSS_X, top], o_ref.at[DIAGONAL, top], to_y)
    x_fwd = copy(6, o_ref.at[ACROSS_Y, low], o_ref.at[DIAGONAL, low], to_x)
    c_x = copy(7, o_ref.at[ACROSS_X], o_ref.at[4 + ACROSS_X], to_c)
    c_y = copy(8, o_ref.at[ACROSS_Y], o_ref.at[4 + ACROSS_Y], to_c)
    c_d = copy(9, o_ref.at[DIAGONAL], o_ref.at[4 + DIAGONAL], to_c)
    for one in (x_top, y_low, x_low, y_top, c_own, own):
        one.start()
    if extra:
        for one in extra[1] + extra[2]:
            one.start()
    x_top.wait_recv()
    y_fwd.start()
    y_low.wait_recv()
    x_fwd.start()
    x_low.wait_recv()
    c_x.start()
    y_top.wait_recv()
    c_y.start()
    y_fwd.wait_recv()
    x_fwd.wait_recv()
    c_d.start()
    for one in (c_own, c_x, c_y, c_d):
        one.wait_recv()
    for one in (x_top, x_low, y_low, y_top, c_own, y_fwd, x_fwd, c_x, c_y, c_d):
        one.wait_send()
    own.wait()
    if extra:
        for one in extra[2] + extra[1]:
            one.wait()


def gather_feature(block):
    rows, width = block.shape
    out = pl.pallas_call(
        gather_kernel,
        out_shape=jax.ShapeDtypeStruct((NF, rows, width), block.dtype),
        in_specs=[vmem_spec()],
        out_specs=hbm_spec(),
        scratch_shapes=[
            pltpu.SemaphoreType.DMA,
            pltpu.SemaphoreType.DMA((10,)),
            pltpu.SemaphoreType.DMA((10,)),
        ],
        compiler_params=pltpu.CompilerParams(
            collective_id=0, has_side_effects=True, vmem_limit_bytes=VMEM_LIMIT
        ),
        cost_estimate=cost(40),
        name="gather_feature",
    )(block)
    return out.reshape(NF * rows, width)


def scatter_flow(
    p_theirs, o_ref, own, other, total, rx, ry, relay, rx_last, ry_last, ssem, rsem,
    peers, begin, stage, ready
):
    x, y, c = feature_place()
    to_x, to_y, to_c = {"x": 1 - x}, {"y": 1 - y}, {"c": 1 - c}
    rows, width = o_ref.shape
    half = rows // 2
    top, low = pl.ds(0, half), pl.ds(half, half)
    step = 16

    def copy(i, src, dst, device):
        return remote(src, dst, ssem.at[i], rsem.at[i], device)

    greet(peers or (to_x, to_y, to_c))
    begin()
    cross = [copy(r, p_theirs(r), other.at[r], to_c) for r in range(4)]

    def add_into(r):
        ready(r)
        cross[r].wait_recv()

        def body(i, none):
            at = pl.ds(pl.multiple_of(i * step, step), step)
            total[r, at] = (own[r, at].astype(f32) + other[r, at].astype(f32)).astype(total.dtype)
            return none

        lax.fori_loop(0, rows // step, body, 0)

    x_diag = copy(4, total.at[DIAGONAL, top], rx.at[1], to_x)
    y_diag = copy(5, total.at[DIAGONAL, low], ry.at[1], to_y)
    x_near = copy(6, total.at[ACROSS_X, top], rx.at[0], to_x)
    y_near = copy(7, total.at[ACROSS_Y, low], ry.at[0], to_y)
    y_last = copy(8, relay.at[0], ry_last, to_y)
    x_last = copy(9, relay.at[1], rx_last, to_x)

    stage(DIAGONAL, cross)
    stage(ACROSS_X, cross)
    add_into(DIAGONAL)
    x_diag.start()
    y_diag.start()
    stage(ACROSS_Y, cross)
    add_into(ACROSS_X)
    x_near.start()
    stage(OWN, cross)
    add_into(ACROSS_Y)
    y_near.start()
    ready(OWN)
    cross[OWN].wait_recv()

    def relay_add(slot, r, start, got):
        def body(i, none):
            at = pl.ds(pl.multiple_of(i * step, step), step)
            here = pl.ds(pl.multiple_of(start + i * step, step), step)
            relay[slot, at] = (total[r, here].astype(f32) + got[1, at].astype(f32)).astype(
                relay.dtype
            )
            return none

        lax.fori_loop(0, half // step, body, 0)

    x_diag.wait_recv()
    relay_add(0, ACROSS_Y, 0, rx)
    y_last.start()
    y_diag.wait_recv()
    relay_add(1, ACROSS_X, half, ry)
    x_last.start()

    def finish(start, near, last):
        def body(i, none):
            at = pl.ds(pl.multiple_of(i * step, step), step)
            here = pl.ds(pl.multiple_of(start + i * step, step), step)
            o_ref[here] = (own[OWN, here].astype(f32) + other[OWN, here].astype(f32)) + (
                near[0, at].astype(f32) + last[at].astype(f32)
            )
            return none

        lax.fori_loop(0, half // step, body, 0)

    x_near.wait_recv()
    y_last.wait_recv()
    finish(0, rx, ry_last)
    y_near.wait_recv()
    x_last.wait_recv()
    finish(half, ry, rx_last)
    for one in cross + [x_diag, y_diag, x_near, y_near, x_last, y_last]:
        one.wait_send()


def scatter_kernel(
    p_ref, o_ref, own, other, total, rx, ry, relay, rx_last, ry_last, lsem, ssem, rsem
):
    loads = [pltpu.make_async_copy(p_ref.at[r], own.at[r], lsem.at[r]) for r in range(4)]
    for r in (DIAGONAL, ACROSS_X, ACROSS_Y, OWN):
        loads[r].start()
    scatter_flow(
        lambda r: p_ref.at[4 + r], o_ref, own, other, total, rx, ry, relay, rx_last, ry_last,
        ssem, rsem, None, lambda: None, lambda r, cross: cross[r].start(),
        lambda r: loads[r].wait(),
    )


def scatter_dot_kernel(
    a_ref, w_ref, b_ref, o_ref, e_ref, theirs, own, other, total, rx, ry, relay, rx_last, ry_last,
    ssem, rsem, local_sem, xssem, xrsem
):
    peers, kept, copies = exchange_parts(FEAT, b_ref, e_ref, local_sem, xssem, xrsem)
    rows, width = o_ref.shape
    tile = 512

    def begin():
        kept.start()
        for one in copies:
            one.start()

    def dot_into(block, ref, r):
        rows_in = a_ref[pl.ds(block * rows, rows)]

        def body(j, none):
            at = pl.ds(pl.multiple_of(j * tile, tile), tile)
            ref[r, :, at] = lax.dot_general(
                rows_in, w_ref[at], contract_last, preferred_element_type=f32
            ).astype(ref.dtype)
            return none

        lax.fori_loop(0, width // tile, body, 0)

    def stage(r, cross):
        dot_into(4 + r, theirs, r)
        cross[r].start()
        dot_into(r, own, r)

    scatter_flow(
        lambda r: theirs.at[r], o_ref, own, other, total, rx, ry, relay, rx_last, ry_last,
        ssem, rsem, peers, begin, stage, lambda r: None,
    )
    for one in copies:
        one.wait()
    kept.wait()


def scatter_dot(rows_in, w, blocks):
    rows, width = rows_in.shape[0] // NF, w.shape[0]
    half = rows // 2
    kind = rows_in.dtype
    four = pltpu.VMEM((4, rows, width), kind)
    two = pltpu.VMEM((2, half, width), kind)
    one = pltpu.VMEM((half, width), kind)
    return pl.pallas_call(
        scatter_dot_kernel,
        out_shape=(
            jax.ShapeDtypeStruct((rows, width), f32),
            jax.ShapeDtypeStruct(blocks.shape, blocks.dtype),
        ),
        in_specs=[vmem_spec()] * 3,
        out_specs=(vmem_spec(), hbm_spec()),
        scratch_shapes=[four] * 4
        + [two] * 3
        + [one] * 2
        + [
            pltpu.SemaphoreType.DMA((10,)),
            pltpu.SemaphoreType.DMA((10,)),
            pltpu.SemaphoreType.DMA,
            pltpu.SemaphoreType.DMA((NF - 1,)),
            pltpu.SemaphoreType.DMA((NF - 1,)),
        ],
        compiler_params=pltpu.CompilerParams(
            collective_id=11, has_side_effects=True, vmem_limit_bytes=VMEM_LIMIT
        ),
        cost_estimate=cost(55),
        name="scatter_dot",
    )(rows_in, w, blocks)


def scatter_feature(partial):
    rows, width = partial.shape[0] // NF, partial.shape[1]
    half = rows // 2
    kind = partial.dtype
    return pl.pallas_call(
        scatter_kernel,
        out_shape=jax.ShapeDtypeStruct((rows, width), f32),
        in_specs=[hbm_spec()],
        out_specs=vmem_spec(),
        scratch_shapes=[
            pltpu.VMEM((4, rows, width), kind),
            pltpu.VMEM((4, rows, width), kind),
            pltpu.VMEM((4, rows, width), kind),
            pltpu.VMEM((2, half, width), kind),
            pltpu.VMEM((2, half, width), kind),
            pltpu.VMEM((2, half, width), kind),
            pltpu.VMEM((half, width), kind),
            pltpu.VMEM((half, width), kind),
            pltpu.SemaphoreType.DMA((4,)),
            pltpu.SemaphoreType.DMA((10,)),
            pltpu.SemaphoreType.DMA((10,)),
        ],
        compiler_params=pltpu.CompilerParams(
            collective_id=1, has_side_effects=True, vmem_limit_bytes=VMEM_LIMIT
        ),
        cost_estimate=cost(45),
        name="scatter_feature",
    )(partial.reshape(NF, rows, width))


def across(value, axis):
    return lax.ppermute(value, axis, [(0, 1), (1, 0)])


def hold(*values):
    return lax.optimization_barrier(values)


def gather_near(block):
    return across(block, "x"), across(block, "y")


def gather_diagonal(by_x, by_y):
    half = by_x.shape[0] // 2
    return across(by_x[:half], "y"), across(by_y[half:], "x")


def gather_chip(block, by_x, by_y, d_top, d_low):
    return jnp.concatenate([block, by_y, by_x, d_top, d_low])


def scatter_halves(mine, got):
    shape = (4, 2, mine.shape[0] // 8, mine.shape[1])
    return mine.reshape(shape), got.reshape(shape)


def add_low(a, b):
    return (a.astype(f32) + b.astype(f32)).astype(a.dtype)


def scatter_sends(mine, got):
    mine, got = scatter_halves(mine, got)
    by_x = add_low(mine[ACROSS_X:, 0], got[ACROSS_X:, 0])
    by_y = add_low(mine[ACROSS_Y::2, 1], got[ACROSS_Y::2, 1])
    return by_x, by_y


def scatter_keeps(mine, got):
    mine, got = scatter_halves(mine, got)
    near_y = add_low(mine[ACROSS_Y, 0], got[ACROSS_Y, 0])
    near_x = add_low(mine[ACROSS_X, 1], got[ACROSS_X, 1])
    return near_y, near_x, add_low(mine[OWN], got[OWN])


def scatter_near(mine, got):
    mine, got = hold(mine, got)
    by_x, by_y = scatter_sends(mine, got)
    by_x, by_y, mine, got = hold(by_x, by_y, mine, got)
    return scatter_keeps(mine, got), across(by_x, "x"), across(by_y, "y")


def scatter_relay(mine, got, by_x, by_y):
    mine, got = scatter_halves(mine, got)

    def joined(chip, side, arrived):
        near = mine[chip, side].astype(f32) + got[chip, side].astype(f32)
        return (near + arrived[1].astype(f32)).astype(arrived.dtype)

    return across(joined(ACROSS_Y, 0, by_x), "y"), across(joined(ACROSS_X, 1, by_y), "x")


def scatter_sum(mine, got, by_x, by_y, y_last, x_last):
    mine, got = scatter_halves(mine, got)
    own = mine[OWN].astype(f32) + got[OWN].astype(f32)
    upper = own[0] + by_x[0].astype(f32) + y_last.astype(f32)
    lower = own[1] + by_y[0].astype(f32) + x_last.astype(f32)
    return jnp.concatenate([upper, lower])


def gather_tail_kernel(x_ref, bx_ref, by_ref, o_ref, lsem, ssem, rsem):
    x, y, c = feature_place()
    to_x, to_y, to_c = {"x": 1 - x}, {"y": 1 - y}, {"c": 1 - c}
    half = x_ref.shape[0] // 2
    top, low = pl.ds(0, half), pl.ds(half, half)

    def copy(i, src, dst, device):
        return remote(src, dst, ssem.at[i], rsem.at[i], device)

    places = ((x_ref, OWN), (by_ref, ACROSS_Y), (bx_ref, ACROSS_X))
    local = [
        pltpu.make_async_copy(ref, o_ref.at[slot], lsem.at[i])
        for i, (ref, slot) in enumerate(places)
    ]
    greet((to_x, to_y, to_c))
    y_fwd = copy(0, bx_ref.at[top], o_ref.at[DIAGONAL, top], to_y)
    x_fwd = copy(1, by_ref.at[low], o_ref.at[DIAGONAL, low], to_x)
    cross = [
        copy(2 + i, ref, o_ref.at[4 + slot], to_c) for i, (ref, slot) in enumerate(places)
    ]
    last = copy(5, o_ref.at[DIAGONAL], o_ref.at[4 + DIAGONAL], to_c)
    for one in [y_fwd, x_fwd] + cross + local:
        one.start()
    y_fwd.wait_recv()
    x_fwd.wait_recv()
    last.start()
    for one in cross + [last]:
        one.wait_recv()
    for one in cross + [y_fwd, x_fwd, last]:
        one.wait_send()
    for one in local:
        one.wait()


def gather_tail(block, by_x, by_y):
    rows, width = block.shape
    out = pl.pallas_call(
        gather_tail_kernel,
        out_shape=jax.ShapeDtypeStruct((NF, rows, width), block.dtype),
        in_specs=[vmem_spec()] * 3,
        out_specs=hbm_spec(),
        scratch_shapes=[
            pltpu.SemaphoreType.DMA((3,)),
            pltpu.SemaphoreType.DMA((6,)),
            pltpu.SemaphoreType.DMA((6,)),
        ],
        compiler_params=pltpu.CompilerParams(
            collective_id=8, has_side_effects=True, vmem_limit_bytes=VMEM_LIMIT
        ),
        cost_estimate=cost(16),
        name="gather_tail",
    )(block, by_x, by_y)
    return out.reshape(NF * rows, width)


def scatter_tail_kernel(
    ny_ref, nx_ref, own_ref, bx_ref, by_ref, o_ref, near, own, bx, by, relay, last, lsem, ssem, rsem
):
    x, y, c = feature_place()
    to_x, to_y = {"x": 1 - x}, {"y": 1 - y}
    half = o_ref.shape[0] // 2
    step = 16

    def load(i, src, dst):
        one = pltpu.make_async_copy(src, dst, lsem.at[i])
        one.start()
        return one

    loads = [
        load(0, ny_ref, near.at[0]),
        load(1, bx_ref, bx),
        load(2, nx_ref, near.at[1]),
        load(3, by_ref, by),
        load(4, own_ref, own),
    ]
    greet((to_x, to_y))
    sends = [
        remote(relay.at[0], last.at[0], ssem.at[0], rsem.at[0], to_y),
        remote(relay.at[1], last.at[1], ssem.at[1], rsem.at[1], to_x),
    ]

    def tiles(body):
        def one(i, none):
            body(pl.ds(pl.multiple_of(i * step, step), step), i * step)
            return none

        lax.fori_loop(0, half // step, one, 0)

    for side, got in ((0, bx), (1, by)):
        loads[2 * side].wait()
        loads[2 * side + 1].wait()

        def add(at, _, side=side, got=got):
            relay[side, at] = (near[side, at].astype(f32) + got[1, at].astype(f32)).astype(
                relay.dtype
            )

        tiles(add)
        sends[side].start()
    loads[4].wait()
    for side, got in ((0, bx), (1, by)):

        def base(at, start, side=side, got=got):
            here = pl.ds(pl.multiple_of(side * half + start, step), step)
            o_ref[here] = own[side, at].astype(f32) + got[0, at].astype(f32)

        tiles(base)
    for side in range(2):
        sends[side].wait_recv()

        def finish(at, start, side=side):
            here = pl.ds(pl.multiple_of(side * half + start, step), step)
            o_ref[here] = o_ref[here] + last[side, at].astype(f32)

        tiles(finish)
    for one in sends:
        one.wait_send()


def scatter_tail(keeps, by_x, by_y):
    _, half, width = by_x.shape
    kind = by_x.dtype
    pair = pltpu.VMEM((2, half, width), kind)
    return pl.pallas_call(
        scatter_tail_kernel,
        out_shape=jax.ShapeDtypeStruct((2 * half, width), f32),
        in_specs=[hbm_spec()] * 5,
        out_specs=vmem_spec(),
        scratch_shapes=[pair] * 6
        + [
            pltpu.SemaphoreType.DMA((5,)),
            pltpu.SemaphoreType.DMA((2,)),
            pltpu.SemaphoreType.DMA((2,)),
        ],
        compiler_params=pltpu.CompilerParams(
            collective_id=9, has_side_effects=True, vmem_limit_bytes=VMEM_LIMIT
        ),
        cost_estimate=cost(16),
        name="scatter_tail",
    )(*keeps, by_x, by_y)


def exchange_parts(axes, x_ref, o_ref, local_sem, ssem, rsem):
    place = [lax.axis_index(name) for name in axes]
    count = 2 ** len(axes)

    def rank(coords):
        total = 0
        for one in coords:
            total = total * 2 + one
        return total

    mine = rank(place)
    own = pltpu.make_async_copy(x_ref.at[mine], o_ref.at[mine], local_sem)
    peers, copies = [], []
    for mask in range(count - 1, 0, -1):
        bits = [(mask // 2 ** (len(axes) - 1 - i)) % 2 for i in range(len(axes))]
        coords = [1 - p if bit else p for p, bit in zip(place, bits)]
        device = {name: q for name, q, bit in zip(axes, coords, bits) if bit}
        peers.append(device)
        copies.append(
            remote(
                x_ref.at[rank(coords)],
                o_ref.at[mine],
                ssem.at[mask - 1],
                rsem.at[mask - 1],
                device,
            )
        )
    return peers, own, copies


def exchange_kernel(axes, *refs):
    count = (len(refs) - 3) // 2
    sources, targets = refs[:count], refs[count : 2 * count]
    local_sem, ssem, rsem = refs[2 * count :]
    parts = [
        exchange_parts(axes, sources[i], targets[i], local_sem.at[i], ssem.at[i], rsem.at[i])
        for i in range(count)
    ]
    for _, own, _ in parts:
        own.start()
    greet(parts[0][0])
    for _, _, copies in parts:
        for one in copies:
            one.start()
    for _, own, copies in parts:
        for one in copies:
            one.wait()
        own.wait()


def exchange(arrays, axes, ident):
    peers = 2 ** len(axes) - 1
    count = len(arrays)
    return pl.pallas_call(
        functools.partial(exchange_kernel, axes),
        out_shape=tuple(jax.ShapeDtypeStruct(a.shape, a.dtype) for a in arrays),
        in_specs=[vmem_spec()] * count,
        out_specs=(hbm_spec(),) * count,
        scratch_shapes=[
            pltpu.SemaphoreType.DMA((count,)),
            pltpu.SemaphoreType.DMA((count, peers)),
            pltpu.SemaphoreType.DMA((count, peers)),
        ],
        compiler_params=pltpu.CompilerParams(
            collective_id=ident, has_side_effects=True, vmem_limit_bytes=VMEM_LIMIT
        ),
        cost_estimate=cost(15),
        name="exchange",
    )(*arrays)


def gather_exchange(block, blocks, smalls, count):
    rows, width = block.shape
    out, got, *small = pl.pallas_call(
        gather_kernel,
        out_shape=(
            jax.ShapeDtypeStruct((NF, rows, width), block.dtype),
            jax.ShapeDtypeStruct(blocks.shape, blocks.dtype),
        )
        + tuple(jax.ShapeDtypeStruct((count,) + a.shape, a.dtype) for a in smalls),
        in_specs=[vmem_spec()] * 4,
        out_specs=(hbm_spec(),) * 2 + (vmem_spec(),) * 2,
        scratch_shapes=[
            pltpu.SemaphoreType.DMA,
            pltpu.SemaphoreType.DMA((10,)),
            pltpu.SemaphoreType.DMA((10,)),
            pltpu.SemaphoreType.DMA,
            pltpu.SemaphoreType.DMA((NF - 1,)),
            pltpu.SemaphoreType.DMA((NF - 1,)),
            pltpu.SemaphoreType.DMA((2,)),
            pltpu.SemaphoreType.DMA((2, count - 1)),
            pltpu.SemaphoreType.DMA((2, count - 1)),
        ],
        compiler_params=pltpu.CompilerParams(
            collective_id=4, has_side_effects=True, vmem_limit_bytes=VMEM_LIMIT
        ),
        cost_estimate=cost(55),
        name="gather_exchange",
    )(block, blocks, *smalls)
    return out.reshape(NF * rows, width), got, *small


def groups_parts(sources, targets, local_sem, ssem, rsem):
    count = targets[0].shape[0]
    z = lax.axis_index("z")
    many = range(len(sources))
    own = [pltpu.make_async_copy(sources[k], targets[k].at[z], local_sem.at[k]) for k in many]
    peers = [{"z": lax.rem(z + hop, count)} for hop in range(1, count)]
    copies = [
        remote(sources[k], targets[k].at[z], ssem.at[k, i], rsem.at[k, i], device)
        for k in many
        for i, device in enumerate(peers)
    ]
    return peers, own, copies


def groups_kernel(*refs):
    many = (len(refs) - 3) // 2
    peers, own, copies = groups_parts(refs[:many], refs[many : 2 * many], *refs[2 * many :])
    for one in own:
        one.start()
    greet(peers)
    for one in copies:
        one.start()
    for one in copies + own:
        one.wait()


def gather_groups(blocks, count, ident):
    many = len(blocks)
    return pl.pallas_call(
        groups_kernel,
        out_shape=tuple(jax.ShapeDtypeStruct((count,) + b.shape, b.dtype) for b in blocks),
        in_specs=[vmem_spec()] * many,
        out_specs=(vmem_spec(),) * many,
        scratch_shapes=[
            pltpu.SemaphoreType.DMA((many,)),
            pltpu.SemaphoreType.DMA((many, count - 1)),
            pltpu.SemaphoreType.DMA((many, count - 1)),
        ],
        compiler_params=pltpu.CompilerParams(collective_id=ident, has_side_effects=True),
        cost_estimate=cost(5),
        name="gather_groups",
    )(*blocks)


def gelu_tanh(values):
    return jax.nn.gelu(values, approximate=True)


def sigmoid(v):
    return 0.5 + 0.5 * jnp.tanh(0.5 * v)


def gelu_pair(v):
    root = 0.7978845608028654
    cube = 0.044715
    square = v * v
    t = jnp.tanh(root * (v + cube * square * v))
    value = 0.5 * v * (1.0 + t)
    slope = 0.5 * (1.0 + t) + 0.5 * v * (1.0 - t * t) * root * (1.0 + 3.0 * cube * square)
    return value, slope


def tile_scan(keep, push, reverse):
    rows = lax.broadcasted_iota(jnp.int32, keep.shape, 0)
    count = keep.shape[0]
    hop = 1
    while hop < count:
        if reverse:
            inside = rows < count - hop
            shift = count - hop
        else:
            inside = rows >= hop
            shift = hop
        keep_near = jnp.where(inside, pltpu.roll(keep, shift, 0), 1.0)
        push_near = jnp.where(inside, pltpu.roll(push, shift, 0), 0.0)
        push = push + keep * push_near
        keep = keep * keep_near
        hop *= 2
    return keep, push


def conv_of(ext, masks, taps, offset, rows):
    value = offset + taps[0:1] * ext[pl.ds(8, rows)]
    for k in range(1, CONV):
        value = value + taps[k : k + 1] * ext[pl.ds(8 - k, rows)] * masks[:, k - 1 : k]
    return value


def forward_kernel(
    order_ref,
    pre_ref,
    halo_ref,
    mask_ref,
    small_ref,
    wa_ref,
    wx_ref,
    branch_ref,
    conved_ref,
    keep_ref,
    prod_ref,
    state_ref,
    ends_ref,
    ext,
    carry,
):
    rows, width = branch_ref.shape
    step = pl.program_id(0)
    branch = pre_ref[:, width : 2 * width].astype(bf16)
    branch_ref[...] = branch

    @pl.when(step == 0)
    def _():
        ext[pl.ds(0, 8)] = halo_ref[...]
        carry[0:1] = jnp.ones_like(carry[0:1])
        carry[1:2] = jnp.zeros_like(carry[1:2])

    @pl.when(step > 0)
    def _():
        ext[pl.ds(0, 8)] = ext[pl.ds(rows, 8)]

    ext[pl.ds(8, rows)] = branch.astype(f32)
    masks = mask_ref[...]
    conved = conv_of(ext, masks, small_ref, small_ref[4:5], rows).astype(bf16)
    conved_ref[...] = conved
    logit_a = jnp.dot(conved, wa_ref[...], preferred_element_type=f32) + small_ref[5:6]
    logit_x = jnp.dot(conved, wx_ref[...], preferred_element_type=f32) + small_ref[6:7]
    decay = jnp.exp(-decay_scale * sigmoid(logit_a) * small_ref[7:8])
    keep_ref[...] = decay * masks[:, 0:1]
    state_ref[...] = (
        jnp.sqrt(1.0 - decay * decay + push_shift) * sigmoid(logit_x) * conved.astype(f32)
    )

    def body(i, held):
        prod_in, state_in = held
        at = pl.ds(pl.multiple_of(i * 8, 8), 8)
        keep, push = tile_scan(keep_ref[at], state_ref[at], False)
        state = push + keep * state_in
        prod = keep * prod_in
        prod_ref[at] = prod
        state_ref[at] = state
        return prod[7:8], state[7:8]

    prod_out, state_out = lax.fori_loop(
        0, rows // 8, body, (carry[0:1], carry[1:2]), unroll=4
    )
    carry[0:1] = prod_out
    carry[1:2] = state_out
    ends_ref[0:1] = prod_out
    ends_ref[1:2] = state_out
    ends_ref[2:8] = jnp.zeros_like(ends_ref[2:8])


def forward_scan(order, rec_pre, halo, masks, small, wa, wx, chunk):
    rows, width = rec_pre.shape[0], rec_pre.shape[1] // 2
    tile = pl.BlockSpec((chunk, width), lambda i, order: (order[i], 0))
    whole = lambda a: pl.BlockSpec(a.shape, lambda i, order: (0, 0))
    full = jax.ShapeDtypeStruct((rows, width), f32)
    low = jax.ShapeDtypeStruct((rows, width), bf16)
    return pl.pallas_call(
        forward_kernel,
        out_shape=(
            low,
            low,
            full,
            full,
            full,
            jax.ShapeDtypeStruct((8, width), f32),
        ),
        grid_spec=pltpu.PrefetchScalarGridSpec(
            num_scalar_prefetch=1,
            grid=(rows // chunk,),
            in_specs=[
                pl.BlockSpec((chunk, 2 * width), lambda i, order: (order[i], 0)),
                whole(halo),
                pl.BlockSpec((chunk, masks.shape[1]), lambda i, order: (i, 0)),
                whole(small),
                whole(wa),
                whole(wx),
            ],
            out_specs=(tile,) * 5 + (pl.BlockSpec((8, width), lambda i, order: (0, 0)),),
            scratch_shapes=[pltpu.VMEM((chunk + 8, width), f32), pltpu.VMEM((8, width), f32)],
        ),
        compiler_params=pltpu.CompilerParams(vmem_limit_bytes=VMEM_LIMIT),
        cost_estimate=cost(15),
        name="forward_scan",
    )(order, rec_pre, halo, masks, small, wa, wx)


def adjoint_kernel(
    order_ref, d_ref, w_ref, pre_ref, keep_ref, d_mixed_ref, prod_ref, adj_ref, heads_ref,
    keep_next, carry
):
    rows = d_ref.shape[0]
    d_mixed = lax.dot_general(d_ref[...], w_ref[...], contract_last, preferred_element_type=f32)
    d_mixed_ref[...] = d_mixed
    step = pl.program_id(0)

    @pl.when(step == 0)
    def _():
        keep_next[pl.ds(rows, 8)] = jnp.ones_like(keep_next[pl.ds(rows, 8)])
        carry[0:1] = jnp.ones_like(carry[0:1])
        carry[1:2] = jnp.zeros_like(carry[1:2])

    @pl.when(step > 0)
    def _():
        keep_next[pl.ds(rows, 8)] = keep_next[pl.ds(0, 8)]

    keep_next[pl.ds(0, rows)] = keep_ref[...]
    prod_ref[...] = keep_next[pl.ds(1, rows)]
    adj_ref[...] = d_mixed * gelu_tanh(pre_ref[:, 0 : adj_ref.shape[1]])
    tiles = rows // 8

    def body(i, held):
        prod_in, adj_in = held
        at = pl.ds(pl.multiple_of((tiles - 1 - i) * 8, 8), 8)
        keep, push = tile_scan(prod_ref[at], adj_ref[at], True)
        adj = push + keep * adj_in
        prod = keep * prod_in
        prod_ref[at] = prod
        adj_ref[at] = adj
        return prod[0:1], adj[0:1]

    prod_out, adj_out = lax.fori_loop(
        0, tiles, body, (carry[0:1], carry[1:2]), unroll=4
    )
    carry[0:1] = prod_out
    carry[1:2] = adj_out
    heads_ref[0:1] = keep_ref[0:1] * prod_out
    heads_ref[1:2] = keep_ref[0:1] * adj_out
    heads_ref[2:8] = jnp.zeros_like(heads_ref[2:8])


def adjoint_scan(order, d_rec, w_out, rec_pre, keep, chunk):
    rows, width = keep.shape
    last = rows // chunk - 1
    tile = pl.BlockSpec((chunk, width), lambda i, order: (order[last - i], 0))
    full = jax.ShapeDtypeStruct((rows, width), f32)
    return pl.pallas_call(
        adjoint_kernel,
        out_shape=(full, full, full, jax.ShapeDtypeStruct((8, width), f32)),
        grid_spec=pltpu.PrefetchScalarGridSpec(
            num_scalar_prefetch=1,
            grid=(rows // chunk,),
            in_specs=[
                pl.BlockSpec((chunk, d_rec.shape[1]), lambda i, order: (order[last - i], 0)),
                pl.BlockSpec((width, d_rec.shape[1]), lambda i, order: (0, 0)),
                pl.BlockSpec((chunk, 2 * width), lambda i, order: (order[last - i], 0)),
                tile,
            ],
            out_specs=(tile, tile, tile, pl.BlockSpec((8, width), lambda i, order: (0, 0))),
            scratch_shapes=[pltpu.VMEM((chunk + 8, width), f32), pltpu.VMEM((8, width), f32)],
        ),
        compiler_params=pltpu.CompilerParams(vmem_limit_bytes=VMEM_LIMIT),
        cost_estimate=cost(12),
        name="adjoint_scan",
    )(order, d_rec, w_out, rec_pre, keep)


def backward_kernel(
    order_ref,
    d_mixed_ref,
    pre_ref,
    state_ref,
    prod_ref,
    state_before_ref,
    prod_before_ref,
    adj_ref,
    adj_prod_ref,
    branch_ref,
    branch_before_ref,
    halo_ref,
    conved_ref,
    mask_ref,
    small_ref,
    enter_ref,
    wa_ref,
    wx_ref,
    d_pre_ref,
    sums_ref,
    edge_ref,
    ga_ref,
    gx_ref,
    ext,
    state_ext,
    later,
):
    rows, width = d_mixed_ref.shape
    step = pl.program_id(0)
    steps = pl.num_programs(0)
    state_in = enter_ref[0:1]
    adj_in = enter_ref[1:2]

    @pl.when(step == 0)
    def _():
        sums_ref[...] = jnp.zeros_like(sums_ref)
        ga_ref[...] = jnp.zeros_like(ga_ref)
        gx_ref[...] = jnp.zeros_like(gx_ref)
        for k in range(TAIL):
            later[k, pl.ds(rows, 8)] = jnp.zeros((8, width), f32)

    @pl.when(step > 0)
    def _():
        for k in range(TAIL):
            later[k, pl.ds(rows, 8)] = later[k, pl.ds(0, 8)]

    first = step == steps - 1

    @pl.when(first)
    def _():
        ext[pl.ds(0, 8)] = halo_ref[...]
        state_ext[pl.ds(0, 8)] = jnp.broadcast_to(state_in, (8, width))

    @pl.when(jnp.logical_not(first))
    def _():
        ext[pl.ds(0, 8)] = branch_before_ref[...].astype(f32)[8:16]
        state_ext[pl.ds(0, 8)] = state_before_ref[...] + prod_before_ref[...] * state_in

    ext[pl.ds(8, rows)] = branch_ref[...].astype(f32)
    state = state_ref[...] + prod_ref[...] * state_in
    state_ext[pl.ds(8, rows)] = state
    _, slope = gelu_pair(pre_ref[:, 0:width])
    d_pre_ref[:, 0:width] = (d_mixed_ref[...] * state * slope).astype(bf16)
    adjoint = adj_ref[...] + adj_prod_ref[...] * adj_in
    state_prev = state_ext[pl.ds(7, rows)]
    masks = mask_ref[...]
    conved_low = conved_ref[...]
    conved = conved_low.astype(f32)
    rates = small_ref[7:8]
    gate_a = sigmoid(
        jnp.dot(conved_low, wa_ref[...], preferred_element_type=f32) + small_ref[5:6]
    )
    gate_x = sigmoid(
        jnp.dot(conved_low, wx_ref[...], preferred_element_type=f32) + small_ref[6:7]
    )
    decay = jnp.exp(-decay_scale * gate_a * rates)
    square = 1.0 - decay * decay + push_shift
    inverse = lax.rsqrt(square)
    root = square * inverse
    d_decay = adjoint * (state_prev * masks[:, 0:1] - gate_x * conved * decay * inverse)
    slope_a = -decay_scale * d_decay * decay * gate_a
    d_logit_a = (slope_a * rates * (1.0 - gate_a)).astype(bf16)
    through = adjoint * root * gate_x
    d_logit_x = (through * conved * (1.0 - gate_x)).astype(bf16)
    d_conved = (
        through
        + lax.dot_general(d_logit_a, wa_ref[...], contract_last, preferred_element_type=f32)
        + lax.dot_general(d_logit_x, wx_ref[...], contract_last, preferred_element_type=f32)
    )
    d_conved = d_conved.astype(bf16).astype(f32)
    ga_ref[...] += lax.dot_general(
        conved_low, d_logit_a, contract_first, preferred_element_type=f32
    )
    gx_ref[...] += lax.dot_general(
        conved_low, d_logit_x, contract_first, preferred_element_type=f32
    )

    def total(v):
        return jnp.sum(v, axis=0, keepdims=True)

    sums_ref[0:1] += total(d_conved * ext[pl.ds(8, rows)])
    for k in range(1, CONV):
        masked = d_conved * masks[:, k - 1 : k]
        later[k - 1, pl.ds(0, rows)] = masked
        sums_ref[k : k + 1] += total(masked * ext[pl.ds(8 - k, rows)])
    sums_ref[4:5] += total(d_conved)
    sums_ref[5:6] += total(d_logit_a.astype(f32))
    sums_ref[6:7] += total(d_logit_x.astype(f32))
    sums_ref[7:8] += total(slope_a)
    d_branch = small_ref[0:1] * d_conved
    for k in range(1, CONV):
        d_branch = d_branch + small_ref[k : k + 1] * later[k - 1, pl.ds(k, rows)]
    d_pre_ref[:, width : 2 * width] = d_branch.astype(bf16)

    @pl.when(first)
    def _():
        for back in range(1, CONV):
            value = jnp.zeros((1, width), f32)
            for k in range(back, CONV):
                value = value + small_ref[k : k + 1] * later[k - 1, pl.ds(k - back, 1)]
            edge_ref[8 - back : 9 - back] = value
        edge_ref[0 : 8 - TAIL] = jnp.zeros((8 - TAIL, width), f32)


def backward_scan(
    order, d_mixed, rec_pre, state, prod, adj, adj_prod, branch_in, halo, conved, masks, small,
    enter, wa, wx, chunk,
):
    rows, width = state.shape
    last = rows // chunk - 1
    tile = pl.BlockSpec((chunk, width), lambda i, order: (order[last - i], 0))

    def before(size):
        per = chunk // size
        return pl.BlockSpec(
            (size, width),
            lambda i, order: (order[jnp.maximum(last - i - 1, 0)] * per + per - 1, 0),
        )

    pinned = lambda shape: pl.BlockSpec(shape, lambda i, order: (0, 0))
    whole = lambda a: pinned(a.shape)
    return pl.pallas_call(
        backward_kernel,
        out_shape=(
            jax.ShapeDtypeStruct((rows, 2 * width), bf16),
            jax.ShapeDtypeStruct((8, width), f32),
            jax.ShapeDtypeStruct((8, width), f32),
            jax.ShapeDtypeStruct((width, width), f32),
            jax.ShapeDtypeStruct((width, width), f32),
        ),
        grid_spec=pltpu.PrefetchScalarGridSpec(
            num_scalar_prefetch=1,
            grid=(rows // chunk,),
            in_specs=[
                tile,
                pl.BlockSpec((chunk, 2 * width), lambda i, order: (order[last - i], 0)),
                tile,
                tile,
                before(8),
                before(8),
                tile,
                tile,
                tile,
                before(16),
                whole(halo),
                tile,
                pl.BlockSpec((chunk, masks.shape[1]), lambda i, order: (last - i, 0)),
                whole(small),
                whole(enter),
                whole(wa),
                whole(wx),
            ],
            out_specs=(
                pl.BlockSpec((chunk, 2 * width), lambda i, order: (order[last - i], 0)),
                pinned((8, width)),
                pinned((8, width)),
                pinned((width, width)),
                pinned((width, width)),
            ),
            scratch_shapes=[
                pltpu.VMEM((chunk + 8, width), f32),
                pltpu.VMEM((chunk + 8, width), f32),
                pltpu.VMEM((TAIL, chunk + 8, width), f32),
            ],
        ),
        compiler_params=pltpu.CompilerParams(vmem_limit_bytes=VMEM_LIMIT),
        cost_estimate=cost(21),
        name="backward_scan",
    )(
        order, d_mixed, rec_pre, state, prod, state, prod, adj, adj_prod, branch_in, branch_in,
        halo, conved, masks, small, enter, wa, wx,
    )


def gated_kernel(n_ref, mine_ref, theirs_ref, w_ref, down_ref, hidden_ref, d_ref):
    ff = down_ref.shape[0]
    tile = 256
    normed = n_ref[...]
    cot = lax.select(
        pl.program_id(0) < pl.num_programs(0) // 2, mine_ref[...], theirs_ref[...]
    )

    def body(j, none):
        at = pl.ds(pl.multiple_of(j * tile, tile), tile)
        up_at = pl.ds(pl.multiple_of(ff + j * tile, tile), tile)
        gate = jnp.dot(normed, w_ref[:, at], preferred_element_type=f32)
        up = jnp.dot(normed, w_ref[:, up_at], preferred_element_type=f32)
        d_hidden = lax.dot_general(cot, down_ref[at], contract_last, preferred_element_type=f32)
        act, slope = gelu_pair(gate)
        hidden_ref[:, at] = (act * up).astype(bf16)
        d_ref[:, at] = (d_hidden * up * slope).astype(bf16)
        d_ref[:, up_at] = (d_hidden * act).astype(bf16)
        return none

    lax.fori_loop(0, ff // tile, body, 0)


def gated_unit(normed, cot_mine, cot_theirs, w_mlp, w_down):
    rows, width = normed.shape
    ff = w_down.shape[0]
    steps = 4
    tile = rows // steps
    row = lambda size: pl.BlockSpec((tile, size), lambda i: (i, 0))
    once = lambda a: pl.BlockSpec(a.shape, lambda i: (0, 0), pipeline_mode=pl.Buffered(1))
    return pl.pallas_call(
        gated_kernel,
        grid=(steps,),
        out_shape=(
            jax.ShapeDtypeStruct((rows, ff), bf16),
            jax.ShapeDtypeStruct((rows, 2 * ff), bf16),
        ),
        in_specs=[
            row(width),
            pl.BlockSpec((tile, width), lambda i: (jnp.minimum(i, steps // 2 - 1), 0)),
            pl.BlockSpec((tile, width), lambda i: (jnp.maximum(i - steps // 2, 0), 0)),
            once(w_mlp),
            once(w_down),
        ],
        out_specs=(row(ff), row(2 * ff)),
        compiler_params=pltpu.CompilerParams(vmem_limit_bytes=VMEM_LIMIT),
        cost_estimate=pl.CostEstimate(
            flops=6 * rows * width * ff, bytes_accessed=40 * 2**20, transcendentals=rows * ff
        ),
        name="gated_unit",
    )(normed, cot_mine, cot_theirs, w_mlp, w_down)


def down_kernel(h_ref, w_ref, mine_ref, theirs_ref):
    width = w_ref.shape[1]
    tile = 1024
    hidden = h_ref[...]

    def into(ref):
        def body(j, none):
            at = pl.ds(pl.multiple_of(j * tile, tile), tile)
            ref[:, at] = jnp.dot(hidden, w_ref[:, at], preferred_element_type=f32).astype(bf16)
            return none

        lax.fori_loop(0, width // tile, body, 0)

    first = pl.program_id(0) < pl.num_programs(0) // 2
    pl.when(first)(lambda: into(mine_ref))
    pl.when(jnp.logical_not(first))(lambda: into(theirs_ref))


def down_rows(hidden, w_down):
    rows, ff = hidden.shape
    width = w_down.shape[1]
    steps = 4
    tile = rows // steps
    part = jax.ShapeDtypeStruct((rows // 2, width), bf16)
    return pl.pallas_call(
        down_kernel,
        grid=(steps,),
        out_shape=(part, part),
        in_specs=[
            pl.BlockSpec((tile, ff), lambda i: (i, 0)),
            pl.BlockSpec((ff, width), lambda i: (0, 0), pipeline_mode=pl.Buffered(1)),
        ],
        out_specs=(
            pl.BlockSpec((tile, width), lambda i: (jnp.minimum(i, steps // 2 - 1), 0)),
            pl.BlockSpec((tile, width), lambda i: (jnp.maximum(i - steps // 2, 0), 0)),
        ),
        compiler_params=pltpu.CompilerParams(vmem_limit_bytes=VMEM_LIMIT),
        cost_estimate=cost(0.1),
        name="down_rows",
    )(hidden, w_down)


def split_kernel(moves, a_ref, b_ref, o_ref):
    for source, block, at, start, size in moves:
        ref = (a_ref, b_ref)[source]
        o_ref[block, :, at : at + size] = ref[:, start : start + size]


def join_kernel(moves, x_ref, a_ref, b_ref, g_ref, oa_ref, ob_ref, og_ref):
    for source, block, at, start, size in moves:
        ref = (oa_ref, ob_ref)[source]
        ref[:, start : start + size] = x_ref[block, :, at : at + size].astype(f32)
    total = jnp.sum(a_ref[...].astype(f32) * oa_ref[...], axis=1, keepdims=True) + jnp.sum(
        b_ref[...].astype(f32) * ob_ref[...], axis=1, keepdims=True
    )
    wide = jnp.broadcast_to(total / g_ref[...], (total.shape[0], LANES))
    og_ref[...] = wide.T[0:1]


def split_blocks(a, b, moves):
    rows, width = a.shape
    return pl.pallas_call(
        functools.partial(split_kernel, moves),
        out_shape=jax.ShapeDtypeStruct((NF, rows, 2 * width // NF), a.dtype),
        compiler_params=pltpu.CompilerParams(vmem_limit_bytes=VMEM_LIMIT),
        cost_estimate=cost(4),
        name="split_blocks",
    )(a, b)


def join_blocks(x, a, b, gain, moves):
    rows, width = a.shape
    out = jax.ShapeDtypeStruct((rows, width), f32)
    return pl.pallas_call(
        functools.partial(join_kernel, moves),
        out_shape=(out, out, jax.ShapeDtypeStruct((1, rows), f32)),
        compiler_params=pltpu.CompilerParams(vmem_limit_bytes=VMEM_LIMIT),
        cost_estimate=cost(5),
        name="join_blocks",
    )(x, a, b, gain)


def pack_kernel(out_ref, ga_ref, gx_ref, sums_ref, o_ref, small):
    spread, _, chan_rows, total = o_ref.shape
    chans, width = out_ref.shape
    extra = total - width
    row = lax.broadcasted_iota(jnp.int32, (chans, chans), 0)
    col = lax.broadcasted_iota(jnp.int32, (chans, chans), 1)
    same = (row < BLK) == (col < BLK)
    at = lax.broadcasted_iota(jnp.int32, (chans, extra), 0)
    at = jnp.where(at < BLK, at, at - BLK)
    to = lax.broadcasted_iota(jnp.int32, (chans, extra), 1)

    def placed(ref, start):
        kept = jnp.where(same, ref[...], 0.0).astype(bf16)
        spot = jnp.where(to == at + start, 1.0, 0.0).astype(bf16)
        return jnp.dot(kept, spot, preferred_element_type=f32)

    rows = jnp.concatenate([sums_ref[...], jnp.zeros_like(sums_ref)]).astype(bf16)
    spot = jnp.where(
        lax.broadcasted_iota(jnp.int32, (16, extra), 0) + 2 * BLK
        == lax.broadcasted_iota(jnp.int32, (16, extra), 1),
        1.0,
        0.0,
    ).astype(bf16)
    small[...] = (
        placed(ga_ref, 0)
        + placed(gx_ref, BLK)
        + lax.dot_general(rows, spot, contract_first, preferred_element_type=f32)
    )
    for unit in range(2):
        for part in range(spread):
            here = pl.ds(unit * BLK + part * chan_rows, chan_rows)
            o_ref[part, unit, :, 0:width] = out_ref[here].astype(bf16)
            o_ref[part, unit, :, width:total] = small[here].astype(bf16)


def pack_sums(grad_out, grad_a, grad_x, sums, spread, chan_rows, total):
    chans, width = grad_out.shape
    return pl.pallas_call(
        pack_kernel,
        out_shape=jax.ShapeDtypeStruct((spread, 2, chan_rows, total), bf16),
        scratch_shapes=[pltpu.VMEM((chans, total - width), f32)],
        compiler_params=pltpu.CompilerParams(vmem_limit_bytes=VMEM_LIMIT),
        cost_estimate=cost(3),
        name="pack_sums",
    )(grad_out, grad_a, grad_x, sums)


def unpack_kernel(x_ref, out_ref, ga_ref, gx_ref, taps_ref, *row_refs):
    width = out_ref.shape[1]
    base = width + 2 * BLK
    out_ref[...] = x_ref[:, 0:width].astype(f32)
    ga_ref[...] = x_ref[:, width : width + BLK].astype(f32)
    gx_ref[...] = x_ref[:, width + BLK : base].astype(f32)
    last = base - base % LANES
    small = x_ref[:, last : last + LANES].astype(f32)
    taps_ref[...] = small[:, base - last : base - last + CONV]
    turned = small.T
    for i, ref in enumerate(row_refs):
        at = base - last + CONV + i
        ref[...] = turned[at : at + 1]


def unpack_sums(x, width):
    rows = x.shape[0]
    shape = lambda *dims: jax.ShapeDtypeStruct(dims, f32)
    return pl.pallas_call(
        unpack_kernel,
        out_shape=(shape(rows, width), shape(rows, BLK), shape(rows, BLK), shape(rows, CONV))
        + (shape(1, rows),) * 4,
        compiler_params=pltpu.CompilerParams(vmem_limit_bytes=VMEM_LIMIT),
        cost_estimate=cost(2),
        name="unpack_sums",
    )(x)


def pad_lanes(rows, width):
    have = rows.shape[-1]
    return jnp.pad(rows, ((0, 0), (0, width - have)))


def inverse_rms(rows):
    return lax.rsqrt(jnp.mean(rows * rows, axis=-1, keepdims=True) + norm_eps)


def norm_back(rows, scale, e):
    return scale * e - rows * (scale * scale * scale) * jnp.mean(e * rows, axis=-1, keepdims=True)


def on_device(
    tokens_in,
    segment_starts,
    cotangent,
    norm1_gain,
    rec_gate_weight,
    rec_in_weight,
    conv_weight,
    conv_bias,
    gate_a_weight,
    gate_a_bias,
    gate_x_weight,
    gate_x_bias,
    decay_rate,
    rec_out_weight,
    norm2_gain,
    mlp_gate_weight,
    mlp_up_weight,
    mlp_down_weight,
):
    count = lax.axis_size("z")
    z = lax.axis_index("z")
    spread = count // 2
    swap_axes = FEAT[len(FEAT) - (spread.bit_length() - 1) :]
    outer = NF // spread
    rows_tok, width = tokens_in.shape
    group_rows = NF * rows_tok
    chan_rows = conv_weight.shape[0]
    chans = chan_rows * count
    rows_w = rec_gate_weight.shape[0]
    ff_rows = mlp_down_weight.shape[0]
    ff = ff_rows * count
    chunk = 256

    chan_moves = [
        (
            source,
            k * spread + e,
            source * chans + zz * BLK,
            ((2 * e + zz) * outer + k) * BLK,
            BLK,
        )
        for source in range(2)
        for k in range(outer)
        for e in range(spread)
        for zz in range(2)
    ]
    ff_moves = [
        (source, f, source * ff + group * ff_rows, (group * NF + f) * ff_rows, ff_rows)
        for source in range(2)
        for f in range(NF)
        for group in range(count)
    ]
    place = [lax.axis_index(name) for name in FEAT]
    time = jnp.arange(NF, dtype=jnp.int32)
    bit = lambda value, here: jnp.where(value == here, 0, 1)
    order = (
        bit(time % 2, place[2]) * 4 + bit(time // 4, place[0]) * 2 + bit((time // 2) % 2, place[1])
    ).astype(jnp.int32)
    final = order[NF - 1] * rows_tok + rows_tok - 8

    pack = jnp.concatenate(
        [
            gate_a_weight,
            gate_x_weight,
            conv_weight,
            conv_bias[:, None],
            gate_a_bias[:, None],
            gate_x_bias[:, None],
            decay_rate[:, None],
        ],
        axis=1,
    )
    used = pack.shape[1]
    extra_width = -(-used // LANES) * LANES
    pack_width = width + extra_width
    pack = pad_lanes(pack, extra_width)

    extra = jnp.concatenate(
        [
            pad_lanes(segment_starts.astype(bf16)[None], 2 * chans),
            pad_lanes(norm1_gain[None], 2 * chans),
            pad_lanes(norm2_gain[None], 2 * chans),
            jnp.zeros((13, 2 * chans), bf16),
        ],
        axis=0,
    )
    rec_send = jnp.concatenate(
        [
            split_blocks(rec_gate_weight, rec_in_weight, chan_moves),
            jnp.broadcast_to(extra[None], (NF, 16, 2 * chans)),
        ],
        axis=1,
    )
    out_all = lax.all_gather(rec_out_weight, "z", axis=0, tiled=True)
    (rec_got,) = exchange([rec_send], FEAT, 3)
    starts = rec_got[:, rows_w, :rows_tok].reshape(group_rows).astype(f32)

    plane_gains = jnp.stack(
        [
            rec_got[:, rows_w + 1, :rows_w].reshape(NF * rows_w),
            rec_got[:, rows_w + 2, :rows_w].reshape(NF * rows_w),
        ]
    ).astype(f32)
    rec_mine = rec_got[:, :rows_w].reshape(NF * rows_w, 2 * chans)
    w_rec = lax.all_gather(rec_mine, "z", axis=0, tiled=True)
    mlp_send = split_blocks(mlp_gate_weight, mlp_up_weight, ff_moves)
    tok_group, mlp_got, gains, pack_all = gather_exchange(
        tokens_in, mlp_send, [jnp.pad(plane_gains, ((0, 6), (0, 0))), pack], count
    )
    tok_group, pack_all, out_all = hold(tok_group, pack_all, out_all)
    out_swap, pack_swap = exchange(
        [
            out_all.reshape(spread, 2, chan_rows, width),
            pack_all.reshape(spread, 2, chan_rows, extra_width),
        ],
        swap_axes,
        12,
    )
    gain_one = gains[:, 0].reshape(1, width)
    gain_two = gains[:, 1].reshape(1, width)

    tok = tokens_in.astype(f32)
    tok_group = tok_group.astype(f32)
    normed = (tok_group * inverse_rms(tok_group) * gain_one).astype(bf16)

    w_mlp = lax.all_gather(mlp_got.reshape(NF * rows_w, 2 * ff), "z", axis=0, tiled=True)
    w_down = lax.all_gather(mlp_down_weight, "z", axis=0, tiled=True)

    w_out = out_swap.transpose(1, 0, 2, 3).reshape(chans, width)
    mine = pack_swap.transpose(1, 0, 2, 3).reshape(chans, extra_width)
    small = mine[:, 2 * BLK : used].astype(f32).T

    unit = lax.broadcasted_iota(jnp.int32, (chans, chans), 0) // BLK
    same_block = unit == lax.broadcasted_iota(jnp.int32, (chans, chans), 1) // BLK

    def block_diag(w):
        return jnp.where(same_block, jnp.concatenate([w, w], axis=1), jnp.zeros((), w.dtype))

    wa = block_diag(mine[:, :BLK])
    wx = block_diag(mine[:, BLK : 2 * BLK])

    open_one = 1.0 - starts
    ahead = jnp.concatenate([jnp.ones((TAIL,), f32), open_one])
    open_two = open_one * ahead[TAIL - 1 : TAIL - 1 + group_rows]
    open_three = open_two * ahead[TAIL - 2 : TAIL - 2 + group_rows]
    masks = jnp.stack([open_one, open_two, open_three], axis=1)
    end = open_one[group_rows - 2 :]
    later_open = jnp.concatenate(
        [jnp.zeros((8 - TAIL,), f32), (end[0] * end[1])[None], end[1:], jnp.ones((1,), f32)]
    )[:, None]

    rec_pre = jnp.dot(normed, w_rec, preferred_element_type=f32)
    rec_pre, cot_own = hold(rec_pre, cotangent)
    cot_x, cot_y = gather_near(cot_own)
    edge_rows = lax.dynamic_slice_in_dim(rec_pre, final, 8, 0)[:, chans:].astype(bf16)
    halo = lax.ppermute(
        edge_rows.astype(f32) * later_open, "z", [(i, i + 1) for i in range(count - 1)]
    )
    branch_in, conved, keep, prod, state_local, ends = forward_scan(
        order, rec_pre, halo, masks, small, wa, wx, chunk
    )
    ends, cot_x, cot_y = hold(ends, cot_x, cot_y)
    cot_top, cot_low = gather_diagonal(cot_x, cot_y)
    (ends,) = gather_groups([ends], count, 2)
    state_in = jnp.zeros((1, chans), f32)
    for hop in range(count - 1):
        state_in = jnp.where(hop < z, ends[hop, 0:1] * state_in + ends[hop, 1:2], state_in)
    mixed = ((state_local + prod * state_in) * gelu_tanh(rec_pre[:, :chans])).astype(bf16)
    mixed_out = jnp.dot(mixed, w_out, preferred_element_type=f32).astype(bf16)
    mixed_out, cot_top, cot_low = hold(mixed_out, cot_top, cot_low)
    cot_chip = gather_chip(cotangent, cot_x, cot_y, cot_top, cot_low)
    cot_got = across(cot_chip, "c")
    middle = tok + scatter_feature(mixed_out)

    scale_two = inverse_rms(middle)
    normed_two = gather_feature((middle * scale_two * gain_two).astype(bf16))
    hidden, d_mlp = gated_unit(normed_two, cot_chip, cot_got, w_mlp, w_down)
    half_rows = group_rows // 2

    def back_rows(d, w):
        return lax.dot_general(d, w, contract_last, preferred_element_type=f32).astype(bf16)

    def over_rows(a, b_mine, b_theirs):
        return (
            lax.dot_general(a[:half_rows], b_mine, contract_first, preferred_element_type=f32)
            + lax.dot_general(a[half_rows:], b_theirs, contract_first, preferred_element_type=f32)
        ).astype(bf16)

    e_theirs = back_rows(d_mlp[half_rows:], w_mlp)
    d_mlp, e_theirs = hold(d_mlp, e_theirs)
    e_got = across(e_theirs, "c")
    e_mine = back_rows(d_mlp[:half_rows], w_mlp)
    e_keeps, e_x, e_y = scatter_near(e_mine, e_got)
    near_y, hidden = hold(e_keeps[0], hidden)
    e_keeps = (near_y,) + e_keeps[1:]
    down_part = over_rows(hidden, cot_chip, cot_got)
    down_part, hidden = hold(down_part, hidden)
    down_sum = lax.psum_scatter(down_part, "z", scatter_dimension=0, tiled=True)
    out_mine, out_theirs = down_rows(hidden, w_down)
    out_mine, out_theirs, e_x, e_y = hold(out_mine, out_theirs, e_x, e_y)
    e_two = gain_two * scatter_tail(e_keeps, e_x, e_y)
    d_middle = cotangent.astype(f32) + norm_back(middle, scale_two, e_two)
    d_own = d_middle.astype(bf16)
    d_x, d_y = gather_near(d_own)
    d_own, d_mlp, out_mine, out_theirs = hold(d_own, d_mlp, out_mine, out_theirs)
    out_got = across(out_theirs, "c")
    mlp_part = lax.dot_general(
        normed_two, d_mlp, contract_first, preferred_element_type=f32
    ).astype(bf16)
    out_x, out_y = scatter_sends(out_mine, out_got)
    d_x, d_y, mlp_part, out_x, out_y = hold(d_x, d_y, mlp_part, out_x, out_y)
    mlp_sum = lax.psum_scatter(mlp_part, "z", scatter_dimension=0, tiled=True)
    d_rec = gather_tail(d_own, d_x, d_y)
    d_rec, down_sum, out_x, out_y = hold(d_rec, down_sum, out_x, out_y)
    out_x, out_y = across(out_x, "x"), across(out_y, "y")

    d_mixed, adj_prod, adj_local, heads = adjoint_scan(
        order, d_rec, w_out, rec_pre, keep, chunk
    )
    from_later = [
        lax.ppermute(heads, "z", [(i + hop, i) for i in range(count - hop)])
        for hop in range(count - 1, 0, -1)
    ]
    *from_later, out_x, out_y = hold(*from_later, out_x, out_y)
    out_last = scatter_relay(out_mine, out_got, out_x, out_y)
    adj_in = jnp.zeros((1, chans), f32)
    for one in from_later:
        adj_in = one[0:1] * adj_in + one[1:2]
    enter = jnp.concatenate([state_in, adj_in, jnp.zeros((6, chans), f32)])
    d_rec_pre, sums, edge, grad_a, grad_x = backward_scan(
        order, d_mixed, rec_pre, state_local, prod, adj_local, adj_prod, branch_in, halo, conved,
        masks, small, enter, wa, wx, chunk,
    )
    after = lax.ppermute(edge, "z", [(i + 1, i) for i in range(count - 1)]) * later_open
    edge, mixed = hold(edge, mixed)
    grad_out = lax.dot_general(mixed, d_rec, contract_first, preferred_element_type=f32)
    after, grad_out = hold(after, grad_out)
    tail_sum = lax.dynamic_slice_in_dim(d_rec_pre, final, 8, 0).astype(f32) + jnp.pad(
        after, ((0, 0), (chans, 0))
    )
    d_rec_pre = lax.dynamic_update_slice_in_dim(d_rec_pre, tail_sum.astype(bf16), final, 0)
    rec_part = lax.dot_general(
        normed, d_rec_pre, contract_first, preferred_element_type=f32
    ).astype(bf16)
    rec_part, d_rec_pre, grad_a, grad_x, sums, *out_last = hold(
        rec_part, d_rec_pre, grad_a, grad_x, sums, *out_last
    )
    layer_out = (middle + scatter_sum(out_mine, out_got, out_x, out_y, *out_last)).astype(bf16)
    rec_sum = lax.psum_scatter(rec_part, "z", scatter_dimension=0, tiled=True)
    back_pack = pack_sums(grad_out, grad_a, grad_x, sums, spread, chan_rows, pack_width)
    (back_swap,) = exchange([back_pack], swap_axes, 5)
    back_swap = back_swap.reshape(count * chan_rows, pack_width)
    grad_down = down_sum.astype(f32)
    back_swap, d_rec_pre, layer_out, grad_down = hold(back_swap, d_rec_pre, layer_out, grad_down)
    mlp_sum, d_rec_pre = hold(mlp_sum, d_rec_pre)
    pack_sum = lax.psum_scatter(back_swap, "z", scatter_dimension=0, tiled=True)
    one_sum, mlp_back = scatter_dot(d_rec_pre, w_rec, mlp_sum.reshape(NF, rows_w, 2 * ff))
    one_sum, rec_sum = hold(one_sum, rec_sum)
    (rec_back,) = exchange([rec_sum.reshape(NF, rows_w, 2 * chans)], FEAT, 10)
    e_one = gain_one * one_sum
    grad_tokens = d_middle + norm_back(tok, inverse_rms(tok), e_one)
    grad_gate, grad_up, grad_gain_two = join_blocks(
        mlp_back, mlp_gate_weight, mlp_up_weight, norm2_gain.astype(f32)[:, None], ff_moves
    )
    grad_rec_gate, grad_rec_in, grad_gain_one = join_blocks(
        rec_back, rec_gate_weight, rec_in_weight, norm1_gain.astype(f32)[:, None], chan_moves
    )

    pack_sum, grad_gain_one, grad_gain_two, grad_tokens = hold(
        pack_sum, grad_gain_one, grad_gain_two, grad_tokens
    )
    grad_out, grad_a, grad_x, grad_taps, *grad_rows = unpack_sums(pack_sum, width)
    grad_offset, grad_a_bias, grad_x_bias, grad_rate = (r.reshape(chan_rows) for r in grad_rows)
    return (
        layer_out,
        grad_tokens,
        grad_gain_one.reshape(rows_w),
        grad_rec_gate,
        grad_rec_in,
        grad_taps,
        grad_offset,
        grad_a,
        grad_a_bias,
        grad_x,
        grad_x_bias,
        grad_rate,
        grad_out,
        grad_gain_two.reshape(rows_w),
        grad_gate,
        grad_up,
        grad_down,
    )


def solution(mesh):
    wide, narrow = mesh.shape["wide"], mesh.shape["narrow"]
    groups = wide * narrow // NF
    grid = Mesh(mesh.devices.reshape((groups,) + (2,) * len(FEAT)), ("z",) + FEAT)
    flat = P(("z",) + FEAT)
    wide_rows = P(("z",) + FEAT, None)
    one, two = flat, wide_rows
    return jax.shard_map(
        on_device,
        mesh=grid,
        in_specs=(
            two, one, two, one, two, two, two, one, two, one, two, one, one, two, one, two, two, two,
        ),
        out_specs=(
            two, two, one, two, two, two, one, two, one, two, one, one, two, one, two, two, two,
        ),
        check_vma=False,
    )
```
